32 devices in a mesh: rows: 2 (over x), gr: 4 (over z), gc: 4 (over y, core).
Axes of the slice: x: 2, y: 2, z: 4, core: 2. Of those that a mesh axis runs over, the one named last changes fastest.
Arguments:
- tokens: bfloat16 [32768, 768], P(('rows', 'gr', 'gc')), may hold values from -6 to 6
- boxes: int32 [4, 32768], P(None, ('rows', 'gr', 'gc')), may hold values from 0 to 1000
- page_ids: int32 [64, 512], P(('rows', 'gr', 'gc')), may hold values from 0 to 3, never falling along the last dimension, each value on 1 to 256 neighbouring positions
- seg_ids: int32 [64, 512], P(('rows', 'gr', 'gc')), may hold values from 0 to 63, never falling along the last dimension, each value on 1 to 24 neighbouring positions
- pair_mask: int32 [2, 2048, 2048], P('rows', 'gr', 'gc'), may hold values 0 or 1
- ln1_gain: float32 [768], replicated, may hold values from 0.5 to 1.5
- ln1_bias: float32 [768], replicated, may hold values from -3 to 3
- query_key_value_weight: bfloat16 [768, 2304], replicated, may hold values from -0.21875 to 0.21875
- attention_output_weight: bfloat16 [768, 768], replicated, may hold values from -0.625 to 0.625
- ln2_gain: float32 [768], replicated, may hold values from 0.5 to 1.5
- ln2_bias: float32 [768], replicated, may hold values from -3 to 3
- up_projection_weight: bfloat16 [768, 3072], replicated, may hold values from -0.21875 to 0.21875
- up_projection_bias: float32 [3072], replicated, may hold values from -3 to 3
- down_projection_weight: bfloat16 [3072, 768], replicated, may hold values from -0.15625 to 0.15625
- box_table: float32 [12, 128], replicated, may hold values from -3 to 3
- rel_left: bfloat16 [768, 768], replicated, may hold values from -0.21875 to 0.21875
- rel_right: bfloat16 [768, 768], replicated, may hold values from -0.21875 to 0.21875
- cot_out: bfloat16 [32768, 768], P(('rows', 'gr', 'gc')), may hold values from -6 to 6
- cot_logits: bfloat16 [2, 2048, 2048], P('rows', 'gr', 'gc'), may hold values from -6 to 6
Outputs:
- layer_out: bfloat16 [32768, 768], P(('rows', 'gr', 'gc'))
- pair_logits: float32 [2, 2048, 2048], P('rows', 'gr', 'gc')
- grad_tokens: float32 [32768, 768], P(('rows', 'gr', 'gc'))
- grad_ln1_gain: float32 [768], replicated
- grad_ln1_bias: float32 [768], replicated
- grad_qkv: float32 [1769472], P(('rows', 'gr', 'gc'))
- grad_out_weight: float32 [589824], P(('rows', 'gr', 'gc'))
- grad_ln2_gain: float32 [768], replicated
- grad_ln2_bias: float32 [768], replicated
- grad_up: float32 [2359296], P(('rows', 'gr', 'gc'))
- grad_up_bias: float32 [3072], replicated
- grad_down: float32 [2359296], P(('rows', 'gr', 'gc'))
- grad_box_table: float32 [12, 128], replicated
- grad_rel_left: float32 [589824], P(('rows', 'gr', 'gc'))
- grad_rel_right: float32 [589824], P(('rows', 'gr', 'gc'))
The draws below stay inside these ranges and needn't reach their ends.
Inputs may be any that keep to these rules, and one draw needn't show every extreme that they name: `page_ids`: within a packed row page ids never fall; each of the 4 pages has 1 to 256 tokens. `seg_ids`: within a packed row segment slots never fall; each of the 64 slots has 1 to 24 tokens.
All inputs are finite; a program needn't handle non-finite values. No bound on the sum of `pair_mask` on one device may be relied on, other than what follows from the above.
Results may differ from the reference program's by a relative error of at most 0.03.
Values may be sent and summed in bfloat16 or wider, within the bound.
A program may use at most 192 MiB of HBM per device.

```python
import math
from functools import partial
import jax
import jax.numpy as jnp
import numpy as np
from jax import lax

D = 768
H = 12
HD = 64
FF = 3072
DR = 768
NBUCK = 64
COORD = 1000
L = 512
SEG = 64
SEG_MOST = 24
PAGES = 4
PAGE_MOST = 256
SEQ_DEV = 2
SEQS = 64
TOKENS = 32768
SEG_DEV = 128
GROUP = 2048
N_ROWS = 2
N_GR = 4
N_GC = 4


def touch_ends(array, own_key, smallest, largest):
    place = [jax.random.randint(jax.random.fold_in(own_key, axis), (), 0, length) for axis, length in enumerate(array.shape)]
    main_axis = array.shape.index(max(array.shape))
    neighbour = place[:main_axis] + [(place[main_axis] + 1) % array.shape[main_axis]] + place[main_axis + 1:]
    return array.at[tuple(place)].set(smallest).at[tuple(neighbour)].set(largest)


def steps_of(stream_key, shape, shards, smallest, top_value):
    gain = 1.0
    for position, shards_of in shards:
        draws = jax.random.uniform(jax.random.fold_in(jax.random.fold_in(stream_key, 6), position), (shards_of,), jnp.float32, smallest / len(shards), top_value / len(shards))
        gain = gain * jnp.repeat(jnp.exp(draws), shape[position] // shards_of).reshape((-1,) + (1,) * (len(shape) - 1 - position))
    return gain


def split_up(count, total, reach, lean):
    loads = [(1 << 20) // math.isqrt(standing ** lean) + 1 for standing in range(2, count + 1)]
    spare, holding = total - reach - (count - 1), [1] * (count - 1)
    while spare > 0:
        movable = [i for i in range(count - 1) if holding[i] < reach]
        mass, left = sum([loads[i] for i in movable]), spare
        for i in movable:
            extra = min(reach - holding[i], max(1, left * loads[i] // mass), spare)
            holding[i] = holding[i] + extra
            spare = spare - extra
    return np.array([reach] + holding)


def ragged_sizes(key, count, total, limit, lean):
    if count == 2:
        one = jax.random.randint(key, (), max(1, total - limit), min(limit, total - 1) + 1)
        return jnp.stack([one, total - one])
    sizes = jnp.asarray(split_up(count, total, limit, lean), jnp.int32)
    twos = (count - 1) // 2
    donor, sink = sizes[1:1 + 2 * twos:2], sizes[2:2 + 2 * twos:2]
    slack = jnp.minimum(donor - 1, limit - sink)
    moved = jax.random.randint(jax.random.fold_in(key, 1), (twos,), 0, 1 << 20) % (slack + 1)
    sizes = sizes.at[1:1 + 2 * twos:2].set(donor - moved).at[2:2 + 2 * twos:2].set(sink + moved)
    return sizes[jax.random.permutation(jax.random.fold_in(key, 2), count)]


def noise(stream_key, extent, spread, reach, cuts=(), kind=jnp.bfloat16):
    drawn = jax.random.normal(stream_key, extent, jnp.float32) * spread
    if len(cuts) > 0:
        drawn = steps_of(stream_key, extent, cuts, -0.22, 0.18) * drawn
    return jnp.clip(drawn, min=-reach, max=reach).astype(kind)


def setup_inputs(seed: int = 0) -> dict:
    key_list = jax.random.split(jax.random.key(seed), 20)
    return {
        "tokens": noise(key_list[0], (TOKENS, D), 1.0, 6.0, ((0, 32),)),
        "boxes": touch_ends(jax.random.randint(key_list[1], (4, TOKENS), 0, COORD + 1), jax.random.fold_in(key_list[1], 1), 0, COORD).astype(jnp.int32),
        "page_ids": jax.vmap(lambda own: jnp.searchsorted(jnp.cumsum(ragged_sizes(own, PAGES, L, PAGE_MOST, 0)), jnp.arange(L), side="right"))(jax.random.split(key_list[2], SEQS)).reshape((SEQS, L)).astype(jnp.int32),
        "seg_ids": jax.vmap(lambda own: jnp.searchsorted(jnp.cumsum(ragged_sizes(own, SEG, L, SEG_MOST, 0)), jnp.arange(L), side="right"))(jax.random.split(key_list[3], SEQS)).reshape((SEQS, L)).astype(jnp.int32),
        "pair_mask": touch_ends((jax.random.randint(key_list[4], (N_ROWS, GROUP, GROUP), 0, 2) < 1).astype(jnp.int32), jax.random.fold_in(key_list[4], 1), 0, 1),
        "ln1_gain": jnp.clip(1.0 + 0.1 * jax.random.normal(key_list[5], (D,), jnp.float32), 0.5, 1.5),
        "ln1_bias": noise(key_list[6], (D,), 0.5, 3.0, (), jnp.float32),
        "query_key_value_weight": noise(key_list[7], (D, 3 * D), D ** -0.5, 0.21875),
        "attention_output_weight": noise(key_list[8], (D, D), (D // 8) ** -0.5, 0.625),
        "ln2_gain": jnp.clip(1.0 + 0.1 * jax.random.normal(key_list[9], (D,), jnp.float32), 0.5, 1.5),
        "ln2_bias": noise(key_list[10], (D,), 0.5, 3.0, (), jnp.float32),
        "up_projection_weight": noise(key_list[11], (D, FF), D ** -0.5, 0.21875),
        "up_projection_bias": noise(key_list[12], (FF,), 0.5, 3.0, (), jnp.float32),
        "down_projection_weight": noise(key_list[13], (FF, D), (FF // 2) ** -0.5, 0.15625),
        "box_table": noise(key_list[14], (H, 2 * NBUCK), 0.5, 3.0, (), jnp.float32),
        "rel_left": noise(key_list[15], (D, DR), D ** -0.5, 0.21875),
        "rel_right": noise(key_list[16], (D, DR), D ** -0.5, 0.21875),
        "cot_out": noise(key_list[17], (TOKENS, D), 1.0, 6.0, ((0, 32),)),
        "cot_logits": noise(key_list[18], (N_ROWS, GROUP, GROUP), 1.0, 6.0, ((0, 2), (1, 4), (2, 4))),
    }


FULL_PRECISION = lax.Precision.HIGHEST
EPSILON = 1e-05

@jax.custom_vjp
def low(v):
    return lax.optimization_barrier(v.astype(jnp.bfloat16)).astype(jnp.float32)

@jax.custom_vjp
def low_back(v):
    return v

def low_keep(v):
    return (low(v), None)

def low_pass(kept, grad):
    return (grad,)

def back_keep(v):
    return (v, None)

def back_low(kept, grad):
    return (low(grad),)
low.defvjp(low_keep, low_pass)
low_back.defvjp(back_keep, back_low)

def layer_norm(values_in, norm_gain, norm_bias):
    average = lax.optimization_barrier(jnp.mean(values_in, axis=-1, keepdims=True))
    centred = values_in - average
    variance = lax.optimization_barrier(jnp.mean(centred * centred, axis=-1, keepdims=True))
    return centred * lax.rsqrt(variance + EPSILON) * norm_gain + norm_bias

def seq_layer(params, block_item):
    layer_inputs, box_rows, page_rows = block_item
    ln1_gain, ln1_bias, query_key_value_weight, attention_output_weight, ln2_gain, ln2_bias, up_projection_weight, up_projection_bias, down_projection_weight, box_table = params
    seq_count = layer_inputs.shape[0]
    first_norm_output = low(layer_norm(layer_inputs, ln1_gain, ln1_bias))
    projected_rows = low(low_back(jnp.einsum('czx,xp->czp', first_norm_output, query_key_value_weight, precision=FULL_PRECISION)))
    queries = projected_rows[..., :D].reshape(seq_count, L, H, HD)
    key_rows = projected_rows[..., D:2 * D].reshape(seq_count, L, H, HD)
    value_rows = projected_rows[..., 2 * D:].reshape(seq_count, L, H, HD)
    products = low_back(jnp.einsum('sihc,sjhc->shij', queries, key_rows, precision=FULL_PRECISION))
    centre_x = (box_rows[:, 0] + box_rows[:, 2]) // 2
    centre_y = (box_rows[:, 1] + box_rows[:, 3]) // 2
    bucket_x = (centre_x[:, None, :] - centre_x[:, :, None] + COORD) * NBUCK // (2 * COORD + 1)
    bucket_y = (centre_y[:, None, :] - centre_y[:, :, None] + COORD) * NBUCK // (2 * COORD + 1) + NBUCK
    box_bias = jnp.moveaxis(box_table[:, bucket_x] + box_table[:, bucket_y], 0, 1)
    same_page = (page_rows[:, :, None] == page_rows[:, None, :])[:, None]
    scores = jnp.where(same_page, products * (1.0 / math.sqrt(HD)) + box_bias, -1e+30)
    softmax_out = low(jax.nn.softmax(scores, axis=-1))
    attended_context = low(low_back(jnp.einsum('shij,sjhc->sihc', softmax_out, value_rows, precision=FULL_PRECISION)))
    attended_context = attended_context.reshape(seq_count, L, D)
    residual_stream = layer_inputs + low_back(jnp.einsum('czx,xp->czp', attended_context, attention_output_weight, precision=FULL_PRECISION))
    second_norm_output = low(layer_norm(residual_stream, ln2_gain, ln2_bias))
    hidden_input_rows = low_back(jnp.einsum('pnw,wx->pnx', second_norm_output, up_projection_weight, precision=FULL_PRECISION) + up_projection_bias)
    activated_hidden = low(jax.nn.gelu(hidden_input_rows, approximate=False))
    return residual_stream + low_back(jnp.einsum('vxz,zq->vxq', activated_hidden, down_projection_weight, precision=FULL_PRECISION))

def forward(boxes, page_ids, seg_ids, pair_mask, tokens, ln1_gain, ln1_bias, query_key_value_weight, attention_output_weight, ln2_gain, ln2_bias, up_projection_weight, up_projection_bias, down_projection_weight, box_table, rel_left, rel_right):
    device_count = N_ROWS * N_GR * N_GC
    params = (ln1_gain, ln1_bias, query_key_value_weight, attention_output_weight, ln2_gain, ln2_bias, up_projection_weight, up_projection_bias, down_projection_weight, box_table)
    layer_inputs = tokens.reshape(device_count, SEQ_DEV, L, D)
    box_rows = jnp.transpose(boxes.reshape(4, device_count, SEQ_DEV, L), (1, 2, 0, 3))
    page_rows = page_ids.reshape(device_count, SEQ_DEV, L)
    layer_full = lax.map(jax.checkpoint(partial(seq_layer, params)), (layer_inputs, box_rows, page_rows))
    layer_out = low(layer_full)
    seg_rows = seg_ids.reshape(device_count, SEQ_DEV, L)
    segment_members = (seg_rows[..., None, :] == jnp.arange(SEG, dtype=jnp.int32)[:, None]).astype(jnp.float32)
    counts = lax.optimization_barrier(jnp.sum(segment_members, axis=-1))
    pooled = jnp.einsum('nsgl,nsld->nsgd', segment_members, layer_out, precision=FULL_PRECISION) / counts[..., None]
    embedded = low(pooled.reshape(N_ROWS, GROUP, D))
    left_seg = low(low_back(jnp.einsum('ngd,de->nge', embedded, rel_left, precision=FULL_PRECISION)))
    right_seg = low(low_back(jnp.einsum('ngd,de->nge', embedded, rel_right, precision=FULL_PRECISION)))
    col_side = jnp.transpose(right_seg.reshape(N_ROWS, N_GR, N_GC, SEG_DEV, DR), (0, 2, 1, 3, 4)).reshape(N_ROWS, GROUP, DR)
    pair_raw = low_back(jnp.einsum('nae,nbe->nab', left_seg, col_side, precision=FULL_PRECISION))
    pair_logits = pair_mask.astype(jnp.float32) * pair_raw * (1.0 / math.sqrt(DR))
    return (layer_out.reshape(TOKENS, D), pair_logits)

def reference(tokens, boxes, page_ids, seg_ids, pair_mask, ln1_gain, ln1_bias, query_key_value_weight, attention_output_weight, ln2_gain, ln2_bias, up_projection_weight, up_projection_bias, down_projection_weight, box_table, rel_left, rel_right, cot_out, cot_logits):
    floats = (tokens.astype(jnp.float32), ln1_gain, ln1_bias, query_key_value_weight.astype(jnp.float32), attention_output_weight.astype(jnp.float32), ln2_gain, ln2_bias, up_projection_weight.astype(jnp.float32), up_projection_bias, down_projection_weight.astype(jnp.float32), box_table, rel_left.astype(jnp.float32), rel_right.astype(jnp.float32))
    forward_fn = partial(forward, boxes, page_ids, seg_ids, pair_mask)
    outputs, pullback = jax.vjp(forward_fn, *floats)
    gradients = pullback((cot_out.astype(jnp.float32), cot_logits.astype(jnp.float32)))
    layer_out, pair_logits = outputs
    return (layer_out.astype(jnp.bfloat16), pair_logits, gradients[0], gradients[1], gradients[2], gradients[3].reshape(-1), gradients[4].reshape(-1), gradients[5], gradients[6], gradients[7].reshape(-1), gradients[8], gradients[9].reshape(-1), gradients[10], gradients[11].reshape(-1), gradients[12].reshape(-1))
```

```python
import functools
import math

import jax
import jax.numpy as jnp
from jax import lax
from jax.experimental import pallas as pl
from jax.experimental.pallas import tpu as pltpu
from jax.sharding import PartitionSpec as P

COORD=1000
SPAN=2*COORD+1
LOG2E=1.4426950408889634
BARRED=-2.0**99
BF=jnp.bfloat16
F32=jnp.float32
NT=(((1,),(1,)),((),()))
NN=(((1,),(0,)),((),()))
def dot(a,b,dims=NN):
    return lax.dot_general(a,b,dims,preferred_element_type=F32)

def whole_and_rest(scaled):
    whole=jnp.floor((scaled+0.5)*(1.0/SPAN))
    return whole, scaled-SPAN*whole

def key_side(low, high, half):
    c=((low+high)>>1).astype(F32)
    return whole_and_rest(c*half)
def query_side(low, high, half):
    c=((low+high)>>1).astype(F32)
    return whole_and_rest((COORD-c)*half)

def hi_lo(v):
    hi=v.astype(BF)
    return hi, (v-hi.astype(F32)).astype(BF)

def fwd_kernel(q_ref,k_ref,v_ref,boxr_ref,boxc_ref,pager_ref,pagec_ref,tab_ref,
               ctx_ref,e_ref,linv_ref,
               ohb_ref,oha_ref,kg_ref,rxy_ref,pg_ref,cx_ref,cy_ref,*,rows):
    length=q_ref.shape[0]
    half=tab_ref.shape[1]//2
    quarter=half//2
    hp=pl.program_id(1)
    lane=lax.broadcasted_iota(jnp.int32,(1,128),1)
    low=lane<64
    @pl.when(hp==0)
    def _():
        bc=boxc_ref[...]
        ax,fax=key_side(bc[:,0:1],bc[:,2:3],half)
        ay,fay=key_side(bc[:,1:2],bc[:,3:4],half)
        bx,fbx=query_side(bc[:,0:1],bc[:,2:3],half)
        by,fby=query_side(bc[:,1:2],bc[:,3:4],half)
        spot=(lane%quarter).astype(F32)
        is_x=(lane%half)<quarter
        oha=jnp.where(jnp.where(is_x,ax,ay)==spot,1.0,0.0)
        ohb=jnp.where(jnp.where(is_x,bx,by)==spot,1.0,0.0)
        ohb_ref[...]=jnp.where(low,ohb,0.0).astype(BF)
        oha_ref[...]=oha.astype(BF)
        page=pagec_ref[...]
        mine=(lane%64)==page
        barred=jnp.where((lane%64)<4,jnp.where(mine,0.0,BARRED),0.0)
        kg_ref[0]=jnp.where(low,oha,barred).astype(BF)
        kg_ref[1]=jnp.where(low,barred,oha).astype(BF)
        pg_ref[...]=jnp.where(mine,1.0,0.0).astype(BF)
        ohx=jnp.where(ax==spot,1.0,0.0)
        ohy=jnp.where(ay==spot,1.0,0.0)
        rxy_ref[pl.ds(0,length),:]=jnp.where(low,ohx,0.0).astype(BF)
        rxy_ref[pl.ds(length,length),:]=jnp.where(low,0.0,ohy).astype(BF)
        br=boxr_ref[...]
        _,gax=key_side(br[0:1],br[2:3],half)
        _,gay=key_side(br[1:2],br[3:4],half)
        cx_ref[...]=jnp.where(gax+fbx>=SPAN,1.0,0.0)
        cy_ref[...]=jnp.where(gay+fby>=SPAN,1.0,0.0)
    k=k_ref[...]
    v=v_ref[...]
    oha=oha_ref[...]
    b_row=lax.broadcasted_iota(jnp.int32,(half,128),0)
    l_col=lax.broadcasted_iota(jnp.int32,(half,128),1)
    row_x=b_row<quarter
    index=jnp.where(row_x,b_row,b_row-quarter+half)+l_col%quarter
    same_axis=row_x==((l_col%half)<quarter)
    d_axis=row_x==(l_col<half)
    heads=[]
    for a in range(2):
        t=jnp.broadcast_to(tab_ref[pl.ds(2*hp+a,1),:],(half,128))
        base=jnp.take_along_axis(t,index,axis=1,mode="promise_in_bounds")
        nxt=jnp.take_along_axis(t,index+1,axis=1,mode="promise_in_bounds")
        hi,lo=hi_lo(base)
        dhi,dlo=hi_lo(nxt-base)
        z=jnp.zeros_like(hi)
        is_hi=(l_col<64)==(a==1)
        g0=jnp.where(same_axis,jnp.where(is_hi,hi.astype(F32),lo.astype(F32)),0.0).astype(BF)
        g1=jnp.where(d_axis,jnp.where((l_col%half)<quarter,dhi.astype(F32),dlo.astype(F32)),0.0).astype(BF)
        hk=jnp.concatenate([g0,g1],axis=1)
        left=dot(ohb_ref[:,0:half],hk).astype(BF)
        if a==0:
            rhs=jnp.concatenate([jnp.where(low,k,oha),kg_ref[0]],axis=1)
            vv=jnp.where(low,v,jnp.ones_like(v))
        else:
            rhs=jnp.concatenate([jnp.where(low,oha,k),kg_ref[1]],axis=1)
            vv=jnp.where(low,jnp.ones_like(v),v)
        heads.append((left,rhs,vv))
    for c in range(length//rows):
        sl=pl.ds(c*rows,rows)
        q=q_ref[sl,:]*jnp.asarray(0.125,BF)
        pg=pg_ref[sl,:]
        outs=[]
        for a in range(2):
            left,rhs,vv=heads[a]
            lc=left[c*rows:(c+1)*rows]
            g0=lc[:,:128]
            if a==0:
                lhs=jnp.concatenate([jnp.where(low,q,g0),jnp.where(low,g0,pg)],axis=1)
            else:
                lhs=jnp.concatenate([jnp.where(low,g0,q),jnp.where(low,pg,g0)],axis=1)
            s=dot(lhs,rhs,NT)
            dxy=dot(lc[:,128:],rxy_ref[...],NT)
            s=s+cx_ref[sl,:]*dxy[:,:length]+cy_ref[sl,:]*dxy[:,length:]
            m=jnp.max(s,axis=1,keepdims=True)
            e=jnp.exp2((s-m)*LOG2E).astype(BF)
            e_ref[a,sl,:]=e
            outs.append(dot(e,vv))
        ctx=jnp.where(low,outs[0],outs[1])
        tot=jnp.where(low,pltpu.roll(outs[0],64,1),pltpu.roll(outs[1],64,1))
        linv=1.0/tot
        linv_ref[sl,:]=linv
        ctx_ref[sl,:]=(ctx*linv).astype(BF)

def attend_forward(qkv,boxes_r,boxes_c,page_r,page_c,table,rows=256):
    tokens,width=qkv.shape
    feats=width//3
    seqs,_,length=page_r.shape
    heads=table.shape[0]
    pairs=heads//2
    return pl.pallas_call(
        functools.partial(fwd_kernel,rows=rows),
        grid=(seqs,pairs),
        in_specs=[
            pl.BlockSpec((length,128),lambda s,h:(s,h)),
            pl.BlockSpec((length,128),lambda s,h:(s,pairs+h)),
            pl.BlockSpec((length,128),lambda s,h:(s,2*pairs+h)),
            pl.BlockSpec((4,length),lambda s,h:(0,s)),
            pl.BlockSpec((length,4),lambda s,h:(s,0)),
            pl.BlockSpec((None,1,length),lambda s,h:(s,0,0)),
            pl.BlockSpec((length,1),lambda s,h:(s,0)),
            pl.BlockSpec(table.shape,lambda s,h:(0,0)),
        ],
        out_specs=[
            pl.BlockSpec((length,128),lambda s,h:(s,h)),
            pl.BlockSpec((2,None,length,length),lambda s,h:(h,s,0,0)),
            pl.BlockSpec((length,128),lambda s,h:(s,h)),
        ],
        out_shape=[jax.ShapeDtypeStruct((tokens,feats),BF),
                   jax.ShapeDtypeStruct((heads,seqs,length,length),BF),
                   jax.ShapeDtypeStruct((tokens,feats),F32)],
        scratch_shapes=[pltpu.VMEM((length,128),BF),pltpu.VMEM((length,128),BF),
                        pltpu.VMEM((2,length,128),BF),pltpu.VMEM((2*length,128),BF),
                        pltpu.VMEM((length,128),BF),
                        pltpu.VMEM((length,length),F32),pltpu.VMEM((length,length),F32)],
        name="attend_forward",
    )(qkv,qkv,qkv,boxes_r,boxes_c,page_r,page_c,table)

def bwd_kernel(q_ref,k_ref,v_ref,e_ref,linv_ref,ctx_ref,gctx_ref,boxr_ref,boxc_ref,
               gq_ref,gk_ref,gv_ref,hist_ref,
               oha_ref,ohbt_ref,cx_ref,cy_ref,g_ref,gx_ref,gy_ref,lt_ref,gt_ref,*,rows):
    length=q_ref.shape[0]
    half=64
    quarter=half//2
    s_id=pl.program_id(0)
    hp=pl.program_id(1)
    lane=lax.broadcasted_iota(jnp.int32,(1,128),1)
    low=lane<64
    @pl.when(hp==0)
    def _():
        bc=boxc_ref[...]
        ax,_=key_side(bc[:,0:1],bc[:,2:3],half)
        ay,_=key_side(bc[:,1:2],bc[:,3:4],half)
        _,fbx=query_side(bc[:,0:1],bc[:,2:3],half)
        _,fby=query_side(bc[:,1:2],bc[:,3:4],half)
        spot=(lane%quarter).astype(F32)
        is_x=(lane%half)<quarter
        oha_ref[...]=jnp.where(jnp.where(is_x,ax,ay)==spot,jnp.where(low,1.0,0.0),0.0).astype(BF)
        br=boxr_ref[...]
        _,gax=key_side(br[0:1],br[2:3],half)
        _,gay=key_side(br[1:2],br[3:4],half)
        rbx,_=query_side(br[0:1],br[2:3],half)
        rby,_=query_side(br[1:2],br[3:4],half)
        row=lax.broadcasted_iota(jnp.int32,(half,length),0)
        rspot=(row%quarter).astype(F32)
        ohbt_ref[...]=jnp.where(jnp.where(row<quarter,rbx,rby)==rspot,1.0,0.0).astype(BF)
        cx_ref[...]=jnp.where(gax+fbx>=SPAN,1.0,0.0).astype(BF)
        cy_ref[...]=jnp.where(gay+fby>=SPAN,1.0,0.0).astype(BF)
    k=k_ref[...]
    v=v_ref[...]
    lt_ref[...]=q_ref[...].astype(F32).T.astype(BF)
    gc=gctx_ref[...].astype(F32)*linv_ref[...]
    gcb=gc.astype(BF)
    gt_ref[...]=gcb.astype(F32).T.astype(BF)
    prod=gc*ctx_ref[...].astype(F32)
    ohbt=ohbt_ref[...]
    kts=[]
    vts=[]
    for a in range(2):
        mine=low if a==0 else jnp.logical_not(low)
        other=64-64*a
        D=jnp.sum(jnp.where(mine,prod,0.0),axis=1,keepdims=True)
        dhi=D.astype(BF).astype(F32)
        dlo=D-dhi
        lhs=jnp.where(mine,gcb.astype(F32),jnp.where(lane==other,dhi,jnp.where(lane==other+1,dlo,0.0))).astype(BF)
        rhs=jnp.where(mine,v,jnp.where((lane==other)|(lane==other+1),-1.0,0.0).astype(BF))
        for c in range(length//rows):
            sl=slice(c*rows,(c+1)*rows)
            gp=dot(lhs[sl],rhs,NT)
            g=(gp*e_ref[a,sl,:].astype(F32)).astype(BF)
            g_ref[a,sl,:]=g
            gx_ref[a,sl,:]=g*cx_ref[sl,:]
            gy_ref[a,sl,:]=g*cy_ref[sl,:]
        left=jnp.concatenate([lt_ref[64*a:64*a+64,:],ohbt],axis=0)
        r0=dot(left,g_ref[a])
        rx=dot(ohbt[:quarter],gx_ref[a])
        ry=dot(ohbt[quarter:],gy_ref[a])
        vts.append(dot(gt_ref[64*a:64*a+64,:],e_ref[a]))
        kts.append(r0[:64])
        w=jnp.concatenate([r0[64:],rx,ry],axis=0)
        whi,wlo=hi_lo(w)
        red=dot(jnp.concatenate([whi,wlo],axis=0),oha_ref[...])
        red=red[:128]+red[128:]
        hist_ref[a]=red
    zero=jnp.zeros_like(k)
    gq=dot(g_ref[0],jnp.where(low,k,zero))+dot(g_ref[1],jnp.where(low,zero,k))
    gq_ref[...]=(gq*0.125).astype(BF)
    gk_ref[...]=(jnp.concatenate(kts,axis=0)*0.125).T.astype(BF)
    gv_ref[...]=jnp.concatenate(vts,axis=0).T.astype(BF)

def attend_backward(qkv,e,linv,ctx,gctx,boxes_r,boxes_c,rows=256):
    tokens,width=qkv.shape
    feats=width//3
    heads,seqs,length,_=e.shape
    pairs=heads//2
    pair=pl.BlockSpec((length,128),lambda s,h:(s,h))
    gq,gk,gv,hist=pl.pallas_call(
        functools.partial(bwd_kernel,rows=rows),
        grid=(seqs,pairs),
        in_specs=[
            pair,
            pl.BlockSpec((length,128),lambda s,h:(s,pairs+h)),
            pl.BlockSpec((length,128),lambda s,h:(s,2*pairs+h)),
            pl.BlockSpec((2,None,length,length),lambda s,h:(h,s,0,0)),
            pair,pair,pair,
            pl.BlockSpec((4,length),lambda s,h:(0,s)),
            pl.BlockSpec((length,4),lambda s,h:(s,0)),
        ],
        out_specs=[pair,pair,pair,pl.BlockSpec((None,2,128,128),lambda s,h:(s,h,0,0))],
        out_shape=[jax.ShapeDtypeStruct((tokens,feats),BF)]*3+[jax.ShapeDtypeStruct((seqs,heads,128,128),F32)],
        scratch_shapes=[pltpu.VMEM((length,128),BF),pltpu.VMEM((64,length),BF),
                        pltpu.VMEM((length,length),BF),pltpu.VMEM((length,length),BF),
                        pltpu.VMEM((2,length,length),BF),pltpu.VMEM((2,length,length),BF),pltpu.VMEM((2,length,length),BF),
                        pltpu.VMEM((128,length),BF),pltpu.VMEM((128,length),BF)],
        name="attend_backward",
    )(qkv,qkv,qkv,e,linv,ctx,gctx,boxes_r,boxes_c)
    return gq,gk,gv,table_gradient(hist)

def table_gradient(hist):
    seqs,heads=hist.shape[:2]
    w=jnp.sum(hist,axis=0)
    quarter=32
    w=w.reshape(heads,2,2,quarter,4,quarter)[:, :, :, :, :2]
    w=jnp.stack([w[:,:,0,:,0],w[:,:,1,:,1]],axis=2)
    plain=w[:,0]-w[:,1]
    carry=w[:,1]
    both=jnp.stack([plain,carry],axis=2).reshape(heads,2,2*quarter*quarter)
    total=lax.iota(jnp.int32,quarter)[:,None]+lax.iota(jnp.int32,quarter)[None,:]
    idx=jnp.stack([total,total+1],0).reshape(-1)
    onehot=(idx[:,None]==lax.iota(jnp.int32,64)[None,:]).astype(F32)
    return jnp.einsum("hak,ke->hae",both,onehot,precision=lax.Precision.HIGHEST).reshape(heads,128)


EPSILON = 1e-05


def norm_stats(rows):
    average = jnp.mean(rows, axis=-1, keepdims=True)
    centred = rows - average
    variance = jnp.mean(centred * centred, axis=-1, keepdims=True)
    return average, lax.rsqrt(variance + EPSILON)


def norm_back(g_out, rows, average, inverse, gain):
    z = (rows - average) * inverse
    g_z = g_out * gain
    grad_in = inverse * (
        g_z
        - jnp.mean(g_z, axis=-1, keepdims=True)
        - z * jnp.mean(g_z * z, axis=-1, keepdims=True)
    )
    return grad_in, jnp.sum(g_out * z, axis=0), jnp.sum(g_out, axis=0)


def gelu_pair(u):
    bell = jnp.exp(u * u * -0.5)
    t = 1.0 / (1.0 + (0.3275911 * math.sqrt(0.5)) * jnp.abs(u))
    series = t * (
        0.254829592
        + t * (-0.284496736 + t * (1.421413741 + t * (-1.453152027 + t * 1.061405429)))
    )
    tail = 0.5 * series * bell
    below = jnp.where(u < 0.0, tail, 1.0 - tail)
    return u * below, below + u * bell * (1.0 / math.sqrt(2.0 * math.pi))


AXES = ("rows", "gr", "gc")


def shares(partial):
    part = lax.psum_scatter(partial.astype(BF), AXES, scatter_dimension=0, tiled=True)
    return part.astype(F32).reshape(-1)


def body(
    tokens, boxes, page_ids, seg_ids, pair_mask, ln1_gain, ln1_bias, query_key_value_weight,
    attention_output_weight, ln2_gain, ln2_bias, up_projection_weight, up_projection_bias,
    down_projection_weight, box_table, rel_left, rel_right, cot_out, cot_logits,
):
    sequences, length = page_ids.shape
    count = sequences * length
    features = tokens.shape[1]
    x = tokens.astype(F32)
    average1, inverse1 = norm_stats(x)
    h1 = ((x - average1) * inverse1 * ln1_gain + ln1_bias).astype(BF)
    qkv = dot(h1, query_key_value_weight).astype(BF)
    boxes_c = boxes.T
    ctx, e, linv = attend_forward(
        qkv, boxes, boxes_c, page_ids[:, None, :], page_ids.reshape(-1, 1), box_table
    )
    r1 = x + dot(ctx, attention_output_weight)
    average2, inverse2 = norm_stats(r1)
    h2 = ((r1 - average2) * inverse2 * ln2_gain + ln2_bias).astype(BF)
    act, slope = gelu_pair(dot(h2, up_projection_weight) + up_projection_bias)
    act = act.astype(BF)
    slope = slope.astype(BF)
    layer_out = (r1 + dot(act, down_projection_weight)).astype(BF)

    slots = 64
    member = seg_ids[:, :, None] == lax.iota(jnp.int32, slots)[None, None, :]
    members = member.astype(BF)
    counts = jnp.sum(member.astype(F32), axis=1)
    pooled = jnp.einsum(
        "stg,std->sgd", members, layer_out.reshape(sequences, length, features),
        preferred_element_type=F32,
    ) / counts[:, :, None]
    embedded = pooled.reshape(sequences * slots, features).astype(BF)
    left = dot(embedded, rel_left).astype(BF)
    right = dot(embedded, rel_right).astype(BF)
    row_side = lax.all_gather(left, "gc", axis=0, tiled=True)
    col_side = lax.all_gather(right, "gr", axis=0, tiled=True)
    pair_scale = 1.0 / math.sqrt(rel_left.shape[1])
    keep = pair_mask[0].astype(F32)
    pair_logits = keep * dot(row_side, col_side, NT) * pair_scale
    g_raw = (cot_logits[0].astype(F32) * pair_scale * keep).astype(BF)
    g_left = lax.psum_scatter(
        dot(g_raw, col_side).astype(BF), "gc", scatter_dimension=0, tiled=True
    )
    g_right = lax.psum_scatter(
        dot(g_raw, row_side, (((0,), (0,)), ((), ()))).astype(BF), "gr",
        scatter_dimension=0, tiled=True,
    )
    TN = (((0,), (0,)), ((), ()))
    grad_rel_left = dot(embedded, g_left, TN)
    grad_rel_right = dot(embedded, g_right, TN)
    left_share = shares(grad_rel_left)
    right_share = shares(grad_rel_right)
    g_emb = dot(g_left, rel_left, NT) + dot(g_right, rel_right, NT)
    g_seg = (g_emb.reshape(sequences, slots, features) / counts[:, :, None])
    seg_hi, seg_lo = hi_lo(g_seg)
    spread = jnp.einsum("stg,sgd->std", members, seg_hi, preferred_element_type=F32) + jnp.einsum(
        "stg,sgd->std", members, seg_lo, preferred_element_type=F32
    )
    g_y = cot_out.astype(F32) + spread.reshape(count, features)
    g_mlp = g_y.astype(BF)
    grad_down = dot(act, g_mlp, TN)
    down_share = shares(grad_down)
    g_u = (dot(g_mlp, down_projection_weight, NT) * slope.astype(F32)).astype(BF)
    grad_up_bias = jnp.sum(g_u.astype(F32), axis=0)
    grad_up = dot(h2, g_u, TN)
    up_share = shares(grad_up)
    g_h2 = dot(g_u, up_projection_weight, NT)
    g_norm2, grad_ln2_gain, grad_ln2_bias = norm_back(g_h2, r1, average2, inverse2, ln2_gain)
    g_r1 = g_y + g_norm2
    g_att = g_r1.astype(BF)
    grad_out = dot(ctx, g_att, TN)
    out_share = shares(grad_out)
    g_ctx = dot(g_att, attention_output_weight, NT).astype(BF)
    g_q, g_k, g_v, grad_table = attend_backward(qkv, e, linv, ctx, g_ctx, boxes, boxes_c)
    g_qkv = jnp.concatenate([g_q, g_k, g_v], axis=1)
    grad_qkv = dot(h1, g_qkv, TN)
    qkv_share = shares(grad_qkv)
    g_h1 = dot(g_qkv, query_key_value_weight, NT)
    g_norm1, grad_ln1_gain, grad_ln1_bias = norm_back(g_h1, x, average1, inverse1, ln1_gain)
    grad_tokens = g_r1 + g_norm1
    small = lax.psum(
        (grad_ln1_gain, grad_ln1_bias, grad_ln2_gain, grad_ln2_bias, grad_up_bias, grad_table), AXES
    )
    return (
        layer_out, pair_logits[None], grad_tokens, small[0], small[1], qkv_share, out_share,
        small[2], small[3], up_share, small[4], down_share, small[5], left_share, right_share,
    )


def solution(mesh):
    whole = P(AXES, None)
    tile = P("rows", "gr", "gc")
    flat = P(AXES)
    one = P()
    in_specs = (
        whole, P(None, AXES), whole, whole, tile, one, one, one, one, one, one, one, one, one, one,
        one, one, whole, tile,
    )
    out_specs = (
        whole, tile, whole, one, one, flat, flat, one, one, flat, one, flat, one, flat, flat,
    )
    return jax.shard_map(body, mesh=mesh, in_specs=in_specs, out_specs=out_specs, check_vma=False)
```

```python
import functools
import math

import jax
import jax.numpy as jnp
from jax import lax
from jax.experimental import pallas as pl
from jax.experimental.pallas import tpu as pltpu
from jax.sharding import PartitionSpec as P

COORD=1000
SPAN=2*COORD+1
LOG2E=1.4426950408889634
BARRED=-2.0**99
BF=jnp.bfloat16
F32=jnp.float32
NT=(((1,),(1,)),((),()))
NN=(((1,),(0,)),((),()))
def dot(a,b,dims=NN):
    return lax.dot_general(a,b,dims,preferred_element_type=F32)

def whole_and_rest(scaled):
    whole=jnp.floor((scaled+0.5)*(1.0/SPAN))
    return whole, scaled-SPAN*whole

def key_side(low, high, half):
    c=((low+high)>>1).astype(F32)
    return whole_and_rest(c*half)
def query_side(low, high, half):
    c=((low+high)>>1).astype(F32)
    return whole_and_rest((COORD-c)*half)

def hi_lo(v):
    hi=v.astype(BF)
    return hi, (v-hi.astype(F32)).astype(BF)

def fwd_kernel(q_ref,k_ref,v_ref,boxr_ref,boxc_ref,pager_ref,pagec_ref,tab_ref,
               ctx_ref,e_ref,linv_ref,
               ohb_ref,oha_ref,kg_ref,rxy_ref,pg_ref,cx_ref,cy_ref,*,rows):
    length=q_ref.shape[0]
    half=tab_ref.shape[1]//2
    quarter=half//2
    hp=pl.program_id(1)
    lane=lax.broadcasted_iota(jnp.int32,(1,128),1)
    low=lane<64
    @pl.when(hp==0)
    def _():
        bc=boxc_ref[...]
        ax,fax=key_side(bc[:,0:1],bc[:,2:3],half)
        ay,fay=key_side(bc[:,1:2],bc[:,3:4],half)
        bx,fbx=query_side(bc[:,0:1],bc[:,2:3],half)
        by,fby=query_side(bc[:,1:2],bc[:,3:4],half)
        spot=(lane%quarter).astype(F32)
        is_x=(lane%half)<quarter
        oha=jnp.where(jnp.where(is_x,ax,ay)==spot,1.0,0.0)
        ohb=jnp.where(jnp.where(is_x,bx,by)==spot,1.0,0.0)
        ohb_ref[...]=jnp.where(low,ohb,0.0).astype(BF)
        oha_ref[...]=oha.astype(BF)
        page=pagec_ref[...]
        mine=(lane%64)==page
        barred=jnp.where((lane%64)<4,jnp.where(mine,0.0,BARRED),0.0)
        kg_ref[0]=jnp.where(low,oha,barred).astype(BF)
        kg_ref[1]=jnp.where(low,barred,oha).astype(BF)
        pg_ref[...]=jnp.where(mine,1.0,0.0).astype(BF)
        ohx=jnp.where(ax==spot,1.0,0.0)
        ohy=jnp.where(ay==spot,1.0,0.0)
        rxy_ref[pl.ds(0,length),:]=jnp.where(low,ohx,0.0).astype(BF)
        rxy_ref[pl.ds(length,length),:]=jnp.where(low,0.0,ohy).astype(BF)
        br=boxr_ref[...]
        _,gax=key_side(br[0:1],br[2:3],half)
        _,gay=key_side(br[1:2],br[3:4],half)
        cx_ref[...]=jnp.where(gax+fbx>=SPAN,1.0,0.0)
        cy_ref[...]=jnp.where(gay+fby>=SPAN,1.0,0.0)
    k=k_ref[...]
    v=v_ref[...]
    oha=oha_ref[...]
    b_row=lax.broadcasted_iota(jnp.int32,(half,128),0)
    l_col=lax.broadcasted_iota(jnp.int32,(half,128),1)
    row_x=b_row<quarter
    index=jnp.where(row_x,b_row,b_row-quarter+half)+l_col%quarter
    same_axis=row_x==((l_col%half)<quarter)
    d_axis=row_x==(l_col<half)
    heads=[]
    for a in range(2):
        t=jnp.broadcast_to(tab_ref[pl.ds(2*hp+a,1),:],(half,128))
        base=jnp.take_along_axis(t,index,axis=1,mode="promise_in_bounds")
        nxt=jnp.take_along_axis(t,index+1,axis=1,mode="promise_in_bounds")
        hi,lo=hi_lo(base)
        dhi,dlo=hi_lo(nxt-base)
        z=jnp.zeros_like(hi)
        is_hi=(l_col<64)==(a==1)
        g0=jnp.where(same_axis,jnp.where(is_hi,hi.astype(F32),lo.astype(F32)),0.0).astype(BF)
        g1=jnp.where(d_axis,jnp.where((l_col%half)<quarter,dhi.astype(F32),dlo.astype(F32)),0.0).astype(BF)
        hk=jnp.concatenate([g0,g1],axis=1)
        left=dot(ohb_ref[:,0:half],hk).astype(BF)
        if a==0:
            rhs=jnp.concatenate([jnp.where(low,k,oha),kg_ref[0]],axis=1)
            vv=jnp.where(low,v,jnp.ones_like(v))
        else:
            rhs=jnp.concatenate([jnp.where(low,oha,k),kg_ref[1]],axis=1)
            vv=jnp.where(low,jnp.ones_like(v),v)
        heads.append((left,rhs,vv))
    for c in range(length//rows):
        sl=pl.ds(c*rows,rows)
        q=q_ref[sl,:]*jnp.asarray(0.125,BF)
        pg=pg_ref[sl,:]
        outs=[]
        for a in range(2):
            left,rhs,vv=heads[a]
            lc=left[c*rows:(c+1)*rows]
            g0=lc[:,:128]
            if a==0:
                lhs=jnp.concatenate([jnp.where(low,q,g0),jnp.where(low,g0,pg)],axis=1)
            else:
                lhs=jnp.concatenate([jnp.where(low,g0,q),jnp.where(low,pg,g0)],axis=1)
            s=dot(lhs,rhs,NT)
            dxy=dot(lc[:,128:],rxy_ref[...],NT)
            s=s+cx_ref[sl,:]*dxy[:,:length]+cy_ref[sl,:]*dxy[:,length:]
            m=jnp.max(s,axis=1,keepdims=True)
            e=jnp.exp2((s-m)*LOG2E).astype(BF)
            e_ref[a,sl,:]=e
            outs.append(dot(e,vv))
        ctx=jnp.where(low,outs[0],outs[1])
        tot=jnp.where(low,pltpu.roll(outs[0],64,1),pltpu.roll(outs[1],64,1))
        linv=1.0/tot
        linv_ref[sl,:]=linv
        ctx_ref[sl,:]=(ctx*linv).astype(BF)

def attend_forward(qkv,boxes_r,boxes_c,page_r,page_c,table,rows=512):
    tokens,width=qkv.shape
    feats=width//3
    seqs,_,length=page_r.shape
    heads=table.shape[0]
    pairs=heads//2
    return pl.pallas_call(
        functools.partial(fwd_kernel,rows=rows),
        grid=(seqs,pairs),
        in_specs=[
            pl.BlockSpec((length,128),lambda s,h:(s,h)),
            pl.BlockSpec((length,128),lambda s,h:(s,pairs+h)),
            pl.BlockSpec((length,128),lambda s,h:(s,2*pairs+h)),
            pl.BlockSpec((4,length),lambda s,h:(0,s)),
            pl.BlockSpec((length,4),lambda s,h:(s,0)),
            pl.BlockSpec((None,1,length),lambda s,h:(s,0,0)),
            pl.BlockSpec((length,1),lambda s,h:(s,0)),
            pl.BlockSpec(table.shape,lambda s,h:(0,0)),
        ],
        out_specs=[
            pl.BlockSpec((length,128),lambda s,h:(s,h)),
            pl.BlockSpec((2,None,length,length),lambda s,h:(h,s,0,0)),
            pl.BlockSpec((length,128),lambda s,h:(s,h)),
        ],
        out_shape=[jax.ShapeDtypeStruct((tokens,feats),BF),
                   jax.ShapeDtypeStruct((heads,seqs,length,length),BF),
                   jax.ShapeDtypeStruct((tokens,feats),F32)],
        scratch_shapes=[pltpu.VMEM((length,128),BF),pltpu.VMEM((length,128),BF),
                        pltpu.VMEM((2,length,128),BF),pltpu.VMEM((2*length,128),BF),
                        pltpu.VMEM((length,128),BF),
                        pltpu.VMEM((length,length),F32),pltpu.VMEM((length,length),F32)],
        name="attend_forward",
    )(qkv,qkv,qkv,boxes_r,boxes_c,page_r,page_c,table)

def bwd_kernel(q_ref,k_ref,v_ref,e_ref,linv_ref,ctx_ref,gctx_ref,boxr_ref,boxc_ref,
               gq_ref,gk_ref,gv_ref,hist_ref,
               oha_ref,ohbt_ref,cx_ref,cy_ref,g_ref,gx_ref,gy_ref,lt_ref,gt_ref,*,rows):
    length=q_ref.shape[0]
    half=64
    quarter=half//2
    s_id=pl.program_id(0)
    hp=pl.program_id(1)
    lane=lax.broadcasted_iota(jnp.int32,(1,128),1)
    low=lane<64
    @pl.when(hp==0)
    def _():
        bc=boxc_ref[...]
        ax,_=key_side(bc[:,0:1],bc[:,2:3],half)
        ay,_=key_side(bc[:,1:2],bc[:,3:4],half)
        _,fbx=query_side(bc[:,0:1],bc[:,2:3],half)
        _,fby=query_side(bc[:,1:2],bc[:,3:4],half)
        spot=(lane%quarter).astype(F32)
        is_x=(lane%half)<quarter
        oha_ref[...]=jnp.where(jnp.where(is_x,ax,ay)==spot,jnp.where(low,1.0,0.0),0.0).astype(BF)
        br=boxr_ref[...]
        _,gax=key_side(br[0:1],br[2:3],half)
        _,gay=key_side(br[1:2],br[3:4],half)
        rbx,_=query_side(br[0:1],br[2:3],half)
        rby,_=query_side(br[1:2],br[3:4],half)
        row=lax.broadcasted_iota(jnp.int32,(half,length),0)
        rspot=(row%quarter).astype(F32)
        ohbt_ref[...]=jnp.where(jnp.where(row<quarter,rbx,rby)==rspot,1.0,0.0).astype(BF)
        cx_ref[...]=jnp.where(gax+fbx>=SPAN,1.0,0.0).astype(BF)
        cy_ref[...]=jnp.where(gay+fby>=SPAN,1.0,0.0).astype(BF)
    k=k_ref[...]
    v=v_ref[...]
    lt_ref[...]=q_ref[...].astype(F32).T.astype(BF)
    gc=gctx_ref[...].astype(F32)*linv_ref[...]
    gcb=gc.astype(BF)
    gt_ref[...]=gcb.astype(F32).T.astype(BF)
    prod=gc*ctx_ref[...].astype(F32)
    ohbt=ohbt_ref[...]
    kts=[]
    vts=[]
    for a in range(2):
        mine=low if a==0 else jnp.logical_not(low)
        other=64-64*a
        D=jnp.sum(jnp.where(mine,prod,0.0),axis=1,keepdims=True)
        dhi=D.astype(BF).astype(F32)
        dlo=D-dhi
        lhs=jnp.where(mine,gcb.astype(F32),jnp.where(lane==other,dhi,jnp.where(lane==other+1,dlo,0.0))).astype(BF)
        rhs=jnp.where(mine,v,jnp.where((lane==other)|(lane==other+1),-1.0,0.0).astype(BF))
        for c in range(length//rows):
            sl=slice(c*rows,(c+1)*rows)
            gp=dot(lhs[sl],rhs,NT)
            g=(gp*e_ref[a,sl,:].astype(F32)).astype(BF)
            g_ref[a,sl,:]=g
            gx_ref[a,sl,:]=g*cx_ref[sl,:]
            gy_ref[a,sl,:]=g*cy_ref[sl,:]
        left=jnp.concatenate([lt_ref[64*a:64*a+64,:],ohbt],axis=0)
        r0=dot(left,g_ref[a])
        rx=dot(ohbt[:quarter],gx_ref[a])
        ry=dot(ohbt[quarter:],gy_ref[a])
        vts.append(dot(gt_ref[64*a:64*a+64,:],e_ref[a]))
        kts.append(r0[:64])
        w=jnp.concatenate([r0[64:],rx,ry],axis=0)
        whi,wlo=hi_lo(w)
        red=dot(jnp.concatenate([whi,wlo],axis=0),oha_ref[...])
        red=red[:128]+red[128:]
        hist_ref[a]=red
    zero=jnp.zeros_like(k)
    gq=dot(g_ref[0],jnp.where(low,k,zero))+dot(g_ref[1],jnp.where(low,zero,k))
    gq_ref[...]=(gq*0.125).astype(BF)
    gk_ref[...]=(jnp.concatenate(kts,axis=0)*0.125).T.astype(BF)
    gv_ref[...]=jnp.concatenate(vts,axis=0).T.astype(BF)

def attend_backward(qkv,e,linv,ctx,gctx,boxes_r,boxes_c,rows=256):
    tokens,width=qkv.shape
    feats=width//3
    heads,seqs,length,_=e.shape
    pairs=heads//2
    pair=pl.BlockSpec((length,128),lambda s,h:(s,h))
    gq,gk,gv,hist=pl.pallas_call(
        functools.partial(bwd_kernel,rows=rows),
        grid=(seqs,pairs),
        in_specs=[
            pair,
            pl.BlockSpec((length,128),lambda s,h:(s,pairs+h)),
            pl.BlockSpec((length,128),lambda s,h:(s,2*pairs+h)),
            pl.BlockSpec((2,None,length,length),lambda s,h:(h,s,0,0)),
            pair,pair,pair,
            pl.BlockSpec((4,length),lambda s,h:(0,s)),
            pl.BlockSpec((length,4),lambda s,h:(s,0)),
        ],
        out_specs=[pair,pair,pair,pl.BlockSpec((None,2,128,128),lambda s,h:(s,h,0,0))],
        out_shape=[jax.ShapeDtypeStruct((tokens,feats),BF)]*3+[jax.ShapeDtypeStruct((seqs,heads,128,128),F32)],
        scratch_shapes=[pltpu.VMEM((length,128),BF),pltpu.VMEM((64,length),BF),
                        pltpu.VMEM((length,length),BF),pltpu.VMEM((length,length),BF),
                        pltpu.VMEM((2,length,length),BF),pltpu.VMEM((2,length,length),BF),pltpu.VMEM((2,length,length),BF),
                        pltpu.VMEM((128,length),BF),pltpu.VMEM((128,length),BF)],
        name="attend_backward",
    )(qkv,qkv,qkv,e,linv,ctx,gctx,boxes_r,boxes_c)
    return gq,gk,gv,table_gradient(hist)

def table_gradient(hist):
    seqs,heads=hist.shape[:2]
    w=jnp.sum(hist,axis=0)
    quarter=32
    w=w.reshape(heads,2,2,quarter,4,quarter)[:, :, :, :, :2]
    w=jnp.stack([w[:,:,0,:,0],w[:,:,1,:,1]],axis=2)
    plain=w[:,0]-w[:,1]
    carry=w[:,1]
    both=jnp.stack([plain,carry],axis=2).reshape(heads,2,2*quarter*quarter)
    total=lax.iota(jnp.int32,quarter)[:,None]+lax.iota(jnp.int32,quarter)[None,:]
    idx=jnp.stack([total,total+1],0).reshape(-1)
    onehot=(idx[:,None]==lax.iota(jnp.int32,64)[None,:]).astype(F32)
    return jnp.einsum("hak,ke->hae",both,onehot,precision=lax.Precision.HIGHEST).reshape(heads,128)


AXES = ("rows", "gr", "gc")
PIECE=384

class Place:
    def __init__(self, n_rows):
        self.n_rows=n_rows
        self.r=lax.axis_index("rows"); self.g=lax.axis_index("gr"); c=lax.axis_index("gc")
        self.core=lax.rem(c,2); self.u=lax.div(c,2)
        self.sibling={"gc":self.u*2+1-self.core}
        self.across={"gc":(1-self.u)*2+self.core}
    def row_peer(self,d): return {"rows":lax.rem(self.r+d,self.n_rows)}
    def gr_peer(self,d): return {"gr":lax.rem(self.g+d,4)}
    def peers(self):
        return [self.sibling,self.across]+[self.row_peer(d) for d in range(1,self.n_rows)]+[self.gr_peer(d) for d in range(1,4)]

def meet(place):
    barrier=pltpu.get_barrier_semaphore()
    peers=place.peers()
    for p in peers:
        pl.semaphore_signal(barrier,inc=1,device_id=p,device_id_type=pl.DeviceIdType.MESH)
    pl.semaphore_wait(barrier,len(peers))

def send(src,dst,s,r,peer):
    return pltpu.make_async_remote_copy(src_ref=src,dst_ref=dst,send_sem=s,recv_sem=r,device_id=peer,device_id_type=pl.DeviceIdType.MESH)

class Shares:
    def __init__(self, place, sources, outs, fins, bufs, sems, orders):
        self.p=place; self.src=sources; self.out=outs; self.fin=fins
        self.own,self.b0,self.b1r,self.b1u,self.b2r,self.b2u,self.b3=bufs
        self.ls,self.ss,self.rs,self.fs,self.fr=sems
        self.units=[]
        for k,ref in enumerate(sources):
            subs,x=ref.shape[3],ref.shape[5]
            for s in range(subs):
                for j in range(x//2//PIECE):
                    self.units.append((k,s,j,orders[k]))
        self.count=len(self.units)
    @staticmethod
    def scratch(shapes, n_rows):
        n=sum(s[3]*(s[5]//2//PIECE) for s in shapes)
        m=shapes[0][4]
        R=n_rows
        bufs=[pltpu.VMEM((n,R,4,2,m,PIECE),BF),pltpu.VMEM((n,R,4,2,m,PIECE),BF),
              pltpu.VMEM((n,R-1,4,2,m,PIECE),BF), pltpu.VMEM((n,R,4,m,PIECE),BF),
              pltpu.VMEM((n,R-1,4,m,PIECE),BF), pltpu.VMEM((n,4,m,PIECE),BF), pltpu.VMEM((n,3,m,PIECE),BF)]
        k=len(shapes)
        P=R+5
        sems=[pltpu.SemaphoreType.DMA((n,)),pltpu.SemaphoreType.DMA((n,P)),pltpu.SemaphoreType.DMA((n,P)),
              pltpu.SemaphoreType.DMA((k,)),pltpu.SemaphoreType.DMA((k,))]
        fins=[pltpu.VMEM((2,s[3]*s[4]//2,s[5]//2),F32) for s in shapes]
        return fins,bufs,sems
    def cols(self,k,j,core):
        half=self.src[k].shape[5]//2
        return pl.ds(pl.multiple_of(core*half+j*PIECE,128),PIECE)
    def send0(self,i):
        k,s,j,_=self.units[i]
        ref=self.src[k]
        return send(ref.at[:,:,:,s,:,self.cols(k,j,1-self.p.core)],self.b0.at[i],self.ss.at[i,0],self.rs.at[i,0],self.p.sibling)
    def keep0(self,i):
        k,s,j,_=self.units[i]
        ref=self.src[k]
        return pltpu.make_async_copy(ref.at[:,:,:,s,:,self.cols(k,j,self.p.core)],self.own.at[i],self.ls.at[i])
    def row_copies(self,i,first):
        p=self.p; out=[]
        for d in range(1,p.n_rows):
            to=lax.rem(p.r+d,p.n_rows)
            src=self.own.at[i,to] if first else self.own.at[i,to,:,p.u]
            dst=(self.b1r if first else self.b2r).at[i,d-1]
            out.append(send(src,dst,self.ss.at[i,1+d],self.rs.at[i,1+d],p.row_peer(d)))
        return out
    def across_copies(self,i,first):
        p=self.p
        src=self.own.at[i,:,:,1-p.u] if first else self.own.at[i,p.r,:,1-p.u]
        dst=(self.b1u if first else self.b2u).at[i]
        return [send(src,dst,self.ss.at[i,1],self.rs.at[i,1],p.across)]
    def gr_copies(self,i):
        p=self.p; out=[]
        for d in range(1,4):
            to=lax.rem(p.g+d,4)
            out.append(send(self.own.at[i,p.r,to,p.u],self.b3.at[i,d-1],self.ss.at[i,p.n_rows+d],self.rs.at[i,p.n_rows+d],p.gr_peer(d)))
        return out
    def copies(self,i,stage):
        rows_first=self.units[i][3]
        if stage==0: return [self.send0(i),self.keep0(i)]
        if stage==3: return self.gr_copies(i)
        return self.row_copies(i,stage==1) if rows_first==(stage==1) else self.across_copies(i,stage==1)
    def start(self,i,stage):
        for c in self.copies(i,stage): c.start()
    def finish(self,i,stage):
        p=self.p
        rows_first=self.units[i][3]
        cs=self.copies(i,stage)
        if stage==0:
            cs[0].wait_recv(); cs[1].wait()
            self.own[i]=(self.own[i].astype(F32)+self.b0[i].astype(F32)).astype(BF)
            return
        for c in cs: c.wait_recv()
        if stage==3:
            k,s,j,_=self.units[i]
            total=self.own[i,p.r,p.g,p.u].astype(F32)
            for d in range(3): total=total+self.b3[i,d].astype(F32)
            subs=self.src[k].shape[3]; m=total.shape[0]
            cs=slice(j*PIECE,(j+1)*PIECE)
            if subs==1:
                self.fin[k][0,:,cs]=total[:m//2]
                self.fin[k][1,:,cs]=total[m//2:]
            else:
                per=subs//2
                self.fin[k][s//per,(s%per)*m:(s%per+1)*m,cs]=total
            return
        if rows_first==(stage==1):
            if stage==1:
                t=self.own[i,p.r].astype(F32)
                for d in range(p.n_rows-1): t=t+self.b1r[i,d].astype(F32)
                self.own[i,p.r]=t.astype(BF)
            else:
                t=self.own[i,p.r,:,p.u].astype(F32)
                for d in range(p.n_rows-1): t=t+self.b2r[i,d].astype(F32)
                self.own[i,p.r,:,p.u]=t.astype(BF)
        else:
            if stage==1:
                self.own[i,:,:,p.u]=(self.own[i,:,:,p.u].astype(F32)+self.b1u[i].astype(F32)).astype(BF)
            else:
                self.own[i,p.r,:,p.u]=(self.own[i,p.r,:,p.u].astype(F32)+self.b2u[i].astype(F32)).astype(BF)
    def last(self,k):
        p=self.p; half=self.src[k].shape[5]//2
        mine=pl.ds(pl.multiple_of(p.core*half,128),half)
        return send(self.fin[k].at[1-p.core],self.out[k].at[:,mine],self.fs.at[k],self.fr.at[k],p.sibling)
    def start_last(self,k):
        p=self.p; half=self.src[k].shape[5]//2
        self.last(k).start()
        mine=pl.ds(pl.multiple_of(p.core*half,128),half)
        self.out[k][:,mine]=self.fin[k][p.core]
    def run_all(self,window,lag,beside):
        n=self.count
        lasts={}
        for i,u in enumerate(self.units): lasts[u[0]]=i
        for i in range(min(window,n)): self.start(i,0)
        for t in range(n+3*lag):
            beside(t)
            if t<n:
                self.finish(t,0)
                if t+window<n: self.start(t+window,0)
                self.start(t,1)
            for stage in (1,2,3):
                i=t-stage*lag
                if 0<=i<n:
                    self.finish(i,stage)
                    if stage<3: self.start(i,stage+1)
                    else:
                        for k,li in lasts.items():
                            if li==i: self.start_last(k)
        for k in range(len(self.src)):
            self.last(k).wait()
        for i in range(n):
            self.send0(i).wait_send()
            for stage in range(1,4):
                for c in self.copies(i,stage): c.wait_send()

class Total:
    def __init__(self, place, source, out, bufs, ss, rs):
        self.p=place; self.src=source; self.out=out
        self.a,self.pair,self.rows,self.high,self.quad=bufs
        self.ss=ss; self.rs=rs
    @staticmethod
    def scratch(shape, n_rows):
        count=n_rows+4
        return ([pltpu.VMEM((3,)+shape,F32),pltpu.VMEM(shape,F32),pltpu.VMEM((n_rows,)+shape,F32),pltpu.VMEM(shape,F32),pltpu.VMEM((4,)+shape,F32)],
                [pltpu.SemaphoreType.DMA((count,)),pltpu.SemaphoreType.DMA((count,))])
    def copies(self,stage):
        p=self.p
        if stage==0: return [send(self.src,self.pair,self.ss.at[0],self.rs.at[0],p.sibling)]
        if stage==1: return [send(self.a.at[0],self.high,self.ss.at[1],self.rs.at[1],p.across)]
        if stage==2: return [send(self.a.at[1],self.rows.at[p.r],self.ss.at[1+d],self.rs.at[1+d],p.row_peer(d)) for d in range(1,p.n_rows)]
        return [send(self.a.at[2],self.quad.at[p.g],self.ss.at[p.n_rows+d],self.rs.at[p.n_rows+d],p.gr_peer(d)) for d in range(1,4)]
    def start(self,stage):
        for c in self.copies(stage): c.start()
    def finish(self,stage):
        p=self.p
        for c in self.copies(stage): c.wait_recv()
        if stage==0: self.a[0]=self.src[...]+self.pair[...]
        elif stage==1: self.a[1]=self.a[0]+self.high[...]
        elif stage==2:
            self.rows[p.r]=self.a[1]
            t=self.rows[0]
            for d in range(1,p.n_rows): t=t+self.rows[d]
            self.a[2]=t
        else:
            self.quad[p.g]=self.a[2]
            self.out[...]=(self.quad[0]+self.quad[1])+(self.quad[2]+self.quad[3])
    def wait_sends(self):
        for stage in range(4):
            for c in self.copies(stage): c.wait_send()

def view(g,n_rows):
    rows,x=g.shape
    sub=rows//(n_rows*8)
    m=48 if sub%48==0 else sub
    return g.reshape(n_rows,4,2,sub//m,m,x)

def shares_kernel(*refs,k,n_rows,orders,window,lag):
    src=refs[:k]; small=refs[k]; out=refs[k+1:2*k+1]; small_out=refs[2*k+1]
    rest=refs[2*k+2:]
    fins=rest[:k]; bufs=rest[k:k+7]; sems=rest[k+7:k+12]; tbufs=rest[k+12:k+17]; ts=rest[k+17:]
    place=Place(n_rows)
    meet(place)
    total=Total(place,small,small_out,tbufs,*ts)
    total.start(0)
    shares=Shares(place,src,out,fins,bufs,sems,orders)
    def beside(t):
        if t in (1,3,5,7):
            stage=t//2
            total.finish(stage)
            if stage<3: total.start(stage+1)
    shares.run_all(window,lag,beside)
    total.wait_sends()

def reduce_shares(grads,small,n_rows,orders,window=6,lag=3):
    views=[view(g,n_rows) for g in grads]
    k=len(views)
    fins,bufs,sems=Shares.scratch([v.shape for v in views],n_rows)
    tbufs,ts=Total.scratch(small.shape,n_rows)
    outs=[jax.ShapeDtypeStruct((v.shape[3]*v.shape[4]//2,v.shape[5]),F32) for v in views]+[jax.ShapeDtypeStruct(small.shape,F32)]
    vm=pl.BlockSpec(memory_space=pltpu.VMEM)
    return pl.pallas_call(functools.partial(shares_kernel,k=k,n_rows=n_rows,orders=orders,window=window,lag=lag),
        in_specs=[pl.BlockSpec(memory_space=pl.ANY)]*k+[vm],
        out_specs=[vm]*(k+1),
        out_shape=outs, scratch_shapes=fins+bufs+sems+tbufs+ts,
        compiler_params=pltpu.CompilerParams(collective_id=1,has_side_effects=True,vmem_limit_bytes=60<<20),
        name="shares")(*views,small)


def reduce_all(grads, smalls, n_rows):
    flat=jnp.concatenate([s.reshape(-1) for s in smalls])
    size=flat.shape[0]
    if (grads[0].shape[0] // (n_rows*8)) % 16:
        parts=[lax.psum_scatter(g,AXES,scatter_dimension=0,tiled=True).astype(F32).reshape(-1) for g in grads]
        total=lax.psum(flat,AXES)
    else:
        rows=-(-size//1024)*8
        packed=jnp.pad(flat,(0,rows*128-size)).reshape(rows,128)
        *parts,total=reduce_shares(grads,packed,n_rows,(True,False,True,False,False,False))
        parts=[part.reshape(-1) for part in parts]
        total=total.reshape(-1)
    out=[]; at=0
    for s in smalls:
        out.append(total[at:at+s.size].reshape(s.shape)); at+=s.size
    return parts,out


EPSILON = 1e-05


def norm_stats(rows):
    average = jnp.mean(rows, axis=-1, keepdims=True)
    centred = rows - average
    variance = jnp.mean(centred * centred, axis=-1, keepdims=True)
    return average, lax.rsqrt(variance + EPSILON)


def norm_back(g_out, rows, average, inverse, gain):
    z = (rows - average) * inverse
    g_z = g_out * gain
    grad_in = inverse * (
        g_z
        - jnp.mean(g_z, axis=-1, keepdims=True)
        - z * jnp.mean(g_z * z, axis=-1, keepdims=True)
    )
    return grad_in, jnp.sum(g_out * z, axis=0), jnp.sum(g_out, axis=0)


def gelu_pair(u):
    bell = jnp.exp(u * u * -0.5)
    t = 1.0 / (1.0 + (0.3275911 * math.sqrt(0.5)) * jnp.abs(u))
    series = t * (
        0.254829592
        + t * (-0.284496736 + t * (1.421413741 + t * (-1.453152027 + t * 1.061405429)))
    )
    tail = 0.5 * series * bell
    below = jnp.where(u < 0.0, tail, 1.0 - tail)
    return u * below, below + u * bell * (1.0 / math.sqrt(2.0 * math.pi))


def body(
    tokens, boxes, page_ids, seg_ids, pair_mask, ln1_gain, ln1_bias, query_key_value_weight,
    attention_output_weight, ln2_gain, ln2_bias, up_projection_weight, up_projection_bias,
    down_projection_weight, box_table, rel_left, rel_right, cot_out, cot_logits,
):
    sequences, length = page_ids.shape
    count = sequences * length
    features = tokens.shape[1]
    x = tokens.astype(F32)
    average1, inverse1 = norm_stats(x)
    h1 = ((x - average1) * inverse1 * ln1_gain + ln1_bias).astype(BF)
    qkv = dot(h1, query_key_value_weight).astype(BF)
    boxes_c = boxes.T
    ctx, e, linv = attend_forward(
        qkv, boxes, boxes_c, page_ids[:, None, :], page_ids.reshape(-1, 1), box_table
    )
    r1 = x + dot(ctx, attention_output_weight)
    average2, inverse2 = norm_stats(r1)
    h2 = ((r1 - average2) * inverse2 * ln2_gain + ln2_bias).astype(BF)
    act, slope = gelu_pair(dot(h2, up_projection_weight) + up_projection_bias)
    act = act.astype(BF)
    slope = slope.astype(BF)
    layer_out = (r1 + dot(act, down_projection_weight)).astype(BF)

    slots = 64
    member = seg_ids[:, :, None] == lax.iota(jnp.int32, slots)[None, None, :]
    members = member.astype(BF)
    counts = jnp.sum(member.astype(F32), axis=1)
    pooled = jnp.einsum(
        "stg,std->sgd", members, layer_out.reshape(sequences, length, features),
        preferred_element_type=F32,
    ) / counts[:, :, None]
    embedded = pooled.reshape(sequences * slots, features).astype(BF)
    left = dot(embedded, rel_left).astype(BF)
    right = dot(embedded, rel_right).astype(BF)
    row_side = lax.all_gather(left, "gc", axis=0, tiled=True)
    col_side = lax.all_gather(right, "gr", axis=0, tiled=True)
    pair_scale = 1.0 / math.sqrt(rel_left.shape[1])
    keep = pair_mask[0].astype(F32)
    pair_logits = keep * dot(row_side, col_side, NT) * pair_scale
    g_raw = (cot_logits[0].astype(F32) * pair_scale * keep).astype(BF)
    g_left = lax.psum_scatter(
        dot(g_raw, col_side).astype(BF), "gc", scatter_dimension=0, tiled=True
    )
    g_right = lax.psum_scatter(
        dot(g_raw, row_side, (((0,), (0,)), ((), ()))).astype(BF), "gr",
        scatter_dimension=0, tiled=True,
    )
    TN = (((0,), (0,)), ((), ()))
    grad_rel_left = dot(embedded, g_left, TN)
    grad_rel_right = dot(embedded, g_right, TN)
    g_emb = dot(g_left, rel_left, NT) + dot(g_right, rel_right, NT)
    g_seg = (g_emb.reshape(sequences, slots, features) / counts[:, :, None])
    seg_hi, seg_lo = hi_lo(g_seg)
    spread = jnp.einsum("stg,sgd->std", members, seg_hi, preferred_element_type=F32) + jnp.einsum(
        "stg,sgd->std", members, seg_lo, preferred_element_type=F32
    )
    g_y = cot_out.astype(F32) + spread.reshape(count, features)
    g_mlp = g_y.astype(BF)
    grad_down = dot(act, g_mlp, TN)
    g_u = (dot(g_mlp, down_projection_weight, NT) * slope.astype(F32)).astype(BF)
    grad_up_bias = jnp.sum(g_u.astype(F32), axis=0)
    grad_up = dot(h2, g_u, TN)
    g_h2 = dot(g_u, up_projection_weight, NT)
    g_norm2, grad_ln2_gain, grad_ln2_bias = norm_back(g_h2, r1, average2, inverse2, ln2_gain)
    g_r1 = g_y + g_norm2
    g_att = g_r1.astype(BF)
    grad_out = dot(ctx, g_att, TN)
    g_ctx = dot(g_att, attention_output_weight, NT).astype(BF)
    g_q, g_k, g_v, grad_table = attend_backward(qkv, e, linv, ctx, g_ctx, boxes, boxes_c)
    g_qkv = jnp.concatenate([g_q, g_k, g_v], axis=1)
    grad_qkv = dot(h1, g_qkv, TN)
    g_h1 = dot(g_qkv, query_key_value_weight, NT)
    g_norm1, grad_ln1_gain, grad_ln1_bias = norm_back(g_h1, x, average1, inverse1, ln1_gain)
    grad_tokens = g_r1 + g_norm1
    parts, small = reduce_all(
        [g.astype(BF) for g in (grad_qkv, grad_down, grad_up, grad_out, grad_rel_left, grad_rel_right)],
        [grad_ln1_gain, grad_ln1_bias, grad_ln2_gain, grad_ln2_bias, grad_up_bias, grad_table],
        lax.axis_size("rows"),
    )
    qkv_share, down_share, up_share, out_share, left_share, right_share = parts
    return (
        layer_out, pair_logits[None], grad_tokens, small[0], small[1], qkv_share, out_share,
        small[2], small[3], up_share, small[4], down_share, small[5], left_share, right_share,
    )


def solution(mesh):
    whole = P(AXES, None)
    tile = P("rows", "gr", "gc")
    flat = P(AXES)
    one = P()
    in_specs = (
        whole, P(None, AXES), whole, whole, tile, one, one, one, one, one, one, one, one, one, one,
        one, one, whole, tile,
    )
    out_specs = (
        whole, tile, whole, one, one, flat, flat, one, one, flat, one, flat, one, flat, flat,
    )
    return jax.shard_map(body, mesh=mesh, in_specs=in_specs, out_specs=out_specs, check_vma=False)
```

```python
import functools
import math

import jax
import jax.numpy as jnp
from jax import lax
from jax.experimental import pallas as pl
from jax.experimental.pallas import tpu as pltpu
from jax.sharding import PartitionSpec as P

COORD=1000
SPAN=2*COORD+1
LOG2E=1.4426950408889634
BARRED=-2.0**99
BF=jnp.bfloat16
F32=jnp.float32
NT=(((1,),(1,)),((),()))
NN=(((1,),(0,)),((),()))
def dot(a,b,dims=NN):
    return lax.dot_general(a,b,dims,preferred_element_type=F32)

def whole_and_rest(scaled):
    whole=jnp.floor((scaled+0.5)*(1.0/SPAN))
    return whole, scaled-SPAN*whole

def key_side(low, high, half):
    c=((low+high)>>1).astype(F32)
    return whole_and_rest(c*half)
def query_side(low, high, half):
    c=((low+high)>>1).astype(F32)
    return whole_and_rest((COORD-c)*half)

def hi_lo(v):
    hi=v.astype(BF)
    return hi, (v-hi.astype(F32)).astype(BF)

def fwd_kernel(q_ref,k_ref,v_ref,boxr_ref,boxc_ref,pager_ref,pagec_ref,tab_ref,
               ctx_ref,e_ref,linv_ref,
               ohb_ref,oha_ref,kg_ref,rxy_ref,pg_ref,cx_ref,cy_ref,*,rows):
    length=q_ref.shape[0]
    half=tab_ref.shape[1]//2
    quarter=half//2
    hp=pl.program_id(1)
    lane=lax.broadcasted_iota(jnp.int32,(1,128),1)
    low=lane<64
    @pl.when(hp==0)
    def _():
        bc=boxc_ref[...]
        ax,fax=key_side(bc[:,0:1],bc[:,2:3],half)
        ay,fay=key_side(bc[:,1:2],bc[:,3:4],half)
        bx,fbx=query_side(bc[:,0:1],bc[:,2:3],half)
        by,fby=query_side(bc[:,1:2],bc[:,3:4],half)
        spot=(lane%quarter).astype(F32)
        is_x=(lane%half)<quarter
        oha=jnp.where(jnp.where(is_x,ax,ay)==spot,1.0,0.0)
        ohb=jnp.where(jnp.where(is_x,bx,by)==spot,1.0,0.0)
        ohb_ref[...]=jnp.where(low,ohb,0.0).astype(BF)
        oha_ref[...]=oha.astype(BF)
        page=pagec_ref[...]
        mine=(lane%64)==page
        barred=jnp.where((lane%64)<4,jnp.where(mine,0.0,BARRED),0.0)
        kg_ref[0]=jnp.where(low,oha,barred).astype(BF)
        kg_ref[1]=jnp.where(low,barred,oha).astype(BF)
        pg_ref[...]=jnp.where(mine,1.0,0.0).astype(BF)
        ohx=jnp.where(ax==spot,1.0,0.0)
        ohy=jnp.where(ay==spot,1.0,0.0)
        rxy_ref[pl.ds(0,length),:]=jnp.where(low,ohx,0.0).astype(BF)
        rxy_ref[pl.ds(length,length),:]=jnp.where(low,0.0,ohy).astype(BF)
        br=boxr_ref[...]
        _,gax=key_side(br[0:1],br[2:3],half)
        _,gay=key_side(br[1:2],br[3:4],half)
        cx_ref[...]=jnp.where(gax+fbx>=SPAN,1.0,0.0)
        cy_ref[...]=jnp.where(gay+fby>=SPAN,1.0,0.0)
    k=k_ref[...]
    v=v_ref[...]
    oha=oha_ref[...]
    b_row=lax.broadcasted_iota(jnp.int32,(half,128),0)
    l_col=lax.broadcasted_iota(jnp.int32,(half,128),1)
    row_x=b_row<quarter
    index=jnp.where(row_x,b_row,b_row-quarter+half)+l_col%quarter
    same_axis=row_x==((l_col%half)<quarter)
    d_axis=row_x==(l_col<half)
    heads=[]
    for a in range(2):
        t=jnp.broadcast_to(tab_ref[pl.ds(2*hp+a,1),:],(half,128))
        base=jnp.take_along_axis(t,index,axis=1,mode="promise_in_bounds")
        nxt=jnp.take_along_axis(t,index+1,axis=1,mode="promise_in_bounds")
        hi,lo=hi_lo(base)
        dhi,dlo=hi_lo(nxt-base)
        z=jnp.zeros_like(hi)
        is_hi=(l_col<64)==(a==1)
        g0=jnp.where(same_axis,jnp.where(is_hi,hi.astype(F32),lo.astype(F32)),0.0).astype(BF)
        g1=jnp.where(d_axis,jnp.where((l_col%half)<quarter,dhi.astype(F32),dlo.astype(F32)),0.0).astype(BF)
        hk=jnp.concatenate([g0,g1],axis=1)
        left=dot(ohb_ref[:,0:half],hk).astype(BF)
        if a==0:
            rhs=jnp.concatenate([jnp.where(low,k,oha),kg_ref[0]],axis=1)
            vv=jnp.where(low,v,jnp.ones_like(v))
        else:
            rhs=jnp.concatenate([jnp.where(low,oha,k),kg_ref[1]],axis=1)
            vv=jnp.where(low,jnp.ones_like(v),v)
        heads.append((left,rhs,vv))
    for c in range(length//rows):
        sl=pl.ds(c*rows,rows)
        q=q_ref[sl,:]*jnp.asarray(0.125,BF)
        pg=pg_ref[sl,:]
        outs=[]
        for a in range(2):
            left,rhs,vv=heads[a]
            lc=left[c*rows:(c+1)*rows]
            g0=lc[:,:128]
            if a==0:
                lhs=jnp.concatenate([jnp.where(low,q,g0),jnp.where(low,g0,pg)],axis=1)
            else:
                lhs=jnp.concatenate([jnp.where(low,g0,q),jnp.where(low,pg,g0)],axis=1)
            s=dot(lhs,rhs,NT)
            dxy=dot(lc[:,128:],rxy_ref[...],NT)
            s=s+cx_ref[sl,:]*dxy[:,:length]+cy_ref[sl,:]*dxy[:,length:]
            m=jnp.max(s,axis=1,keepdims=True)
            e=jnp.exp2((s-m)*LOG2E).astype(BF)
            e_ref[a,sl,:]=e
            outs.append(dot(e,vv))
        ctx=jnp.where(low,outs[0],outs[1])
        tot=jnp.where(low,pltpu.roll(outs[0],64,1),pltpu.roll(outs[1],64,1))
        linv=1.0/tot
        linv_ref[sl,:]=linv
        ctx_ref[sl,:]=(ctx*linv).astype(BF)

def attend_forward(qkv,boxes_r,boxes_c,page_r,page_c,table,rows=512):
    tokens,width=qkv.shape
    feats=width//3
    seqs,_,length=page_r.shape
    heads=table.shape[0]
    pairs=heads//2
    return pl.pallas_call(
        functools.partial(fwd_kernel,rows=rows),
        grid=(seqs,pairs),
        in_specs=[
            pl.BlockSpec((length,128),lambda s,h:(s,h)),
            pl.BlockSpec((length,128),lambda s,h:(s,pairs+h)),
            pl.BlockSpec((length,128),lambda s,h:(s,2*pairs+h)),
            pl.BlockSpec((4,length),lambda s,h:(0,s)),
            pl.BlockSpec((length,4),lambda s,h:(s,0)),
            pl.BlockSpec((None,1,length),lambda s,h:(s,0,0)),
            pl.BlockSpec((length,1),lambda s,h:(s,0)),
            pl.BlockSpec(table.shape,lambda s,h:(0,0)),
        ],
        out_specs=[
            pl.BlockSpec((length,128),lambda s,h:(s,h)),
            pl.BlockSpec((2,None,length,length),lambda s,h:(h,s,0,0)),
            pl.BlockSpec((length,128),lambda s,h:(s,h)),
        ],
        out_shape=[jax.ShapeDtypeStruct((tokens,feats),BF),
                   jax.ShapeDtypeStruct((heads,seqs,length,length),BF),
                   jax.ShapeDtypeStruct((tokens,feats),F32)],
        scratch_shapes=[pltpu.VMEM((length,128),BF),pltpu.VMEM((length,128),BF),
                        pltpu.VMEM((2,length,128),BF),pltpu.VMEM((2*length,128),BF),
                        pltpu.VMEM((length,128),BF),
                        pltpu.VMEM((length,length),F32),pltpu.VMEM((length,length),F32)],
        name="attend_forward",
    )(qkv,qkv,qkv,boxes_r,boxes_c,page_r,page_c,table)


AXES = ("rows", "gr", "gc")
MESH = pl.DeviceIdType.MESH
PIECE = 384


class Place:
    def __init__(self, n_rows):
        self.n_rows = n_rows
        self.r = lax.axis_index("rows")
        self.g = lax.axis_index("gr")
        self.c = lax.axis_index("gc")
        self.core = lax.rem(self.c, 2)
        self.u = lax.div(self.c, 2)
        self.sibling = {"gc": self.u * 2 + 1 - self.core}
        self.across = {"gc": (1 - self.u) * 2 + self.core}

    def row_peer(self, d):
        return {"rows": lax.rem(self.r + d, self.n_rows)}

    def gr_peer(self, d):
        return {"gr": lax.rem(self.g + d, 4)}

    def peers(self):
        return (
            [self.sibling, self.across]
            + [self.row_peer(d) for d in range(1, self.n_rows)]
            + [self.gr_peer(d) for d in range(1, 4)]
        )


def meet(peers):
    barrier = pltpu.get_barrier_semaphore()
    for peer in peers:
        pl.semaphore_signal(barrier, inc=1, device_id=peer, device_id_type=MESH)
    pl.semaphore_wait(barrier, len(peers))


def send(src, dst, send_sem, recv_sem, peer):
    return pltpu.make_async_remote_copy(
        src_ref=src, dst_ref=dst, send_sem=send_sem, recv_sem=recv_sem, device_id=peer,
        device_id_type=MESH,
    )


class Shares:
    def __init__(self, place, units, arrays, staging, fins, got, bufs, sems):
        self.p = place
        self.units = units
        self.arrays = arrays
        self.staging = staging
        self.fin = fins
        self.got = got
        self.own, self.b0, self.b1r, self.b1u, self.b2r, self.b2u, self.b3 = bufs
        self.ls, self.ss, self.rs, self.fs, self.fr = sems
        self.count = len(units)
        self.place = [sum(u[3] == unit[3] for u in units[:i]) for i, unit in enumerate(units)]

    @staticmethod
    def scratch(units, sizes, n_rows):
        n, m, r = len(units), 48, n_rows
        by_rows = sum(unit[3] for unit in units)
        bufs = [
            pltpu.VMEM((n, r, 4, 2, m, PIECE), BF),
            pltpu.VMEM((n, r, 4, 2, m, PIECE), BF),
            pltpu.VMEM((by_rows, r - 1, 4, 2, m, PIECE), BF),
            pltpu.VMEM((n - by_rows, r, 4, m, PIECE), BF),
            pltpu.VMEM((n - by_rows, r - 1, 4, m, PIECE), BF),
            pltpu.VMEM((by_rows, 4, m, PIECE), BF),
            pltpu.VMEM((n, 3, m, PIECE), BF),
        ]
        dma = pltpu.SemaphoreType.DMA
        k = len(sizes)
        sems = [dma((n,)), dma((n, r + 4)), dma((n, r + 4)), dma((k,)), dma((k,))]
        fins = [pltpu.VMEM((2, rows, x // 2), F32) for rows, x in sizes]
        got = [pltpu.VMEM((rows, x // 2), F32) for rows, x in sizes]
        return fins, got, bufs, sems

    def columns(self, j, core):
        return pl.ds(pl.multiple_of(j * 2 * PIECE + core * PIECE, 128), PIECE)

    def swap(self, i):
        k, s, j, _, staged = self.units[i]
        theirs = 1 - self.p.core
        if staged is None:
            src = self.arrays[k].at[:, :, :, s, :, self.columns(j, theirs)]
        else:
            src = self.staging.at[staged, theirs]
        return send(src, self.b0.at[i], self.ss.at[i, 0], self.rs.at[i, 0], self.p.sibling)

    def keep(self, i):
        k, s, j, _, _ = self.units[i]
        src = self.arrays[k].at[:, :, :, s, :, self.columns(j, self.p.core)]
        return pltpu.make_async_copy(src, self.own.at[i], self.ls.at[i])

    def along_rows(self, i, first):
        p = self.p
        out = []
        for d in range(1, p.n_rows):
            to = lax.rem(p.r + d, p.n_rows)
            src = self.own.at[i, to] if first else self.own.at[i, to, :, p.u]
            dst = (self.b1r if first else self.b2r).at[self.place[i], d - 1]
            out.append(send(src, dst, self.ss.at[i, 1 + d], self.rs.at[i, 1 + d], p.row_peer(d)))
        return out

    def across(self, i, first):
        p = self.p
        src = self.own.at[i, :, :, 1 - p.u] if first else self.own.at[i, p.r, :, 1 - p.u]
        dst = (self.b1u if first else self.b2u).at[self.place[i]]
        return [send(src, dst, self.ss.at[i, 1], self.rs.at[i, 1], p.across)]

    def along_gr(self, i):
        p = self.p
        out = []
        for d in range(1, 4):
            src = self.own.at[i, p.r, lax.rem(p.g + d, 4), p.u]
            at = p.n_rows + d
            out.append(
                send(src, self.b3.at[i, d - 1], self.ss.at[i, at], self.rs.at[i, at], p.gr_peer(d))
            )
        return out

    def copies(self, i, stage):
        if stage == 0:
            return [self.swap(i)]
        if stage == 3:
            return self.along_gr(i)
        if self.units[i][3] == (stage == 1):
            return self.along_rows(i, stage == 1)
        return self.across(i, stage == 1)

    def start(self, i, stage):
        if stage == 0 and self.units[i][4] is None:
            self.keep(i).start()
        for copy in self.copies(i, stage):
            copy.start()

    def finish(self, i, stage):
        p = self.p
        k, s, j, rows_first, staged = self.units[i]
        if stage == 0 and staged is None:
            self.keep(i).wait()
        for copy in self.copies(i, stage):
            copy.wait_recv()
        wide = lambda v: v.astype(F32)
        at = self.place[i]
        if stage == 0:
            mine = self.own[i] if staged is None else self.staging[staged, p.core]
            self.own[i] = (wide(mine) + wide(self.b0[i])).astype(BF)
        elif stage == 3:
            total = wide(self.own[i, p.r, p.g, p.u])
            for d in range(3):
                total = total + wide(self.b3[i, d])
            m = total.shape[0]
            span = slice(j * PIECE, (j + 1) * PIECE)
            rows = self.fin[k].shape[1]
            if rows < m:
                self.fin[k][0, :, span] = total[:rows]
                self.fin[k][1, :, span] = total[rows:]
            else:
                per = rows // m
                self.fin[k][s // per, (s % per) * m : (s % per + 1) * m, span] = total
        elif rows_first == (stage == 1):
            if stage == 1:
                total = wide(self.own[i, p.r])
                for d in range(p.n_rows - 1):
                    total = total + wide(self.b1r[at, d])
                self.own[i, p.r] = total.astype(BF)
            else:
                total = wide(self.own[i, p.r, :, p.u])
                for d in range(p.n_rows - 1):
                    total = total + wide(self.b2r[at, d])
                self.own[i, p.r, :, p.u] = total.astype(BF)
        elif stage == 1:
            self.own[i, :, :, p.u] = (wide(self.own[i, :, :, p.u]) + wide(self.b1u[at])).astype(BF)
        else:
            self.own[i, p.r, :, p.u] = (
                wide(self.own[i, p.r, :, p.u]) + wide(self.b2u[at])
            ).astype(BF)

    def last(self, k):
        return send(
            self.fin[k].at[1 - self.p.core], self.got[k], self.fs.at[k], self.fr.at[k],
            self.p.sibling,
        )

    def tick(self, t, window, lag):
        n = self.count
        if t < n:
            self.finish(t, 0)
            self.start(t, 1)
            if t + window < n and self.units[t + window][4] is None:
                self.start(t + window, 0)
        for stage in (1, 2, 3):
            i = t - stage * lag
            if 0 <= i < n:
                self.finish(i, stage)
                if stage < 3:
                    self.start(i, stage + 1)
                else:
                    k = self.units[i][0]
                    if all(unit[0] != k for unit in self.units[i + 1 :]):
                        self.last(k).start()

    def ticks(self, lag):
        return self.count + 3 * lag

    def deliver(self, outs, spans):
        core = self.p.core
        for k, out in enumerate(outs):
            self.last(k).wait()
            for value, owner in ((self.fin[k][core], core), (self.got[k][...], 1 - core)):
                at = 0
                for base, step, width in spans[k]:
                    where = pl.ds(pl.multiple_of(base + owner * step, 128), width)
                    out[:, where] = value[:, at : at + width]
                    at += width

    def wait_sends(self):
        for i in range(self.count):
            for stage in range(4):
                for copy in self.copies(i, stage):
                    copy.wait_send()


class Total:
    def __init__(self, place, source, out, bufs, sems):
        self.p = place
        self.src = source
        self.out = out
        self.part, self.pair, self.high, self.rows, self.quad = bufs
        self.ss, self.rs = sems

    @staticmethod
    def scratch(shape, n_rows):
        dma = pltpu.SemaphoreType.DMA
        bufs = [
            pltpu.VMEM((3,) + shape, F32), pltpu.VMEM(shape, F32), pltpu.VMEM(shape, F32),
            pltpu.VMEM((n_rows,) + shape, F32), pltpu.VMEM((4,) + shape, F32),
        ]
        return bufs, [dma((n_rows + 4,)), dma((n_rows + 4,))]

    def copies(self, stage):
        p = self.p
        if stage == 0:
            return [send(self.src, self.pair, self.ss.at[0], self.rs.at[0], p.sibling)]
        if stage == 1:
            return [send(self.part.at[0], self.high, self.ss.at[1], self.rs.at[1], p.across)]
        if stage == 2:
            return [
                send(
                    self.part.at[1], self.rows.at[p.r], self.ss.at[1 + d], self.rs.at[1 + d],
                    p.row_peer(d),
                )
                for d in range(1, p.n_rows)
            ]
        return [
            send(
                self.part.at[2], self.quad.at[p.g], self.ss.at[p.n_rows + d],
                self.rs.at[p.n_rows + d], p.gr_peer(d),
            )
            for d in range(1, 4)
        ]

    def start(self, stage):
        for copy in self.copies(stage):
            copy.start()

    def finish(self, stage):
        p = self.p
        for copy in self.copies(stage):
            copy.wait_recv()
        if stage == 0:
            self.part[0] = self.src[...] + self.pair[...]
        elif stage == 1:
            self.part[1] = self.part[0] + self.high[...]
        elif stage == 2:
            self.rows[p.r] = self.part[1]
            total = self.rows[0]
            for d in range(1, p.n_rows):
                total = total + self.rows[d]
            self.part[2] = total
        else:
            self.quad[p.g] = self.part[2]
            self.out[...] = (self.quad[0] + self.quad[1]) + (self.quad[2] + self.quad[3])

    def wait_sends(self):
        for stage in range(4):
            for copy in self.copies(stage):
                copy.wait_send()


def view(g, n_rows):
    rows, x = g.shape
    per = rows // (n_rows * 8)
    return g.reshape(n_rows, 4, 2, per // 48, 48, x)


def back_kernel(*refs, n_ext, units, spans, n_rows, comm, lag, window):
    (q_ref, k_ref, v_ref, e_ref, linv_ref, ctx_ref, gctx_ref, boxr_ref, boxc_ref, wq_ref, wk_ref,
     wv_ref, h1_ref, x_ref, gr1_ref, gain_ref, small_ref) = refs[:17]
    at = 17
    arrays = refs[at : at + n_ext]
    at += n_ext
    gx_ref = refs[at]
    small_out = refs[at + 1]
    at += 2
    if comm:
        outs = refs[at : at + n_ext + 1]
        at += n_ext + 1
    else:
        grad_ref = refs[at]
        at += 1
    (oha_ref, ohbt_ref, cx_ref, cy_ref, g_ref, gcx_ref, gcy_ref, lt_ref, gt_ref, pair_ref, h1t_ref,
     acc_ref, hist_ref, h1_buf, x_buf, gr1_buf, pack_ref, in_sem) = refs[at : at + 18]
    at += 18
    length = q_ref.shape[0]
    half, quarter = 64, 32
    pairs, seqs = pl.num_programs(0), pl.num_programs(1)
    hp = pl.program_id(0)
    s_id = pl.program_id(1)
    n_seq = cx_ref.shape[0]
    n_pair = hist_ref.shape[0] // 2
    lane = lax.broadcasted_iota(jnp.int32, (1, 128), 1)
    low = lane < 64
    if comm:
        place = Place(n_rows)
        staging = refs[at]
        fins = refs[at + 1 : at + n_ext + 2]
        at += n_ext + 2
        got = refs[at : at + n_ext + 1]
        at += n_ext + 1
        shares = Shares(
            place, units, arrays, staging, fins, got, refs[at : at + 7], refs[at + 7 : at + 12]
        )
        at += 12
        total = Total(place, pack_ref, small_out, refs[at : at + 5], refs[at + 5 : at + 7])

    def inputs():
        return (
            pltpu.make_async_copy(h1_ref, h1_buf, in_sem.at[0]),
            pltpu.make_async_copy(x_ref, x_buf, in_sem.at[1]),
            pltpu.make_async_copy(gr1_ref, gr1_buf, in_sem.at[2]),
        )

    @pl.when((hp == 0) & (s_id == 0))
    def _():
        for copy in inputs():
            copy.start()
        acc_ref[...] = jnp.zeros_like(acc_ref)
        hist_ref[...] = jnp.zeros_like(hist_ref)
        if comm:
            meet(place.peers())
            for i, unit in enumerate(units[:window]):
                if unit[4] is None:
                    shares.start(i, 0)

    @pl.when(hp == 0)
    def _():
        bc = boxc_ref[...]
        ax, _ = key_side(bc[:, 0:1], bc[:, 2:3], half)
        ay, _ = key_side(bc[:, 1:2], bc[:, 3:4], half)
        _, fbx = query_side(bc[:, 0:1], bc[:, 2:3], half)
        _, fby = query_side(bc[:, 1:2], bc[:, 3:4], half)
        spot = (lane % quarter).astype(F32)
        is_x = (lane % half) < quarter
        oha = jnp.where(jnp.where(is_x, ax, ay) == spot, jnp.where(low, 1.0, 0.0), 0.0)
        oha_ref[s_id] = oha.astype(BF)
        br = boxr_ref[...]
        _, gax = key_side(br[0:1], br[2:3], half)
        _, gay = key_side(br[1:2], br[3:4], half)
        rbx, _ = query_side(br[0:1], br[2:3], half)
        rby, _ = query_side(br[1:2], br[3:4], half)
        row = lax.broadcasted_iota(jnp.int32, (half, length), 0)
        rspot = (row % quarter).astype(F32)
        ohbt_ref[s_id] = jnp.where(jnp.where(row < quarter, rbx, rby) == rspot, 1.0, 0.0).astype(BF)
        cx_ref[s_id] = jnp.where(gax + fbx >= SPAN, 1.0, 0.0).astype(BF)
        cy_ref[s_id] = jnp.where(gay + fby >= SPAN, 1.0, 0.0).astype(BF)

    @pl.when((hp == 0) & (s_id == n_seq - 1))
    def _():
        inputs()[0].wait()
        for c in range(h1_buf.shape[0] // 128):
            sl = slice(c * 128, (c + 1) * 128)
            h1t_ref[:, sl] = h1_buf[sl, :].astype(F32).T.astype(BF)

    k = k_ref[...]
    v = v_ref[...]
    lt_ref[...] = q_ref[...].astype(F32).T.astype(BF)
    gc = gctx_ref[...].astype(F32) * linv_ref[...]
    gcb = gc.astype(BF)
    gt_ref[...] = gcb.astype(F32).T.astype(BF)
    prod = gc * ctx_ref[...].astype(F32)
    ohbt = ohbt_ref[s_id]
    kts = []
    vts = []
    rows = 256
    for a in range(2):
        mine = low if a == 0 else jnp.logical_not(low)
        other = 64 - 64 * a
        d = jnp.sum(jnp.where(mine, prod, 0.0), axis=1, keepdims=True)
        dhi = d.astype(BF).astype(F32)
        extra = jnp.where(lane == other, dhi, jnp.where(lane == other + 1, d - dhi, 0.0))
        lhs = jnp.where(mine, gcb.astype(F32), extra).astype(BF)
        minus = jnp.where((lane == other) | (lane == other + 1), -1.0, 0.0).astype(BF)
        rhs = jnp.where(mine, v, minus)
        for c in range(length // rows):
            sl = slice(c * rows, (c + 1) * rows)
            gp = dot(lhs[sl], rhs, NT)
            g = (gp * e_ref[a, sl, :].astype(F32)).astype(BF)
            g_ref[a, sl, :] = g
            gcx_ref[a, sl, :] = g * cx_ref[s_id, sl, :]
            gcy_ref[a, sl, :] = g * cy_ref[s_id, sl, :]
        left = jnp.concatenate([lt_ref[64 * a : 64 * a + 64, :], ohbt], axis=0)
        r0 = dot(left, g_ref[a])
        rx = dot(ohbt[:quarter], gcx_ref[a])
        ry = dot(ohbt[quarter:], gcy_ref[a])
        vts.append(dot(gt_ref[64 * a : 64 * a + 64, :], e_ref[a]))
        kts.append(r0[:64])
        w = jnp.concatenate([r0[64:], rx, ry], axis=0)
        whi, wlo = hi_lo(w)
        red = dot(jnp.concatenate([whi, wlo], axis=0), oha_ref[s_id])
        hist_ref[2 * hp + a] += red[:128] + red[128:]
    zero = jnp.zeros_like(k)
    gq = dot(g_ref[0], jnp.where(low, k, zero)) + dot(g_ref[1], jnp.where(low, zero, k))
    g_pair = jnp.concatenate(
        [
            (gq * 0.125).astype(BF),
            (jnp.concatenate(kts, axis=0) * 0.125).T.astype(BF),
            jnp.concatenate(vts, axis=0).T.astype(BF),
        ],
        axis=1,
    )
    own_rows = pl.ds(pl.multiple_of(s_id * length, length), length)
    pair_ref[own_rows, :] = g_pair
    w_pair = jnp.concatenate([wq_ref[...], wk_ref[...], wv_ref[...]], axis=1)
    acc_ref[own_rows, :] += dot(g_pair, w_pair, NT)

    @pl.when(s_id == n_seq - 1)
    def _():
        piece = dot(h1t_ref[...], pair_ref[...]).astype(BF)
        if comm:
            staging[lax.div(hp, 2), lax.rem(hp, 2)] = piece.reshape(staging.shape[2:])
        else:
            grad_ref[0] = piece[:, :128]
            grad_ref[1] = piece[:, 128:256]
            grad_ref[2] = piece[:, 256:]

    if comm:
        n_step = n_pair * n_seq
        step = hp * n_seq + s_id
        waits = {}
        for i, unit in enumerate(units):
            if unit[4] is not None:
                waits[i] = (2 * unit[4] + 2) * n_seq - 1
        for at_step in range(n_step):
            @pl.when(step == at_step)
            def _(at_step=at_step):
                for i, ready in waits.items():
                    if ready == at_step:
                        shares.start(i, 0)
                if at_step < n_step - 1:
                    shares.tick(at_step, window, lag)

    @pl.when((hp == n_pair - 1) & (s_id == n_seq - 1))
    def _():
        inputs()[1].wait()
        inputs()[2].wait()
        gain = gain_ref[...]
        count, width = acc_ref.shape
        chunk = 256
        gain_sum = jnp.zeros((1, width), F32)
        bias_sum = jnp.zeros((1, width), F32)
        for c in range(count // chunk):
            sl = slice(c * chunk, (c + 1) * chunk)
            x = x_buf[sl, :].astype(F32)
            average, inverse = norm_stats(x)
            g_out = acc_ref[sl, :]
            z = (x - average) * inverse
            g_z = g_out * gain
            mean_g = jnp.mean(g_z, axis=-1, keepdims=True)
            mean_gz = jnp.mean(g_z * z, axis=-1, keepdims=True)
            gx_ref[sl, :] = gr1_buf[sl, :] + inverse * (g_z - mean_g - z * mean_gz)
            gain_sum = gain_sum + jnp.sum(g_out * z, axis=0, keepdims=True)
            bias_sum = bias_sum + jnp.sum(g_out, axis=0, keepdims=True)
        pack_ref[...] = small_ref[...]
        lines = width // 128
        for j in range(lines):
            pack_ref[j : j + 1, :] = gain_sum[:, j * 128 : (j + 1) * 128]
            pack_ref[lines + j : lines + j + 1, :] = bias_sum[:, j * 128 : (j + 1) * 128]
        base = pack_ref.shape[0] - 16
        for h in range(2 * n_pair):
            w = hist_ref[h]
            line = jnp.zeros((1, 128), F32)
            for axis in range(2):
                plain = w[axis * quarter : (axis + 1) * quarter]
                carry = w[half + axis * quarter : half + (axis + 1) * quarter]
                keep = (lane >= axis * quarter) & (lane < (axis + 1) * quarter)
                stay = jnp.where(keep, plain - carry, 0.0)
                move = jnp.where(keep, carry, 0.0)
                shift = axis * (half - quarter)
                stay = pltpu.roll(stay, shift, 1, stride=1, stride_axis=0)
                move = pltpu.roll(move, shift + 1, 1, stride=1, stride_axis=0)
                line = line + jnp.sum(stay + move, axis=0, keepdims=True)
            pack_ref[base + h : base + h + 1, :] = line
        if comm:
            total.start(0)
            first = n_pair * n_seq - 1
            for t in range(first, shares.ticks(lag)):
                shares.tick(t, window, lag)
                stage = t - first
                if stage < 4:
                    total.finish(stage)
                    if stage < 3:
                        total.start(stage + 1)
            shares.deliver(outs, spans)
            total.wait_sends()
            shares.wait_sends()
        else:
            small_out[...] = pack_ref[...]


def attend_and_project_backward(
    qkv, e, linv, ctx, gctx, boxes_r, boxes_c, weight, h1, tokens, g_r1, gain, small, arrays, n_rows, comm
):
    count, width = qkv.shape
    feats = width // 3
    heads, seqs, length, _ = e.shape
    pairs = heads // 2
    rows_of = lambda off: pl.BlockSpec((length, 128), lambda h, s: (s, off + h))
    cols_of = lambda off: pl.BlockSpec((feats, 128), lambda h, s: (0, off + h))
    any_ref = pl.BlockSpec(memory_space=pl.ANY)
    vm = pl.BlockSpec(memory_space=pltpu.VMEM)
    views = [view(g, n_rows) for g in arrays] if comm else []
    n_ext = len(views)
    lag, window = 3, 4
    external = []
    for k, g in enumerate(views):
        for s in range(g.shape[3]):
            for j in range(g.shape[5] // (2 * PIECE)):
                external.append((k, s, j, len(external) % 2 == 0, None))
    units = list(external)
    for t in range(pairs // 2):
        units.insert(min(len(units), (2 * t + 2) * seqs), (n_ext, 0, t, t % 2 == 0, t))
    units = tuple(units)
    out_shape = [jax.ShapeDtypeStruct((count, feats), F32), jax.ShapeDtypeStruct(small.shape, F32)]
    out_specs = [vm, vm]
    spans = []
    scratch = [
        pltpu.VMEM((seqs, length, 128), BF), pltpu.VMEM((seqs, 64, length), BF),
        pltpu.VMEM((seqs, length, length), BF), pltpu.VMEM((seqs, length, length), BF),
        pltpu.VMEM((2, length, length), BF), pltpu.VMEM((2, length, length), BF),
        pltpu.VMEM((2, length, length), BF), pltpu.VMEM((128, length), BF),
        pltpu.VMEM((128, length), BF), pltpu.VMEM((count, 384), BF), pltpu.VMEM((feats, count), BF),
        pltpu.VMEM((count, feats), F32), pltpu.VMEM((heads, 128, 128), F32),
        pltpu.VMEM((count, feats), BF), pltpu.VMEM((count, feats), BF),
        pltpu.VMEM((count, feats), F32), pltpu.VMEM(small.shape, F32), pltpu.SemaphoreType.DMA((3,)),
    ]
    params = dict(vmem_limit_bytes=63 << 20, dimension_semantics=("arbitrary", "arbitrary"))
    if comm:
        sizes = [(g.shape[3] * 24, g.shape[5]) for g in views] + [(24, width)]
        for rows, x in sizes[:-1]:
            spans.append([(j * 2 * PIECE, PIECE, PIECE) for j in range(x // (2 * PIECE))])
        spans.append(
            [(p * feats + t * 256, 128, 128) for t in range(pairs // 2) for p in range(3)]
        )
        out_shape += [jax.ShapeDtypeStruct(size, F32) for size in sizes]
        out_specs += [vm] * len(sizes)
        fins, got, bufs, sems = Shares.scratch(units, sizes, n_rows)
        tbufs, tsems = Total.scratch(small.shape, n_rows)
        scratch += [pltpu.VMEM((pairs // 2, 2, n_rows, 4, 2, 48, PIECE), BF)]
        scratch += fins + got + bufs + sems + tbufs + tsems
        params.update(collective_id=2, has_side_effects=True)
    else:
        out_shape.append(jax.ShapeDtypeStruct((3, feats, feats), BF))
        out_specs.append(pl.BlockSpec((3, feats, 128), lambda h, s: (0, 0, h)))
    results = pl.pallas_call(
        functools.partial(
            back_kernel, n_ext=n_ext, units=units, spans=spans, n_rows=n_rows, comm=comm, lag=lag,
            window=window,
        ),
        grid=(pairs, seqs),
        in_specs=[
            rows_of(0), rows_of(pairs), rows_of(2 * pairs),
            pl.BlockSpec((2, None, length, length), lambda h, s: (h, s, 0, 0)),
            rows_of(0), rows_of(0), rows_of(0),
            pl.BlockSpec((4, length), lambda h, s: (0, s)),
            pl.BlockSpec((length, 4), lambda h, s: (s, 0)),
            cols_of(0), cols_of(pairs), cols_of(2 * pairs),
            any_ref, any_ref, any_ref, vm, vm,
        ] + [any_ref] * n_ext,
        out_specs=out_specs,
        out_shape=out_shape,
        scratch_shapes=scratch,
        compiler_params=pltpu.CompilerParams(**params),
        name="attend_backward",
    )(
        qkv, qkv, qkv, e, linv, ctx, gctx, boxes_r, boxes_c, weight, weight, weight, h1, tokens, g_r1,
        gain.reshape(1, feats), small, *views,
    )
    return results


EPSILON = 1e-05


def norm_stats(rows):
    average = jnp.mean(rows, axis=-1, keepdims=True)
    centred = rows - average
    variance = jnp.mean(centred * centred, axis=-1, keepdims=True)
    return average, lax.rsqrt(variance + EPSILON)


def norm_back(g_out, rows, average, inverse, gain):
    z = (rows - average) * inverse
    g_z = g_out * gain
    grad_in = inverse * (
        g_z
        - jnp.mean(g_z, axis=-1, keepdims=True)
        - z * jnp.mean(g_z * z, axis=-1, keepdims=True)
    )
    return grad_in, jnp.sum(g_out * z, axis=0), jnp.sum(g_out, axis=0)


def gelu_pair(u):
    bell = jnp.exp(u * u * -0.5)
    t = 1.0 / (1.0 + (0.3275911 * math.sqrt(0.5)) * jnp.abs(u))
    series = t * (
        0.254829592
        + t * (-0.284496736 + t * (1.421413741 + t * (-1.453152027 + t * 1.061405429)))
    )
    tail = 0.5 * series * bell
    below = jnp.where(u < 0.0, tail, 1.0 - tail)
    return u * below, below + u * bell * (1.0 / math.sqrt(2.0 * math.pi))


def body(
    tokens, boxes, page_ids, seg_ids, pair_mask, ln1_gain, ln1_bias, query_key_value_weight,
    attention_output_weight, ln2_gain, ln2_bias, up_projection_weight, up_projection_bias,
    down_projection_weight, box_table, rel_left, rel_right, cot_out, cot_logits,
):
    sequences, length = page_ids.shape
    count = sequences * length
    features = tokens.shape[1]
    x = tokens.astype(F32)
    average1, inverse1 = norm_stats(x)
    h1 = ((x - average1) * inverse1 * ln1_gain + ln1_bias).astype(BF)
    qkv = dot(h1, query_key_value_weight).astype(BF)
    boxes_c = boxes.T
    ctx, e, linv = attend_forward(
        qkv, boxes, boxes_c, page_ids[:, None, :], page_ids.reshape(-1, 1), box_table
    )
    r1 = x + dot(ctx, attention_output_weight)
    average2, inverse2 = norm_stats(r1)
    h2 = ((r1 - average2) * inverse2 * ln2_gain + ln2_bias).astype(BF)
    act, slope = gelu_pair(dot(h2, up_projection_weight) + up_projection_bias)
    act = act.astype(BF)
    slope = slope.astype(BF)
    layer_out = (r1 + dot(act, down_projection_weight)).astype(BF)

    slots = 64
    member = seg_ids[:, :, None] == lax.iota(jnp.int32, slots)[None, None, :]
    members = member.astype(BF)
    counts = jnp.sum(member.astype(F32), axis=1)
    pooled = jnp.einsum(
        "stg,std->sgd", members, layer_out.reshape(sequences, length, features),
        preferred_element_type=F32,
    ) / counts[:, :, None]
    embedded = pooled.reshape(sequences * slots, features).astype(BF)
    left = dot(embedded, rel_left).astype(BF)
    right = dot(embedded, rel_right).astype(BF)
    row_side = lax.all_gather(left, "gc", axis=0, tiled=True)
    col_side = lax.all_gather(right, "gr", axis=0, tiled=True)
    pair_scale = 1.0 / math.sqrt(rel_left.shape[1])
    keep = pair_mask[0].astype(F32)
    pair_logits = keep * dot(row_side, col_side, NT) * pair_scale
    g_raw = (cot_logits[0].astype(F32) * pair_scale * keep).astype(BF)
    g_left = lax.psum_scatter(
        dot(g_raw, col_side).astype(BF), "gc", scatter_dimension=0, tiled=True
    )
    g_right = lax.psum_scatter(
        dot(g_raw, row_side, (((0,), (0,)), ((), ()))).astype(BF), "gr",
        scatter_dimension=0, tiled=True,
    )
    TN = (((0,), (0,)), ((), ()))
    grad_rel_left = dot(embedded, g_left, TN)
    grad_rel_right = dot(embedded, g_right, TN)
    g_emb = dot(g_left, rel_left, NT) + dot(g_right, rel_right, NT)
    g_seg = (g_emb.reshape(sequences, slots, features) / counts[:, :, None])
    seg_hi, seg_lo = hi_lo(g_seg)
    spread = jnp.einsum("stg,sgd->std", members, seg_hi, preferred_element_type=F32) + jnp.einsum(
        "stg,sgd->std", members, seg_lo, preferred_element_type=F32
    )
    g_y = cot_out.astype(F32) + spread.reshape(count, features)
    g_mlp = g_y.astype(BF)
    grad_down = dot(act, g_mlp, TN)
    g_u = (dot(g_mlp, down_projection_weight, NT) * slope.astype(F32)).astype(BF)
    grad_up_bias = jnp.sum(g_u.astype(F32), axis=0)
    grad_up = dot(h2, g_u, TN)
    g_h2 = dot(g_u, up_projection_weight, NT)
    g_norm2, grad_ln2_gain, grad_ln2_bias = norm_back(g_h2, r1, average2, inverse2, ln2_gain)
    g_r1 = g_y + g_norm2
    g_att = g_r1.astype(BF)
    grad_out = dot(ctx, g_att, TN)
    g_ctx = dot(g_att, attention_output_weight, NT).astype(BF)
    n_rows = lax.axis_size("rows")
    comm = n_rows * 8 * 48 <= features
    lines = jnp.concatenate([grad_ln2_gain, grad_ln2_bias, grad_up_bias]).reshape(-1, 128)
    small = jnp.pad(lines, ((2 * features // 128, 16), (0, 0)))
    grads = [g.astype(BF) for g in (grad_rel_left, grad_rel_right, grad_out, grad_down, grad_up)]
    grad_tokens, small, *shares = attend_and_project_backward(
        qkv, e, linv, ctx, g_ctx, boxes, boxes_c, query_key_value_weight, h1, tokens, g_r1, ln1_gain,
        small, grads, n_rows, comm,
    )
    if not comm:
        grads.append(jnp.concatenate([shares[0][0], shares[0][1], shares[0][2]], axis=1))
        shares = [
            lax.psum_scatter(g, AXES, scatter_dimension=0, tiled=True).astype(F32) for g in grads
        ]
        small = lax.psum(small, AXES)
    left_share, right_share, out_share, down_share, up_share, qkv_share = (
        share.reshape(-1) for share in shares
    )
    small = small.reshape(-1)
    ends = (0, features, 2 * features, 3 * features, 4 * features, 4 * features + grad_up_bias.shape[0])
    norms = [small[ends[n] : ends[n + 1]] for n in range(5)]
    grad_table = small[ends[5] : ends[5] + box_table.size].reshape(box_table.shape)
    return (
        layer_out, pair_logits[None], grad_tokens, norms[0], norms[1], qkv_share, out_share,
        norms[2], norms[3], up_share, norms[4], down_share, grad_table, left_share, right_share,
    )


def solution(mesh):
    whole = P(AXES, None)
    tile = P("rows", "gr", "gc")
    flat = P(AXES)
    one = P()
    in_specs = (
        whole, P(None, AXES), whole, whole, tile, one, one, one, one, one, one, one, one, one, one,
        one, one, whole, tile,
    )
    out_specs = (
        whole, tile, whole, one, one, flat, flat, one, one, flat, one, flat, one, flat, flat,
    )
    return jax.shard_map(body, mesh=mesh, in_specs=in_specs, out_specs=out_specs, check_vma=False)
```

```python
import functools
import math

import jax
import jax.numpy as jnp
from jax import lax
from jax.experimental import pallas as pl
from jax.experimental.pallas import tpu as pltpu
from jax.sharding import PartitionSpec as P

COORD=1000
SPAN=2*COORD+1
LOG2E=1.4426950408889634
BARRED=-2.0**99
BF=jnp.bfloat16
F32=jnp.float32
NT=(((1,),(1,)),((),()))
NN=(((1,),(0,)),((),()))
def dot(a,b,dims=NN):
    return lax.dot_general(a,b,dims,preferred_element_type=F32)

def whole_and_rest(scaled):
    whole=jnp.floor((scaled+0.5)*(1.0/SPAN))
    return whole, scaled-SPAN*whole

def key_side(low, high, half):
    c=((low+high)>>1).astype(F32)
    return whole_and_rest(c*half)
def query_side(low, high, half):
    c=((low+high)>>1).astype(F32)
    return whole_and_rest((COORD-c)*half)

def hi_lo(v):
    hi=v.astype(BF)
    return hi, (v-hi.astype(F32)).astype(BF)

def fwd_kernel(q_ref,k_ref,v_ref,boxr_ref,boxc_ref,pager_ref,pagec_ref,tab_ref,mask_ref,cot_ref,
               ctx_ref,e_ref,linv_ref,rowp_ref,colp_ref,
               ohb_ref,oha_ref,kg_ref,rxy_ref,pg_ref,cx_ref,cy_ref,*panel_refs,rows,pair_scale):
    length=q_ref.shape[0]
    half=tab_ref.shape[1]//2
    quarter=half//2
    hp=pl.program_id(1)
    seq=pl.program_id(0)
    place=Place(1)
    panels=Panels(place,*panel_refs[:4],panel_refs[4:])
    @pl.when((hp==0)&(seq==0))
    def _():
        meet([place.gc_peer(d) for d in (1,2,3)]+[place.gr_peer(d) for d in (1,2,3)])
        panels.fill(mask_ref,cot_ref,pair_scale)
    @pl.when((hp==1)&(seq==0))
    def _():
        panels.start()
    lane=lax.broadcasted_iota(jnp.int32,(1,128),1)
    low=lane<64
    @pl.when(hp==0)
    def _():
        bc=boxc_ref[...]
        ax,fax=key_side(bc[:,0:1],bc[:,2:3],half)
        ay,fay=key_side(bc[:,1:2],bc[:,3:4],half)
        bx,fbx=query_side(bc[:,0:1],bc[:,2:3],half)
        by,fby=query_side(bc[:,1:2],bc[:,3:4],half)
        spot=(lane%quarter).astype(F32)
        is_x=(lane%half)<quarter
        oha=jnp.where(jnp.where(is_x,ax,ay)==spot,1.0,0.0)
        ohb=jnp.where(jnp.where(is_x,bx,by)==(quarter-1)-spot,1.0,0.0)
        ohb_ref[...]=jnp.where(low,ohb,0.0).astype(BF)
        oha_ref[...]=oha.astype(BF)
        page=pagec_ref[...]
        mine=(lane%64)==page
        barred=jnp.where((lane%64)<4,jnp.where(mine,0.0,BARRED),0.0)
        kg_ref[0]=jnp.where(low,oha,barred).astype(BF)
        kg_ref[1]=jnp.where(low,barred,oha).astype(BF)
        pg_ref[...]=jnp.where(mine,1.0,0.0).astype(BF)
        ohx=jnp.where(ax==spot,1.0,0.0)
        ohy=jnp.where(ay==spot,1.0,0.0)
        rxy_ref[pl.ds(0,length),:]=jnp.where(low,ohx,0.0).astype(BF)
        rxy_ref[pl.ds(length,length),:]=jnp.where(low,0.0,ohy).astype(BF)
        br=boxr_ref[...]
        _,gax=key_side(br[0:1],br[2:3],half)
        _,gay=key_side(br[1:2],br[3:4],half)
        cx_ref[...]=jnp.where(gax+fbx>=SPAN,1.0,0.0)
        cy_ref[...]=jnp.where(gay+fby>=SPAN,1.0,0.0)
    k=k_ref[...]
    v=v_ref[...]
    oha=oha_ref[...]
    b_row=lax.broadcasted_iota(jnp.int32,(half,128),0)
    l_col=lax.broadcasted_iota(jnp.int32,(half,128),1)
    row_x=b_row<quarter
    same_axis=row_x==((l_col%half)<quarter)
    d_axis=row_x==(l_col<half)
    heads=[]
    for a in range(2):
        t=tab_ref[pl.ds(2*hp+a,1),:]
        both=[jnp.where(low,t,0.0)+pltpu.roll(jnp.where(low,t,0.0),64,1),
              jnp.where(low,0.0,t)+pltpu.roll(jnp.where(low,0.0,t),64,1)]
        tiles=[]
        for b in both:
            spreads=[]
            for first in (0,1):
                whole=jnp.broadcast_to(b,(quarter,128))
                turned=pltpu.roll(whole,128-(quarter-1)-first,1,stride=1,stride_axis=0)
                lowq=jnp.where(lane<quarter,turned,0.0)
                pair=lowq+pltpu.roll(lowq,quarter,1)
                spreads.append(pair+pltpu.roll(pair,64,1))
            tiles.append(spreads)
        base=jnp.concatenate([tiles[0][0],tiles[1][0]],axis=0)
        nxt=jnp.concatenate([tiles[0][1],tiles[1][1]],axis=0)
        hi,lo=hi_lo(base)
        dhi,dlo=hi_lo(nxt-base)
        z=jnp.zeros_like(hi)
        is_hi=(l_col<64)==(a==1)
        g0=jnp.where(same_axis,jnp.where(is_hi,hi.astype(F32),lo.astype(F32)),0.0).astype(BF)
        g1=jnp.where(d_axis,jnp.where((l_col%half)<quarter,dhi.astype(F32),dlo.astype(F32)),0.0).astype(BF)
        hk=jnp.concatenate([g0,g1],axis=1)
        left=dot(ohb_ref[:,0:half],hk).astype(BF)
        if a==0:
            rhs=jnp.concatenate([jnp.where(low,k,oha),kg_ref[0]],axis=1)
            vv=jnp.where(low,v,jnp.ones_like(v))
        else:
            rhs=jnp.concatenate([jnp.where(low,oha,k),kg_ref[1]],axis=1)
            vv=jnp.where(low,jnp.ones_like(v),v)
        heads.append((left,rhs,vv))
    for c in range(length//rows):
        sl=pl.ds(c*rows,rows)
        q=q_ref[sl,:]*jnp.asarray(0.125,BF)
        pg=pg_ref[sl,:]
        outs=[]
        for a in range(2):
            left,rhs,vv=heads[a]
            lc=left[c*rows:(c+1)*rows]
            g0=lc[:,:128]
            if a==0:
                lhs=jnp.concatenate([jnp.where(low,q,g0),jnp.where(low,g0,pg)],axis=1)
            else:
                lhs=jnp.concatenate([jnp.where(low,g0,q),jnp.where(low,pg,g0)],axis=1)
            s=dot(lhs,rhs,NT)
            dxy=dot(lc[:,128:],rxy_ref[...],NT)
            s=s+cx_ref[sl,:]*dxy[:,:length]+cy_ref[sl,:]*dxy[:,length:]
            m=jnp.max(s,axis=1,keepdims=True)
            e=jnp.exp2((s-m)*LOG2E).astype(BF)
            e_ref[a,sl,:]=e
            outs.append(dot(e,vv))
        ctx=jnp.where(low,outs[0],outs[1])
        tot=jnp.where(low,pltpu.roll(outs[0],64,1),pltpu.roll(outs[1],64,1))
        linv=1.0/tot
        linv_ref[sl,:]=linv
        ctx_ref[sl,:]=(ctx*linv).astype(BF)
    @pl.when((hp==pl.num_programs(1)-1)&(seq==pl.num_programs(0)-1))
    def _():
        panels.collect(rowp_ref,colp_ref)

def attend_forward(qkv,boxes_r,boxes_c,page_r,page_c,table,mask,cot,pair_scale,rows=512):
    tokens,width=qkv.shape
    feats=width//3
    seqs,_,length=page_r.shape
    heads=table.shape[0]
    pairs=heads//2
    return pl.pallas_call(
        functools.partial(fwd_kernel,rows=rows,pair_scale=pair_scale),
        grid=(seqs,pairs),
        in_specs=[
            pl.BlockSpec((length,128),lambda s,h:(s,h)),
            pl.BlockSpec((length,128),lambda s,h:(s,pairs+h)),
            pl.BlockSpec((length,128),lambda s,h:(s,2*pairs+h)),
            pl.BlockSpec((4,length),lambda s,h:(0,s)),
            pl.BlockSpec((length,4),lambda s,h:(s,0)),
            pl.BlockSpec((None,1,length),lambda s,h:(s,0,0)),
            pl.BlockSpec((length,1),lambda s,h:(s,0)),
            pl.BlockSpec(table.shape,lambda s,h:(0,0)),
            pl.BlockSpec(memory_space=pltpu.VMEM),
            pl.BlockSpec(memory_space=pltpu.VMEM),
        ],
        out_specs=[
            pl.BlockSpec((length,128),lambda s,h:(s,h)),
            pl.BlockSpec((2,None,length,length),lambda s,h:(h,s,0,0)),
            pl.BlockSpec((length,128),lambda s,h:(s,h)),
            pl.BlockSpec(memory_space=pltpu.VMEM),
            pl.BlockSpec(memory_space=pltpu.VMEM),
        ],
        out_shape=[jax.ShapeDtypeStruct((tokens,feats),BF),
                   jax.ShapeDtypeStruct((heads,seqs,length,length),BF),
                   jax.ShapeDtypeStruct((tokens,feats),F32)]
                  +[jax.ShapeDtypeStruct((4,mask.shape[0]//4,mask.shape[0]),BF)]*2,
        scratch_shapes=[pltpu.VMEM((length,128),BF),pltpu.VMEM((length,128),BF),
                        pltpu.VMEM((2,length,128),BF),pltpu.VMEM((2*length,128),BF),
                        pltpu.VMEM((length,128),BF),
                        pltpu.VMEM((length,length),F32),pltpu.VMEM((length,length),F32)]
                       +Panels.scratch(mask.shape[0]),
        compiler_params=pltpu.CompilerParams(collective_id=4,has_side_effects=True,vmem_limit_bytes=60<<20),
        name="attend_forward",
    )(qkv,qkv,qkv,boxes_r,boxes_c,page_r,page_c,table,mask,cot)


AXES = ("rows", "gr", "gc")
MESH = pl.DeviceIdType.MESH
PIECE = 384


class Place:
    def __init__(self, n_rows):
        self.n_rows = n_rows
        self.r = lax.axis_index("rows")
        self.g = lax.axis_index("gr")
        self.c = lax.axis_index("gc")
        self.core = lax.rem(self.c, 2)
        self.u = lax.div(self.c, 2)
        self.sibling = {"gc": self.u * 2 + 1 - self.core}
        self.across = {"gc": (1 - self.u) * 2 + self.core}

    def row_peer(self, d):
        return {"rows": lax.rem(self.r + d, self.n_rows)}

    def gr_peer(self, d):
        return {"gr": lax.rem(self.g + d, 4)}

    def gc_peer(self, d):
        return {"gc": lax.rem(self.c + d, 4)}

    def peers(self):
        return (
            [self.sibling, self.across]
            + [self.row_peer(d) for d in range(1, self.n_rows)]
            + [self.gr_peer(d) for d in range(1, 4)]
        )


def meet(peers):
    barrier = pltpu.get_barrier_semaphore()
    for peer in peers:
        pl.semaphore_signal(barrier, inc=1, device_id=peer, device_id_type=MESH)
    pl.semaphore_wait(barrier, len(peers))


def send(src, dst, send_sem, recv_sem, peer):
    return pltpu.make_async_remote_copy(
        src_ref=src, dst_ref=dst, send_sem=send_sem, recv_sem=recv_sem, device_id=peer,
        device_id_type=MESH,
    )


class Shares:
    def __init__(self, place, slots, arrays, staging, fins, got, bufs, sems):
        self.p = place
        units = tuple(unit for unit in slots if unit is not None)
        self.units = units
        order = iter(range(len(units)))
        self.slots = [None if unit is None else next(order) for unit in slots]
        self.external = [i for i, unit in enumerate(units) if unit[4] is None]
        self.arrays = arrays
        self.staging = staging
        self.fin = fins
        self.got = got
        self.own, self.b0, self.b1r, self.b1u, self.b2r, self.b2u, self.b3 = bufs
        self.ls, self.ss, self.rs, self.fs, self.fr = sems
        self.count = len(units)
        self.place = [sum(u[3] == unit[3] for u in units[:i]) for i, unit in enumerate(units)]

    @staticmethod
    def scratch(slots, sizes, n_rows):
        units = [unit for unit in slots if unit is not None]
        n, m, r = len(units), 48, n_rows
        by_rows = sum(unit[3] for unit in units)
        bufs = [
            pltpu.VMEM((n, r, 4, 2, m, PIECE), BF),
            pltpu.VMEM((n, r, 4, 2, m, PIECE), BF),
            pltpu.VMEM((by_rows, r - 1, 4, 2, m, PIECE), BF),
            pltpu.VMEM((n - by_rows, r, 4, m, PIECE), BF),
            pltpu.VMEM((n - by_rows, r - 1, 4, m, PIECE), BF),
            pltpu.VMEM((by_rows, 4, m, PIECE), BF),
            pltpu.VMEM((n, 3, m, PIECE), BF),
        ]
        dma = pltpu.SemaphoreType.DMA
        k = len(sizes)
        sems = [dma((n,)), dma((n, r + 4)), dma((n, r + 4)), dma((k,)), dma((k,))]
        fins = [pltpu.VMEM((2, rows, x // 2), F32) for rows, x in sizes]
        got = [pltpu.VMEM((rows, x // 2), F32) for rows, x in sizes]
        return fins, got, bufs, sems

    def columns(self, j, core):
        return pl.ds(pl.multiple_of(j * 2 * PIECE + core * PIECE, 128), PIECE)

    def swap(self, i):
        k, s, j, _, staged = self.units[i]
        theirs = 1 - self.p.core
        if staged is None:
            src = self.arrays[k].at[:, :, :, s, :, self.columns(j, theirs)]
        else:
            src = self.staging.at[staged, theirs]
        return send(src, self.b0.at[i], self.ss.at[i, 0], self.rs.at[i, 0], self.p.sibling)

    def keep(self, i):
        k, s, j, _, _ = self.units[i]
        src = self.arrays[k].at[:, :, :, s, :, self.columns(j, self.p.core)]
        return pltpu.make_async_copy(src, self.own.at[i], self.ls.at[i])

    def along_rows(self, i, first):
        p = self.p
        out = []
        for d in range(1, p.n_rows):
            to = lax.rem(p.r + d, p.n_rows)
            src = self.own.at[i, to] if first else self.own.at[i, to, :, p.u]
            dst = (self.b1r if first else self.b2r).at[self.place[i], d - 1]
            out.append(send(src, dst, self.ss.at[i, 1 + d], self.rs.at[i, 1 + d], p.row_peer(d)))
        return out

    def across(self, i, first):
        p = self.p
        src = self.own.at[i, :, :, 1 - p.u] if first else self.own.at[i, p.r, :, 1 - p.u]
        dst = (self.b1u if first else self.b2u).at[self.place[i]]
        return [send(src, dst, self.ss.at[i, 1], self.rs.at[i, 1], p.across)]

    def along_gr(self, i):
        p = self.p
        out = []
        for d in range(1, 4):
            src = self.own.at[i, p.r, lax.rem(p.g + d, 4), p.u]
            at = p.n_rows + d
            out.append(
                send(src, self.b3.at[i, d - 1], self.ss.at[i, at], self.rs.at[i, at], p.gr_peer(d))
            )
        return out

    def copies(self, i, stage):
        if stage == 0:
            return [self.swap(i)]
        if stage == 3:
            return self.along_gr(i)
        if self.units[i][3] == (stage == 1):
            return self.along_rows(i, stage == 1)
        return self.across(i, stage == 1)

    def start(self, i, stage):
        if stage == 0 and self.units[i][4] is None:
            self.keep(i).start()
        for copy in self.copies(i, stage):
            copy.start()

    def finish(self, i, stage):
        p = self.p
        k, s, j, rows_first, staged = self.units[i]
        if stage == 0 and staged is None:
            self.keep(i).wait()
        for copy in self.copies(i, stage):
            copy.wait_recv()
        wide = lambda v: v.astype(F32)
        at = self.place[i]
        if stage == 0:
            mine = self.own[i] if staged is None else self.staging[staged, p.core]
            self.own[i] = (wide(mine) + wide(self.b0[i])).astype(BF)
        elif stage == 3:
            total = wide(self.own[i, p.r, p.g, p.u])
            for d in range(3):
                total = total + wide(self.b3[i, d])
            m = total.shape[0]
            span = slice(j * PIECE, (j + 1) * PIECE)
            rows = self.fin[k].shape[1]
            if rows < m:
                self.fin[k][0, :, span] = total[:rows]
                self.fin[k][1, :, span] = total[rows:]
            else:
                per = self.arrays[k].shape[3] // 2
                row = (s % per) * m if rows > m else 0
                self.fin[k][s // per, row : row + m, span] = total
        elif rows_first == (stage == 1):
            if stage == 1:
                total = wide(self.own[i, p.r])
                for d in range(p.n_rows - 1):
                    total = total + wide(self.b1r[at, d])
                self.own[i, p.r] = total.astype(BF)
            else:
                total = wide(self.own[i, p.r, :, p.u])
                for d in range(p.n_rows - 1):
                    total = total + wide(self.b2r[at, d])
                self.own[i, p.r, :, p.u] = total.astype(BF)
        elif stage == 1:
            self.own[i, :, :, p.u] = (wide(self.own[i, :, :, p.u]) + wide(self.b1u[at])).astype(BF)
        else:
            self.own[i, p.r, :, p.u] = (
                wide(self.own[i, p.r, :, p.u]) + wide(self.b2u[at])
            ).astype(BF)

    def last(self, k):
        return send(
            self.fin[k].at[1 - self.p.core], self.got[k], self.fs.at[k], self.fr.at[k],
            self.p.sibling,
        )

    def begin(self, window):
        for i in self.external[:window]:
            self.start(i, 0)

    def tick(self, t, window, lag):
        def at(beat):
            return self.slots[beat] if 0 <= beat < len(self.slots) else None

        i = at(t)
        if i is not None:
            self.finish(i, 0)
            self.start(i, 1)
            if i in self.external:
                later = self.external.index(i) + window
                if later < len(self.external):
                    self.start(self.external[later], 0)
        for stage in (1, 2, 3):
            i = at(t - stage * lag)
            if i is not None:
                self.finish(i, stage)
                if stage < 3:
                    self.start(i, stage + 1)
                else:
                    k = self.units[i][0]
                    later = self.slots[self.slots.index(i) + 1 :]
                    if all(n is None or self.units[n][0] != k for n in later):
                        self.last(k).start()

    def ticks(self, lag):
        return len(self.slots) + 3 * lag

    def deliver(self, outs, spans):
        core = self.p.core
        for k, out in enumerate(outs):
            self.last(k).wait()
            for value, owner in ((self.fin[k][core], core), (self.got[k][...], 1 - core)):
                at = 0
                for base, step, width in spans[k]:
                    where = pl.ds(pl.multiple_of(base + owner * step, 128), width)
                    out[:, where] = value[:, at : at + width]
                    at += width

    def wait_sends(self):
        for i in range(self.count):
            for stage in range(4):
                for copy in self.copies(i, stage):
                    copy.wait_send()


class Total:
    def __init__(self, place, source, out, bufs, sems):
        self.p = place
        self.src = source
        self.out = out
        self.part, self.pair, self.high, self.rows, self.quad = bufs
        self.ss, self.rs = sems

    @staticmethod
    def scratch(shape, n_rows):
        dma = pltpu.SemaphoreType.DMA
        bufs = [
            pltpu.VMEM((3,) + shape, F32), pltpu.VMEM(shape, F32), pltpu.VMEM(shape, F32),
            pltpu.VMEM((n_rows,) + shape, F32), pltpu.VMEM((4,) + shape, F32),
        ]
        return bufs, [dma((n_rows + 4,)), dma((n_rows + 4,))]

    def copies(self, stage):
        p = self.p
        if stage == 0:
            return [send(self.src, self.pair, self.ss.at[0], self.rs.at[0], p.sibling)]
        if stage == 1:
            return [send(self.part.at[0], self.high, self.ss.at[1], self.rs.at[1], p.across)]
        if stage == 2:
            return [
                send(
                    self.part.at[1], self.rows.at[p.r], self.ss.at[1 + d], self.rs.at[1 + d],
                    p.row_peer(d),
                )
                for d in range(1, p.n_rows)
            ]
        return [
            send(
                self.part.at[2], self.quad.at[p.g], self.ss.at[p.n_rows + d],
                self.rs.at[p.n_rows + d], p.gr_peer(d),
            )
            for d in range(1, 4)
        ]

    def start(self, stage):
        for copy in self.copies(stage):
            copy.start()

    def finish(self, stage):
        p = self.p
        for copy in self.copies(stage):
            copy.wait_recv()
        if stage == 0:
            self.part[0] = self.src[...] + self.pair[...]
        elif stage == 1:
            self.part[1] = self.part[0] + self.high[...]
        elif stage == 2:
            self.rows[p.r] = self.part[1]
            total = self.rows[0]
            for d in range(1, p.n_rows):
                total = total + self.rows[d]
            self.part[2] = total
        else:
            self.quad[p.g] = self.part[2]
            self.out[...] = (self.quad[0] + self.quad[1]) + (self.quad[2] + self.quad[3])

    def wait_sends(self):
        for stage in range(4):
            for copy in self.copies(stage):
                copy.wait_send()


def view(g, n_rows):
    rows, x = g.shape
    per = rows // (n_rows * 8)
    return g.reshape(n_rows, 4, 2, per // 48, 48, x)


class Panels:
    def __init__(self, place, tile, tile_t, rows, cols, sems):
        self.p = place
        self.tile, self.tile_t, self.rows, self.cols = tile, tile_t, rows, cols
        self.ss, self.rs = sems

    @staticmethod
    def scratch(size):
        dma = pltpu.SemaphoreType.DMA
        part = size // 4
        return [
            pltpu.VMEM((4, part, size), BF), pltpu.VMEM((4, part, size), BF),
            pltpu.VMEM((3, part, size), BF), pltpu.VMEM((3, part, size), BF), dma((6,)), dma((6,)),
        ]

    def copies(self):
        p = self.p
        out = []
        for d in range(1, 4):
            for n, (src, dst, peer, at) in enumerate((
                (self.tile, self.rows, p.gc_peer(d), p.c), (self.tile_t, self.cols, p.gr_peer(d), p.g),
            )):
                at_sem = 3 * n + d - 1
                out.append(
                    send(
                        src.at[lax.rem(at + d, 4)], dst.at[d - 1], self.ss.at[at_sem],
                        self.rs.at[at_sem], peer,
                    )
                )
        return out

    def fill(self, mask, cot, scale):
        g_raw = cot[...].astype(F32) * scale * mask[...].astype(F32)
        self.tile[...] = g_raw.astype(BF).reshape(self.tile.shape)
        self.tile_t[...] = g_raw.T.astype(BF).reshape(self.tile_t.shape)

    def start(self):
        for copy in self.copies():
            copy.start()

    def collect(self, row_out, col_out):
        p = self.p
        for copy in self.copies():
            copy.wait()
        row_out[p.c] = self.tile[p.c]
        col_out[p.g] = self.tile_t[p.g]
        for d in range(1, 4):
            row_out[lax.rem(p.c + 4 - d, 4)] = self.rows[d - 1]
            col_out[lax.rem(p.g + 4 - d, 4)] = self.cols[d - 1]


class Spread:
    def __init__(self, place, blocks, sems):
        self.p = place
        self.e = blocks
        self.ss, self.rs = sems
        self.near = lax.rem(place.c + 2, 4)

    @staticmethod
    def scratch(shape):
        dma = pltpu.SemaphoreType.DMA
        return [pltpu.VMEM((4, 4) + shape, BF), dma((4, 4, 3)), dma((4, 4))]

    def hop(self, row, col, kind, peer):
        block = self.e.at[row, col]
        return send(block, block, self.ss.at[row, col, kind], self.rs.at[row, col], peer)

    def own(self, step, waiting):
        p = self.p
        for sign in (1, -1) if step else (0,):
            row = p.g + sign * step
            inside = (row >= 0) & (row <= 3)

            @pl.when(inside)
            def _(row=row, sign=sign):
                if step and not waiting:
                    self.hop(row, p.c, 0, p.sibling).wait_recv()
                go = "wait_send" if waiting else "start"
                getattr(self.hop(row, p.c, 0, p.sibling), go)()
                getattr(self.hop(row, p.c, 1, p.across), go)()
                for way in (1, -1) if step == 0 else (-sign,):
                    to = p.g + way

                    @pl.when((to >= 0) & (to <= 3))
                    def _(to=to, way=way):
                        if step == 0 and way == -1:
                            copy = send(
                                self.e.at[row, p.c], self.e.at[row, p.c], self.down.at[0],
                                self.rs.at[row, p.c], {"gr": to},
                            )
                        else:
                            copy = self.hop(row, p.c, 2, {"gr": to})
                        getattr(copy, go)()

    def relay(self, step, waiting):
        p = self.p
        for sign in (1, -1) if step else (0,):
            row = p.g + sign * step

            @pl.when((row >= 0) & (row <= 3))
            def _(row=row):
                copy = self.hop(row, self.near, 0, p.sibling)
                if waiting:
                    copy.wait_send()
                else:
                    copy.wait_recv()
                    copy.start()

    def arrive(self, rows, cols):
        for row in rows:
            for col in cols:
                self.hop(row, col, 0, self.p.sibling).wait_recv()


def pair_kernel(
    emb_ref, left_ref, right_ref, rowp_ref, colp_ref, mask_ref,
    logits_ref, gleft_ref, gright_ref, gemb_ref, e_ref, ss, rs, down, *, scale,
):
    place = Place(1)
    meet([place.sibling, place.across] + [place.gr_peer(d) for d in (1, 2, 3)])
    spread = Spread(place, e_ref, (ss, rs))
    spread.down = down
    p = place
    e_ref[p.g, p.c] = emb_ref[...]
    part, width = emb_ref.shape
    spread.own(0, False)
    spread.own(1, False)
    spread.relay(0, False)
    sib = p.u * 2 + 1 - p.core
    far = (1 - p.u) * 2 + 1 - p.core
    spread.arrive([p.g], [sib, far])
    left_rows = dot(e_ref[p.g].reshape(4 * part, width), left_ref[...]).astype(BF)
    spread.own(2, False)
    spread.relay(1, False)
    spread.own(3, False)
    right_cols = dot(e_ref[:, p.c].reshape(4 * part, width), right_ref[...]).astype(BF)
    spread.relay(2, False)
    logits_ref[...] = mask_ref[...].astype(F32) * dot(left_rows, right_cols, NT) * scale
    spread.relay(3, False)
    for d in range(1, 4):
        spread.arrive([lax.rem(p.g + d, 4)], [sib, far])
    row_sum = jnp.zeros((part, width), F32)
    col_sum = jnp.zeros((part, width), F32)
    for n in range(4):
        row_sum = row_sum + dot(rowp_ref[n], e_ref[:, n].reshape(4 * part, width))
        col_sum = col_sum + dot(colp_ref[n], e_ref[n].reshape(4 * part, width))

    def through(total, weight):
        high, low = hi_lo(total)
        return (dot(high, weight) + dot(low, weight)).astype(BF)

    g_left = through(row_sum, right_ref[...])
    g_right = through(col_sum, left_ref[...])
    emb_t = emb_ref[...].astype(F32).T.astype(BF)
    gleft_ref[...] = dot(emb_t, g_left).astype(BF)
    gright_ref[...] = dot(emb_t, g_right).astype(BF)
    gemb_ref[...] = dot(g_left, left_ref[...], NT) + dot(g_right, right_ref[...], NT)
    for step in range(4):
        spread.own(step, True)
        spread.relay(step, True)


def pair_head(emb, rel_left, rel_right, row_panel, col_panel, mask, scale):
    part, width = emb.shape
    size = mask.shape[0]
    vm = pl.BlockSpec(memory_space=pltpu.VMEM)
    dma = pltpu.SemaphoreType.DMA
    return pl.pallas_call(
        functools.partial(pair_kernel, scale=scale),
        in_specs=[vm] * 6,
        out_specs=[vm] * 4,
        out_shape=[
            jax.ShapeDtypeStruct((size, size), F32), jax.ShapeDtypeStruct(rel_left.shape, BF),
            jax.ShapeDtypeStruct(rel_right.shape, BF), jax.ShapeDtypeStruct((part, width), F32),
        ],
        scratch_shapes=Spread.scratch((part, width)) + [dma((1,))],
        compiler_params=pltpu.CompilerParams(
            collective_id=5, has_side_effects=True, vmem_limit_bytes=50 << 20
        ),
        name="pair_head",
    )(emb, rel_left, rel_right, row_panel, col_panel, mask)


def norm_back_chunk(g_out, rows, gain):
    average, inverse = norm_stats(rows)
    z = (rows - average) * inverse
    g_z = g_out * gain
    mean_g = jnp.mean(g_z, axis=-1, keepdims=True)
    mean_gz = jnp.mean(g_z * z, axis=-1, keepdims=True)
    return inverse * (g_z - mean_g - z * mean_gz), jnp.sum(g_out * z, axis=0, keepdims=True)


def put_lines(ref, at, row):
    for j in range(row.shape[1] // 128):
        ref[at + j : at + j + 1, :] = row[:, j * 128 : (j + 1) * 128]


def mlp_back_kernel(*refs, n_ext, units, spans, n_rows, comm, lag, window):
    (slope_ref, wd_ref, wu_ref, gmlp_ref, h2_ref, r1_ref, gy_ref, ctx_ref, wo_ref, gain_ref) = refs[:10]
    at = 10
    arrays = refs[at : at + n_ext]
    at += n_ext
    gup_ref, gr1_ref, gout_ref, gctx_ref, small_ref = refs[at : at + 5]
    at += 5
    outs = refs[at : at + len(spans)]
    at += len(spans)
    h2_buf, h2t_ref, acc_ref, r1_buf, gy_buf, ctx_buf, ctxt_ref, wo_buf, gatt_ref, in_sem = refs[at : at + 10]
    at += 10
    n_step = pl.num_programs(0)
    step = pl.program_id(0)
    count, feats = acc_ref.shape
    lines = feats // 128
    steps = (small_ref.shape[0] - 16) // lines - 4
    if comm:
        place = Place(n_rows)
        n = len(spans)
        shares = Shares(
            place, units, arrays, None, refs[at : at + n], refs[at + n : at + 2 * n],
            refs[at + 2 * n : at + 2 * n + 7], refs[at + 2 * n + 7 : at + 2 * n + 12],
        )

    def inputs():
        pairs = (
            (h2_ref, h2_buf), (ctx_ref, ctx_buf), (r1_ref, r1_buf), (gy_ref, gy_buf), (wo_ref, wo_buf),
        )
        return [pltpu.make_async_copy(a, b, in_sem.at[i]) for i, (a, b) in enumerate(pairs)]

    @pl.when(step == 0)
    def _():
        for copy in inputs():
            copy.start()
        if comm:
            meet(place.peers())
            shares.begin(window)
        acc_ref[...] = jnp.zeros_like(acc_ref)
        small_ref[...] = jnp.zeros_like(small_ref)

    def beat(part):
        if comm:
            for at_step in range(steps):
                @pl.when(step == at_step)
                def _(at_step=at_step):
                    shares.tick(2 * at_step + part, window, lag)

    g_act = dot(gmlp_ref[...], wd_ref[...], NT)
    g_wide = g_act * slope_ref[...].astype(F32)
    g_u = g_wide.astype(BF)
    bias = jnp.sum(g_u.astype(F32), axis=0, keepdims=True)
    acc_ref[...] += dot(g_u, wu_ref[...], NT)
    beat(0)

    @pl.when(step == 0)
    def _():
        inputs()[0].wait()
        for c in range(count // 128):
            sl = slice(c * 128, (c + 1) * 128)
            h2t_ref[:, sl] = h2_buf[sl, :].astype(F32).T.astype(BF)

    gup_ref[...] = dot(h2t_ref[...], g_u).astype(BF)
    for at_step in range(steps):
        @pl.when(step == at_step)
        def _(at_step=at_step):
            put_lines(small_ref, (4 + at_step) * lines, bias)
    beat(1)

    @pl.when(step == n_step - 1)
    def _():
        for copy in inputs()[1:]:
            copy.wait()
        gain_sum = jnp.zeros((1, feats), F32)
        bias_sum = jnp.zeros((1, feats), F32)
        chunk = 256
        for c in range(count // chunk):
            sl = slice(c * chunk, (c + 1) * chunk)
            g_out = acc_ref[sl, :]
            g_in, part = norm_back_chunk(g_out, r1_buf[sl, :], gain_ref[...])
            gain_sum = gain_sum + part
            bias_sum = bias_sum + jnp.sum(g_out, axis=0, keepdims=True)
            g_r1 = gy_buf[sl, :] + g_in
            gr1_ref[sl, :] = g_r1
            gatt_ref[sl, :] = g_r1.astype(BF)
        put_lines(small_ref, 2 * lines, gain_sum)
        put_lines(small_ref, 3 * lines, bias_sum)
        if comm:
            shares.tick(2 * steps, window, lag)
        for c in range(count // 128):
            sl = slice(c * 128, (c + 1) * 128)
            ctxt_ref[:, sl] = ctx_buf[sl, :].astype(F32).T.astype(BF)
        gctx_ref[...] = dot(gatt_ref[...], wo_buf[...], NT).astype(BF)
        if comm:
            shares.tick(2 * steps + 1, window, lag)
        gout_ref[...] = dot(ctxt_ref[...], gatt_ref[...]).astype(BF)
        if comm:
            for t in range(2 * steps + 2, shares.ticks(lag)):
                shares.tick(t, window, lag)
            shares.deliver(outs, spans)
            shares.wait_sends()


def mlp_backward(
    slope, w_down, w_up, g_mlp, h2, r1, g_y, ctx, w_out, gain, small_rows, left, right, down, n_rows, comm
):
    count, feats = g_mlp.shape
    hidden = slope.shape[1]
    steps = hidden // feats
    vm = pl.BlockSpec(memory_space=pltpu.VMEM)
    any_ref = pl.BlockSpec(memory_space=pl.ANY)
    lag, window = 2, 4
    units, sizes, spans = (), [], []
    views = []
    if comm:
        views = [view(g, n_rows) for g in (left, right, down)]
        units = (
            (0, 0, 0, True, None), (2, 0, 0, False, None), (1, 0, 0, True, None), (2, 2, 0, False, None),
        )
        sizes = [(24, feats), (24, feats), (48, feats)]
        spans = [[(0, PIECE, PIECE)]] * 3
    scratch = [
        pltpu.VMEM((count, feats), BF), pltpu.VMEM((feats, count), BF), pltpu.VMEM((count, feats), F32),
        pltpu.VMEM((count, feats), F32), pltpu.VMEM((count, feats), F32), pltpu.VMEM((count, feats), BF),
        pltpu.VMEM((feats, count), BF), pltpu.VMEM((feats, feats), BF), pltpu.VMEM((count, feats), BF),
        pltpu.SemaphoreType.DMA((5,)),
    ]
    params = dict(vmem_limit_bytes=63 << 20, dimension_semantics=("arbitrary",))
    if comm:
        fins, got, bufs, sems = Shares.scratch(units, sizes, n_rows)
        scratch += fins + got + bufs + sems
        params.update(collective_id=3, has_side_effects=True)
    return pl.pallas_call(
        functools.partial(
            mlp_back_kernel, n_ext=len(views), units=units, spans=spans, n_rows=n_rows, comm=comm,
            lag=lag, window=window,
        ),
        grid=(steps,),
        in_specs=[
            pl.BlockSpec((count, feats), lambda f: (0, f)),
            pl.BlockSpec((feats, feats), lambda f: (f, 0)),
            pl.BlockSpec((feats, feats), lambda f: (0, f)),
            vm, any_ref, any_ref, any_ref, any_ref, any_ref, vm,
        ] + [any_ref] * len(views),
        out_specs=[pl.BlockSpec((feats, feats), lambda f: (0, f)), vm, vm, vm, vm] + [vm] * len(sizes),
        out_shape=[
            jax.ShapeDtypeStruct((feats, hidden), BF), jax.ShapeDtypeStruct((count, feats), F32),
            jax.ShapeDtypeStruct((feats, feats), BF), jax.ShapeDtypeStruct((count, feats), BF),
            jax.ShapeDtypeStruct((small_rows, 128), F32),
        ] + [jax.ShapeDtypeStruct(size, F32) for size in sizes],
        scratch_shapes=scratch,
        compiler_params=pltpu.CompilerParams(**params),
        name="mlp_backward",
    )(slope, w_down, w_up, g_mlp, h2, r1, g_y, ctx, w_out, gain.reshape(1, feats), *views)


def deliver_kernel(gx_ref, small_ref, *refs, parts, heads):
    n_in = sum(parts)
    ins, outs = refs[:n_in], refs[n_in:]
    outs[0][...] = gx_ref[...]

    @pl.when(pl.program_id(0) == 0)
    def _():
        at = 0
        for k, n in enumerate(parts):
            out = outs[1 + k]
            row = 0
            for ref in ins[at : at + n]:
                rows, x = ref.shape
                per = x // 128
                for j in range(per):
                    out[pl.ds(row + j, rows, stride=per), :] = ref[:, j * 128 : (j + 1) * 128]
                row += rows * per
            at += n
        line = 0
        for out in outs[1 + len(parts) :]:
            if len(out.shape) == 1:
                for j in range(out.shape[0] // 128):
                    out[j * 128 : (j + 1) * 128] = small_ref[line]
                    line += 1
            else:
                out[...] = small_ref[line : line + out.shape[0], :]


def deliver(g_tokens, small, shares, features, hidden, heads):
    count = g_tokens.shape[0]
    flat = [p for group in shares for p in group]
    vm = pl.BlockSpec(memory_space=pltpu.VMEM)
    block = count // 4
    sizes = [sum(p.size for p in group) for group in shares]
    results = pl.pallas_call(
        functools.partial(deliver_kernel, parts=tuple(len(group) for group in shares), heads=heads),
        grid=(4,),
        in_specs=[pl.BlockSpec((block, features), lambda i: (i, 0)), vm] + [vm] * len(flat),
        out_specs=[pl.BlockSpec((block, features), lambda i: (i, 0))] + [vm] * (len(shares) + 6),
        out_shape=[jax.ShapeDtypeStruct(g_tokens.shape, F32)]
        + [jax.ShapeDtypeStruct((size // 128, 128), F32) for size in sizes]
        + [jax.ShapeDtypeStruct((features,), F32)] * 4
        + [jax.ShapeDtypeStruct((hidden,), F32), jax.ShapeDtypeStruct((heads, 128), F32)],
        name="deliver",
    )(g_tokens, small, *flat)
    return (
        results[0], [r.reshape(-1) for r in results[1 : 1 + len(shares)]], results[1 + len(shares) :]
    )


def back_kernel(*refs, n_ext, units, spans, n_rows, comm, lag, window):
    (q_ref, k_ref, v_ref, e_ref, linv_ref, ctx_ref, gctx_ref, boxr_ref, boxc_ref, w_ref, h1_ref,
     x_ref, gr1_ref, gain_ref, small_ref) = refs[:15]
    at = 15
    arrays = refs[at : at + n_ext]
    at += n_ext
    gx_ref = refs[at]
    small_out = refs[at + 1]
    at += 2
    if comm:
        outs = refs[at : at + n_ext + 1]
        at += n_ext + 1
    else:
        grad_ref = refs[at]
        at += 1
    (oha_ref, ohbt_ref, cx_ref, cy_ref, g_ref, gcx_ref, gcy_ref, lt_ref, gt_ref, gall_ref, h1t_ref,
     hist_ref, h1_buf, x_buf, gr1_buf, w_buf, pack_ref, in_sem) = refs[at : at + 18]
    at += 18
    length = q_ref.shape[0]
    half, quarter = 64, 32
    pairs, seqs = pl.num_programs(0), pl.num_programs(1)
    hp = pl.program_id(0)
    s_id = pl.program_id(1)
    n_seq = cx_ref.shape[0]
    n_pair = hist_ref.shape[0] // 2
    lane = lax.broadcasted_iota(jnp.int32, (1, 128), 1)
    low = lane < 64
    if comm:
        place = Place(n_rows)
        staging = refs[at]
        fins = refs[at + 1 : at + n_ext + 2]
        at += n_ext + 2
        got = refs[at : at + n_ext + 1]
        at += n_ext + 1
        shares = Shares(
            place, units, arrays, staging, fins, got, refs[at : at + 7], refs[at + 7 : at + 12]
        )
        at += 12
        total = Total(place, pack_ref, small_out, refs[at : at + 5], refs[at + 5 : at + 7])

    def inputs():
        return (
            pltpu.make_async_copy(h1_ref, h1_buf, in_sem.at[0]),
            pltpu.make_async_copy(x_ref, x_buf, in_sem.at[1]),
            pltpu.make_async_copy(gr1_ref, gr1_buf, in_sem.at[2]),
            pltpu.make_async_copy(w_ref, w_buf, in_sem.at[3]),
        )

    @pl.when((hp == 0) & (s_id == 0))
    def _():
        for copy in inputs():
            copy.start()
        hist_ref[...] = jnp.zeros_like(hist_ref)
        if comm:
            meet(place.peers())
            shares.begin(window)

    @pl.when(hp == 0)
    def _():
        bc = boxc_ref[...]
        ax, _ = key_side(bc[:, 0:1], bc[:, 2:3], half)
        ay, _ = key_side(bc[:, 1:2], bc[:, 3:4], half)
        _, fbx = query_side(bc[:, 0:1], bc[:, 2:3], half)
        _, fby = query_side(bc[:, 1:2], bc[:, 3:4], half)
        spot = (lane % quarter).astype(F32)
        is_x = (lane % half) < quarter
        oha = jnp.where(jnp.where(is_x, ax, ay) == spot, jnp.where(low, 1.0, 0.0), 0.0)
        oha_ref[s_id] = oha.astype(BF)
        br = boxr_ref[...]
        _, gax = key_side(br[0:1], br[2:3], half)
        _, gay = key_side(br[1:2], br[3:4], half)
        rbx, _ = query_side(br[0:1], br[2:3], half)
        rby, _ = query_side(br[1:2], br[3:4], half)
        row = lax.broadcasted_iota(jnp.int32, (half, length), 0)
        rspot = (row % quarter).astype(F32)
        ohbt_ref[s_id] = jnp.where(jnp.where(row < quarter, rbx, rby) == rspot, 1.0, 0.0).astype(BF)
        cx_ref[s_id] = jnp.where(gax + fbx >= SPAN, 1.0, 0.0).astype(BF)
        cy_ref[s_id] = jnp.where(gay + fby >= SPAN, 1.0, 0.0).astype(BF)

    @pl.when((hp == 0) & (s_id == n_seq - 1))
    def _():
        inputs()[0].wait()
        for c in range(h1_buf.shape[0] // 128):
            sl = slice(c * 128, (c + 1) * 128)
            h1t_ref[:, sl] = h1_buf[sl, :].astype(F32).T.astype(BF)

    k = k_ref[...]
    v = v_ref[...]
    lt_ref[...] = q_ref[...].astype(F32).T.astype(BF)
    gc = gctx_ref[...].astype(F32) * linv_ref[...]
    gcb = gc.astype(BF)
    gt_ref[...] = gcb.astype(F32).T.astype(BF)
    prod = gc * ctx_ref[...].astype(F32)
    ohbt = ohbt_ref[s_id]
    kts = []
    vts = []
    rows = 256
    n_step = n_pair * n_seq
    step = hp * n_seq + s_id
    for a in range(2):
        if comm and a == 1:
            for at_step in range(n_step):
                @pl.when(step == at_step)
                def _(at_step=at_step):
                    shares.tick(2 * at_step, window, lag)
        mine = low if a == 0 else jnp.logical_not(low)
        other = 64 - 64 * a
        d = jnp.sum(jnp.where(mine, prod, 0.0), axis=1, keepdims=True)
        dhi = d.astype(BF).astype(F32)
        extra = jnp.where(lane == other, dhi, jnp.where(lane == other + 1, d - dhi, 0.0))
        lhs = jnp.where(mine, gcb.astype(F32), extra).astype(BF)
        minus = jnp.where((lane == other) | (lane == other + 1), -1.0, 0.0).astype(BF)
        rhs = jnp.where(mine, v, minus)
        for c in range(length // rows):
            sl = slice(c * rows, (c + 1) * rows)
            gp = dot(lhs[sl], rhs, NT)
            g = (gp * e_ref[a, sl, :].astype(F32)).astype(BF)
            g_ref[a, sl, :] = g
            gcx_ref[a, sl, :] = g * cx_ref[s_id, sl, :]
            gcy_ref[a, sl, :] = g * cy_ref[s_id, sl, :]
        left = jnp.concatenate([lt_ref[64 * a : 64 * a + 64, :], ohbt], axis=0)
        r0 = dot(left, g_ref[a])
        rx = dot(ohbt[:quarter], gcx_ref[a])
        ry = dot(ohbt[quarter:], gcy_ref[a])
        vts.append(dot(gt_ref[64 * a : 64 * a + 64, :], e_ref[a]))
        kts.append(r0[:64])
        w = jnp.concatenate([r0[64:], rx, ry], axis=0)
        whi, wlo = hi_lo(w)
        red = dot(jnp.concatenate([whi, wlo], axis=0), oha_ref[s_id])
        hist_ref[2 * hp + a] += red[:128] + red[128:]
    zero = jnp.zeros_like(k)
    gq = dot(g_ref[0], jnp.where(low, k, zero)) + dot(g_ref[1], jnp.where(low, zero, k))
    own_rows = pl.ds(pl.multiple_of(s_id * length, length), length)
    feats = h1_buf.shape[1]
    parts = [pl.ds(pl.multiple_of(p * feats + hp * 128, 128), 128) for p in range(3)]
    gall_ref[own_rows, parts[0]] = (gq * 0.125).astype(BF)
    gall_ref[own_rows, parts[1]] = (jnp.concatenate(kts, axis=0) * 0.125).T.astype(BF)
    gall_ref[own_rows, parts[2]] = jnp.concatenate(vts, axis=0).T.astype(BF)

    @pl.when(s_id == n_seq - 1)
    def _():
        g_pair = jnp.concatenate([gall_ref[:, part] for part in parts], axis=1)
        piece = dot(h1t_ref[...], g_pair).astype(BF)
        if comm:
            staging[lax.div(hp, 2), lax.rem(hp, 2)] = piece.reshape(staging.shape[2:])
        else:
            grad_ref[0] = piece[:, :128]
            grad_ref[1] = piece[:, 128:256]
            grad_ref[2] = piece[:, 256:]

    if comm:
        for at_step in range(n_step):
            @pl.when(step == at_step)
            def _(at_step=at_step):
                for i, unit in enumerate(shares.units):
                    if unit[4] is not None and (2 * unit[4] + 2) * n_seq - 1 == at_step:
                        shares.start(i, 0)
                if at_step < n_step - 1:
                    shares.tick(2 * at_step + 1, window, lag)

    @pl.when((hp == n_pair - 1) & (s_id == n_seq - 1))
    def _():
        for copy in inputs()[1:]:
            copy.wait()
        gain = gain_ref[...]
        count = x_buf.shape[0]
        chunk = 256
        beat = 2 * n_step - 1
        gain_sum = jnp.zeros((1, feats), F32)
        bias_sum = jnp.zeros((1, feats), F32)
        pack_ref[...] = small_ref[...]
        base = pack_ref.shape[0] - 16
        for h in range(2 * n_pair):
            w = hist_ref[h]
            line = jnp.zeros((1, 128), F32)
            for axis in range(2):
                plain = w[axis * quarter : (axis + 1) * quarter]
                carry = w[half + axis * quarter : half + (axis + 1) * quarter]
                keep = (lane >= axis * quarter) & (lane < (axis + 1) * quarter)
                stay = jnp.where(keep, plain - carry, 0.0)
                move = jnp.where(keep, carry, 0.0)
                shift = axis * (half - quarter)
                stay = pltpu.roll(stay, shift, 1, stride=1, stride_axis=0)
                move = pltpu.roll(move, shift + 1, 1, stride=1, stride_axis=0)
                line = line + jnp.sum(stay + move, axis=0, keepdims=True)
            pack_ref[base + h : base + h + 1, :] = line
        for c in range(count // chunk):
            sl = slice(c * chunk, (c + 1) * chunk)
            g_out = dot(gall_ref[sl, :], w_buf[...], NT)
            g_in, part = norm_back_chunk(g_out, x_buf[sl, :].astype(F32), gain)
            gx_ref[sl, :] = gr1_buf[sl, :] + g_in
            gain_sum = gain_sum + part
            bias_sum = bias_sum + jnp.sum(g_out, axis=0, keepdims=True)
            if comm:
                for t in range(beat, beat + 2):
                    shares.tick(t, window, lag)
                beat += 2
        lines = feats // 128
        put_lines(pack_ref, 0, gain_sum)
        put_lines(pack_ref, lines, bias_sum)
        if comm:
            total.start(0)
            stage = 0
            for t in range(beat, shares.ticks(lag)):
                shares.tick(t, window, lag)
                if (t - beat) % 2 == 1 and stage < 4:
                    total.finish(stage)
                    if stage < 3:
                        total.start(stage + 1)
                    stage += 1
            shares.deliver(outs, spans)
            total.wait_sends()
            shares.wait_sends()
        else:
            small_out[...] = pack_ref[...]


def attend_and_project_backward(
    qkv, e, linv, ctx, gctx, boxes_r, boxes_c, weight, h1, tokens, g_r1, gain, small, arrays,
    chosen, n_rows, comm
):
    count, width = qkv.shape
    feats = width // 3
    heads, seqs, length, _ = e.shape
    pairs = heads // 2
    rows_of = lambda off: pl.BlockSpec((length, 128), lambda h, s: (s, off + h))
    any_ref = pl.BlockSpec(memory_space=pl.ANY)
    vm = pl.BlockSpec(memory_space=pltpu.VMEM)
    views = [view(g, n_rows) for g in arrays] if comm else []
    n_ext = len(views)
    lag, window = 8, 4
    external = [
        (k, s, j, n % 2 == 0, None) for n, (k, s, j) in enumerate(chosen)
    ] if comm else []
    units = [None] * (4 * pairs + 3)
    for t in range(pairs // 2):
        units[8 * t + 9] = (n_ext, 0, t, t % 2 == 0, t)
    for unit, slot in zip(external, (0, 2, 4, 7, 12, 14, 20)):
        units[slot] = unit
    units = tuple(units)
    out_shape = [jax.ShapeDtypeStruct((count, feats), F32), jax.ShapeDtypeStruct(small.shape, F32)]
    out_specs = [vm, vm]
    spans = []
    scratch = [
        pltpu.VMEM((seqs, length, 128), BF), pltpu.VMEM((seqs, 64, length), BF),
        pltpu.VMEM((seqs, length, length), BF), pltpu.VMEM((seqs, length, length), BF),
        pltpu.VMEM((2, length, length), BF), pltpu.VMEM((2, length, length), BF),
        pltpu.VMEM((2, length, length), BF), pltpu.VMEM((128, length), BF),
        pltpu.VMEM((128, length), BF), pltpu.VMEM((count, width), BF), pltpu.VMEM((feats, count), BF),
        pltpu.VMEM((heads, 128, 128), F32), pltpu.VMEM((count, feats), BF),
        pltpu.VMEM((count, feats), BF), pltpu.VMEM((count, feats), F32), pltpu.VMEM((feats, width), BF),
        pltpu.VMEM(small.shape, F32), pltpu.SemaphoreType.DMA((4,)),
    ]
    params = dict(vmem_limit_bytes=63 << 20, dimension_semantics=("arbitrary", "arbitrary"))
    if comm:
        sizes = [(24 if g.shape[3] == 1 else 48, g.shape[5]) for g in views] + [(24, width)]
        for rows, x in sizes[:-1]:
            spans.append([(j * 2 * PIECE, PIECE, PIECE) for j in range(x // (2 * PIECE))])
        spans.append(
            [(p * feats + t * 256, 128, 128) for t in range(pairs // 2) for p in range(3)]
        )
        out_shape += [jax.ShapeDtypeStruct(size, F32) for size in sizes]
        out_specs += [vm] * len(sizes)
        fins, got, bufs, sems = Shares.scratch(units, sizes, n_rows)
        tbufs, tsems = Total.scratch(small.shape, n_rows)
        scratch += [pltpu.VMEM((pairs // 2, 2, n_rows, 4, 2, 48, PIECE), BF)]
        scratch += fins + got + bufs + sems + tbufs + tsems
        params.update(collective_id=2, has_side_effects=True)
    else:
        out_shape.append(jax.ShapeDtypeStruct((3, feats, feats), BF))
        out_specs.append(pl.BlockSpec((3, feats, 128), lambda h, s: (0, 0, h)))
    results = pl.pallas_call(
        functools.partial(
            back_kernel, n_ext=n_ext, units=units, spans=spans, n_rows=n_rows, comm=comm, lag=lag,
            window=window,
        ),
        grid=(pairs, seqs),
        in_specs=[
            rows_of(0), rows_of(pairs), rows_of(2 * pairs),
            pl.BlockSpec((2, None, length, length), lambda h, s: (h, s, 0, 0)),
            rows_of(0), rows_of(0), rows_of(0),
            pl.BlockSpec((4, length), lambda h, s: (0, s)),
            pl.BlockSpec((length, 4), lambda h, s: (s, 0)),
            any_ref, any_ref, any_ref, any_ref, vm, vm,
        ] + [any_ref] * n_ext,
        out_specs=out_specs,
        out_shape=out_shape,
        scratch_shapes=scratch,
        compiler_params=pltpu.CompilerParams(**params),
        name="attend_backward",
    )(
        qkv, qkv, qkv, e, linv, ctx, gctx, boxes_r, boxes_c, weight, h1, tokens, g_r1,
        gain.reshape(1, feats), small, *views,
    )
    return results


EPSILON = 1e-05


def norm_stats(rows):
    average = jnp.mean(rows, axis=-1, keepdims=True)
    centred = rows - average
    variance = jnp.mean(centred * centred, axis=-1, keepdims=True)
    return average, lax.rsqrt(variance + EPSILON)


def gelu_pair(u):
    bell = jnp.exp(u * u * -0.5)
    t = 1.0 / (1.0 + (0.3275911 * math.sqrt(0.5)) * jnp.abs(u))
    series = t * (
        0.254829592
        + t * (-0.284496736 + t * (1.421413741 + t * (-1.453152027 + t * 1.061405429)))
    )
    tail = 0.5 * series * bell
    below = jnp.where(u < 0.0, tail, 1.0 - tail)
    return u * below, below + u * bell * (1.0 / math.sqrt(2.0 * math.pi))


def body(
    tokens, boxes, page_ids, seg_ids, pair_mask, ln1_gain, ln1_bias, query_key_value_weight,
    attention_output_weight, ln2_gain, ln2_bias, up_projection_weight, up_projection_bias,
    down_projection_weight, box_table, rel_left, rel_right, cot_out, cot_logits,
):
    sequences, length = page_ids.shape
    count = sequences * length
    features = tokens.shape[1]
    x = tokens.astype(F32)
    average1, inverse1 = norm_stats(x)
    h1 = ((x - average1) * inverse1 * ln1_gain + ln1_bias).astype(BF)
    qkv = dot(h1, query_key_value_weight).astype(BF)
    boxes_c = boxes.T
    pair_scale = 1.0 / math.sqrt(rel_left.shape[1])
    ctx, e, linv, row_panel, col_panel = attend_forward(
        qkv, boxes, boxes_c, page_ids[:, None, :], page_ids.reshape(-1, 1), box_table, pair_mask[0],
        cot_logits[0], pair_scale,
    )
    r1 = x + dot(ctx, attention_output_weight)
    average2, inverse2 = norm_stats(r1)
    h2 = ((r1 - average2) * inverse2 * ln2_gain + ln2_bias).astype(BF)
    act, slope = gelu_pair(dot(h2, up_projection_weight) + up_projection_bias)
    act = act.astype(BF)
    slope = slope.astype(BF)
    layer_out = (r1 + dot(act, down_projection_weight)).astype(BF)

    slots = 64
    member = seg_ids[:, :, None] == lax.iota(jnp.int32, slots)[None, None, :]
    members = member.astype(BF)
    counts = jnp.sum(member.astype(F32), axis=1)
    pooled = jnp.einsum(
        "stg,std->sgd", members, layer_out.reshape(sequences, length, features),
        preferred_element_type=F32,
    ) / counts[:, :, None]
    embedded = pooled.reshape(sequences * slots, features).astype(BF)
    pair_logits, grad_rel_left, grad_rel_right, g_emb = pair_head(
        embedded, rel_left, rel_right, row_panel, col_panel, pair_mask[0], pair_scale
    )
    TN = (((0,), (0,)), ((), ()))
    g_seg = (g_emb.reshape(sequences, slots, features) / counts[:, :, None])
    seg_hi, seg_lo = hi_lo(g_seg)
    spread = jnp.einsum("stg,sgd->std", members, seg_hi, preferred_element_type=F32) + jnp.einsum(
        "stg,sgd->std", members, seg_lo, preferred_element_type=F32
    )
    g_y = cot_out.astype(F32) + spread.reshape(count, features)
    g_mlp = g_y.astype(BF)
    grad_down = dot(act, g_mlp, TN).astype(BF)
    n_rows = lax.axis_size("rows")
    comm = n_rows * 8 * 48 <= features
    heads = box_table.shape[0]
    hidden = slope.shape[1]
    small_rows = (4 * features + hidden) // 128 + 16
    grad_up, g_r1, grad_out, g_ctx, small, *early = mlp_backward(
        slope, down_projection_weight, up_projection_weight, g_mlp, h2, r1, g_y, ctx,
        attention_output_weight, ln2_gain, small_rows, grad_rel_left, grad_rel_right, grad_down,
        n_rows, comm,
    )
    g_tokens, small, *late = attend_and_project_backward(
        qkv, e, linv, ctx, g_ctx, boxes, boxes_c, query_key_value_weight, h1, tokens, g_r1, ln1_gain,
        small, (grad_down, grad_out, grad_up),
        ((0, 1, 0), (0, 3, 0), (1, 0, 0), (2, 0, 0), (2, 0, 1), (2, 0, 2), (2, 0, 3)), n_rows, comm,
    )
    if comm:
        down, out, up, qkv_part = late
        shares = [[early[0]], [early[1]], [out], [early[2], down], [up], [qkv_part]]
    else:
        grad_qkv = jnp.concatenate([late[0][0], late[0][1], late[0][2]], axis=1)
        flats = [
            lax.psum_scatter(g, AXES, scatter_dimension=0, tiled=True).astype(F32).reshape(-1)
            for g in (grad_rel_left, grad_rel_right, grad_out, grad_down, grad_up, grad_qkv)
        ]
        shares = [[flat.reshape(-1, 128)] for flat in flats]
        small = lax.psum(small, AXES)
    grad_tokens, flats, vectors = deliver(g_tokens, small, shares, features, hidden, heads)
    left_share, right_share, out_share, down_share, up_share, qkv_share = flats
    return (
        layer_out, pair_logits[None], grad_tokens, vectors[0], vectors[1], qkv_share, out_share,
        vectors[2], vectors[3], up_share, vectors[4], down_share, vectors[5], left_share, right_share,
    )


def solution(mesh):
    whole = P(AXES, None)
    tile = P("rows", "gr", "gc")
    flat = P(AXES)
    one = P()
    in_specs = (
        whole, P(None, AXES), whole, whole, tile, one, one, one, one, one, one, one, one, one, one,
        one, one, whole, tile,
    )
    out_specs = (
        whole, tile, whole, one, one, flat, flat, one, one, flat, one, flat, one, flat, flat,
    )
    return jax.shard_map(body, mesh=mesh, in_specs=in_specs, out_specs=out_specs, check_vma=False)
```

```python
import functools
import math

import jax
import jax.numpy as jnp
from jax import lax
from jax.experimental import pallas as pl
from jax.experimental.pallas import tpu as pltpu
from jax.sharding import PartitionSpec as P

COORD=1000
SPAN=2*COORD+1
LOG2E=1.4426950408889634
BARRED=-2.0**99
SLOTS=64
BF=jnp.bfloat16
F32=jnp.float32
NT=(((1,),(1,)),((),()))
NN=(((1,),(0,)),((),()))
def dot(a,b,dims=NN):
    return lax.dot_general(a,b,dims,preferred_element_type=F32)

def whole_and_rest(scaled):
    whole=jnp.floor((scaled+0.5)*(1.0/SPAN))
    return whole, scaled-SPAN*whole

def key_side(low, high, half):
    c=jnp.floor((low+high).astype(F32)*0.5)
    return whole_and_rest(c*half)
def query_side(low, high, half):
    c=jnp.floor((low+high).astype(F32)*0.5)
    return whole_and_rest((COORD-c)*half)

def hi_lo(v):
    hi=v.astype(BF)
    return hi, (v-hi.astype(F32)).astype(BF)

def fwd_kernel(q_ref,k_ref,v_ref,boxr_ref,boxc_ref,tab_ref,mask_ref,cot_ref,
               ctx_ref,e_ref,linv_ref,rowp_ref,colp_ref,
               ohb_ref,oha_ref,kg_ref,rxy_ref,pg_ref,cx_ref,cy_ref,*panel_refs,rows,pair_scale):
    length=q_ref.shape[0]
    half=tab_ref.shape[1]//2
    quarter=half//2
    hp=pl.program_id(1)
    seq=pl.program_id(0)
    place=Place(1)
    mask_buf,cot_buf,in_sem=panel_refs[:3]
    panels=Panels(place,*panel_refs[3:7],panel_refs[7:])
    def inputs():
        return (pltpu.make_async_copy(mask_ref,mask_buf,in_sem.at[0]),
                pltpu.make_async_copy(cot_ref,cot_buf,in_sem.at[1]))
    @pl.when((hp==0)&(seq==0))
    def _():
        for copy in inputs():
            copy.start()
    @pl.when((hp==1)&(seq==0))
    def _():
        for copy in inputs():
            copy.wait()
        panels.fill(mask_buf,cot_buf,pair_scale)
        meet([place.gc_peer(d) for d in (1,2,3)]+[place.gr_peer(d) for d in (1,2,3)])
    @pl.when((hp==2)&(seq==0))
    def _():
        panels.start()
    lane=lax.broadcasted_iota(jnp.int32,(1,128),1)
    low=lane<64
    @pl.when(hp==0)
    def _():
        bc=boxc_ref[...]
        ax,fax=key_side(bc[:,0:1],bc[:,2:3],half)
        ay,fay=key_side(bc[:,1:2],bc[:,3:4],half)
        bx,fbx=query_side(bc[:,0:1],bc[:,2:3],half)
        by,fby=query_side(bc[:,1:2],bc[:,3:4],half)
        spot=(lane%quarter).astype(F32)
        is_x=(lane%half)<quarter
        oha=jnp.where(jnp.where(is_x,ax,ay)==spot,1.0,0.0)
        ohb=jnp.where(jnp.where(is_x,bx,by)==(quarter-1)-spot,1.0,0.0)
        ohb_ref[...]=jnp.where(low,ohb,0.0).astype(BF)
        oha_ref[...]=oha.astype(BF)
        page=bc[:,4:5].astype(jnp.int32)
        mine=(lane%64)==page
        barred=jnp.where((lane%64)<4,jnp.where(mine,0.0,BARRED),0.0)
        kg_ref[0]=jnp.where(low,oha,barred).astype(BF)
        kg_ref[1]=jnp.where(low,barred,oha).astype(BF)
        pg_ref[...]=jnp.where(mine,1.0,0.0).astype(BF)
        ohx=jnp.where(ax==spot,1.0,0.0)
        ohy=jnp.where(ay==spot,1.0,0.0)
        rxy_ref[pl.ds(0,length),:]=jnp.where(low,ohx,0.0).astype(BF)
        rxy_ref[pl.ds(length,length),:]=jnp.where(low,0.0,ohy).astype(BF)
        br=boxr_ref[...]
        _,gax=key_side(br[0:1],br[2:3],half)
        _,gay=key_side(br[1:2],br[3:4],half)
        cx_ref[...]=jnp.where(gax+fbx>=SPAN,1.0,0.0)
        cy_ref[...]=jnp.where(gay+fby>=SPAN,1.0,0.0)
    k=k_ref[...]
    v=v_ref[...]
    oha=oha_ref[...]
    b_row=lax.broadcasted_iota(jnp.int32,(half,128),0)
    l_col=lax.broadcasted_iota(jnp.int32,(half,128),1)
    row_x=b_row<quarter
    same_axis=row_x==((l_col%half)<quarter)
    d_axis=row_x==(l_col<half)
    heads=[]
    for a in range(2):
        t=tab_ref[pl.ds(2*hp+a,1),:]
        both=[jnp.where(low,t,0.0)+pltpu.roll(jnp.where(low,t,0.0),64,1),
              jnp.where(low,0.0,t)+pltpu.roll(jnp.where(low,0.0,t),64,1)]
        tiles=[]
        for b in both:
            spreads=[]
            for first in (0,1):
                whole=jnp.broadcast_to(b,(quarter,128))
                turned=pltpu.roll(whole,128-(quarter-1)-first,1,stride=1,stride_axis=0)
                lowq=jnp.where(lane<quarter,turned,0.0)
                pair=lowq+pltpu.roll(lowq,quarter,1)
                spreads.append(pair+pltpu.roll(pair,64,1))
            tiles.append(spreads)
        base=jnp.concatenate([tiles[0][0],tiles[1][0]],axis=0)
        nxt=jnp.concatenate([tiles[0][1],tiles[1][1]],axis=0)
        hi,lo=hi_lo(base)
        dhi,dlo=hi_lo(nxt-base)
        z=jnp.zeros_like(hi)
        is_hi=(l_col<64)==(a==1)
        g0=jnp.where(same_axis,jnp.where(is_hi,hi.astype(F32),lo.astype(F32)),0.0).astype(BF)
        g1=jnp.where(d_axis,jnp.where((l_col%half)<quarter,dhi.astype(F32),dlo.astype(F32)),0.0).astype(BF)
        hk=jnp.concatenate([g0,g1],axis=1)
        left=dot(ohb_ref[:,0:half],hk).astype(BF)
        if a==0:
            rhs=jnp.concatenate([jnp.where(low,k,oha),kg_ref[0]],axis=1)
            vv=jnp.where(low,v,jnp.ones_like(v))
        else:
            rhs=jnp.concatenate([jnp.where(low,oha,k),kg_ref[1]],axis=1)
            vv=jnp.where(low,jnp.ones_like(v),v)
        heads.append((left,rhs,vv))
    for c in range(length//rows):
        sl=pl.ds(c*rows,rows)
        q=q_ref[sl,:]*jnp.asarray(0.125,BF)
        pg=pg_ref[sl,:]
        outs=[]
        for a in range(2):
            left,rhs,vv=heads[a]
            lc=left[c*rows:(c+1)*rows]
            g0=lc[:,:128]
            if a==0:
                lhs=jnp.concatenate([jnp.where(low,q,g0),jnp.where(low,g0,pg)],axis=1)
            else:
                lhs=jnp.concatenate([jnp.where(low,g0,q),jnp.where(low,pg,g0)],axis=1)
            s=dot(lhs,rhs,NT)
            dxy=dot(lc[:,128:],rxy_ref[...],NT)
            s=s+cx_ref[sl,:]*dxy[:,:length]+cy_ref[sl,:]*dxy[:,length:]
            m=jnp.max(s,axis=1,keepdims=True)
            e=jnp.exp2((s-m)*LOG2E).astype(BF)
            e_ref[a,sl,:]=e
            outs.append(dot(e,vv))
        ctx=jnp.where(low,outs[0],outs[1])
        tot=jnp.where(low,pltpu.roll(outs[0],64,1),pltpu.roll(outs[1],64,1))
        linv=1.0/tot
        linv_ref[sl,:]=linv
        ctx_ref[sl,:]=(ctx*linv).astype(BF)
    @pl.when((hp==pl.num_programs(1)-1)&(seq==pl.num_programs(0)-1))
    def _():
        panels.collect(rowp_ref,colp_ref)

def attend_forward(qkv,boxes_r,boxes_c,seqs,table,mask,cot,pair_scale,rows=512):
    tokens,width=qkv.shape
    feats=width//3
    length=tokens//seqs
    heads=table.shape[0]
    pairs=heads//2
    return pl.pallas_call(
        functools.partial(fwd_kernel,rows=rows,pair_scale=pair_scale),
        grid=(seqs,pairs),
        in_specs=[
            pl.BlockSpec((length,128),lambda s,h:(s,h)),
            pl.BlockSpec((length,128),lambda s,h:(s,pairs+h)),
            pl.BlockSpec((length,128),lambda s,h:(s,2*pairs+h)),
            pl.BlockSpec((4,length),lambda s,h:(0,s)),
            pl.BlockSpec((length,128),lambda s,h:(s,0)),
            pl.BlockSpec(table.shape,lambda s,h:(0,0)),
            pl.BlockSpec(memory_space=pl.ANY),
            pl.BlockSpec(memory_space=pl.ANY),
        ],
        out_specs=[
            pl.BlockSpec((length,128),lambda s,h:(s,h)),
            pl.BlockSpec((2,None,length,length),lambda s,h:(h,s,0,0)),
            pl.BlockSpec((length,128),lambda s,h:(s,h)),
            pl.BlockSpec(memory_space=pltpu.VMEM),
            pl.BlockSpec(memory_space=pltpu.VMEM),
        ],
        out_shape=[jax.ShapeDtypeStruct((tokens,feats),BF),
                   jax.ShapeDtypeStruct((heads,seqs,length,length),BF),
                   jax.ShapeDtypeStruct((tokens,feats),F32)]
                  +[jax.ShapeDtypeStruct((4,mask.shape[0]//4,mask.shape[0]),BF)]*2,
        scratch_shapes=[pltpu.VMEM((length,128),BF),pltpu.VMEM((length,128),BF),
                        pltpu.VMEM((2,length,128),BF),pltpu.VMEM((2*length,128),BF),
                        pltpu.VMEM((length,128),BF),
                        pltpu.VMEM((length,length),F32),pltpu.VMEM((length,length),F32)]
                       +[pltpu.VMEM(mask.shape,jnp.int32),pltpu.VMEM(cot.shape,BF),pltpu.SemaphoreType.DMA((2,))]
                       +Panels.scratch(mask.shape[0]),
        compiler_params=pltpu.CompilerParams(collective_id=4,has_side_effects=True,vmem_limit_bytes=60<<20),
        name="attend_forward",
    )(qkv,qkv,qkv,boxes_r,boxes_c,table,mask,cot)


AXES = ("rows", "gr", "gc")
MESH = pl.DeviceIdType.MESH
PIECE = 384


class Place:
    def __init__(self, n_rows):
        self.n_rows = n_rows
        self.r = lax.axis_index("rows")
        self.g = lax.axis_index("gr")
        self.c = lax.axis_index("gc")
        self.core = lax.rem(self.c, 2)
        self.u = lax.div(self.c, 2)
        self.sibling = {"gc": self.u * 2 + 1 - self.core}
        self.across = {"gc": (1 - self.u) * 2 + self.core}

    def row_peer(self, d):
        return {"rows": lax.rem(self.r + d, self.n_rows)}

    def gr_peer(self, d):
        return {"gr": lax.rem(self.g + d, 4)}

    def gc_peer(self, d):
        return {"gc": lax.rem(self.c + d, 4)}

    def peers(self):
        return (
            [self.sibling, self.across]
            + [self.row_peer(d) for d in range(1, self.n_rows)]
            + [self.gr_peer(d) for d in range(1, 4)]
        )


def meet(peers):
    barrier = pltpu.get_barrier_semaphore()
    for peer in peers:
        pl.semaphore_signal(barrier, inc=1, device_id=peer, device_id_type=MESH)
    pl.semaphore_wait(barrier, len(peers))


def send(src, dst, send_sem, recv_sem, peer):
    return pltpu.make_async_remote_copy(
        src_ref=src, dst_ref=dst, send_sem=send_sem, recv_sem=recv_sem, device_id=peer,
        device_id_type=MESH,
    )


def by_step(step, first, end, action):
    if end - first == 1:
        action(first)
        return
    middle = (first + end) // 2
    pl.when(step < middle)(lambda: by_step(step, first, middle, action))
    pl.when(step >= middle)(lambda: by_step(step, middle, end, action))


class Unit:
    def __init__(self, array, part, block, rows_first, beats, source=None, leave=None):
        self.array, self.part, self.block = array, part, block
        self.rows_first, self.beats, self.source, self.leave = rows_first, beats, source, leave
        self.stages = sorted(stage for stage in beats if stage != "in")
        self.fresh = self.stages[0] == 0

    def does(self, stage):
        return stage in self.beats


class Shares:
    def __init__(self, place, units, piece, arrays, staging, carried, fins, got, bufs, sems, ends):
        self.p = place
        self.units = units
        self.piece = piece
        self.arrays = arrays
        self.staging = staging
        self.carried = carried
        self.fin = fins
        self.got = got
        self.own, self.b0, self.b1r, self.b1u, self.b2r, self.b2u, self.b3 = bufs
        self.ls, self.ss, self.rs = sems
        self.fs, self.fr = ends
        external = [i for i, unit in enumerate(units) if unit.source is None]
        self.external = sorted(external, key=lambda i: units[i].beats[0])

    def number(self, i, test):
        return sum(test(unit) for unit in self.units[:i])

    @staticmethod
    def kinds():
        return (
            lambda unit: True,
            lambda unit: unit.does(0),
            lambda unit: unit.does(1) and unit.rows_first,
            lambda unit: unit.does(1) and not unit.rows_first,
            lambda unit: unit.does(2) and not unit.rows_first,
            lambda unit: unit.does(2) and unit.rows_first,
            lambda unit: unit.does(3),
        )

    @staticmethod
    def scratch(units, piece, n_rows):
        n, m, r = len(units), 48, n_rows
        shapes = (
            (r, 4, 2, m), (r, 4, 2, m), (r - 1, 4, 2, m), (r, 4, m), (r - 1, 4, m), (4, m), (3, m),
        )
        bufs = [
            pltpu.VMEM((max(1, sum(map(test, units))),) + shape + (piece,), BF)
            for test, shape in zip(Shares.kinds(), shapes)
        ]
        dma = pltpu.SemaphoreType.DMA
        return bufs + [dma((n,)), dma((n, r + 4)), dma((n, r + 4))]

    @staticmethod
    def result_scratch(sizes):
        dma = pltpu.SemaphoreType.DMA
        k = len(sizes)
        fins = [pltpu.VMEM((2, rows, x // 2), F32) for rows, x in sizes]
        got = [pltpu.VMEM((rows, x // 2), F32) for rows, x in sizes]
        return fins + got + [dma((k,)), dma((k,))]

    def buffer(self, kind, i):
        bufs = (self.own, self.b0, self.b1r, self.b1u, self.b2r, self.b2u, self.b3)
        return bufs[kind].at[self.number(i, self.kinds()[kind])]

    def piece_of(self, i, core):
        unit = self.units[i]
        if unit.source is None:
            at = unit.block * 2 * self.piece + core * self.piece
            columns = pl.ds(pl.multiple_of(at, 128), self.piece)
            return self.arrays[unit.array].at[:, :, :, unit.part, :, columns]
        _, n, column = unit.source
        return self.staging.at[n, core, :, :, :, :, column : column + self.piece]

    def swap(self, i):
        src = self.piece_of(i, 1 - self.p.core)
        return send(src, self.buffer(1, i), self.ss.at[i, 0], self.rs.at[i, 0], self.p.sibling)

    def keep(self, i):
        unit, p = self.units[i], self.p
        if unit.source is None:
            src, to = self.piece_of(i, p.core), self.own.at[i]
        else:
            src = self.carried[unit.source[1]].at[unit.source[2]]
            if unit.does(2):
                to = self.own.at[i, p.r] if unit.rows_first else self.own.at[i, :, :, p.u]
            else:
                to = self.own.at[i, p.r, :, p.u]
        return pltpu.make_async_copy(src, to, self.ls.at[i])

    def along_rows(self, i, first):
        p = self.p
        out = []
        for d in range(1, p.n_rows):
            to = lax.rem(p.r + d, p.n_rows)
            src = self.own.at[i, to] if first else self.own.at[i, to, :, p.u]
            dst = self.buffer(2 if first else 4, i).at[d - 1]
            out.append(send(src, dst, self.ss.at[i, 1 + d], self.rs.at[i, 1 + d], p.row_peer(d)))
        return out

    def across(self, i, first):
        p = self.p
        src = self.own.at[i, :, :, 1 - p.u] if first else self.own.at[i, p.r, :, 1 - p.u]
        dst = self.buffer(3 if first else 5, i)
        return [send(src, dst, self.ss.at[i, 1], self.rs.at[i, 1], p.across)]

    def along_gr(self, i):
        p = self.p
        out = []
        for d in range(1, 4):
            src = self.own.at[i, p.r, lax.rem(p.g + d, 4), p.u]
            at = p.n_rows + d
            dst = self.buffer(6, i).at[d - 1]
            out.append(send(src, dst, self.ss.at[i, at], self.rs.at[i, at], p.gr_peer(d)))
        return out

    def copies(self, i, stage):
        if stage == 0:
            return [self.swap(i)]
        if stage == 3:
            return self.along_gr(i)
        if self.units[i].rows_first == (stage == 1):
            return self.along_rows(i, stage == 1)
        return self.across(i, stage == 1)

    def start(self, i, stage):
        if stage == 0 and self.units[i].source is None:
            self.keep(i).start()
        for copy in self.copies(i, stage):
            copy.start()

    def finish(self, i, stage):
        p, unit = self.p, self.units[i]
        if stage == 0 and unit.source is None:
            self.keep(i).wait()
        for copy in self.copies(i, stage):
            copy.wait_recv()
        if stage == 0:
            mine = self.own[i] if unit.source is None else self.piece_of(i, p.core)[...]
            self.own[i] = mine + self.buffer(1, i)[...]
            return
        if stage == 3:
            total = self.own[i, p.r, p.g, p.u].astype(F32)
            for d in range(3):
                total = total + self.buffer(6, i)[d].astype(F32)
            m = total.shape[0]
            fin = self.fin[unit.array]
            rows = fin.shape[1]
            span = slice(unit.block * self.piece, (unit.block + 1) * self.piece)
            if rows < m:
                fin[0, :, span] = total[:rows]
                fin[1, :, span] = total[rows:]
            else:
                per = rows // m
                row = (unit.part % per) * m
                fin[unit.part // per, row : row + m, span] = total
            return
        if stage == 2:
            to = self.own.at[i, p.r, :, p.u]
        else:
            to = self.own.at[i, p.r] if unit.rows_first else self.own.at[i, :, :, p.u]
        total = to[...]
        if unit.rows_first == (stage == 1):
            for d in range(p.n_rows - 1):
                total = total + self.buffer(2 if stage == 1 else 4, i)[d]
        else:
            total = total + self.buffer(3 if stage == 1 else 5, i)[...]
        if unit.leave is not None and stage == unit.stages[-1]:
            self.carried[unit.leave[0]][unit.leave[1]] = total
        else:
            to[...] = total

    def last(self, k):
        return send(
            self.fin[k].at[1 - self.p.core], self.got[k], self.fs.at[k], self.fr.at[k],
            self.p.sibling,
        )

    def begin(self, window):
        for i, unit in enumerate(self.units):
            if not unit.fresh:
                self.keep(i).start()
        for i in self.external[:window]:
            self.start(i, 0)

    def tick(self, t, window, done):
        due = []
        for i, unit in enumerate(self.units):
            for stage, beat in unit.beats.items():
                if beat == t:
                    due.append((-1 if stage == "in" else stage, i))
        for stage, i in sorted(due, reverse=True):
            unit = self.units[i]
            if stage < 0:
                self.keep(i).wait()
                self.start(i, unit.stages[0])
                continue
            self.finish(i, stage)
            if stage == 0 and i in self.external:
                later = self.external.index(i) + window
                if later < len(self.external):
                    self.start(self.external[later], 0)
            if stage == 3:
                final, count = done[unit.array]
                if t == final:
                    done[unit.array] = final, count - 1
                    if count == 1:
                        self.last(unit.array).start()
            elif stage < unit.stages[-1]:
                self.start(i, stage + 1)

    def ticks(self):
        return 1 + max(beat for unit in self.units for beat in unit.beats.values())

    def deliver(self, k, out, spans):
        core = self.p.core
        self.last(k).wait()
        for value, owner in ((self.fin[k][core], core), (self.got[k][...], 1 - core)):
            at = 0
            for base, step, width in spans:
                where = pl.ds(pl.multiple_of(base + owner * step, 128), width)
                out[:, where] = value[:, at : at + width]
                at += width

    def wait_sends(self):
        for i, unit in enumerate(self.units):
            for stage in unit.stages:
                for copy in self.copies(i, stage):
                    copy.wait_send()


def on_the_way(units, arrays):
    beats = [[unit.beats[3] for unit in units if unit.array == k and unit.does(3)] for k in range(arrays)]
    return [(max(of), of.count(max(of))) if of else (-1, 0) for of in beats]


class Total:
    def __init__(self, place, source, out, bufs, sems):
        self.p = place
        self.src = source
        self.out = out
        self.part, self.pair, self.high, self.rows, self.quad = bufs
        self.ss, self.rs = sems

    @staticmethod
    def scratch(shape, n_rows):
        dma = pltpu.SemaphoreType.DMA
        bufs = [
            pltpu.VMEM((3,) + shape, F32), pltpu.VMEM(shape, F32), pltpu.VMEM(shape, F32),
            pltpu.VMEM((n_rows,) + shape, F32), pltpu.VMEM((4,) + shape, F32),
        ]
        return bufs, [dma((n_rows + 4,)), dma((n_rows + 4,))]

    def copies(self, stage):
        p = self.p
        if stage == 0:
            return [send(self.src, self.pair, self.ss.at[0], self.rs.at[0], p.sibling)]
        if stage == 1:
            return [send(self.part.at[0], self.high, self.ss.at[1], self.rs.at[1], p.across)]
        if stage == 2:
            return [
                send(
                    self.part.at[1], self.rows.at[p.r], self.ss.at[1 + d], self.rs.at[1 + d],
                    p.row_peer(d),
                )
                for d in range(1, p.n_rows)
            ]
        return [
            send(
                self.part.at[2], self.quad.at[p.g], self.ss.at[p.n_rows + d],
                self.rs.at[p.n_rows + d], p.gr_peer(d),
            )
            for d in range(1, 4)
        ]

    def start(self, stage):
        for copy in self.copies(stage):
            copy.start()

    def finish(self, stage):
        p = self.p
        for copy in self.copies(stage):
            copy.wait_recv()
        if stage == 0:
            self.part[0] = self.src[...] + self.pair[...]
        elif stage == 1:
            self.part[1] = self.part[0] + self.high[...]
        elif stage == 2:
            self.rows[p.r] = self.part[1]
            total = self.rows[0]
            for d in range(1, p.n_rows):
                total = total + self.rows[d]
            self.part[2] = total
        else:
            self.quad[p.g] = self.part[2]
            self.out[...] = (self.quad[0] + self.quad[1]) + (self.quad[2] + self.quad[3])

    def wait_sends(self):
        for stage in range(4):
            for copy in self.copies(stage):
                copy.wait_send()


def view(g, n_rows):
    rows, x = g.shape
    per = rows // (n_rows * 8)
    return g.reshape(n_rows, 4, 2, per // 48, 48, x)


def project_kernel(x_ref, gain_ref, bias_ref, w_ref, box_ref, page_ref, h1_ref, qkv_ref, cols_ref):
    @pl.when(pl.program_id(0) == 0)
    def _():
        chunk = 256
        count = x_ref.shape[0]
        for c in range(count // chunk):
            sl = slice(c * chunk, (c + 1) * chunk)
            x = x_ref[sl, :].astype(F32)
            average, inverse = norm_stats(x)
            h1_ref[sl, :] = ((x - average) * inverse * gain_ref[...].reshape(1, -1) + bias_ref[...].reshape(1, -1)).astype(BF)
        pages = jnp.concatenate([page_ref[s : s + 1, :] for s in range(page_ref.shape[0])], axis=1)
        lines = jnp.concatenate(
            [box_ref[...].astype(F32), pages.astype(F32), jnp.zeros((123, count), F32)], axis=0
        )
        cols_ref[...] = lines.T

    qkv_ref[...] = dot(h1_ref[...], w_ref[...]).astype(BF)


def project_forward(tokens, gain, bias, weight, boxes, page_ids):
    count, feats = tokens.shape
    width = weight.shape[1]
    block = 384
    vm = pl.BlockSpec(memory_space=pltpu.VMEM)
    return pl.pallas_call(
        project_kernel,
        grid=(width // block,),
        in_specs=[
            pl.BlockSpec((count, feats), lambda j: (0, 0)), vm, vm,
            pl.BlockSpec((feats, block), lambda j: (0, j)), vm, vm,
        ],
        out_specs=[vm, pl.BlockSpec((count, block), lambda j: (0, j)), vm],
        out_shape=[
            jax.ShapeDtypeStruct((count, feats), BF), jax.ShapeDtypeStruct((count, width), BF),
            jax.ShapeDtypeStruct((count, 128), F32),
        ],
        compiler_params=pltpu.CompilerParams(vmem_limit_bytes=40 << 20),
        name="project_forward",
    )(tokens, gain, bias, weight, boxes, page_ids)


def slot_members(seg_row, slots):
    ids = lax.broadcasted_iota(jnp.int32, (slots, seg_row.shape[1]), 0)
    return jnp.where(ids == seg_row, 1.0, 0.0)


def mlp_forward_kernel(
    ctx_ref, wo_ref, x_ref, gain_ref, bias_ref, wu_ref, bu_ref, wd_ref, seg_ref,
    r1_ref, h2_ref, act_ref, slope_ref, out_ref, emb_ref, acc_ref,
):
    step = pl.program_id(0)
    count = x_ref.shape[0]
    chunk = 256

    @pl.when(step == 0)
    def _():
        for c in range(count // chunk):
            sl = slice(c * chunk, (c + 1) * chunk)
            r1 = x_ref[sl, :].astype(F32) + dot(ctx_ref[sl, :], wo_ref[...])
            average, inverse = norm_stats(r1)
            r1_ref[sl, :] = r1
            acc_ref[sl, :] = r1
            h2_ref[sl, :] = ((r1 - average) * inverse * gain_ref[...].reshape(1, -1) + bias_ref[...].reshape(1, -1)).astype(BF)

    for c in range(count // chunk):
        sl = slice(c * chunk, (c + 1) * chunk)
        act, slope = gelu_pair(dot(h2_ref[sl, :], wu_ref[...]) + bu_ref[...])
        act = act.astype(BF)
        act_ref[sl, :] = act
        slope_ref[sl, :] = slope.astype(BF)
        acc_ref[sl, :] += dot(act, wd_ref[...])

    @pl.when(step == pl.num_programs(0) - 1)
    def _():
        out_ref[...] = acc_ref[...].astype(BF)
        seqs, length = seg_ref.shape
        slots = emb_ref.shape[0] // seqs
        for s in range(seqs):
            members = slot_members(seg_ref[s : s + 1, :], slots)
            total = dot(members.astype(BF), out_ref[s * length : (s + 1) * length, :])
            sizes = jnp.sum(members, axis=1, keepdims=True)
            emb_ref[s * slots : (s + 1) * slots, :] = (total / sizes).astype(BF)


def mlp_forward(ctx, w_out, tokens, gain, bias, w_up, b_up, w_down, seg_ids, slots):
    count, feats = tokens.shape
    hidden = w_up.shape[1]
    vm = pl.BlockSpec(memory_space=pltpu.VMEM)
    return pl.pallas_call(
        mlp_forward_kernel,
        grid=(hidden // feats,),
        in_specs=[
            vm, vm, vm, vm, vm, pl.BlockSpec((feats, feats), lambda f: (0, f)),
            pl.BlockSpec((1, feats), lambda f: (0, f)), pl.BlockSpec((feats, feats), lambda f: (f, 0)), vm,
        ],
        out_specs=[
            vm, vm, pl.BlockSpec((count, feats), lambda f: (0, f)),
            pl.BlockSpec((count, feats), lambda f: (0, f)), vm, vm,
        ],
        out_shape=[
            jax.ShapeDtypeStruct((count, feats), F32), jax.ShapeDtypeStruct((count, feats), BF),
            jax.ShapeDtypeStruct((count, hidden), BF), jax.ShapeDtypeStruct((count, hidden), BF),
            jax.ShapeDtypeStruct((count, feats), BF),
            jax.ShapeDtypeStruct((seg_ids.shape[0] * slots, feats), BF),
        ],
        scratch_shapes=[pltpu.VMEM((count, feats), F32)],
        compiler_params=pltpu.CompilerParams(vmem_limit_bytes=50 << 20),
        name="mlp_forward",
    )(
        ctx, w_out, tokens, gain, bias, w_up,
        b_up.reshape(1, hidden), w_down, seg_ids,
    )


class Panels:
    def __init__(self, place, tile, tile_t, rows, cols, sems):
        self.p = place
        self.tile, self.tile_t, self.rows, self.cols = tile, tile_t, rows, cols
        self.ss, self.rs = sems

    @staticmethod
    def scratch(size):
        dma = pltpu.SemaphoreType.DMA
        part = size // 4
        return [
            pltpu.VMEM((4, part, size), BF), pltpu.VMEM((4, part, size), BF),
            pltpu.VMEM((3, part, size), BF), pltpu.VMEM((3, part, size), BF), dma((6,)), dma((6,)),
        ]

    def copies(self):
        p = self.p
        out = []
        for d in range(1, 4):
            for n, (src, dst, peer, at) in enumerate((
                (self.tile, self.rows, p.gc_peer(d), p.c), (self.tile_t, self.cols, p.gr_peer(d), p.g),
            )):
                at_sem = 3 * n + d - 1
                out.append(
                    send(
                        src.at[lax.rem(at + d, 4)], dst.at[d - 1], self.ss.at[at_sem],
                        self.rs.at[at_sem], peer,
                    )
                )
        return out

    def fill(self, mask, cot, scale):
        g_raw = cot[...].astype(F32) * scale * mask[...].astype(F32)
        self.tile[...] = g_raw.astype(BF).reshape(self.tile.shape)
        self.tile_t[...] = g_raw.T.astype(BF).reshape(self.tile_t.shape)

    def start(self):
        for copy in self.copies():
            copy.start()

    def collect(self, row_out, col_out):
        p = self.p
        for copy in self.copies():
            copy.wait()
        row_out[p.c] = self.tile[p.c]
        col_out[p.g] = self.tile_t[p.g]
        for d in range(1, 4):
            row_out[lax.rem(p.c + 4 - d, 4)] = self.rows[d - 1]
            col_out[lax.rem(p.g + 4 - d, 4)] = self.cols[d - 1]


class Spread:
    def __init__(self, place, blocks, sems):
        self.p = place
        self.e = blocks
        self.ss, self.rs = sems
        self.near = lax.rem(place.c + 2, 4)

    @staticmethod
    def scratch(shape):
        dma = pltpu.SemaphoreType.DMA
        return [pltpu.VMEM((4, 4) + shape, BF), dma((4, 4, 3)), dma((4, 4))]

    def hop(self, row, col, kind, peer):
        block = self.e.at[row, col]
        return send(block, block, self.ss.at[row, col, kind], self.rs.at[row, col], peer)

    def own(self, step, waiting):
        p = self.p
        for sign in (1, -1) if step else (0,):
            row = p.g + sign * step
            inside = (row >= 0) & (row <= 3)

            @pl.when(inside)
            def _(row=row, sign=sign):
                if step and not waiting:
                    self.hop(row, p.c, 0, p.sibling).wait_recv()
                go = "wait_send" if waiting else "start"
                getattr(self.hop(row, p.c, 0, p.sibling), go)()
                getattr(self.hop(row, p.c, 1, p.across), go)()
                for way in (1, -1) if step == 0 else (-sign,):
                    to = p.g + way

                    @pl.when((to >= 0) & (to <= 3))
                    def _(to=to, way=way):
                        if step == 0 and way == -1:
                            copy = send(
                                self.e.at[row, p.c], self.e.at[row, p.c], self.down.at[0],
                                self.rs.at[row, p.c], {"gr": to},
                            )
                        else:
                            copy = self.hop(row, p.c, 2, {"gr": to})
                        getattr(copy, go)()

    def relay(self, step, waiting):
        p = self.p
        for sign in (1, -1) if step else (0,):
            row = p.g + sign * step

            @pl.when((row >= 0) & (row <= 3))
            def _(row=row):
                copy = self.hop(row, self.near, 0, p.sibling)
                if waiting:
                    copy.wait_send()
                else:
                    copy.wait_recv()
                    copy.start()

    def arrive(self, rows, cols):
        for row in rows:
            for col in cols:
                self.hop(row, col, 0, self.p.sibling).wait_recv()


def pair_kernel(
    emb_ref, left_ref, right_ref, rowp_ref, colp_ref, mask_ref, cot_ref, seg_ref,
    logits_ref, gleft_ref, gright_ref, gy_ref, gmlp_ref, e_ref, ss, rs, down, *, scale,
):
    place = Place(1)
    meet([place.sibling, place.across] + [place.gr_peer(d) for d in (1, 2, 3)])
    spread = Spread(place, e_ref, (ss, rs))
    spread.down = down
    p = place
    e_ref[p.g, p.c] = emb_ref[...]
    part, width = emb_ref.shape
    spread.own(0, False)
    spread.own(1, False)
    spread.relay(0, False)
    sib = p.u * 2 + 1 - p.core
    far = (1 - p.u) * 2 + 1 - p.core
    spread.arrive([p.g], [sib, far])
    left_rows = dot(e_ref[p.g].reshape(4 * part, width), left_ref[...]).astype(BF)
    spread.own(2, False)
    spread.relay(1, False)
    spread.own(3, False)
    right_cols = dot(e_ref[:, p.c].reshape(4 * part, width), right_ref[...]).astype(BF)
    spread.relay(2, False)
    logits_ref[...] = mask_ref[...].astype(F32) * dot(left_rows, right_cols, NT) * scale
    spread.relay(3, False)
    for d in range(1, 4):
        spread.arrive([lax.rem(p.g + d, 4)], [sib, far])
    row_sum = jnp.zeros((part, width), F32)
    col_sum = jnp.zeros((part, width), F32)
    for n in range(4):
        row_sum = row_sum + dot(rowp_ref[n], e_ref[:, n].reshape(4 * part, width))
        col_sum = col_sum + dot(colp_ref[n], e_ref[n].reshape(4 * part, width))

    def through(total, weight):
        high, low = hi_lo(total)
        return (dot(high, weight) + dot(low, weight)).astype(BF)

    g_left = through(row_sum, right_ref[...])
    g_right = through(col_sum, left_ref[...])
    emb_t = emb_ref[...].astype(F32).T.astype(BF)
    gleft_ref[...] = dot(emb_t, g_left).astype(BF)
    gright_ref[...] = dot(emb_t, g_right).astype(BF)
    g_emb = dot(g_left, left_ref[...], NT) + dot(g_right, right_ref[...], NT)
    seqs, length = seg_ref.shape
    slots = part // seqs
    for n in range(seqs):
        members = slot_members(seg_ref[n : n + 1, :], slots)
        g_seg = g_emb[n * slots : (n + 1) * slots] / jnp.sum(members, axis=1, keepdims=True)
        high, low = hi_lo(g_seg)
        twice = jnp.concatenate([members, members], axis=0).T.astype(BF)
        sl = slice(n * length, (n + 1) * length)
        g_y = cot_ref[sl, :].astype(F32) + dot(twice, jnp.concatenate([high, low], axis=0))
        gy_ref[sl, :] = g_y
        gmlp_ref[sl, :] = g_y.astype(BF)
    for step in range(4):
        spread.own(step, True)
        spread.relay(step, True)


def pair_head(emb, rel_left, rel_right, row_panel, col_panel, mask, cot_out, seg_ids, scale):
    part, width = emb.shape
    size = mask.shape[0]
    vm = pl.BlockSpec(memory_space=pltpu.VMEM)
    dma = pltpu.SemaphoreType.DMA
    return pl.pallas_call(
        functools.partial(pair_kernel, scale=scale),
        in_specs=[vm] * 8,
        out_specs=[vm] * 5,
        out_shape=[
            jax.ShapeDtypeStruct((size, size), F32), jax.ShapeDtypeStruct(rel_left.shape, BF),
            jax.ShapeDtypeStruct(rel_right.shape, BF), jax.ShapeDtypeStruct(cot_out.shape, F32),
            jax.ShapeDtypeStruct(cot_out.shape, BF),
        ],
        scratch_shapes=Spread.scratch((part, width)) + [dma((1,))],
        compiler_params=pltpu.CompilerParams(
            collective_id=5, has_side_effects=True, vmem_limit_bytes=50 << 20
        ),
        name="pair_head",
    )(emb, rel_left, rel_right, row_panel, col_panel, mask, cot_out, seg_ids)


def norm_back_chunk(g_out, rows, gain):
    average, inverse = norm_stats(rows)
    z = (rows - average) * inverse
    g_z = g_out * gain
    mean_g = jnp.mean(g_z, axis=-1, keepdims=True)
    mean_gz = jnp.mean(g_z * z, axis=-1, keepdims=True)
    return inverse * (g_z - mean_g - z * mean_gz), jnp.sum(g_out * z, axis=0, keepdims=True)


def put_lines(ref, at, row):
    for j in range(row.shape[1] // 128):
        ref[at + j : at + j + 1, :] = row[:, j * 128 : (j + 1) * 128]


def mlp_back_kernel(*refs, n_ext, units, n_rows, comm, window):
    (slope_ref, wd_ref, wu_ref, gmlp_ref, h2_ref, r1_ref, gy_ref, ctx_ref, wo_ref, gain_ref) = refs[:10]
    at = 10
    arrays = refs[at : at + n_ext]
    at += n_ext
    gup_ref, gr1_ref, gout_ref, gctx_ref, small_ref = refs[at : at + 5]
    at += 5
    carried, outs = refs[at : at + 3], refs[at + 3 : at + 5]
    at += 5 if comm else 0
    h2_buf, h2t_ref, acc_ref, r1_buf, gy_buf, ctx_buf, ctxt_ref, wo_buf, gatt_ref, in_sem = refs[at : at + 10]
    at += 10
    n_step = pl.num_programs(0)
    step = pl.program_id(0)
    count, feats = acc_ref.shape
    lines = feats // 128
    steps = (small_ref.shape[0] - 16) // lines - 4
    if comm:
        place = Place(n_rows)
        shares = Shares(
            place, units, PIECE, arrays, None, carried, refs[at : at + 2], refs[at + 2 : at + 4],
            refs[at + 6 : at + 13], refs[at + 13 : at + 16], refs[at + 4 : at + 6],
        )
        done = on_the_way(units, 3)

    def inputs():
        pairs = (
            (h2_ref, h2_buf), (ctx_ref, ctx_buf), (r1_ref, r1_buf), (gy_ref, gy_buf), (wo_ref, wo_buf),
        )
        return [pltpu.make_async_copy(a, b, in_sem.at[i]) for i, (a, b) in enumerate(pairs)]

    @pl.when(step == 0)
    def _():
        for copy in inputs():
            copy.start()
        if comm:
            meet(place.peers())
            shares.begin(window)
        acc_ref[...] = jnp.zeros_like(acc_ref)
        small_ref[...] = jnp.zeros_like(small_ref)

    def beat(part):
        if comm:
            by_step(step, 0, steps, lambda n: shares.tick(2 * n + part, window, done))

    g_act = dot(gmlp_ref[...], wd_ref[...], NT)
    g_wide = g_act * slope_ref[...].astype(F32)
    g_u = g_wide.astype(BF)
    bias = jnp.sum(g_u.astype(F32), axis=0, keepdims=True)
    acc_ref[...] += dot(g_u, wu_ref[...], NT)
    beat(0)

    @pl.when(step == 0)
    def _():
        inputs()[0].wait()
        for c in range(count // 128):
            sl = slice(c * 128, (c + 1) * 128)
            h2t_ref[:, sl] = h2_buf[sl, :].astype(F32).T.astype(BF)

    gup_ref[...] = dot(h2t_ref[...], g_u).astype(BF)
    for at_step in range(steps):
        @pl.when(step == at_step)
        def _(at_step=at_step):
            put_lines(small_ref, (4 + at_step) * lines, bias)
    beat(1)

    @pl.when(step == n_step - 1)
    def _():
        for copy in inputs()[1:]:
            copy.wait()
        gain_sum = jnp.zeros((1, feats), F32)
        bias_sum = jnp.zeros((1, feats), F32)
        chunk = 256
        for c in range(count // chunk):
            sl = slice(c * chunk, (c + 1) * chunk)
            g_out = acc_ref[sl, :]
            g_in, part = norm_back_chunk(g_out, r1_buf[sl, :], gain_ref[...].reshape(1, -1))
            gain_sum = gain_sum + part
            bias_sum = bias_sum + jnp.sum(g_out, axis=0, keepdims=True)
            g_r1 = gy_buf[sl, :] + g_in
            gr1_ref[sl, :] = g_r1
            gatt_ref[sl, :] = g_r1.astype(BF)
        put_lines(small_ref, 2 * lines, gain_sum)
        put_lines(small_ref, 3 * lines, bias_sum)
        if comm:
            shares.tick(2 * steps, window, done)
        for c in range(count // 128):
            sl = slice(c * 128, (c + 1) * 128)
            ctxt_ref[:, sl] = ctx_buf[sl, :].astype(F32).T.astype(BF)
        gctx_ref[...] = dot(gatt_ref[...], wo_buf[...], NT).astype(BF)
        if comm:
            shares.tick(2 * steps + 1, window, done)
        gout_ref[...] = dot(ctxt_ref[...], gatt_ref[...]).astype(BF)
        if comm:
            for t in range(2 * steps + 2, shares.ticks()):
                shares.tick(t, window, done)
            for n, out in enumerate(outs):
                shares.deliver(n, out, ((0, PIECE, PIECE),))
            shares.wait_sends()


def early_units():
    whole, most, some = {0: 0, 1: 3, 2: 6, 3: 9}, {0: 2, 1: 5, 2: 8}, {0: 4, 1: 9}
    return (
        Unit(0, 0, 0, True, whole), Unit(1, 0, 0, False, whole),
        Unit(2, 0, 0, True, most, leave=(2, 0)), Unit(2, 1, 0, False, most, leave=(2, 1)),
        Unit(2, 2, 0, True, some, leave=(0, 0)), Unit(2, 3, 0, False, some, leave=(1, 0)),
    )


def mlp_backward(
    slope, w_down, w_up, g_mlp, h2, r1, g_y, ctx, w_out, gain, small_rows, left, right, down, n_rows, comm
):
    count, feats = g_mlp.shape
    hidden = slope.shape[1]
    steps = hidden // feats
    vm = pl.BlockSpec(memory_space=pltpu.VMEM)
    any_ref = pl.BlockSpec(memory_space=pl.ANY)
    views = [view(g, n_rows) for g in (left, right, down)] if comm else []
    units = early_units()
    extra = []
    if comm:
        extra = [
            jax.ShapeDtypeStruct((1, 4, 2, 48, PIECE), BF),
            jax.ShapeDtypeStruct((1, n_rows, 4, 48, PIECE), BF),
            jax.ShapeDtypeStruct((2, 4, 48, PIECE), BF),
            jax.ShapeDtypeStruct((24, feats), F32),
            jax.ShapeDtypeStruct((24, feats), F32),
        ]
    scratch = [
        pltpu.VMEM((count, feats), BF), pltpu.VMEM((feats, count), BF), pltpu.VMEM((count, feats), F32),
        pltpu.VMEM((count, feats), F32), pltpu.VMEM((count, feats), F32), pltpu.VMEM((count, feats), BF),
        pltpu.VMEM((feats, count), BF), pltpu.VMEM((feats, feats), BF), pltpu.VMEM((count, feats), BF),
        pltpu.SemaphoreType.DMA((5,)),
    ]
    params = dict(vmem_limit_bytes=63 << 20, dimension_semantics=("arbitrary",))
    if comm:
        scratch += Shares.result_scratch([(24, feats)] * 2) + Shares.scratch(units, PIECE, n_rows)
        params.update(collective_id=3, has_side_effects=True)
    return pl.pallas_call(
        functools.partial(
            mlp_back_kernel, n_ext=len(views), units=units, n_rows=n_rows, comm=comm, window=2,
        ),
        grid=(steps,),
        in_specs=[
            pl.BlockSpec((count, feats), lambda f: (0, f)),
            pl.BlockSpec((feats, feats), lambda f: (f, 0)),
            pl.BlockSpec((feats, feats), lambda f: (0, f)),
            vm, any_ref, any_ref, any_ref, any_ref, any_ref, vm,
        ] + [any_ref] * len(views),
        out_specs=[pl.BlockSpec((feats, feats), lambda f: (0, f)), vm, vm, vm, vm] + [vm] * len(extra),
        out_shape=[
            jax.ShapeDtypeStruct((feats, hidden), BF), jax.ShapeDtypeStruct((count, feats), F32),
            jax.ShapeDtypeStruct((feats, feats), BF), jax.ShapeDtypeStruct((count, feats), BF),
            jax.ShapeDtypeStruct((small_rows, 128), F32),
        ] + extra,
        scratch_shapes=scratch,
        compiler_params=pltpu.CompilerParams(**params),
        name="mlp_backward",
    )(slope, w_down, w_up, g_mlp, h2, r1, g_y, ctx, w_out, gain, *views)


def deliver_kernel(gx_ref, small_ref, *refs, parts, heads):
    n_in = sum(parts)
    ins, outs = refs[:n_in], refs[n_in:]
    outs[0][...] = gx_ref[...]

    @pl.when(pl.program_id(0) == 0)
    def _():
        at = 0
        for k, n in enumerate(parts):
            out = outs[1 + k]
            row = 0
            for ref in ins[at : at + n]:
                rows, x = ref.shape
                per = x // 128
                for j in range(per):
                    out[pl.ds(row + j, rows, stride=per), :] = ref[:, j * 128 : (j + 1) * 128]
                row += rows * per
            at += n
        line = 0
        for out in outs[1 + len(parts) :]:
            if len(out.shape) == 1:
                for j in range(out.shape[0] // 128):
                    out[j * 128 : (j + 1) * 128] = small_ref[line]
                    line += 1
            else:
                out[...] = small_ref[line : line + out.shape[0], :]


def deliver(g_tokens, small, shares, features, hidden, heads):
    count = g_tokens.shape[0]
    flat = [p for group in shares for p in group]
    vm = pl.BlockSpec(memory_space=pltpu.VMEM)
    block = count // 4
    sizes = [sum(p.size for p in group) for group in shares]
    results = pl.pallas_call(
        functools.partial(deliver_kernel, parts=tuple(len(group) for group in shares), heads=heads),
        grid=(4,),
        in_specs=[pl.BlockSpec((block, features), lambda i: (i, 0)), vm] + [vm] * len(flat),
        out_specs=[pl.BlockSpec((block, features), lambda i: (i, 0))] + [vm] * (len(shares) + 6),
        out_shape=[jax.ShapeDtypeStruct(g_tokens.shape, F32)]
        + [jax.ShapeDtypeStruct((size // 128, 128), F32) for size in sizes]
        + [jax.ShapeDtypeStruct((features,), F32)] * 4
        + [jax.ShapeDtypeStruct((hidden,), F32), jax.ShapeDtypeStruct((heads, 128), F32)],
        name="deliver",
    )(g_tokens, small, *flat)
    return (
        results[0], [r.reshape(-1) for r in results[1 : 1 + len(shares)]], results[1 + len(shares) :]
    )


def back_kernel(*refs, n_ext, units, tail, spans, n_rows, comm, window):
    (q_ref, k_ref, v_ref, e_ref, linv_ref, ctx_ref, gctx_ref, boxr_ref, boxc_ref, w_ref, h1_ref,
     x_ref, gr1_ref, gain_ref, small_ref) = refs[:15]
    at = 15
    arrays = refs[at : at + n_ext]
    at += n_ext
    carried = refs[at : at + 3] if comm else ()
    at += len(carried)
    n_out = len(spans)
    gx_ref = refs[at]
    small_out = refs[at + 1]
    at += 2
    if comm:
        outs = refs[at : at + n_out]
        at += n_out
    else:
        grad_ref = refs[at]
        at += 1
    (oha_ref, ohbt_ref, cx_ref, cy_ref, g_ref, gcx_ref, gcy_ref, lt_ref, gt_ref, gall_ref, h1t_ref,
     hist_ref, h1_buf, x_buf, gr1_buf, w_buf, pack_ref, in_sem) = refs[at : at + 18]
    at += 18
    length = q_ref.shape[0]
    half, quarter = 64, 32
    pairs, seqs = pl.num_programs(0), pl.num_programs(1)
    hp = pl.program_id(0)
    s_id = pl.program_id(1)
    n_seq = cx_ref.shape[0]
    n_pair = hist_ref.shape[0] // 2
    lane = lax.broadcasted_iota(jnp.int32, (1, 128), 1)
    low = lane < 64
    if comm:
        place = Place(n_rows)
        staging = refs[at]
        fins = refs[at + 1 : at + n_out + 1]
        at += n_out + 1
        got = refs[at : at + n_out]
        at += n_out
        known = (None,) + tuple(arrays) + (None,)
        ends = refs[at : at + 2]
        at += 2
        shares = Shares(
            place, units, PIECE, known, staging, carried, fins, got, refs[at : at + 7],
            refs[at + 7 : at + 10], ends,
        )
        at += 10
        thirds = Shares(
            place, tail, PIECE // 3, known, staging, carried, fins, got, refs[at : at + 7],
            refs[at + 7 : at + 10], ends,
        )
        at += 10
        done = on_the_way(units + tail, n_out)
        total = Total(place, pack_ref, small_out, refs[at : at + 5], refs[at + 5 : at + 7])

    def inputs():
        return (
            pltpu.make_async_copy(h1_ref, h1_buf, in_sem.at[0]),
            pltpu.make_async_copy(x_ref, x_buf, in_sem.at[1]),
            pltpu.make_async_copy(gr1_ref, gr1_buf, in_sem.at[2]),
            pltpu.make_async_copy(w_ref, w_buf, in_sem.at[3]),
        )

    @pl.when((hp == 0) & (s_id == 0))
    def _():
        for copy in inputs():
            copy.start()
        hist_ref[...] = jnp.zeros_like(hist_ref)
        if comm:
            meet(place.peers())
            shares.begin(window)

    @pl.when(hp == 0)
    def _():
        bc = boxc_ref[...]
        ax, _ = key_side(bc[:, 0:1], bc[:, 2:3], half)
        ay, _ = key_side(bc[:, 1:2], bc[:, 3:4], half)
        _, fbx = query_side(bc[:, 0:1], bc[:, 2:3], half)
        _, fby = query_side(bc[:, 1:2], bc[:, 3:4], half)
        spot = (lane % quarter).astype(F32)
        is_x = (lane % half) < quarter
        oha = jnp.where(jnp.where(is_x, ax, ay) == spot, jnp.where(low, 1.0, 0.0), 0.0)
        oha_ref[s_id] = oha.astype(BF)
        br = boxr_ref[...]
        _, gax = key_side(br[0:1], br[2:3], half)
        _, gay = key_side(br[1:2], br[3:4], half)
        rbx, _ = query_side(br[0:1], br[2:3], half)
        rby, _ = query_side(br[1:2], br[3:4], half)
        row = lax.broadcasted_iota(jnp.int32, (half, length), 0)
        rspot = (row % quarter).astype(F32)
        ohbt_ref[s_id] = jnp.where(jnp.where(row < quarter, rbx, rby) == rspot, 1.0, 0.0).astype(BF)
        cx_ref[s_id] = jnp.where(gax + fbx >= SPAN, 1.0, 0.0).astype(BF)
        cy_ref[s_id] = jnp.where(gay + fby >= SPAN, 1.0, 0.0).astype(BF)

    @pl.when((hp == 0) & (s_id == n_seq - 1))
    def _():
        inputs()[0].wait()
        for c in range(h1_buf.shape[0] // 128):
            sl = slice(c * 128, (c + 1) * 128)
            h1t_ref[:, sl] = h1_buf[sl, :].astype(F32).T.astype(BF)

    k = k_ref[...]
    v = v_ref[...]
    lt_ref[...] = q_ref[...].astype(F32).T.astype(BF)
    gc = gctx_ref[...].astype(F32) * linv_ref[...]
    gcb = gc.astype(BF)
    gt_ref[...] = gcb.astype(F32).T.astype(BF)
    prod = gc * ctx_ref[...].astype(F32)
    ohbt = ohbt_ref[s_id]
    kts = []
    vts = []
    rows = 256
    n_step = n_pair * n_seq
    step = hp * n_seq + s_id
    for a in range(2):
        if comm and a == 1:
            by_step(step, 0, n_step, lambda n: shares.tick(2 * n, window, done))
        mine = low if a == 0 else jnp.logical_not(low)
        other = 64 - 64 * a
        d = jnp.sum(jnp.where(mine, prod, 0.0), axis=1, keepdims=True)
        dhi = d.astype(BF).astype(F32)
        extra = jnp.where(lane == other, dhi, jnp.where(lane == other + 1, d - dhi, 0.0))
        lhs = jnp.where(mine, gcb.astype(F32), extra).astype(BF)
        minus = jnp.where((lane == other) | (lane == other + 1), -1.0, 0.0).astype(BF)
        rhs = jnp.where(mine, v, minus)
        for c in range(length // rows):
            sl = slice(c * rows, (c + 1) * rows)
            gp = dot(lhs[sl], rhs, NT)
            g = (gp * e_ref[a, sl, :].astype(F32)).astype(BF)
            g_ref[a, sl, :] = g
            gcx_ref[a, sl, :] = g * cx_ref[s_id, sl, :]
            gcy_ref[a, sl, :] = g * cy_ref[s_id, sl, :]
        left = jnp.concatenate([lt_ref[64 * a : 64 * a + 64, :], ohbt], axis=0)
        r0 = dot(left, g_ref[a])
        rx = dot(ohbt[:quarter], gcx_ref[a])
        ry = dot(ohbt[quarter:], gcy_ref[a])
        vts.append(dot(gt_ref[64 * a : 64 * a + 64, :], e_ref[a]))
        kts.append(r0[:64])
        w = jnp.concatenate([r0[64:], rx, ry], axis=0)
        whi, wlo = hi_lo(w)
        red = dot(jnp.concatenate([whi, wlo], axis=0), oha_ref[s_id])
        hist_ref[2 * hp + a] += red[:128] + red[128:]
    zero = jnp.zeros_like(k)
    gq = dot(g_ref[0], jnp.where(low, k, zero)) + dot(g_ref[1], jnp.where(low, zero, k))
    own_rows = pl.ds(pl.multiple_of(s_id * length, length), length)
    feats = h1_buf.shape[1]
    parts = [pl.ds(pl.multiple_of(p * feats + hp * 128, 128), 128) for p in range(3)]
    gall_ref[own_rows, parts[0]] = (gq * 0.125).astype(BF)
    gall_ref[own_rows, parts[1]] = (jnp.concatenate(kts, axis=0) * 0.125).T.astype(BF)
    gall_ref[own_rows, parts[2]] = jnp.concatenate(vts, axis=0).T.astype(BF)

    @pl.when(s_id == n_seq - 1)
    def _():
        g_pair = jnp.concatenate([gall_ref[:, part] for part in parts], axis=1)
        piece = dot(h1t_ref[...], g_pair).astype(BF)
        if comm:
            staging[lax.div(hp, 2), lax.rem(hp, 2)] = piece.reshape(staging.shape[2:])
        else:
            grad_ref[0] = piece[:, :128]
            grad_ref[1] = piece[:, 128:256]
            grad_ref[2] = piece[:, 256:]

    if comm:
        def beat_of(at_step):
            for part in (shares, thirds):
                for i, unit in enumerate(part.units):
                    source = unit.source or ("", 0)
                    if source[0] == "own" and (2 * source[1] + 2) * n_seq - 1 == at_step:
                        part.start(i, 0)
            if at_step < n_step - 1:
                shares.tick(2 * at_step + 1, window, done)

        by_step(step, 0, n_step, beat_of)

    @pl.when((hp == n_pair - 1) & (s_id == n_seq - 1))
    def _():
        for copy in inputs()[1:]:
            copy.wait()
        gain = gain_ref[...].reshape(1, -1)
        count = x_buf.shape[0]
        chunk = 256
        beat = 2 * n_step - 1
        gain_sum = jnp.zeros((1, feats), F32)
        bias_sum = jnp.zeros((1, feats), F32)
        pack_ref[...] = small_ref[...]
        base = pack_ref.shape[0] - 16
        for h in range(2 * n_pair):
            w = hist_ref[h]
            line = jnp.zeros((1, 128), F32)
            for axis in range(2):
                plain = w[axis * quarter : (axis + 1) * quarter]
                carry = w[half + axis * quarter : half + (axis + 1) * quarter]
                keep = (lane >= axis * quarter) & (lane < (axis + 1) * quarter)
                stay = jnp.where(keep, plain - carry, 0.0)
                move = jnp.where(keep, carry, 0.0)
                shift = axis * (half - quarter)
                stay = pltpu.roll(stay, shift, 1, stride=1, stride_axis=0)
                move = pltpu.roll(move, shift + 1, 1, stride=1, stride_axis=0)
                line = line + jnp.sum(stay + move, axis=0, keepdims=True)
            pack_ref[base + h : base + h + 1, :] = line
        for c in range(count // chunk):
            sl = slice(c * chunk, (c + 1) * chunk)
            g_out = dot(gall_ref[sl, :], w_buf[...], NT)
            g_in, part = norm_back_chunk(g_out, x_buf[sl, :].astype(F32), gain)
            gx_ref[sl, :] = gr1_buf[sl, :] + g_in
            gain_sum = gain_sum + part
            bias_sum = bias_sum + jnp.sum(g_out, axis=0, keepdims=True)
            if comm:
                for t in range(beat, beat + 2):
                    shares.tick(t, window, done)
                    thirds.tick(t, window, done)
                beat += 2
        lines = feats // 128
        put_lines(pack_ref, 0, gain_sum)
        put_lines(pack_ref, lines, bias_sum)
        if comm:
            total.start(0)
            stage = 0
            for t in range(beat, max(shares.ticks(), thirds.ticks())):
                shares.tick(t, window, done)
                thirds.tick(t, window, done)
                if (t - beat) % 2 == 1 and stage < 4:
                    total.finish(stage)
                    if stage < 3:
                        total.start(stage + 1)
                    stage += 1
            for stage in range(stage, 4):
                total.finish(stage)
                if stage < 3:
                    total.start(stage + 1)
            for n, out in enumerate(outs):
                shares.deliver(n, out, spans[n])
            thirds.wait_sends()
            total.wait_sends()
            shares.wait_sends()
        else:
            small_out[...] = pack_ref[...]


def late_units():
    units = (
        Unit(0, 0, 0, True, {"in": 0, 3: 5}, source=("mid", 2, 0)),
        Unit(0, 1, 0, False, {"in": 0, 3: 5}, source=("mid", 2, 1)),
        Unit(0, 2, 0, True, {"in": 0, 2: 3, 3: 8}, source=("mid", 0, 0)),
        Unit(0, 3, 0, False, {"in": 0, 2: 3, 3: 8}, source=("mid", 1, 0)),
        Unit(2, 0, 0, True, {0: 1, 1: 6, 2: 11, 3: 15}),
        Unit(2, 0, 1, False, {0: 2, 1: 7, 2: 12, 3: 16}),
        Unit(1, 0, 0, True, {0: 5, 1: 11, 2: 15, 3: 19}),
        Unit(2, 0, 2, False, {0: 7, 1: 13, 2: 17, 3: 21}),
        Unit(2, 0, 3, True, {0: 12, 1: 18, 2: 22, 3: 26}),
        Unit(3, 0, 0, False, {0: 10, 1: 15, 2: 19, 3: 23}, source=("own", 0, 0)),
        Unit(3, 0, 1, False, {0: 18, 1: 23, 2: 26, 3: 29}, source=("own", 1, 0)),
    )
    tail = tuple(
        Unit(
            3, 0, 6 + n, n != 1, {0: 25, 1: 28 + n // 2, 2: 31 + n // 2, 3: 34 + n // 2},
            source=("own", 2, n * PIECE // 3),
        )
        for n in range(3)
    )
    return units, tail


def attend_and_project_backward(
    qkv, e, linv, ctx, gctx, boxes_r, boxes_c, weight, h1, tokens, g_r1, gain, small, arrays,
    carried, n_rows, comm
):
    count, width = qkv.shape
    feats = width // 3
    heads, seqs, length, _ = e.shape
    pairs = heads // 2
    rows_of = lambda off: pl.BlockSpec((length, 128), lambda h, s: (s, off + h))
    any_ref = pl.BlockSpec(memory_space=pl.ANY)
    vm = pl.BlockSpec(memory_space=pltpu.VMEM)
    views = [view(g, n_rows) for g in arrays] if comm else []
    n_ext = len(views)
    units, tail = late_units() if comm else ((), ())
    out_shape = [jax.ShapeDtypeStruct((count, feats), F32), jax.ShapeDtypeStruct(small.shape, F32)]
    out_specs = [vm, vm]
    spans = []
    scratch = [
        pltpu.VMEM((seqs, length, 128), BF), pltpu.VMEM((seqs, 64, length), BF),
        pltpu.VMEM((seqs, length, length), BF), pltpu.VMEM((seqs, length, length), BF),
        pltpu.VMEM((2, length, length), BF), pltpu.VMEM((2, length, length), BF),
        pltpu.VMEM((2, length, length), BF), pltpu.VMEM((128, length), BF),
        pltpu.VMEM((128, length), BF), pltpu.VMEM((count, width), BF), pltpu.VMEM((feats, count), BF),
        pltpu.VMEM((heads, 128, 128), F32), pltpu.VMEM((count, feats), BF),
        pltpu.VMEM((count, feats), BF), pltpu.VMEM((count, feats), F32), pltpu.VMEM((feats, width), BF),
        pltpu.VMEM(small.shape, F32), pltpu.SemaphoreType.DMA((4,)),
    ]
    params = dict(vmem_limit_bytes=63 << 20, dimension_semantics=("arbitrary", "arbitrary"))
    if comm:
        hidden = views[-1].shape[5]
        sizes = [(24 * hidden // feats, feats), (24, feats), (24, hidden), (24, width)]
        for rows, x in sizes[:-1]:
            spans.append([(j * 2 * PIECE, PIECE, PIECE) for j in range(x // (2 * PIECE))])
        spans.append(
            [(p * feats + t * 256, 128, 128) for t in range(pairs // 2) for p in range(3)]
        )
        out_shape += [jax.ShapeDtypeStruct(size, F32) for size in sizes]
        out_specs += [vm] * len(sizes)
        tbufs, tsems = Total.scratch(small.shape, n_rows)
        scratch += [pltpu.VMEM((pairs // 2, 2, n_rows, 4, 2, 48, PIECE), BF)]
        scratch += Shares.result_scratch(sizes) + Shares.scratch(units, PIECE, n_rows)
        scratch += Shares.scratch(tail, PIECE // 3, n_rows) + tbufs + tsems
        params.update(collective_id=2, has_side_effects=True)
    else:
        out_shape.append(jax.ShapeDtypeStruct((3, feats, feats), BF))
        out_specs.append(pl.BlockSpec((3, feats, 128), lambda h, s: (0, 0, h)))
    results = pl.pallas_call(
        functools.partial(
            back_kernel, n_ext=n_ext, units=units, tail=tail, spans=spans, n_rows=n_rows, comm=comm, window=2,
        ),
        grid=(pairs, seqs),
        in_specs=[
            rows_of(0), rows_of(pairs), rows_of(2 * pairs),
            pl.BlockSpec((2, None, length, length), lambda h, s: (h, s, 0, 0)),
            rows_of(0), rows_of(0), rows_of(0),
            pl.BlockSpec((4, length), lambda h, s: (0, s)),
            pl.BlockSpec((length, 128), lambda h, s: (s, 0)),
            any_ref, any_ref, any_ref, any_ref, vm, vm,
        ] + [any_ref] * (n_ext + len(carried)),
        out_specs=out_specs,
        out_shape=out_shape,
        scratch_shapes=scratch,
        compiler_params=pltpu.CompilerParams(**params),
        name="attend_backward",
    )(
        qkv, qkv, qkv, e, linv, ctx, gctx, boxes_r, boxes_c, weight, h1, tokens, g_r1,
        gain, small, *views, *carried,
    )
    return results


EPSILON = 1e-05


def norm_stats(rows):
    average = jnp.mean(rows, axis=-1, keepdims=True)
    centred = rows - average
    variance = jnp.mean(centred * centred, axis=-1, keepdims=True)
    return average, lax.rsqrt(variance + EPSILON)


def gelu_pair(u):
    bell = jnp.exp2(u * u * (-0.5 * LOG2E))
    below = 0.5 + 0.5 * lax.erf(u * math.sqrt(0.5))
    return u * below, below + u * bell * (1.0 / math.sqrt(2.0 * math.pi))


def body(
    tokens, boxes, page_ids, seg_ids, pair_mask, ln1_gain, ln1_bias, query_key_value_weight,
    attention_output_weight, ln2_gain, ln2_bias, up_projection_weight, up_projection_bias,
    down_projection_weight, box_table, rel_left, rel_right, cot_out, cot_logits,
):
    features = tokens.shape[1]
    h1, qkv, boxes_c = project_forward(
        tokens, ln1_gain, ln1_bias, query_key_value_weight, boxes, page_ids
    )
    pair_scale = 1.0 / math.sqrt(rel_left.shape[1])
    ctx, e, linv, row_panel, col_panel = attend_forward(
        qkv, boxes, boxes_c, page_ids.shape[0], box_table, pair_mask[0], cot_logits[0], pair_scale
    )
    r1, h2, act, slope, layer_out, embedded = mlp_forward(
        ctx, attention_output_weight, tokens, ln2_gain, ln2_bias, up_projection_weight,
        up_projection_bias, down_projection_weight, seg_ids, SLOTS,
    )
    pair_logits, grad_rel_left, grad_rel_right, g_y, g_mlp = pair_head(
        embedded, rel_left, rel_right, row_panel, col_panel, pair_mask[0], cot_out, seg_ids, pair_scale
    )
    grad_down = dot(act, g_mlp, (((0,), (0,)), ((), ()))).astype(BF)
    n_rows = lax.axis_size("rows")
    comm = n_rows * 8 * 48 <= features
    heads = box_table.shape[0]
    hidden = slope.shape[1]
    small_rows = (4 * features + hidden) // 128 + 16
    grad_up, g_r1, grad_out, g_ctx, small, *early = mlp_backward(
        slope, down_projection_weight, up_projection_weight, g_mlp, h2, r1, g_y, ctx,
        attention_output_weight, ln2_gain, small_rows, grad_rel_left, grad_rel_right, grad_down,
        n_rows, comm,
    )
    g_tokens, small, *late = attend_and_project_backward(
        qkv, e, linv, ctx, g_ctx, boxes, boxes_c, query_key_value_weight, h1, tokens, g_r1, ln1_gain,
        small, (grad_out, grad_up), early[:3], n_rows, comm,
    )
    early = early[3:]
    if comm:
        down, out, up, qkv_part = late
        shares = [[early[0]], [early[1]], [out], [down], [up], [qkv_part]]
    else:
        grad_qkv = jnp.concatenate([late[0][0], late[0][1], late[0][2]], axis=1)
        flats = [
            lax.psum_scatter(g, AXES, scatter_dimension=0, tiled=True).astype(F32).reshape(-1)
            for g in (grad_rel_left, grad_rel_right, grad_out, grad_down, grad_up, grad_qkv)
        ]
        shares = [[flat.reshape(-1, 128)] for flat in flats]
        small = lax.psum(small, AXES)
    grad_tokens, flats, vectors = deliver(g_tokens, small, shares, features, hidden, heads)
    left_share, right_share, out_share, down_share, up_share, qkv_share = flats
    return (
        layer_out, pair_logits[None], grad_tokens, vectors[0], vectors[1], qkv_share, out_share,
        vectors[2], vectors[3], up_share, vectors[4], down_share, vectors[5], left_share, right_share,
    )


def solution(mesh):
    whole = P(AXES, None)
    tile = P("rows", "gr", "gc")
    flat = P(AXES)
    one = P()
    in_specs = (
        whole, P(None, AXES), whole, whole, tile, one, one, one, one, one, one, one, one, one, one,
        one, one, whole, tile,
    )
    out_specs = (
        whole, tile, whole, one, one, flat, flat, one, one, flat, one, flat, one, flat, flat,
    )
    return jax.shard_map(body, mesh=mesh, in_specs=in_specs, out_specs=out_specs, check_vma=False)
```

```python
import functools
import math

import jax
import jax.numpy as jnp
from jax import lax
from jax.experimental import pallas as pl
from jax.experimental.pallas import tpu as pltpu
from jax.sharding import PartitionSpec as P

COORD=1000
SPAN=2*COORD+1
LOG2E=1.4426950408889634
BARRED=-2.0**99
SLOTS=64
BF=jnp.bfloat16
F32=jnp.float32
NT=(((1,),(1,)),((),()))
NN=(((1,),(0,)),((),()))
def dot(a,b,dims=NN):
    return lax.dot_general(a,b,dims,preferred_element_type=F32)

def whole_and_rest(scaled):
    whole=jnp.floor((scaled+0.5)*(1.0/SPAN))
    return whole, scaled-SPAN*whole

def key_side(low, high, half):
    c=jnp.floor((low+high).astype(F32)*0.5)
    return whole_and_rest(c*half)
def query_side(low, high, half):
    c=jnp.floor((low+high).astype(F32)*0.5)
    return whole_and_rest((COORD-c)*half)

def hi_lo(v):
    hi=v.astype(BF)
    return hi, (v-hi.astype(F32)).astype(BF)

def fwd_kernel(q_ref,k_ref,v_ref,boxr_ref,boxc_ref,tab_ref,mask_ref,cot_ref,
               ctx_ref,e_ref,linv_ref,rowp_ref,colp_ref,
               ohb_ref,oha_ref,kg_ref,rxy_ref,pg_ref,cx_ref,cy_ref,*panel_refs,rows,pair_scale):
    length=q_ref.shape[0]
    half=tab_ref.shape[1]//2
    quarter=half//2
    hp=pl.program_id(1)
    seq=pl.program_id(0)
    place=Place(1)
    mask_buf,cot_buf,in_sem=panel_refs[:3]
    panels=Panels(place,*panel_refs[3:7],panel_refs[7:])
    def inputs():
        return (pltpu.make_async_copy(mask_ref,mask_buf,in_sem.at[0]),
                pltpu.make_async_copy(cot_ref,cot_buf,in_sem.at[1]))
    @pl.when((hp==0)&(seq==0))
    def _():
        for copy in inputs():
            copy.start()
    @pl.when((hp==1)&(seq==0))
    def _():
        for copy in inputs():
            copy.wait()
        panels.fill(mask_buf,cot_buf,pair_scale)
        meet([place.gc_peer(d) for d in (1,2,3)]+[place.gr_peer(d) for d in (1,2,3)])
    @pl.when((hp==2)&(seq==0))
    def _():
        panels.start()
    lane=lax.broadcasted_iota(jnp.int32,(1,128),1)
    low=lane<64
    @pl.when(hp==0)
    def _():
        bc=boxc_ref[...]
        ax,fax=key_side(bc[:,0:1],bc[:,2:3],half)
        ay,fay=key_side(bc[:,1:2],bc[:,3:4],half)
        bx,fbx=query_side(bc[:,0:1],bc[:,2:3],half)
        by,fby=query_side(bc[:,1:2],bc[:,3:4],half)
        spot=(lane%quarter).astype(F32)
        is_x=(lane%half)<quarter
        oha=jnp.where(jnp.where(is_x,ax,ay)==spot,1.0,0.0)
        ohb=jnp.where(jnp.where(is_x,bx,by)==(quarter-1)-spot,1.0,0.0)
        ohb_ref[...]=jnp.where(low,ohb,0.0).astype(BF)
        oha_ref[...]=oha.astype(BF)
        page=bc[:,4:5].astype(jnp.int32)
        mine=(lane%64)==page
        barred=jnp.where((lane%64)<4,jnp.where(mine,0.0,BARRED),0.0)
        kg_ref[0]=jnp.where(low,oha,barred).astype(BF)
        kg_ref[1]=jnp.where(low,barred,oha).astype(BF)
        pg_ref[...]=jnp.where(mine,1.0,0.0).astype(BF)
        ohx=jnp.where(ax==spot,1.0,0.0)
        ohy=jnp.where(ay==spot,1.0,0.0)
        rxy_ref[pl.ds(0,length),:]=jnp.where(low,ohx,0.0).astype(BF)
        rxy_ref[pl.ds(length,length),:]=jnp.where(low,0.0,ohy).astype(BF)
        br=boxr_ref[...]
        _,gax=key_side(br[0:1],br[2:3],half)
        _,gay=key_side(br[1:2],br[3:4],half)
        cx_ref[...]=jnp.where(gax+fbx>=SPAN,1.0,0.0)
        cy_ref[...]=jnp.where(gay+fby>=SPAN,1.0,0.0)
    k=k_ref[...]
    v=v_ref[...]
    oha=oha_ref[...]
    b_row=lax.broadcasted_iota(jnp.int32,(half,128),0)
    l_col=lax.broadcasted_iota(jnp.int32,(half,128),1)
    row_x=b_row<quarter
    same_axis=row_x==((l_col%half)<quarter)
    d_axis=row_x==(l_col<half)
    heads=[]
    for a in range(2):
        t=tab_ref[pl.ds(2*hp+a,1),:]
        both=[jnp.where(low,t,0.0)+pltpu.roll(jnp.where(low,t,0.0),64,1),
              jnp.where(low,0.0,t)+pltpu.roll(jnp.where(low,0.0,t),64,1)]
        tiles=[]
        for b in both:
            spreads=[]
            for first in (0,1):
                whole=jnp.broadcast_to(b,(quarter,128))
                turned=pltpu.roll(whole,128-(quarter-1)-first,1,stride=1,stride_axis=0)
                lowq=jnp.where(lane<quarter,turned,0.0)
                pair=lowq+pltpu.roll(lowq,quarter,1)
                spreads.append(pair+pltpu.roll(pair,64,1))
            tiles.append(spreads)
        base=jnp.concatenate([tiles[0][0],tiles[1][0]],axis=0)
        nxt=jnp.concatenate([tiles[0][1],tiles[1][1]],axis=0)
        hi,lo=hi_lo(base)
        dhi,dlo=hi_lo(nxt-base)
        z=jnp.zeros_like(hi)
        is_hi=(l_col<64)==(a==1)
        g0=jnp.where(same_axis,jnp.where(is_hi,hi.astype(F32),lo.astype(F32)),0.0).astype(BF)
        g1=jnp.where(d_axis,jnp.where((l_col%half)<quarter,dhi.astype(F32),dlo.astype(F32)),0.0).astype(BF)
        hk=jnp.concatenate([g0,g1],axis=1)
        left=dot(ohb_ref[:,0:half],hk).astype(BF)
        if a==0:
            rhs=jnp.concatenate([jnp.where(low,k,oha),kg_ref[0]],axis=1)
            vv=jnp.where(low,v,jnp.ones_like(v))
        else:
            rhs=jnp.concatenate([jnp.where(low,oha,k),kg_ref[1]],axis=1)
            vv=jnp.where(low,jnp.ones_like(v),v)
        heads.append((left,rhs,vv))
    for c in range(length//rows):
        sl=pl.ds(c*rows,rows)
        q=q_ref[sl,:]*jnp.asarray(0.125,BF)
        pg=pg_ref[sl,:]
        outs=[]
        for a in range(2):
            left,rhs,vv=heads[a]
            lc=left[c*rows:(c+1)*rows]
            g0=lc[:,:128]
            if a==0:
                lhs=jnp.concatenate([jnp.where(low,q,g0),jnp.where(low,g0,pg)],axis=1)
            else:
                lhs=jnp.concatenate([jnp.where(low,g0,q),jnp.where(low,pg,g0)],axis=1)
            s=dot(lhs,rhs,NT)
            dxy=dot(lc[:,128:],rxy_ref[...],NT)
            s=s+cx_ref[sl,:]*dxy[:,:length]+cy_ref[sl,:]*dxy[:,length:]
            m=jnp.max(s,axis=1,keepdims=True)
            e=jnp.exp2((s-m)*LOG2E).astype(BF)
            e_ref[a,sl,:]=e
            outs.append(dot(e,vv))
        ctx=jnp.where(low,outs[0],outs[1])
        tot=jnp.where(low,pltpu.roll(outs[0],64,1),pltpu.roll(outs[1],64,1))
        linv=1.0/tot
        linv_ref[sl,:]=linv
        ctx_ref[sl,:]=(ctx*linv).astype(BF)
    @pl.when((hp==pl.num_programs(1)-1)&(seq==pl.num_programs(0)-1))
    def _():
        panels.collect(rowp_ref,colp_ref)

def attend_forward(qkv,boxes_r,boxes_c,seqs,table,mask,cot,pair_scale,rows=512):
    tokens,width=qkv.shape
    feats=width//3
    length=tokens//seqs
    heads=table.shape[0]
    pairs=heads//2
    return pl.pallas_call(
        functools.partial(fwd_kernel,rows=rows,pair_scale=pair_scale),
        grid=(seqs,pairs),
        in_specs=[
            pl.BlockSpec((length,128),lambda s,h:(s,h)),
            pl.BlockSpec((length,128),lambda s,h:(s,pairs+h)),
            pl.BlockSpec((length,128),lambda s,h:(s,2*pairs+h)),
            pl.BlockSpec((4,length),lambda s,h:(0,s)),
            pl.BlockSpec((length,128),lambda s,h:(s,0)),
            pl.BlockSpec(table.shape,lambda s,h:(0,0)),
            pl.BlockSpec(memory_space=pl.ANY),
            pl.BlockSpec(memory_space=pl.ANY),
        ],
        out_specs=[
            pl.BlockSpec((length,128),lambda s,h:(s,h)),
            pl.BlockSpec((2,None,length,length),lambda s,h:(h,s,0,0)),
            pl.BlockSpec((length,128),lambda s,h:(s,h)),
            pl.BlockSpec(memory_space=pltpu.VMEM),
            pl.BlockSpec(memory_space=pltpu.VMEM),
        ],
        out_shape=[jax.ShapeDtypeStruct((tokens,feats),BF),
                   jax.ShapeDtypeStruct((heads,seqs,length,length),BF),
                   jax.ShapeDtypeStruct((tokens,feats),F32)]
                  +[jax.ShapeDtypeStruct((4,mask.shape[0]//4,mask.shape[0]),BF)]*2,
        scratch_shapes=[pltpu.VMEM((length,128),BF),pltpu.VMEM((length,128),BF),
                        pltpu.VMEM((2,length,128),BF),pltpu.VMEM((2*length,128),BF),
                        pltpu.VMEM((length,128),BF),
                        pltpu.VMEM((length,length),F32),pltpu.VMEM((length,length),F32)]
                       +[pltpu.VMEM(mask.shape,jnp.int32),pltpu.VMEM(cot.shape,BF),pltpu.SemaphoreType.DMA((2,))]
                       +Panels.scratch(mask.shape[0]),
        compiler_params=pltpu.CompilerParams(collective_id=4,has_side_effects=True,vmem_limit_bytes=60<<20),
        name="attend_forward",
    )(qkv,qkv,qkv,boxes_r,boxes_c,table,mask,cot)


AXES = ("rows", "gr", "gc")
MESH = pl.DeviceIdType.MESH
PIECE = 384


class Place:
    def __init__(self, n_rows):
        self.n_rows = n_rows
        self.r = lax.axis_index("rows")
        self.g = lax.axis_index("gr")
        self.c = lax.axis_index("gc")
        self.core = lax.rem(self.c, 2)
        self.u = lax.div(self.c, 2)
        self.sibling = {"gc": self.u * 2 + 1 - self.core}
        self.across = {"gc": (1 - self.u) * 2 + self.core}

    def row_peer(self, d):
        return {"rows": lax.rem(self.r + d, self.n_rows)}

    def gr_peer(self, d):
        return {"gr": lax.rem(self.g + d, 4)}

    def gc_peer(self, d):
        return {"gc": lax.rem(self.c + d, 4)}

    def peers(self):
        return (
            [self.sibling, self.across]
            + [self.row_peer(d) for d in range(1, self.n_rows)]
            + [self.gr_peer(d) for d in range(1, 4)]
        )


def meet(peers):
    barrier = pltpu.get_barrier_semaphore()
    for peer in peers:
        pl.semaphore_signal(barrier, inc=1, device_id=peer, device_id_type=MESH)
    pl.semaphore_wait(barrier, len(peers))


def send(src, dst, send_sem, recv_sem, peer):
    return pltpu.make_async_remote_copy(
        src_ref=src, dst_ref=dst, send_sem=send_sem, recv_sem=recv_sem, device_id=peer,
        device_id_type=MESH,
    )


def by_step(step, first, end, action):
    if end - first == 1:
        action(first)
        return
    middle = (first + end) // 2
    pl.when(step < middle)(lambda: by_step(step, first, middle, action))
    pl.when(step >= middle)(lambda: by_step(step, middle, end, action))


class Unit:
    def __init__(self, array, part, block, rows_first, beats, source=None, leave=None):
        self.array, self.part, self.block = array, part, block
        self.rows_first, self.beats, self.source, self.leave = rows_first, beats, source, leave
        self.stages = sorted(stage for stage in beats if stage != "in")
        self.fresh = self.stages[0] == 0

    def does(self, stage):
        return stage in self.beats


class Shares:
    def __init__(self, place, units, piece, arrays, staging, carried, fins, got, bufs, sems, ends):
        self.p = place
        self.units = units
        self.piece = piece
        self.arrays = arrays
        self.staging = staging
        self.carried = carried
        self.fin = fins
        self.got = got
        self.own, self.b0, self.b1r, self.b1u, self.b2r, self.b2u, self.b3 = bufs
        self.ls, self.ss, self.rs = sems
        self.fs, self.fr = ends
        external = [i for i, unit in enumerate(units) if unit.source is None]
        self.external = sorted(external, key=lambda i: units[i].beats[0])

    def number(self, i, test):
        return sum(test(unit) for unit in self.units[:i])

    @staticmethod
    def kinds():
        return (
            lambda unit: True,
            lambda unit: unit.does(0),
            lambda unit: unit.does(1) and unit.rows_first,
            lambda unit: unit.does(1) and not unit.rows_first,
            lambda unit: unit.does(2) and not unit.rows_first,
            lambda unit: unit.does(2) and unit.rows_first,
            lambda unit: unit.does(3),
        )

    @staticmethod
    def scratch(units, piece, n_rows):
        n, m, r = len(units), 48, n_rows
        shapes = (
            (r, 4, 2, m), (r, 4, 2, m), (r - 1, 4, 2, m), (r, 4, m), (r - 1, 4, m), (4, m), (3, m),
        )
        bufs = [
            pltpu.VMEM((max(1, sum(map(test, units))),) + shape + (piece,), BF)
            for test, shape in zip(Shares.kinds(), shapes)
        ]
        dma = pltpu.SemaphoreType.DMA
        return bufs + [dma((n,)), dma((n, r + 4)), dma((n, r + 4))]

    @staticmethod
    def result_scratch(sizes):
        dma = pltpu.SemaphoreType.DMA
        k = len(sizes)
        fins = [pltpu.VMEM((2, rows, x // 2), F32) for rows, x in sizes]
        got = [pltpu.VMEM((rows, x // 2), F32) for rows, x in sizes]
        return fins + got + [dma((k,)), dma((k,))]

    def buffer(self, kind, i):
        bufs = (self.own, self.b0, self.b1r, self.b1u, self.b2r, self.b2u, self.b3)
        return bufs[kind].at[self.number(i, self.kinds()[kind])]

    def piece_of(self, i, core):
        unit = self.units[i]
        if unit.source is None:
            at = unit.block * 2 * self.piece + core * self.piece
            columns = pl.ds(pl.multiple_of(at, 128), self.piece)
            return self.arrays[unit.array].at[:, :, :, unit.part, :, columns]
        _, n, column = unit.source
        return self.staging.at[n, core, :, :, :, :, column : column + self.piece]

    def swap(self, i):
        src = self.piece_of(i, 1 - self.p.core)
        return send(src, self.buffer(1, i), self.ss.at[i, 0], self.rs.at[i, 0], self.p.sibling)

    def keep(self, i):
        unit, p = self.units[i], self.p
        if unit.source is None:
            src, to = self.piece_of(i, p.core), self.own.at[i]
        else:
            src = self.carried[unit.source[1]].at[unit.source[2]]
            if unit.does(2):
                to = self.own.at[i, p.r] if unit.rows_first else self.own.at[i, :, :, p.u]
            else:
                to = self.own.at[i, p.r, :, p.u]
        return pltpu.make_async_copy(src, to, self.ls.at[i])

    def along_rows(self, i, first):
        p = self.p
        out = []
        for d in range(1, p.n_rows):
            to = lax.rem(p.r + d, p.n_rows)
            src = self.own.at[i, to] if first else self.own.at[i, to, :, p.u]
            dst = self.buffer(2 if first else 4, i).at[d - 1]
            out.append(send(src, dst, self.ss.at[i, 1 + d], self.rs.at[i, 1 + d], p.row_peer(d)))
        return out

    def across(self, i, first):
        p = self.p
        src = self.own.at[i, :, :, 1 - p.u] if first else self.own.at[i, p.r, :, 1 - p.u]
        dst = self.buffer(3 if first else 5, i)
        return [send(src, dst, self.ss.at[i, 1], self.rs.at[i, 1], p.across)]

    def along_gr(self, i):
        p = self.p
        out = []
        for d in range(1, 4):
            src = self.own.at[i, p.r, lax.rem(p.g + d, 4), p.u]
            at = p.n_rows + d
            dst = self.buffer(6, i).at[d - 1]
            out.append(send(src, dst, self.ss.at[i, at], self.rs.at[i, at], p.gr_peer(d)))
        return out

    def copies(self, i, stage):
        if stage == 0:
            return [self.swap(i)]
        if stage == 3:
            return self.along_gr(i)
        if self.units[i].rows_first == (stage == 1):
            return self.along_rows(i, stage == 1)
        return self.across(i, stage == 1)

    def start(self, i, stage):
        if stage == 0 and self.units[i].source is None:
            self.keep(i).start()
        for copy in self.copies(i, stage):
            copy.start()

    def finish(self, i, stage):
        p, unit = self.p, self.units[i]
        if stage == 0 and unit.source is None:
            self.keep(i).wait()
        for copy in self.copies(i, stage):
            copy.wait_recv()
        if stage == 0:
            to = self.own.at[i]
            mine = to if unit.source is None else self.piece_of(i, p.core)
            theirs = self.buffer(1, i)

            @pl.loop(0, 4)
            def _(n):
                to[:, n] = mine[:, n] + theirs[:, n]

            return
        if stage == 3:
            total = self.own[i, p.r, p.g, p.u].astype(F32)
            for d in range(3):
                total = total + self.buffer(6, i)[d].astype(F32)
            m = total.shape[0]
            fin = self.fin[unit.array]
            rows = fin.shape[1]
            span = slice(unit.block * self.piece, (unit.block + 1) * self.piece)
            if rows < m:
                fin[0, :, span] = total[:rows]
                fin[1, :, span] = total[rows:]
            else:
                per = rows // m
                row = (unit.part % per) * m
                fin[unit.part // per, row : row + m, span] = total
            return
        if stage == 2:
            to = self.own.at[i, p.r, :, p.u]
        else:
            to = self.own.at[i, p.r] if unit.rows_first else self.own.at[i, :, :, p.u]
        if unit.rows_first == (stage == 1):
            terms = [self.buffer(2 if stage == 1 else 4, i).at[d] for d in range(p.n_rows - 1)]
        else:
            terms = [self.buffer(3 if stage == 1 else 5, i)]
        out = to
        if unit.leave is not None and stage == unit.stages[-1]:
            out = self.carried[unit.leave[0]].at[unit.leave[1]]
        if stage == 1:
            @pl.loop(0, 4)
            def _(n):
                at = n if unit.rows_first else (slice(None), n)
                total = to[at]
                for term in terms:
                    total = total + term[at]
                out[at] = total
        else:
            total = to[...]
            for term in terms:
                total = total + term[...]
            out[...] = total

    def last(self, k):
        return send(
            self.fin[k].at[1 - self.p.core], self.got[k], self.fs.at[k], self.fr.at[k],
            self.p.sibling,
        )

    def begin(self, window):
        for i, unit in enumerate(self.units):
            if not unit.fresh:
                self.keep(i).start()
        for i in self.external[:window]:
            self.start(i, 0)

    def tick(self, t, window, done):
        due = []
        for i, unit in enumerate(self.units):
            for stage, beat in unit.beats.items():
                if beat == t:
                    due.append((-1 if stage == "in" else stage, i))
        for stage, i in sorted(due, key=lambda entry: (-entry[0], entry[1])):
            unit = self.units[i]
            if stage < 0:
                self.keep(i).wait()
                self.start(i, unit.stages[0])
                continue
            self.finish(i, stage)
            if stage == 0 and i in self.external:
                later = self.external.index(i) + window
                if later < len(self.external):
                    self.start(self.external[later], 0)
            if stage == 3:
                final, count = done[unit.array]
                if t == final:
                    done[unit.array] = final, count - 1
                    if count == 1:
                        self.last(unit.array).start()
            elif stage < unit.stages[-1]:
                self.start(i, stage + 1)

    def ticks(self):
        return 1 + max(beat for unit in self.units for beat in unit.beats.values())

    def deliver(self, k, out, spans):
        core = self.p.core
        self.last(k).wait()
        for value, owner in ((self.fin[k][core], core), (self.got[k][...], 1 - core)):
            at = 0
            for base, step, width in spans:
                where = pl.ds(pl.multiple_of(base + owner * step, 128), width)
                out[:, where] = value[:, at : at + width]
                at += width

    def wait_sends(self):
        for i, unit in enumerate(self.units):
            for stage in unit.stages:
                for copy in self.copies(i, stage):
                    copy.wait_send()


def on_the_way(units, arrays):
    beats = [[unit.beats[3] for unit in units if unit.array == k and unit.does(3)] for k in range(arrays)]
    return [(max(of), of.count(max(of))) if of else (-1, 0) for of in beats]


class Total:
    def __init__(self, place, source, out, bufs, sems):
        self.p = place
        self.src = source
        self.out = out
        self.part, self.pair, self.high, self.rows, self.quad = bufs
        self.ss, self.rs = sems

    @staticmethod
    def scratch(shape, n_rows):
        dma = pltpu.SemaphoreType.DMA
        bufs = [
            pltpu.VMEM((3,) + shape, F32), pltpu.VMEM(shape, F32), pltpu.VMEM(shape, F32),
            pltpu.VMEM((n_rows,) + shape, F32), pltpu.VMEM((4,) + shape, F32),
        ]
        return bufs, [dma((n_rows + 4,)), dma((n_rows + 4,))]

    def copies(self, stage):
        p = self.p
        if stage == 0:
            return [send(self.src, self.pair, self.ss.at[0], self.rs.at[0], p.sibling)]
        if stage == 1:
            return [send(self.part.at[0], self.high, self.ss.at[1], self.rs.at[1], p.across)]
        if stage == 2:
            return [
                send(
                    self.part.at[1], self.rows.at[p.r], self.ss.at[1 + d], self.rs.at[1 + d],
                    p.row_peer(d),
                )
                for d in range(1, p.n_rows)
            ]
        return [
            send(
                self.part.at[2], self.quad.at[p.g], self.ss.at[p.n_rows + d],
                self.rs.at[p.n_rows + d], p.gr_peer(d),
            )
            for d in range(1, 4)
        ]

    def start(self, stage):
        for copy in self.copies(stage):
            copy.start()

    def finish(self, stage):
        p = self.p
        for copy in self.copies(stage):
            copy.wait_recv()
        if stage == 0:
            self.part[0] = self.src[...] + self.pair[...]
        elif stage == 1:
            self.part[1] = self.part[0] + self.high[...]
        elif stage == 2:
            self.rows[p.r] = self.part[1]
            total = self.rows[0]
            for d in range(1, p.n_rows):
                total = total + self.rows[d]
            self.part[2] = total
        else:
            self.quad[p.g] = self.part[2]
            self.out[...] = (self.quad[0] + self.quad[1]) + (self.quad[2] + self.quad[3])

    def wait_sends(self):
        for stage in range(4):
            for copy in self.copies(stage):
                copy.wait_send()


def view(g, n_rows):
    rows, x = g.shape
    per = rows // (n_rows * 8)
    return g.reshape(n_rows, 4, 2, per // 48, 48, x)


def project_kernel(x_ref, gain_ref, bias_ref, w_ref, box_ref, page_ref, h1_ref, qkv_ref, cols_ref):
    @pl.when(pl.program_id(0) == 0)
    def _():
        chunk = 256
        count = x_ref.shape[0]

        @pl.loop(0, count // chunk)
        def _(c):
            sl = pl.ds(pl.multiple_of(c * chunk, chunk), chunk)
            x = x_ref[sl, :].astype(F32)
            average, inverse = norm_stats(x)
            h1_ref[sl, :] = ((x - average) * inverse * gain_ref[...].reshape(1, -1) + bias_ref[...].reshape(1, -1)).astype(BF)
        pages = jnp.concatenate([page_ref[s : s + 1, :] for s in range(page_ref.shape[0])], axis=1)
        lines = jnp.concatenate(
            [box_ref[...].astype(F32), pages.astype(F32), jnp.zeros((123, count), F32)], axis=0
        )
        cols_ref[...] = lines.T

    qkv_ref[...] = dot(h1_ref[...], w_ref[...]).astype(BF)


def project_forward(tokens, gain, bias, weight, boxes, page_ids):
    count, feats = tokens.shape
    width = weight.shape[1]
    block = 384
    vm = pl.BlockSpec(memory_space=pltpu.VMEM)
    return pl.pallas_call(
        project_kernel,
        grid=(width // block,),
        in_specs=[
            pl.BlockSpec((count, feats), lambda j: (0, 0)), vm, vm,
            pl.BlockSpec((feats, block), lambda j: (0, j)), vm, vm,
        ],
        out_specs=[vm, pl.BlockSpec((count, block), lambda j: (0, j)), vm],
        out_shape=[
            jax.ShapeDtypeStruct((count, feats), BF), jax.ShapeDtypeStruct((count, width), BF),
            jax.ShapeDtypeStruct((count, 128), F32),
        ],
        compiler_params=pltpu.CompilerParams(vmem_limit_bytes=63 << 20),
        name="project_forward",
    )(tokens, gain, bias, weight, boxes, page_ids)


def slot_members(seg_row, slots):
    ids = lax.broadcasted_iota(jnp.int32, (slots, seg_row.shape[1]), 0)
    return jnp.where(ids == seg_row, 1.0, 0.0)


def mlp_forward_kernel(
    ctx_ref, wo_ref, x_ref, gain_ref, bias_ref, wu_ref, bu_ref, wd_ref, seg_ref,
    r1_ref, h2_ref, act_ref, slope_ref, out_ref, emb_ref, acc_ref,
):
    step = pl.program_id(0)
    count = x_ref.shape[0]
    chunk = 256

    @pl.when(step == 0)
    def _():
        @pl.loop(0, count // chunk)
        def _(c):
            sl = pl.ds(pl.multiple_of(c * chunk, chunk), chunk)
            r1 = x_ref[sl, :].astype(F32) + dot(ctx_ref[sl, :], wo_ref[...])
            average, inverse = norm_stats(r1)
            r1_ref[sl, :] = r1
            acc_ref[sl, :] = r1
            h2_ref[sl, :] = ((r1 - average) * inverse * gain_ref[...].reshape(1, -1) + bias_ref[...].reshape(1, -1)).astype(BF)

    for c in range(count // chunk):
        sl = slice(c * chunk, (c + 1) * chunk)
        act, slope = gelu_pair(dot(h2_ref[sl, :], wu_ref[...]) + bu_ref[...])
        act = act.astype(BF)
        act_ref[sl, :] = act
        slope_ref[sl, :] = slope.astype(BF)
        acc_ref[sl, :] += dot(act, wd_ref[...])

    @pl.when(step == pl.num_programs(0) - 1)
    def _():
        out_ref[...] = acc_ref[...].astype(BF)
        seqs, length = seg_ref.shape
        slots = emb_ref.shape[0] // seqs
        for s in range(seqs):
            members = slot_members(seg_ref[s : s + 1, :], slots)
            total = dot(members.astype(BF), out_ref[s * length : (s + 1) * length, :])
            sizes = jnp.sum(members, axis=1, keepdims=True)
            emb_ref[s * slots : (s + 1) * slots, :] = (total / sizes).astype(BF)


def mlp_forward(ctx, w_out, tokens, gain, bias, w_up, b_up, w_down, seg_ids, slots):
    count, feats = tokens.shape
    hidden = w_up.shape[1]
    vm = pl.BlockSpec(memory_space=pltpu.VMEM)
    return pl.pallas_call(
        mlp_forward_kernel,
        grid=(hidden // feats,),
        in_specs=[
            vm, vm, vm, vm, vm, pl.BlockSpec((feats, feats), lambda f: (0, f)),
            pl.BlockSpec((1, feats), lambda f: (0, f)), pl.BlockSpec((feats, feats), lambda f: (f, 0)), vm,
        ],
        out_specs=[
            vm, vm, pl.BlockSpec((count, feats), lambda f: (0, f)),
            pl.BlockSpec((count, feats), lambda f: (0, f)), vm, vm,
        ],
        out_shape=[
            jax.ShapeDtypeStruct((count, feats), F32), jax.ShapeDtypeStruct((count, feats), BF),
            jax.ShapeDtypeStruct((count, hidden), BF), jax.ShapeDtypeStruct((count, hidden), BF),
            jax.ShapeDtypeStruct((count, feats), BF),
            jax.ShapeDtypeStruct((seg_ids.shape[0] * slots, feats), BF),
        ],
        scratch_shapes=[pltpu.VMEM((count, feats), F32)],
        compiler_params=pltpu.CompilerParams(vmem_limit_bytes=50 << 20),
        name="mlp_forward",
    )(
        ctx, w_out, tokens, gain, bias, w_up,
        b_up.reshape(1, hidden), w_down, seg_ids,
    )


class Panels:
    def __init__(self, place, tile, tile_t, rows, cols, sems):
        self.p = place
        self.tile, self.tile_t, self.rows, self.cols = tile, tile_t, rows, cols
        self.ss, self.rs = sems

    @staticmethod
    def scratch(size):
        dma = pltpu.SemaphoreType.DMA
        part = size // 4
        return [
            pltpu.VMEM((4, part, size), BF), pltpu.VMEM((4, part, size), BF),
            pltpu.VMEM((3, part, size), BF), pltpu.VMEM((3, part, size), BF), dma((6,)), dma((6,)),
        ]

    def copies(self):
        p = self.p
        out = []
        for d in range(1, 4):
            for n, (src, dst, peer, at) in enumerate((
                (self.tile, self.rows, p.gc_peer(d), p.c), (self.tile_t, self.cols, p.gr_peer(d), p.g),
            )):
                at_sem = 3 * n + d - 1
                out.append(
                    send(
                        src.at[lax.rem(at + d, 4)], dst.at[d - 1], self.ss.at[at_sem],
                        self.rs.at[at_sem], peer,
                    )
                )
        return out

    def fill(self, mask, cot, scale):
        g_raw = cot[...].astype(F32) * scale * mask[...].astype(F32)
        self.tile[...] = g_raw.astype(BF).reshape(self.tile.shape)
        self.tile_t[...] = g_raw.T.astype(BF).reshape(self.tile_t.shape)

    def start(self):
        for copy in self.copies():
            copy.start()

    def collect(self, row_out, col_out):
        p = self.p
        for copy in self.copies():
            copy.wait()
        row_out[p.c] = self.tile[p.c]
        col_out[p.g] = self.tile_t[p.g]
        for d in range(1, 4):
            row_out[lax.rem(p.c + 4 - d, 4)] = self.rows[d - 1]
            col_out[lax.rem(p.g + 4 - d, 4)] = self.cols[d - 1]


class Spread:
    def __init__(self, place, blocks, sems):
        self.p = place
        self.e = blocks
        self.ss, self.rs = sems
        self.near = lax.rem(place.c + 2, 4)

    @staticmethod
    def scratch(shape):
        dma = pltpu.SemaphoreType.DMA
        return [pltpu.VMEM((4, 4) + shape, BF), dma((4, 4, 3)), dma((4, 4))]

    def hop(self, row, col, kind, peer):
        block = self.e.at[row, col]
        return send(block, block, self.ss.at[row, col, kind], self.rs.at[row, col], peer)

    def own(self, step, waiting):
        p = self.p
        for sign in (1, -1) if step else (0,):
            row = p.g + sign * step
            inside = (row >= 0) & (row <= 3)

            @pl.when(inside)
            def _(row=row, sign=sign):
                if step and not waiting:
                    self.hop(row, p.c, 0, p.sibling).wait_recv()
                go = "wait_send" if waiting else "start"
                getattr(self.hop(row, p.c, 0, p.sibling), go)()
                getattr(self.hop(row, p.c, 1, p.across), go)()
                for way in (1, -1) if step == 0 else (-sign,):
                    to = p.g + way

                    @pl.when((to >= 0) & (to <= 3))
                    def _(to=to, way=way):
                        if step == 0 and way == -1:
                            copy = send(
                                self.e.at[row, p.c], self.e.at[row, p.c], self.down.at[0],
                                self.rs.at[row, p.c], {"gr": to},
                            )
                        else:
                            copy = self.hop(row, p.c, 2, {"gr": to})
                        getattr(copy, go)()

    def relay(self, step, waiting):
        p = self.p
        for sign in (1, -1) if step else (0,):
            row = p.g + sign * step

            @pl.when((row >= 0) & (row <= 3))
            def _(row=row):
                copy = self.hop(row, self.near, 0, p.sibling)
                if waiting:
                    copy.wait_send()
                else:
                    copy.wait_recv()
                    copy.start()

    def arrive(self, rows, cols):
        for row in rows:
            for col in cols:
                self.hop(row, col, 0, self.p.sibling).wait_recv()


def pair_kernel(
    emb_ref, left_ref, right_ref, rowp_ref, colp_ref, mask_ref, cot_ref, seg_ref,
    logits_ref, gleft_ref, gright_ref, gy_ref, gmlp_ref, e_ref, ss, rs, down, *, scale,
):
    place = Place(1)
    meet([place.sibling, place.across] + [place.gr_peer(d) for d in (1, 2, 3)])
    spread = Spread(place, e_ref, (ss, rs))
    spread.down = down
    p = place
    e_ref[p.g, p.c] = emb_ref[...]
    part, width = emb_ref.shape
    spread.own(0, False)
    spread.own(1, False)
    spread.relay(0, False)
    sib = p.u * 2 + 1 - p.core
    far = (1 - p.u) * 2 + 1 - p.core
    spread.arrive([p.g], [sib, far])
    left_rows = dot(e_ref[p.g].reshape(4 * part, width), left_ref[...]).astype(BF)
    spread.own(2, False)
    spread.relay(1, False)
    spread.own(3, False)
    right_cols = dot(e_ref[:, p.c].reshape(4 * part, width), right_ref[...]).astype(BF)
    spread.relay(2, False)
    logits_ref[...] = mask_ref[...].astype(F32) * dot(left_rows, right_cols, NT) * scale
    spread.relay(3, False)
    for d in range(1, 4):
        spread.arrive([lax.rem(p.g + d, 4)], [sib, far])
    row_sum = jnp.zeros((part, width), F32)
    col_sum = jnp.zeros((part, width), F32)
    for n in range(4):
        row_sum = row_sum + dot(rowp_ref[n], e_ref[:, n].reshape(4 * part, width))
        col_sum = col_sum + dot(colp_ref[n], e_ref[n].reshape(4 * part, width))

    def through(total, weight):
        high, low = hi_lo(total)
        return (dot(high, weight) + dot(low, weight)).astype(BF)

    g_left = through(row_sum, right_ref[...])
    g_right = through(col_sum, left_ref[...])
    emb_t = emb_ref[...].astype(F32).T.astype(BF)
    gleft_ref[...] = dot(emb_t, g_left).astype(BF)
    gright_ref[...] = dot(emb_t, g_right).astype(BF)
    g_emb = dot(g_left, left_ref[...], NT) + dot(g_right, right_ref[...], NT)
    seqs, length = seg_ref.shape
    slots = part // seqs
    for n in range(seqs):
        members = slot_members(seg_ref[n : n + 1, :], slots)
        g_seg = g_emb[n * slots : (n + 1) * slots] / jnp.sum(members, axis=1, keepdims=True)
        high, low = hi_lo(g_seg)
        twice = jnp.concatenate([members, members], axis=0).T.astype(BF)
        sl = slice(n * length, (n + 1) * length)
        g_y = cot_ref[sl, :].astype(F32) + dot(twice, jnp.concatenate([high, low], axis=0))
        gy_ref[sl, :] = g_y
        gmlp_ref[sl, :] = g_y.astype(BF)
    for step in range(4):
        spread.own(step, True)
        spread.relay(step, True)


def pair_head(emb, rel_left, rel_right, row_panel, col_panel, mask, cot_out, seg_ids, scale):
    part, width = emb.shape
    size = mask.shape[0]
    vm = pl.BlockSpec(memory_space=pltpu.VMEM)
    dma = pltpu.SemaphoreType.DMA
    return pl.pallas_call(
        functools.partial(pair_kernel, scale=scale),
        in_specs=[vm] * 8,
        out_specs=[vm] * 5,
        out_shape=[
            jax.ShapeDtypeStruct((size, size), F32), jax.ShapeDtypeStruct(rel_left.shape, BF),
            jax.ShapeDtypeStruct(rel_right.shape, BF), jax.ShapeDtypeStruct(cot_out.shape, F32),
            jax.ShapeDtypeStruct(cot_out.shape, BF),
        ],
        scratch_shapes=Spread.scratch((part, width)) + [dma((1,))],
        compiler_params=pltpu.CompilerParams(
            collective_id=5, has_side_effects=True, vmem_limit_bytes=50 << 20
        ),
        name="pair_head",
    )(emb, rel_left, rel_right, row_panel, col_panel, mask, cot_out, seg_ids)


def norm_back_chunk(g_out, rows, gain):
    average, inverse = norm_stats(rows)
    z = (rows - average) * inverse
    g_z = g_out * gain
    mean_g = jnp.mean(g_z, axis=-1, keepdims=True)
    mean_gz = jnp.mean(g_z * z, axis=-1, keepdims=True)
    return inverse * (g_z - mean_g - z * mean_gz), jnp.sum(g_out * z, axis=0, keepdims=True)


def turn(source, target):
    @pl.loop(0, source.shape[0] // 128, unroll=2)
    def _(c):
        sl = pl.ds(pl.multiple_of(c * 128, 128), 128)
        target[:, sl] = source[sl, :].astype(F32).T.astype(BF)


def put_lines(ref, at, row):
    for j in range(row.shape[1] // 128):
        ref[at + j : at + j + 1, :] = row[:, j * 128 : (j + 1) * 128]


def mlp_back_kernel(*refs, n_ext, units, n_rows, comm, window):
    (slope_ref, wd_ref, wu_ref, gmlp_ref, h2_ref, r1_ref, gy_ref, ctx_ref, wo_ref, gain_ref) = refs[:10]
    at = 10
    arrays = refs[at : at + n_ext]
    at += n_ext
    gup_ref, gr1_ref, gout_ref, gctx_ref, small_ref = refs[at : at + 5]
    at += 5
    carried = refs[at : at + 2]
    at += 2 if comm else 0
    h2_buf, h2t_ref, acc_ref, r1_buf, gy_buf, ctx_buf, ctxt_ref, wo_buf, gatt_ref, in_sem = refs[at : at + 10]
    at += 10
    n_step = pl.num_programs(0)
    step = pl.program_id(0)
    count, feats = acc_ref.shape
    lines = feats // 128
    steps = (small_ref.shape[0] - 16) // lines - 4
    if comm:
        place = Place(n_rows)
        shares = Shares(
            place, units, PIECE, arrays, None, carried, (), (), refs[at : at + 7],
            refs[at + 7 : at + 10], (None, None),
        )
        done = on_the_way(units, 3)

    def inputs():
        pairs = (
            (h2_ref, h2_buf), (ctx_ref, ctx_buf), (r1_ref, r1_buf), (gy_ref, gy_buf), (wo_ref, wo_buf),
        )
        return [pltpu.make_async_copy(a, b, in_sem.at[i]) for i, (a, b) in enumerate(pairs)]

    @pl.when(step == 0)
    def _():
        for copy in inputs():
            copy.start()
        if comm:
            meet(place.peers())
            shares.begin(window)
        acc_ref[...] = jnp.zeros_like(acc_ref)
        small_ref[...] = jnp.zeros_like(small_ref)

    def beat(part):
        if comm:
            by_step(step, 0, steps, lambda n: shares.tick(2 * n + part, window, done))

    g_act = dot(gmlp_ref[...], wd_ref[...], NT)
    g_wide = g_act * slope_ref[...].astype(F32)
    g_u = g_wide.astype(BF)
    bias = jnp.sum(g_u.astype(F32), axis=0, keepdims=True)
    acc_ref[...] += dot(g_u, wu_ref[...], NT)
    beat(0)

    @pl.when(step == 0)
    def _():
        inputs()[0].wait()
        turn(h2_buf, h2t_ref)

    gup_ref[...] = dot(h2t_ref[...], g_u).astype(BF)
    for at_step in range(steps):
        @pl.when(step == at_step)
        def _(at_step=at_step):
            put_lines(small_ref, (4 + at_step) * lines, bias)
    beat(1)

    @pl.when(step == n_step - 1)
    def _():
        for copy in inputs()[1:]:
            copy.wait()
        chunk = 256

        def back(c, sums):
            sl = pl.ds(pl.multiple_of(c * chunk, chunk), chunk)
            g_out = acc_ref[sl, :]
            g_in, part = norm_back_chunk(g_out, r1_buf[sl, :], gain_ref[...].reshape(1, -1))
            g_r1 = gy_buf[sl, :] + g_in
            gr1_ref[sl, :] = g_r1
            gatt_ref[sl, :] = g_r1.astype(BF)
            return sums[0] + part, sums[1] + jnp.sum(g_out, axis=0, keepdims=True)

        nothing = jnp.zeros((1, feats), F32)
        gain_sum, bias_sum = lax.fori_loop(0, count // chunk, back, (nothing, nothing), unroll=2)
        put_lines(small_ref, 2 * lines, gain_sum)
        put_lines(small_ref, 3 * lines, bias_sum)
        if comm:
            shares.tick(2 * steps, window, done)
        turn(ctx_buf, ctxt_ref)
        gctx_ref[...] = dot(gatt_ref[...], wo_buf[...], NT).astype(BF)
        if comm:
            shares.tick(2 * steps + 1, window, done)
        gout_ref[...] = dot(ctxt_ref[...], gatt_ref[...]).astype(BF)
        if comm:
            for t in range(2 * steps + 2, shares.ticks()):
                shares.tick(t, window, done)
            shares.wait_sends()


def early_units():
    order = ((0, 0), (1, 0), (2, 0), (2, 1), (2, 2), (2, 3))
    return tuple(
        Unit(k, s, 0, n % 2 == 0, {0: 1 + n // 2 * 2, 1: 4 + n // 2 * 2}, leave=(n % 2, n // 2))
        for n, (k, s) in enumerate(order)
    )


def mlp_backward(
    slope, w_down, w_up, g_mlp, h2, r1, g_y, ctx, w_out, gain, small_rows, left, right, down, n_rows, comm
):
    count, feats = g_mlp.shape
    hidden = slope.shape[1]
    steps = hidden // feats
    vm = pl.BlockSpec(memory_space=pltpu.VMEM)
    any_ref = pl.BlockSpec(memory_space=pl.ANY)
    views = [view(g, n_rows) for g in (left, right, down)] if comm else []
    units = early_units()
    extra = []
    if comm:
        extra = [
            jax.ShapeDtypeStruct((3, 4, 2, 48, PIECE), BF),
            jax.ShapeDtypeStruct((3, n_rows, 4, 48, PIECE), BF),
        ]
    scratch = [
        pltpu.VMEM((count, feats), BF), pltpu.VMEM((feats, count), BF), pltpu.VMEM((count, feats), F32),
        pltpu.VMEM((count, feats), F32), pltpu.VMEM((count, feats), F32), pltpu.VMEM((count, feats), BF),
        pltpu.VMEM((feats, count), BF), pltpu.VMEM((feats, feats), BF), pltpu.VMEM((count, feats), BF),
        pltpu.SemaphoreType.DMA((5,)),
    ]
    params = dict(vmem_limit_bytes=63 << 20, dimension_semantics=("arbitrary",))
    if comm:
        scratch += Shares.scratch(units, PIECE, n_rows)
        params.update(collective_id=3, has_side_effects=True)
    return pl.pallas_call(
        functools.partial(
            mlp_back_kernel, n_ext=len(views), units=units, n_rows=n_rows, comm=comm, window=2,
        ),
        grid=(steps,),
        in_specs=[
            pl.BlockSpec((count, feats), lambda f: (0, f)),
            pl.BlockSpec((feats, feats), lambda f: (f, 0)),
            pl.BlockSpec((feats, feats), lambda f: (0, f)),
            vm, any_ref, any_ref, any_ref, any_ref, any_ref, vm,
        ] + [any_ref] * len(views),
        out_specs=[pl.BlockSpec((feats, feats), lambda f: (0, f)), vm, vm, vm, vm] + [vm] * len(extra),
        out_shape=[
            jax.ShapeDtypeStruct((feats, hidden), BF), jax.ShapeDtypeStruct((count, feats), F32),
            jax.ShapeDtypeStruct((feats, feats), BF), jax.ShapeDtypeStruct((count, feats), BF),
            jax.ShapeDtypeStruct((small_rows, 128), F32),
        ] + extra,
        scratch_shapes=scratch,
        compiler_params=pltpu.CompilerParams(**params),
        name="mlp_backward",
    )(slope, w_down, w_up, g_mlp, h2, r1, g_y, ctx, w_out, gain, *views)


def deliver_kernel(gx_ref, small_ref, *refs, parts, heads):
    n_in = sum(parts)
    ins, outs = refs[:n_in], refs[n_in:]
    outs[0][...] = gx_ref[...]

    @pl.when(pl.program_id(0) == 0)
    def _():
        at = 0
        for k, n in enumerate(parts):
            out = outs[1 + k]
            row = 0
            for ref in ins[at : at + n]:
                rows, x = ref.shape
                per = x // 128
                for j in range(per):
                    out[pl.ds(row + j, rows, stride=per), :] = ref[:, j * 128 : (j + 1) * 128]
                row += rows * per
            at += n
        line = 0
        for out in outs[1 + len(parts) :]:
            if len(out.shape) == 1:
                for j in range(out.shape[0] // 128):
                    out[j * 128 : (j + 1) * 128] = small_ref[line]
                    line += 1
            else:
                out[...] = small_ref[line : line + out.shape[0], :]


def deliver(g_tokens, small, shares, features, hidden, heads):
    count = g_tokens.shape[0]
    flat = [p for group in shares for p in group]
    vm = pl.BlockSpec(memory_space=pltpu.VMEM)
    block = count // 4
    sizes = [sum(p.size for p in group) for group in shares]
    results = pl.pallas_call(
        functools.partial(deliver_kernel, parts=tuple(len(group) for group in shares), heads=heads),
        grid=(4,),
        in_specs=[pl.BlockSpec((block, features), lambda i: (i, 0)), vm] + [vm] * len(flat),
        out_specs=[pl.BlockSpec((block, features), lambda i: (i, 0))] + [vm] * (len(shares) + 6),
        out_shape=[jax.ShapeDtypeStruct(g_tokens.shape, F32)]
        + [jax.ShapeDtypeStruct((size // 128, 128), F32) for size in sizes]
        + [jax.ShapeDtypeStruct((features,), F32)] * 4
        + [jax.ShapeDtypeStruct((hidden,), F32), jax.ShapeDtypeStruct((heads, 128), F32)],
        name="deliver",
    )(g_tokens, small, *flat)
    return (
        results[0], [r.reshape(-1) for r in results[1 : 1 + len(shares)]], results[1 + len(shares) :]
    )


def back_kernel(*refs, n_ext, units, tail, spans, n_rows, comm, window):
    (q_ref, k_ref, v_ref, e_ref, linv_ref, ctx_ref, gctx_ref, boxr_ref, boxc_ref, w_ref, h1_ref,
     x_ref, gr1_ref, gain_ref, small_ref) = refs[:15]
    at = 15
    arrays = refs[at : at + n_ext]
    at += n_ext
    carried = refs[at : at + 2] if comm else ()
    at += len(carried)
    n_out = len(spans)
    gx_ref = refs[at]
    small_out = refs[at + 1]
    at += 2
    if comm:
        outs = refs[at : at + n_out]
        at += n_out
    else:
        grad_ref = refs[at]
        at += 1
    (oha_ref, ohbt_ref, cx_ref, cy_ref, g_ref, gcx_ref, gcy_ref, lt_ref, gt_ref, gall_ref, h1t_ref,
     hist_ref, h1_buf, x_buf, gr1_buf, w_buf, pack_ref, in_sem) = refs[at : at + 18]
    at += 18
    length = q_ref.shape[0]
    half, quarter = 64, 32
    pairs, seqs = pl.num_programs(0), pl.num_programs(1)
    hp = pl.program_id(0)
    s_id = pl.program_id(1)
    n_seq = cx_ref.shape[0]
    n_pair = hist_ref.shape[0] // 2
    lane = lax.broadcasted_iota(jnp.int32, (1, 128), 1)
    low = lane < 64
    if comm:
        place = Place(n_rows)
        staging = refs[at]
        fins = refs[at + 1 : at + n_out + 1]
        at += n_out + 1
        got = refs[at : at + n_out]
        at += n_out
        known = (None,) * 3 + tuple(arrays) + (None,)
        ends = refs[at : at + 2]
        at += 2
        shares = Shares(
            place, units, PIECE, known, staging, carried, fins, got, refs[at : at + 7],
            refs[at + 7 : at + 10], ends,
        )
        at += 10
        thirds = Shares(
            place, tail, PIECE // 3, known, staging, carried, fins, got, refs[at : at + 7],
            refs[at + 7 : at + 10], ends,
        )
        at += 10
        done = on_the_way(units + tail, n_out)
        total = Total(place, pack_ref, small_out, refs[at : at + 5], refs[at + 5 : at + 7])

    def inputs():
        return (
            pltpu.make_async_copy(h1_ref, h1_buf, in_sem.at[0]),
            pltpu.make_async_copy(x_ref, x_buf, in_sem.at[1]),
            pltpu.make_async_copy(gr1_ref, gr1_buf, in_sem.at[2]),
            pltpu.make_async_copy(w_ref, w_buf, in_sem.at[3]),
        )

    @pl.when((hp == 0) & (s_id == 0))
    def _():
        for copy in inputs():
            copy.start()
        hist_ref[...] = jnp.zeros_like(hist_ref)
        if comm:
            meet(place.peers())
            shares.begin(window)

    @pl.when(hp == 0)
    def _():
        bc = boxc_ref[...]
        ax, _ = key_side(bc[:, 0:1], bc[:, 2:3], half)
        ay, _ = key_side(bc[:, 1:2], bc[:, 3:4], half)
        _, fbx = query_side(bc[:, 0:1], bc[:, 2:3], half)
        _, fby = query_side(bc[:, 1:2], bc[:, 3:4], half)
        spot = (lane % quarter).astype(F32)
        is_x = (lane % half) < quarter
        oha = jnp.where(jnp.where(is_x, ax, ay) == spot, jnp.where(low, 1.0, 0.0), 0.0)
        oha_ref[s_id] = oha.astype(BF)
        br = boxr_ref[...]
        _, gax = key_side(br[0:1], br[2:3], half)
        _, gay = key_side(br[1:2], br[3:4], half)
        rbx, _ = query_side(br[0:1], br[2:3], half)
        rby, _ = query_side(br[1:2], br[3:4], half)
        row = lax.broadcasted_iota(jnp.int32, (half, length), 0)
        rspot = (row % quarter).astype(F32)
        ohbt_ref[s_id] = jnp.where(jnp.where(row < quarter, rbx, rby) == rspot, 1.0, 0.0).astype(BF)
        cx_ref[s_id] = jnp.where(gax + fbx >= SPAN, 1.0, 0.0).astype(BF)
        cy_ref[s_id] = jnp.where(gay + fby >= SPAN, 1.0, 0.0).astype(BF)

    @pl.when((hp == 0) & (s_id == n_seq - 1))
    def _():
        inputs()[0].wait()
        turn(h1_buf, h1t_ref)

    k = k_ref[...]
    v = v_ref[...]
    lt_ref[...] = q_ref[...].astype(F32).T.astype(BF)
    gc = gctx_ref[...].astype(F32) * linv_ref[...]
    gcb = gc.astype(BF)
    gt_ref[...] = gcb.astype(F32).T.astype(BF)
    prod = gc * ctx_ref[...].astype(F32)
    ohbt = ohbt_ref[s_id]
    kts = []
    vts = []
    rows = 256
    n_step = n_pair * n_seq
    step = hp * n_seq + s_id
    for a in range(2):
        if comm and a == 1:
            by_step(step, 0, n_step, lambda n: shares.tick(2 * n, window, done))
        mine = low if a == 0 else jnp.logical_not(low)
        other = 64 - 64 * a
        d = jnp.sum(jnp.where(mine, prod, 0.0), axis=1, keepdims=True)
        dhi = d.astype(BF).astype(F32)
        extra = jnp.where(lane == other, dhi, jnp.where(lane == other + 1, d - dhi, 0.0))
        lhs = jnp.where(mine, gcb.astype(F32), extra).astype(BF)
        minus = jnp.where((lane == other) | (lane == other + 1), -1.0, 0.0).astype(BF)
        rhs = jnp.where(mine, v, minus)
        for c in range(length // rows):
            sl = slice(c * rows, (c + 1) * rows)
            gp = dot(lhs[sl], rhs, NT)
            g = (gp * e_ref[a, sl, :].astype(F32)).astype(BF)
            g_ref[a, sl, :] = g
            gcx_ref[a, sl, :] = g * cx_ref[s_id, sl, :]
            gcy_ref[a, sl, :] = g * cy_ref[s_id, sl, :]
        left = jnp.concatenate([lt_ref[64 * a : 64 * a + 64, :], ohbt], axis=0)
        r0 = dot(left, g_ref[a])
        rx = dot(ohbt[:quarter], gcx_ref[a])
        ry = dot(ohbt[quarter:], gcy_ref[a])
        vts.append(dot(gt_ref[64 * a : 64 * a + 64, :], e_ref[a]))
        kts.append(r0[:64])
        w = jnp.concatenate([r0[64:], rx, ry], axis=0)
        whi, wlo = hi_lo(w)
        red = dot(jnp.concatenate([whi, wlo], axis=0), oha_ref[s_id])
        hist_ref[2 * hp + a] += red[:128] + red[128:]
    zero = jnp.zeros_like(k)
    gq = dot(g_ref[0], jnp.where(low, k, zero)) + dot(g_ref[1], jnp.where(low, zero, k))
    own_rows = pl.ds(pl.multiple_of(s_id * length, length), length)
    feats = h1_buf.shape[1]
    parts = [pl.ds(pl.multiple_of(p * feats + hp * 128, 128), 128) for p in range(3)]
    gall_ref[own_rows, parts[0]] = (gq * 0.125).astype(BF)
    gall_ref[own_rows, parts[1]] = (jnp.concatenate(kts, axis=0) * 0.125).T.astype(BF)
    gall_ref[own_rows, parts[2]] = jnp.concatenate(vts, axis=0).T.astype(BF)

    @pl.when(s_id == n_seq - 1)
    def _():
        g_pair = jnp.concatenate([gall_ref[:, part] for part in parts], axis=1)
        piece = dot(h1t_ref[...], g_pair).astype(BF)
        if comm:
            staging[lax.div(hp, 2), lax.rem(hp, 2)] = piece.reshape(staging.shape[2:])
        else:
            grad_ref[0] = piece[:, :128]
            grad_ref[1] = piece[:, 128:256]
            grad_ref[2] = piece[:, 256:]

    if comm:
        def beat_of(at_step):
            for part in (shares, thirds):
                for i, unit in enumerate(part.units):
                    source = unit.source or ("", 0)
                    if source[0] == "own" and (2 * source[1] + 2) * n_seq - 1 == at_step:
                        part.start(i, 0)
            if at_step < n_step - 1:
                shares.tick(2 * at_step + 1, window, done)

        by_step(step, 0, n_step, beat_of)

    @pl.when((hp == n_pair - 1) & (s_id == n_seq - 1))
    def _():
        for copy in inputs()[1:]:
            copy.wait()
        gain = gain_ref[...].reshape(1, -1)
        count = x_buf.shape[0]
        chunk = 256
        beat = 2 * n_step - 1
        gain_sum = jnp.zeros((1, feats), F32)
        bias_sum = jnp.zeros((1, feats), F32)
        pack_ref[...] = small_ref[...]
        base = pack_ref.shape[0] - 16
        for h in range(2 * n_pair):
            w = hist_ref[h]
            line = jnp.zeros((1, 128), F32)
            for axis in range(2):
                plain = w[axis * quarter : (axis + 1) * quarter]
                carry = w[half + axis * quarter : half + (axis + 1) * quarter]
                keep = (lane >= axis * quarter) & (lane < (axis + 1) * quarter)
                stay = jnp.where(keep, plain - carry, 0.0)
                move = jnp.where(keep, carry, 0.0)
                shift = axis * (half - quarter)
                stay = pltpu.roll(stay, shift, 1, stride=1, stride_axis=0)
                move = pltpu.roll(move, shift + 1, 1, stride=1, stride_axis=0)
                line = line + jnp.sum(stay + move, axis=0, keepdims=True)
            pack_ref[base + h : base + h + 1, :] = line
        for c in range(count // chunk):
            sl = slice(c * chunk, (c + 1) * chunk)
            g_out = dot(gall_ref[sl, :], w_buf[...], NT)
            g_in, part = norm_back_chunk(g_out, x_buf[sl, :].astype(F32), gain)
            gx_ref[sl, :] = gr1_buf[sl, :] + g_in
            gain_sum = gain_sum + part
            bias_sum = bias_sum + jnp.sum(g_out, axis=0, keepdims=True)
            if comm:
                for t in range(beat, beat + 2):
                    shares.tick(t, window, done)
                    thirds.tick(t, window, done)
                beat += 2
        lines = feats // 128
        put_lines(pack_ref, 0, gain_sum)
        put_lines(pack_ref, lines, bias_sum)
        if comm:
            total.start(0)
            stage = 0
            for t in range(beat, max(shares.ticks(), thirds.ticks())):
                shares.tick(t, window, done)
                thirds.tick(t, window, done)
                if t in SUM_BEATS:
                    total.finish(stage)
                    if stage < 3:
                        total.start(stage + 1)
                    stage += 1
            for stage in range(stage, 4):
                total.finish(stage)
                if stage < 3:
                    total.start(stage + 1)
            for n, out in enumerate(outs):
                shares.deliver(n, out, spans[n])
            thirds.wait_sends()
            total.wait_sends()
            shares.wait_sends()
        else:
            small_out[...] = pack_ref[...]


SUM_BEATS = (34, 39, 43, 46)


def late_units():
    rest = ((0, 4, 8), (0, 4, 9), (3, 7, 11), (3, 7, 12), (5, 8, 14), (5, 8, 16))
    units = [
        Unit(
            unit.array, unit.part, 0, unit.rows_first, {"in": enter, 2: second, 3: third},
            source=("mid",) + unit.leave,
        )
        for unit, (enter, second, third) in zip(early_units(), rest)
    ]
    whole = (
        (4, 0, True, (7, 12, 18, 22)), (4, 1, False, (7, 12, 17, 20)), (3, 0, True, (11, 16, 19, 23)),
        (4, 2, False, (11, 16, 23, 28)), (4, 3, True, (22, 27, 33, 42)),
    )
    units += [Unit(k, 0, j, first, dict(enumerate(beats))) for k, j, first, beats in whole]
    own = ((True, (12, 21, 23, 31)), (False, (18, 23, 29, 37)))
    units += [
        Unit(5, 0, t, first, dict(enumerate(beats)), source=("own", t, 0))
        for t, (first, beats) in enumerate(own)
    ]
    thirds = ((True, (27, 32, 38, 44)), (True, (27, 35, 40, 45)), (False, (27, 36, 41, 47)))
    tail = tuple(
        Unit(5, 0, 6 + n, first, dict(enumerate(beats)), source=("own", 2, n * PIECE // 3))
        for n, (first, beats) in enumerate(thirds)
    )
    return tuple(units), tail


def attend_and_project_backward(
    qkv, e, linv, ctx, gctx, boxes_r, boxes_c, weight, h1, tokens, g_r1, gain, small, arrays,
    carried, n_rows, comm
):
    count, width = qkv.shape
    feats = width // 3
    heads, seqs, length, _ = e.shape
    pairs = heads // 2
    rows_of = lambda off: pl.BlockSpec((length, 128), lambda h, s: (s, off + h))
    any_ref = pl.BlockSpec(memory_space=pl.ANY)
    vm = pl.BlockSpec(memory_space=pltpu.VMEM)
    views = [view(g, n_rows) for g in arrays] if comm else []
    n_ext = len(views)
    units, tail = late_units() if comm else ((), ())
    out_shape = [jax.ShapeDtypeStruct((count, feats), F32), jax.ShapeDtypeStruct(small.shape, F32)]
    out_specs = [vm, vm]
    spans = []
    scratch = [
        pltpu.VMEM((seqs, length, 128), BF), pltpu.VMEM((seqs, 64, length), BF),
        pltpu.VMEM((seqs, length, length), BF), pltpu.VMEM((seqs, length, length), BF),
        pltpu.VMEM((2, length, length), BF), pltpu.VMEM((2, length, length), BF),
        pltpu.VMEM((2, length, length), BF), pltpu.VMEM((128, length), BF),
        pltpu.VMEM((128, length), BF), pltpu.VMEM((count, width), BF), pltpu.VMEM((feats, count), BF),
        pltpu.VMEM((heads, 128, 128), F32), pltpu.VMEM((count, feats), BF),
        pltpu.VMEM((count, feats), BF), pltpu.VMEM((count, feats), F32), pltpu.VMEM((feats, width), BF),
        pltpu.VMEM(small.shape, F32), pltpu.SemaphoreType.DMA((4,)),
    ]
    params = dict(vmem_limit_bytes=63 << 20, dimension_semantics=("arbitrary", "arbitrary"))
    if comm:
        hidden = views[-1].shape[5]
        sizes = [(24, feats), (24, feats), (24 * hidden // feats, feats), (24, feats), (24, hidden), (24, width)]
        for rows, x in sizes[:-1]:
            spans.append([(j * 2 * PIECE, PIECE, PIECE) for j in range(x // (2 * PIECE))])
        spans.append(
            [(p * feats + t * 256, 128, 128) for t in range(pairs // 2) for p in range(3)]
        )
        out_shape += [jax.ShapeDtypeStruct(size, F32) for size in sizes]
        out_specs += [vm] * len(sizes)
        tbufs, tsems = Total.scratch(small.shape, n_rows)
        scratch += [pltpu.VMEM((pairs // 2, 2, n_rows, 4, 2, 48, PIECE), BF)]
        scratch += Shares.result_scratch(sizes) + Shares.scratch(units, PIECE, n_rows)
        scratch += Shares.scratch(tail, PIECE // 3, n_rows) + tbufs + tsems
        params.update(collective_id=2, has_side_effects=True)
    else:
        out_shape.append(jax.ShapeDtypeStruct((3, feats, feats), BF))
        out_specs.append(pl.BlockSpec((3, feats, 128), lambda h, s: (0, 0, h)))
    results = pl.pallas_call(
        functools.partial(
            back_kernel, n_ext=n_ext, units=units, tail=tail, spans=spans, n_rows=n_rows, comm=comm, window=2,
        ),
        grid=(pairs, seqs),
        in_specs=[
            rows_of(0), rows_of(pairs), rows_of(2 * pairs),
            pl.BlockSpec((2, None, length, length), lambda h, s: (h, s, 0, 0)),
            rows_of(0), rows_of(0), rows_of(0),
            pl.BlockSpec((4, length), lambda h, s: (0, s)),
            pl.BlockSpec((length, 128), lambda h, s: (s, 0)),
            any_ref, any_ref, any_ref, any_ref, vm, vm,
        ] + [any_ref] * (n_ext + len(carried)),
        out_specs=out_specs,
        out_shape=out_shape,
        scratch_shapes=scratch,
        compiler_params=pltpu.CompilerParams(**params),
        name="attend_backward",
    )(
        qkv, qkv, qkv, e, linv, ctx, gctx, boxes_r, boxes_c, weight, h1, tokens, g_r1,
        gain, small, *views, *carried,
    )
    return results


EPSILON = 1e-05


def norm_stats(rows):
    average = jnp.mean(rows, axis=-1, keepdims=True)
    centred = rows - average
    variance = jnp.mean(centred * centred, axis=-1, keepdims=True)
    return average, lax.rsqrt(variance + EPSILON)


def gelu_pair(u):
    bell = jnp.exp2(u * u * (-0.5 * LOG2E))
    below = 0.5 + 0.5 * lax.erf(u * math.sqrt(0.5))
    return u * below, below + u * bell * (1.0 / math.sqrt(2.0 * math.pi))


def body(
    tokens, boxes, page_ids, seg_ids, pair_mask, ln1_gain, ln1_bias, query_key_value_weight,
    attention_output_weight, ln2_gain, ln2_bias, up_projection_weight, up_projection_bias,
    down_projection_weight, box_table, rel_left, rel_right, cot_out, cot_logits,
):
    features = tokens.shape[1]
    h1, qkv, boxes_c = project_forward(
        tokens, ln1_gain, ln1_bias, query_key_value_weight, boxes, page_ids
    )
    pair_scale = 1.0 / math.sqrt(rel_left.shape[1])
    ctx, e, linv, row_panel, col_panel = attend_forward(
        qkv, boxes, boxes_c, page_ids.shape[0], box_table, pair_mask[0], cot_logits[0], pair_scale
    )
    r1, h2, act, slope, layer_out, embedded = mlp_forward(
        ctx, attention_output_weight, tokens, ln2_gain, ln2_bias, up_projection_weight,
        up_projection_bias, down_projection_weight, seg_ids, SLOTS,
    )
    pair_logits, grad_rel_left, grad_rel_right, g_y, g_mlp = pair_head(
        embedded, rel_left, rel_right, row_panel, col_panel, pair_mask[0], cot_out, seg_ids, pair_scale
    )
    grad_down = dot(act, g_mlp, (((0,), (0,)), ((), ()))).astype(BF)
    n_rows = lax.axis_size("rows")
    comm = n_rows * 8 * 48 <= features
    heads = box_table.shape[0]
    hidden = slope.shape[1]
    small_rows = (4 * features + hidden) // 128 + 16
    grad_up, g_r1, grad_out, g_ctx, small, *early = mlp_backward(
        slope, down_projection_weight, up_projection_weight, g_mlp, h2, r1, g_y, ctx,
        attention_output_weight, ln2_gain, small_rows, grad_rel_left, grad_rel_right, grad_down,
        n_rows, comm,
    )
    g_tokens, small, *late = attend_and_project_backward(
        qkv, e, linv, ctx, g_ctx, boxes, boxes_c, query_key_value_weight, h1, tokens, g_r1, ln1_gain,
        small, (grad_out, grad_up), early, n_rows, comm,
    )
    if comm:
        left, right, down, out, up, qkv_part = late
        shares = [[left], [right], [out], [down], [up], [qkv_part]]
    else:
        grad_qkv = jnp.concatenate([late[0][0], late[0][1], late[0][2]], axis=1)
        flats = [
            lax.psum_scatter(g, AXES, scatter_dimension=0, tiled=True).astype(F32).reshape(-1)
            for g in (grad_rel_left, grad_rel_right, grad_out, grad_down, grad_up, grad_qkv)
        ]
        shares = [[flat.reshape(-1, 128)] for flat in flats]
        small = lax.psum(small, AXES)
    grad_tokens, flats, vectors = deliver(g_tokens, small, shares, features, hidden, heads)
    left_share, right_share, out_share, down_share, up_share, qkv_share = flats
    return (
        layer_out, pair_logits[None], grad_tokens, vectors[0], vectors[1], qkv_share, out_share,
        vectors[2], vectors[3], up_share, vectors[4], down_share, vectors[5], left_share, right_share,
    )


def solution(mesh):
    whole = P(AXES, None)
    tile = P("rows", "gr", "gc")
    flat = P(AXES)
    one = P()
    in_specs = (
        whole, P(None, AXES), whole, whole, tile, one, one, one, one, one, one, one, one, one, one,
        one, one, whole, tile,
    )
    out_specs = (
        whole, tile, whole, one, one, flat, flat, one, one, flat, one, flat, one, flat, flat,
    )
    return jax.shard_map(body, mesh=mesh, in_specs=in_specs, out_specs=out_specs, check_vma=False)
```

```python
import functools
import math

import jax
import jax.numpy as jnp
from jax import lax
from jax.experimental import pallas as pl
from jax.experimental.pallas import tpu as pltpu
from jax.sharding import PartitionSpec as P

COORD=1000
SPAN=2*COORD+1
LOG2E=1.4426950408889634
BARRED=-2.0**99
SLOTS=64
BF=jnp.bfloat16
F32=jnp.float32
NT=(((1,),(1,)),((),()))
NN=(((1,),(0,)),((),()))
def dot(a,b,dims=NN):
    return lax.dot_general(a,b,dims,preferred_element_type=F32)

def whole_and_rest(scaled):
    whole=jnp.floor((scaled+0.5)*(1.0/SPAN))
    return whole, scaled-SPAN*whole

def key_side(low, high, half):
    c=jnp.floor((low+high).astype(F32)*0.5)
    return whole_and_rest(c*half)
def query_side(low, high, half):
    c=jnp.floor((low+high).astype(F32)*0.5)
    return whole_and_rest((COORD-c)*half)

def hi_lo(v):
    hi=v.astype(BF)
    return hi, (v-hi.astype(F32)).astype(BF)

def fwd_kernel(q_ref,k_ref,v_ref,boxr_ref,boxc_ref,tab_ref,mask_ref,cot_ref,
               ctx_ref,e_ref,linv_ref,rowp_ref,colp_ref,
               ohb_ref,oha_ref,kg_ref,rxy_ref,pg_ref,cx_ref,cy_ref,*panel_refs,rows,pair_scale):
    length=q_ref.shape[0]
    half=tab_ref.shape[1]//2
    quarter=half//2
    hp=pl.program_id(1)
    seq=pl.program_id(0)
    place=Place(1)
    mask_buf,cot_buf,in_sem=panel_refs[:3]
    panels=Panels(place,*panel_refs[3:7],panel_refs[7:])
    def inputs():
        return (pltpu.make_async_copy(mask_ref,mask_buf,in_sem.at[0]),
                pltpu.make_async_copy(cot_ref,cot_buf,in_sem.at[1]))
    @pl.when((hp==0)&(seq==0))
    def _():
        for copy in inputs():
            copy.start()
    @pl.when((hp==1)&(seq==0))
    def _():
        for copy in inputs():
            copy.wait()
        panels.fill(mask_buf,cot_buf,pair_scale)
        meet([place.gc_peer(d) for d in (1,2,3)]+[place.gr_peer(d) for d in (1,2,3)])
    @pl.when((hp==2)&(seq==0))
    def _():
        panels.start()
    lane=lax.broadcasted_iota(jnp.int32,(1,128),1)
    low=lane<64
    @pl.when(hp==0)
    def _():
        bc=boxc_ref[...]
        ax,fax=key_side(bc[:,0:1],bc[:,2:3],half)
        ay,fay=key_side(bc[:,1:2],bc[:,3:4],half)
        bx,fbx=query_side(bc[:,0:1],bc[:,2:3],half)
        by,fby=query_side(bc[:,1:2],bc[:,3:4],half)
        spot=(lane%quarter).astype(F32)
        is_x=(lane%half)<quarter
        oha=jnp.where(jnp.where(is_x,ax,ay)==spot,1.0,0.0)
        ohb=jnp.where(jnp.where(is_x,bx,by)==(quarter-1)-spot,1.0,0.0)
        ohb_ref[...]=jnp.where(low,ohb,0.0).astype(BF)
        oha_ref[...]=oha.astype(BF)
        page=bc[:,4:5].astype(jnp.int32)
        mine=(lane%64)==page
        barred=jnp.where((lane%64)<4,jnp.where(mine,0.0,BARRED),0.0)
        kg_ref[0]=jnp.where(low,oha,barred).astype(BF)
        kg_ref[1]=jnp.where(low,barred,oha).astype(BF)
        pg_ref[...]=jnp.where(mine,1.0,0.0).astype(BF)
        ohx=jnp.where(ax==spot,1.0,0.0)
        ohy=jnp.where(ay==spot,1.0,0.0)
        rxy_ref[pl.ds(0,length),:]=jnp.where(low,ohx,0.0).astype(BF)
        rxy_ref[pl.ds(length,length),:]=jnp.where(low,0.0,ohy).astype(BF)
        br=boxr_ref[...]
        _,gax=key_side(br[0:1],br[2:3],half)
        _,gay=key_side(br[1:2],br[3:4],half)
        cx_ref[...]=jnp.where(gax+fbx>=SPAN,1.0,0.0)
        cy_ref[...]=jnp.where(gay+fby>=SPAN,1.0,0.0)
    k=k_ref[...]
    v=v_ref[...]
    oha=oha_ref[...]
    b_row=lax.broadcasted_iota(jnp.int32,(half,128),0)
    l_col=lax.broadcasted_iota(jnp.int32,(half,128),1)
    row_x=b_row<quarter
    same_axis=row_x==((l_col%half)<quarter)
    d_axis=row_x==(l_col<half)
    heads=[]
    for a in range(2):
        t=tab_ref[pl.ds(2*hp+a,1),:]
        both=[jnp.where(low,t,0.0)+pltpu.roll(jnp.where(low,t,0.0),64,1),
              jnp.where(low,0.0,t)+pltpu.roll(jnp.where(low,0.0,t),64,1)]
        tiles=[]
        for b in both:
            spreads=[]
            for first in (0,1):
                whole=jnp.broadcast_to(b,(quarter,128))
                turned=pltpu.roll(whole,128-(quarter-1)-first,1,stride=1,stride_axis=0)
                lowq=jnp.where(lane<quarter,turned,0.0)
                pair=lowq+pltpu.roll(lowq,quarter,1)
                spreads.append(pair+pltpu.roll(pair,64,1))
            tiles.append(spreads)
        base=jnp.concatenate([tiles[0][0],tiles[1][0]],axis=0)
        nxt=jnp.concatenate([tiles[0][1],tiles[1][1]],axis=0)
        hi,lo=hi_lo(base)
        dhi,dlo=hi_lo(nxt-base)
        z=jnp.zeros_like(hi)
        is_hi=(l_col<64)==(a==1)
        g0=jnp.where(same_axis,jnp.where(is_hi,hi.astype(F32),lo.astype(F32)),0.0).astype(BF)
        g1=jnp.where(d_axis,jnp.where((l_col%half)<quarter,dhi.astype(F32),dlo.astype(F32)),0.0).astype(BF)
        hk=jnp.concatenate([g0,g1],axis=1)
        left=dot(ohb_ref[:,0:half],hk).astype(BF)
        if a==0:
            rhs=jnp.concatenate([jnp.where(low,k,oha),kg_ref[0]],axis=1)
            vv=jnp.where(low,v,jnp.ones_like(v))
        else:
            rhs=jnp.concatenate([jnp.where(low,oha,k),kg_ref[1]],axis=1)
            vv=jnp.where(low,jnp.ones_like(v),v)
        heads.append((left,rhs,vv))
    for c in range(length//rows):
        sl=pl.ds(c*rows,rows)
        q=q_ref[sl,:]*jnp.asarray(0.125,BF)
        pg=pg_ref[sl,:]
        outs=[]
        for a in range(2):
            left,rhs,vv=heads[a]
            lc=left[c*rows:(c+1)*rows]
            g0=lc[:,:128]
            if a==0:
                lhs=jnp.concatenate([jnp.where(low,q,g0),jnp.where(low,g0,pg)],axis=1)
            else:
                lhs=jnp.concatenate([jnp.where(low,g0,q),jnp.where(low,pg,g0)],axis=1)
            s=dot(lhs,rhs,NT)
            s=s+cx_ref[sl,:]*dot(lc[:,128:],rxy_ref[pl.ds(0,length),:],NT)
            s=s+cy_ref[sl,:]*dot(lc[:,128:],rxy_ref[pl.ds(length,length),:],NT)
            m=jnp.max(s,axis=1,keepdims=True)
            e=jnp.exp2((s-m)*LOG2E).astype(BF)
            e_ref[a,sl,:]=e
            outs.append(dot(e,vv))
        ctx=jnp.where(low,outs[0],outs[1])
        tot=jnp.where(low,pltpu.roll(outs[0],64,1),pltpu.roll(outs[1],64,1))
        linv=1.0/tot
        linv_ref[sl,:]=linv
        ctx_ref[sl,:]=(ctx*linv).astype(BF)
    @pl.when((hp==pl.num_programs(1)-1)&(seq==pl.num_programs(0)-1))
    def _():
        panels.collect(rowp_ref,colp_ref)

def attend_forward(qkv,boxes_r,boxes_c,seqs,table,mask,cot,pair_scale,rows=512):
    tokens,width=qkv.shape
    feats=width//3
    length=tokens//seqs
    heads=table.shape[0]
    pairs=heads//2
    return pl.pallas_call(
        functools.partial(fwd_kernel,rows=rows,pair_scale=pair_scale),
        grid=(seqs,pairs),
        in_specs=[
            pl.BlockSpec((length,128),lambda s,h:(s,h)),
            pl.BlockSpec((length,128),lambda s,h:(s,pairs+h)),
            pl.BlockSpec((length,128),lambda s,h:(s,2*pairs+h)),
            pl.BlockSpec((4,length),lambda s,h:(0,s)),
            pl.BlockSpec((length,128),lambda s,h:(s,0)),
            pl.BlockSpec(table.shape,lambda s,h:(0,0)),
            pl.BlockSpec(memory_space=pl.ANY),
            pl.BlockSpec(memory_space=pl.ANY),
        ],
        out_specs=[
            pl.BlockSpec((length,128),lambda s,h:(s,h)),
            pl.BlockSpec((2,None,length,length),lambda s,h:(h,s,0,0)),
            pl.BlockSpec((length,128),lambda s,h:(s,h)),
            pl.BlockSpec(memory_space=pltpu.VMEM),
            pl.BlockSpec(memory_space=pltpu.VMEM),
        ],
        out_shape=[jax.ShapeDtypeStruct((tokens,feats),BF),
                   jax.ShapeDtypeStruct((heads,seqs,length,length),BF),
                   jax.ShapeDtypeStruct((tokens,feats),F32)]
                  +[jax.ShapeDtypeStruct((4,mask.shape[0]//4,mask.shape[0]),BF)]*2,
        scratch_shapes=[pltpu.VMEM((length,128),BF),pltpu.VMEM((length,128),BF),
                        pltpu.VMEM((2,length,128),BF),pltpu.VMEM((2*length,128),BF),
                        pltpu.VMEM((length,128),BF),
                        pltpu.VMEM((length,length),F32),pltpu.VMEM((length,length),F32)]
                       +[pltpu.VMEM(mask.shape,jnp.int32),pltpu.VMEM(cot.shape,BF),pltpu.SemaphoreType.DMA((2,))]
                       +Panels.scratch(mask.shape[0]),
        compiler_params=pltpu.CompilerParams(collective_id=4,has_side_effects=True,vmem_limit_bytes=60<<20),
        name="attend_forward",
    )(qkv,qkv,qkv,boxes_r,boxes_c,table,mask,cot)


AXES = ("rows", "gr", "gc")
MESH = pl.DeviceIdType.MESH
PIECE = 384


class Place:
    def __init__(self, n_rows):
        self.n_rows = n_rows
        self.r = lax.axis_index("rows")
        self.g = lax.axis_index("gr")
        self.c = lax.axis_index("gc")
        self.core = lax.rem(self.c, 2)
        self.u = lax.div(self.c, 2)
        self.sibling = {"gc": self.u * 2 + 1 - self.core}
        self.across = {"gc": (1 - self.u) * 2 + self.core}

    def row_peer(self, d):
        return {"rows": lax.rem(self.r + d, self.n_rows)}

    def gr_peer(self, d):
        return {"gr": lax.rem(self.g + d, 4)}

    def gc_peer(self, d):
        return {"gc": lax.rem(self.c + d, 4)}

    def peers(self):
        return (
            [self.sibling, self.across]
            + [self.row_peer(d) for d in range(1, self.n_rows)]
            + [self.gr_peer(d) for d in range(1, 4)]
        )


def meet(peers):
    barrier = pltpu.get_barrier_semaphore()
    for peer in peers:
        pl.semaphore_signal(barrier, inc=1, device_id=peer, device_id_type=MESH)
    pl.semaphore_wait(barrier, len(peers))


def send(src, dst, send_sem, recv_sem, peer):
    return pltpu.make_async_remote_copy(
        src_ref=src, dst_ref=dst, send_sem=send_sem, recv_sem=recv_sem, device_id=peer,
        device_id_type=MESH,
    )


def by_step(step, first, end, action):
    if end - first == 1:
        action(first)
        return
    middle = (first + end) // 2
    pl.when(step < middle)(lambda: by_step(step, first, middle, action))
    pl.when(step >= middle)(lambda: by_step(step, middle, end, action))


class Unit:
    def __init__(self, array, part, block, rows_first, beats, source=None, leave=None):
        self.array, self.part, self.block = array, part, block
        self.rows_first, self.beats, self.source, self.leave = rows_first, beats, source, leave
        self.stages = sorted(stage for stage in beats if stage != "in")
        self.fresh = self.stages[0] == 0

    def does(self, stage):
        return stage in self.beats


class Shares:
    def __init__(self, place, units, piece, arrays, staging, carried, fins, got, bufs, sems, ends):
        self.p = place
        self.units = units
        self.piece = piece
        self.arrays = arrays
        self.staging = staging
        self.carried = carried
        self.fin = fins
        self.got = got
        self.own, self.b0, self.b1r, self.b1u, self.b2r, self.b2u, self.b3 = bufs
        self.ls, self.ss, self.rs = sems
        self.fs, self.fr = ends
        external = [i for i, unit in enumerate(units) if unit.source is None]
        self.external = sorted(external, key=lambda i: units[i].beats[0])

    def number(self, i, test):
        return sum(test(unit) for unit in self.units[:i])

    @staticmethod
    def kinds():
        return (
            lambda unit: True,
            lambda unit: unit.does(0),
            lambda unit: unit.does(1) and unit.rows_first,
            lambda unit: unit.does(1) and not unit.rows_first,
            lambda unit: unit.does(2) and not unit.rows_first,
            lambda unit: unit.does(2) and unit.rows_first,
            lambda unit: unit.does(3),
        )

    @staticmethod
    def scratch(units, piece, n_rows):
        n, m, r = len(units), 48, n_rows
        shapes = (
            (r, 4, 2, m), (r, 4, 2, m), (r - 1, 4, 2, m), (r, 4, m), (r - 1, 4, m), (4, m), (3, m),
        )
        bufs = [
            pltpu.VMEM((max(1, sum(map(test, units))),) + shape + (piece,), BF)
            for test, shape in zip(Shares.kinds(), shapes)
        ]
        dma = pltpu.SemaphoreType.DMA
        return bufs + [dma((n,)), dma((n, r + 4)), dma((n, r + 4))]

    @staticmethod
    def result_scratch(sizes):
        dma = pltpu.SemaphoreType.DMA
        k = len(sizes)
        fins = [pltpu.VMEM((2, rows, x // 2), F32) for rows, x in sizes]
        got = [pltpu.VMEM((rows, x // 2), F32) for rows, x in sizes]
        return fins + got + [dma((k,)), dma((k,))]

    def buffer(self, kind, i):
        bufs = (self.own, self.b0, self.b1r, self.b1u, self.b2r, self.b2u, self.b3)
        return bufs[kind].at[self.number(i, self.kinds()[kind])]

    def piece_of(self, i, core):
        unit = self.units[i]
        if unit.source is None:
            at = unit.block * 2 * self.piece + core * self.piece
            columns = pl.ds(pl.multiple_of(at, 128), self.piece)
            return self.arrays[unit.array].at[:, :, :, unit.part, :, columns]
        _, n, column = unit.source
        return self.staging.at[n, core, :, :, :, :, column : column + self.piece]

    def swap(self, i):
        src = self.piece_of(i, 1 - self.p.core)
        return send(src, self.buffer(1, i), self.ss.at[i, 0], self.rs.at[i, 0], self.p.sibling)

    def keep(self, i):
        unit, p = self.units[i], self.p
        if unit.source is None:
            src, to = self.piece_of(i, p.core), self.own.at[i]
        else:
            src = self.carried[unit.source[1]].at[unit.source[2]]
            if unit.does(2):
                to = self.own.at[i, p.r] if unit.rows_first else self.own.at[i, :, :, p.u]
            else:
                to = self.own.at[i, p.r, :, p.u]
        return pltpu.make_async_copy(src, to, self.ls.at[i])

    def along_rows(self, i, first):
        p = self.p
        out = []
        for d in range(1, p.n_rows):
            to = lax.rem(p.r + d, p.n_rows)
            src = self.own.at[i, to] if first else self.own.at[i, to, :, p.u]
            dst = self.buffer(2 if first else 4, i).at[d - 1]
            out.append(send(src, dst, self.ss.at[i, 1 + d], self.rs.at[i, 1 + d], p.row_peer(d)))
        return out

    def across(self, i, first):
        p = self.p
        src = self.own.at[i, :, :, 1 - p.u] if first else self.own.at[i, p.r, :, 1 - p.u]
        dst = self.buffer(3 if first else 5, i)
        return [send(src, dst, self.ss.at[i, 1], self.rs.at[i, 1], p.across)]

    def along_gr(self, i):
        p = self.p
        out = []
        for d in range(1, 4):
            src = self.own.at[i, p.r, lax.rem(p.g + d, 4), p.u]
            at = p.n_rows + d
            dst = self.buffer(6, i).at[d - 1]
            out.append(send(src, dst, self.ss.at[i, at], self.rs.at[i, at], p.gr_peer(d)))
        return out

    def copies(self, i, stage):
        if stage == 0:
            return [self.swap(i)]
        if stage == 3:
            return self.along_gr(i)
        if self.units[i].rows_first == (stage == 1):
            return self.along_rows(i, stage == 1)
        return self.across(i, stage == 1)

    def start(self, i, stage):
        if stage == 0 and self.units[i].source is None:
            self.keep(i).start()
        for copy in self.copies(i, stage):
            copy.start()

    def finish(self, i, stage):
        p, unit = self.p, self.units[i]
        if stage == 0 and unit.source is None:
            self.keep(i).wait()
        for copy in self.copies(i, stage):
            copy.wait_recv()
        if stage == 0:
            to = self.own.at[i]
            mine = to if unit.source is None else self.piece_of(i, p.core)
            theirs = self.buffer(1, i)

            @pl.loop(0, 4)
            def _(n):
                to[:, n] = mine[:, n] + theirs[:, n]

            return
        if stage == 3:
            total = self.own[i, p.r, p.g, p.u].astype(F32)
            for d in range(3):
                total = total + self.buffer(6, i)[d].astype(F32)
            m = total.shape[0]
            fin = self.fin[unit.array]
            rows = fin.shape[1]
            span = slice(unit.block * self.piece, (unit.block + 1) * self.piece)
            if rows < m:
                fin[0, :, span] = total[:rows]
                fin[1, :, span] = total[rows:]
            else:
                per = rows // m
                row = (unit.part % per) * m
                fin[unit.part // per, row : row + m, span] = total
            return
        if stage == 2:
            to = self.own.at[i, p.r, :, p.u]
        else:
            to = self.own.at[i, p.r] if unit.rows_first else self.own.at[i, :, :, p.u]
        if unit.rows_first == (stage == 1):
            terms = [self.buffer(2 if stage == 1 else 4, i).at[d] for d in range(p.n_rows - 1)]
        else:
            terms = [self.buffer(3 if stage == 1 else 5, i)]
        out = to
        if unit.leave is not None and stage == unit.stages[-1]:
            out = self.carried[unit.leave[0]].at[unit.leave[1]]
        if stage == 1:
            @pl.loop(0, 4)
            def _(n):
                at = n if unit.rows_first else (slice(None), n)
                total = to[at]
                for term in terms:
                    total = total + term[at]
                out[at] = total
        else:
            total = to[...]
            for term in terms:
                total = total + term[...]
            out[...] = total

    def last(self, k):
        return send(
            self.fin[k].at[1 - self.p.core], self.got[k], self.fs.at[k], self.fr.at[k],
            self.p.sibling,
        )

    def begin(self, window):
        for i, unit in enumerate(self.units):
            if not unit.fresh:
                self.keep(i).start()
        for i in self.external[:window]:
            self.start(i, 0)

    def tick(self, t, window, done):
        due = []
        for i, unit in enumerate(self.units):
            for stage, beat in unit.beats.items():
                if beat == t:
                    due.append((-1 if stage == "in" else stage, i))
        for stage, i in sorted(due, key=lambda entry: (-entry[0], entry[1])):
            unit = self.units[i]
            if stage < 0:
                self.keep(i).wait()
                self.start(i, unit.stages[0])
                continue
            self.finish(i, stage)
            if stage == 0 and i in self.external:
                later = self.external.index(i) + window
                if later < len(self.external):
                    self.start(self.external[later], 0)
            if stage == 3:
                final, count = done[unit.array]
                if t == final:
                    done[unit.array] = final, count - 1
                    if count == 1:
                        self.last(unit.array).start()
            elif stage < unit.stages[-1]:
                self.start(i, stage + 1)

    def ticks(self):
        return 1 + max(beat for unit in self.units for beat in unit.beats.values())

    def deliver(self, k, out, spans):
        core = self.p.core
        self.last(k).wait()
        for value, owner in ((self.fin[k][core], core), (self.got[k][...], 1 - core)):
            at = 0
            for base, step, width in spans:
                where = pl.ds(pl.multiple_of(base + owner * step, 128), width)
                out[:, where] = value[:, at : at + width]
                at += width

    def wait_sends(self):
        for i, unit in enumerate(self.units):
            for stage in unit.stages:
                for copy in self.copies(i, stage):
                    copy.wait_send()


def on_the_way(units, arrays):
    beats = [[unit.beats[3] for unit in units if unit.array == k and unit.does(3)] for k in range(arrays)]
    return [(max(of), of.count(max(of))) if of else (-1, 0) for of in beats]


class Total:
    def __init__(self, place, source, out, bufs, sems):
        self.p = place
        self.src = source
        self.out = out
        self.part, self.pair, self.high, self.rows, self.quad = bufs
        self.ss, self.rs = sems

    @staticmethod
    def scratch(shape, n_rows):
        dma = pltpu.SemaphoreType.DMA
        bufs = [
            pltpu.VMEM((3,) + shape, F32), pltpu.VMEM(shape, F32), pltpu.VMEM(shape, F32),
            pltpu.VMEM((n_rows,) + shape, F32), pltpu.VMEM((4,) + shape, F32),
        ]
        return bufs, [dma((n_rows + 4,)), dma((n_rows + 4,))]

    def copies(self, stage):
        p = self.p
        if stage == 0:
            return [send(self.src, self.pair, self.ss.at[0], self.rs.at[0], p.sibling)]
        if stage == 1:
            return [send(self.part.at[0], self.high, self.ss.at[1], self.rs.at[1], p.across)]
        if stage == 2:
            return [
                send(
                    self.part.at[1], self.rows.at[p.r], self.ss.at[1 + d], self.rs.at[1 + d],
                    p.row_peer(d),
                )
                for d in range(1, p.n_rows)
            ]
        return [
            send(
                self.part.at[2], self.quad.at[p.g], self.ss.at[p.n_rows + d],
                self.rs.at[p.n_rows + d], p.gr_peer(d),
            )
            for d in range(1, 4)
        ]

    def start(self, stage):
        for copy in self.copies(stage):
            copy.start()

    def finish(self, stage):
        p = self.p
        for copy in self.copies(stage):
            copy.wait_recv()
        if stage == 0:
            self.part[0] = self.src[...] + self.pair[...]
        elif stage == 1:
            self.part[1] = self.part[0] + self.high[...]
        elif stage == 2:
            self.rows[p.r] = self.part[1]
            total = self.rows[0]
            for d in range(1, p.n_rows):
                total = total + self.rows[d]
            self.part[2] = total
        else:
            self.quad[p.g] = self.part[2]
            self.out[...] = (self.quad[0] + self.quad[1]) + (self.quad[2] + self.quad[3])

    def wait_sends(self):
        for stage in range(4):
            for copy in self.copies(stage):
                copy.wait_send()


def view(g, n_rows):
    rows, x = g.shape
    per = rows // (n_rows * 8)
    return g.reshape(n_rows, 4, 2, per // 48, 48, x)


def project_kernel(x_ref, gain_ref, bias_ref, w_ref, box_ref, page_ref, h1_ref, qkv_ref, cols_ref):
    @pl.when(pl.program_id(0) == 0)
    def _():
        chunk = 256
        count = x_ref.shape[0]

        @pl.loop(0, count // chunk)
        def _(c):
            sl = pl.ds(pl.multiple_of(c * chunk, chunk), chunk)
            x = x_ref[sl, :].astype(F32)
            average, inverse = norm_stats(x)
            h1_ref[sl, :] = ((x - average) * inverse * gain_ref[...].reshape(1, -1) + bias_ref[...].reshape(1, -1)).astype(BF)
        pages = jnp.concatenate([page_ref[s : s + 1, :] for s in range(page_ref.shape[0])], axis=1)
        lines = jnp.concatenate(
            [box_ref[...].astype(F32), pages.astype(F32), jnp.zeros((123, count), F32)], axis=0
        )
        cols_ref[...] = lines.T

    qkv_ref[...] = dot(h1_ref[...], w_ref[...]).astype(BF)


def project_forward(tokens, gain, bias, weight, boxes, page_ids):
    count, feats = tokens.shape
    width = weight.shape[1]
    block = feats
    vm = pl.BlockSpec(memory_space=pltpu.VMEM)
    return pl.pallas_call(
        project_kernel,
        grid=(width // block,),
        in_specs=[
            pl.BlockSpec((count, feats), lambda j: (0, 0)), vm, vm,
            pl.BlockSpec((feats, block), lambda j: (0, j)), vm, vm,
        ],
        out_specs=[vm, pl.BlockSpec((count, block), lambda j: (0, j)), vm],
        out_shape=[
            jax.ShapeDtypeStruct((count, feats), BF), jax.ShapeDtypeStruct((count, width), BF),
            jax.ShapeDtypeStruct((count, 128), F32),
        ],
        compiler_params=pltpu.CompilerParams(vmem_limit_bytes=63 << 20),
        name="project_forward",
    )(tokens, gain, bias, weight, boxes, page_ids)


def slot_members(seg_row, slots):
    ids = lax.broadcasted_iota(jnp.int32, (slots, seg_row.shape[1]), 0)
    return jnp.where(ids == seg_row, 1.0, 0.0)


def mlp_forward_kernel(
    ctx_ref, wo_ref, x_ref, gain_ref, bias_ref, wu_ref, bu_ref, wd_ref, seg_ref,
    r1_ref, h2_ref, act_ref, slope_ref, out_ref, emb_ref, acc_ref,
):
    step = pl.program_id(0)
    count = x_ref.shape[0]
    chunk = 512

    @pl.when(step == 0)
    def _():
        @pl.loop(0, count // chunk)
        def _(c):
            sl = pl.ds(pl.multiple_of(c * chunk, chunk), chunk)
            r1 = x_ref[sl, :].astype(F32) + dot(ctx_ref[sl, :], wo_ref[...])
            average, inverse = norm_stats(r1)
            r1_ref[sl, :] = r1
            acc_ref[sl, :] = r1
            h2_ref[sl, :] = ((r1 - average) * inverse * gain_ref[...].reshape(1, -1) + bias_ref[...].reshape(1, -1)).astype(BF)

    for c in range(count // chunk):
        sl = slice(c * chunk, (c + 1) * chunk)
        act, slope = gelu_pair(dot(h2_ref[sl, :], wu_ref[...]) + bu_ref[...])
        act = act.astype(BF)
        act_ref[sl, :] = act
        slope_ref[sl, :] = slope.astype(BF)
        acc_ref[sl, :] += dot(act, wd_ref[...])

    @pl.when(step == pl.num_programs(0) - 1)
    def _():
        out_ref[...] = acc_ref[...].astype(BF)
        seqs, length = seg_ref.shape
        slots = emb_ref.shape[0] // seqs
        for s in range(seqs):
            members = slot_members(seg_ref[s : s + 1, :], slots)
            total = dot(members.astype(BF), out_ref[s * length : (s + 1) * length, :])
            sizes = jnp.sum(members, axis=1, keepdims=True)
            emb_ref[s * slots : (s + 1) * slots, :] = (total / sizes).astype(BF)


def mlp_forward(ctx, w_out, tokens, gain, bias, w_up, b_up, w_down, seg_ids, slots):
    count, feats = tokens.shape
    hidden = w_up.shape[1]
    vm = pl.BlockSpec(memory_space=pltpu.VMEM)
    return pl.pallas_call(
        mlp_forward_kernel,
        grid=(hidden // feats,),
        in_specs=[
            vm, vm, vm, vm, vm, pl.BlockSpec((feats, feats), lambda f: (0, f)),
            pl.BlockSpec((1, feats), lambda f: (0, f)), pl.BlockSpec((feats, feats), lambda f: (f, 0)), vm,
        ],
        out_specs=[
            vm, vm, pl.BlockSpec((count, feats), lambda f: (0, f)),
            pl.BlockSpec((count, feats), lambda f: (0, f)), vm, vm,
        ],
        out_shape=[
            jax.ShapeDtypeStruct((count, feats), F32), jax.ShapeDtypeStruct((count, feats), BF),
            jax.ShapeDtypeStruct((count, hidden), BF), jax.ShapeDtypeStruct((count, hidden), BF),
            jax.ShapeDtypeStruct((count, feats), BF),
            jax.ShapeDtypeStruct((seg_ids.shape[0] * slots, feats), BF),
        ],
        scratch_shapes=[pltpu.VMEM((count, feats), F32)],
        compiler_params=pltpu.CompilerParams(vmem_limit_bytes=50 << 20),
        name="mlp_forward",
    )(
        ctx, w_out, tokens, gain, bias, w_up,
        b_up.reshape(1, hidden), w_down, seg_ids,
    )


class Panels:
    def __init__(self, place, tile, tile_t, rows, cols, sems):
        self.p = place
        self.tile, self.tile_t, self.rows, self.cols = tile, tile_t, rows, cols
        self.ss, self.rs = sems

    @staticmethod
    def scratch(size):
        dma = pltpu.SemaphoreType.DMA
        part = size // 4
        return [
            pltpu.VMEM((4, part, size), BF), pltpu.VMEM((4, part, size), BF),
            pltpu.VMEM((3, part, size), BF), pltpu.VMEM((3, part, size), BF), dma((6,)), dma((6,)),
        ]

    def copies(self):
        p = self.p
        out = []
        for d in range(1, 4):
            for n, (src, dst, peer, at) in enumerate((
                (self.tile, self.rows, p.gc_peer(d), p.c), (self.tile_t, self.cols, p.gr_peer(d), p.g),
            )):
                at_sem = 3 * n + d - 1
                out.append(
                    send(
                        src.at[lax.rem(at + d, 4)], dst.at[d - 1], self.ss.at[at_sem],
                        self.rs.at[at_sem], peer,
                    )
                )
        return out

    def fill(self, mask, cot, scale):
        g_raw = cot[...].astype(F32) * scale * mask[...].astype(F32)
        self.tile[...] = g_raw.astype(BF).reshape(self.tile.shape)
        self.tile_t[...] = g_raw.T.astype(BF).reshape(self.tile_t.shape)

    def start(self):
        for copy in self.copies():
            copy.start()

    def collect(self, row_out, col_out):
        p = self.p
        for copy in self.copies():
            copy.wait()
        row_out[p.c] = self.tile[p.c]
        col_out[p.g] = self.tile_t[p.g]
        for d in range(1, 4):
            row_out[lax.rem(p.c + 4 - d, 4)] = self.rows[d - 1]
            col_out[lax.rem(p.g + 4 - d, 4)] = self.cols[d - 1]


class Spread:
    def __init__(self, place, blocks, sems):
        self.p = place
        self.e = blocks
        self.ss, self.rs = sems
        self.near = lax.rem(place.c + 2, 4)

    @staticmethod
    def scratch(shape):
        dma = pltpu.SemaphoreType.DMA
        return [pltpu.VMEM((4, 4) + shape, BF), dma((4, 4, 3)), dma((4, 4))]

    def hop(self, row, col, kind, peer):
        block = self.e.at[row, col]
        return send(block, block, self.ss.at[row, col, kind], self.rs.at[row, col], peer)

    def own(self, step, waiting):
        p = self.p
        for sign in (1, -1) if step else (0,):
            row = p.g + sign * step
            inside = (row >= 0) & (row <= 3)

            @pl.when(inside)
            def _(row=row, sign=sign):
                if step and not waiting:
                    self.hop(row, p.c, 0, p.sibling).wait_recv()
                go = "wait_send" if waiting else "start"
                getattr(self.hop(row, p.c, 0, p.sibling), go)()
                getattr(self.hop(row, p.c, 1, p.across), go)()
                for way in (1, -1) if step == 0 else (-sign,):
                    to = p.g + way

                    @pl.when((to >= 0) & (to <= 3))
                    def _(to=to, way=way):
                        if step == 0 and way == -1:
                            copy = send(
                                self.e.at[row, p.c], self.e.at[row, p.c], self.down.at[0],
                                self.rs.at[row, p.c], {"gr": to},
                            )
                        else:
                            copy = self.hop(row, p.c, 2, {"gr": to})
                        getattr(copy, go)()

    def relay(self, step, waiting):
        p = self.p
        for sign in (1, -1) if step else (0,):
            row = p.g + sign * step

            @pl.when((row >= 0) & (row <= 3))
            def _(row=row):
                copy = self.hop(row, self.near, 0, p.sibling)
                if waiting:
                    copy.wait_send()
                else:
                    copy.wait_recv()
                    copy.start()

    def arrive(self, rows, cols):
        for row in rows:
            for col in cols:
                self.hop(row, col, 0, self.p.sibling).wait_recv()


def pair_kernel(
    emb_ref, left_ref, right_ref, rowp_ref, colp_ref, mask_ref, cot_ref, seg_ref,
    logits_ref, gleft_ref, gright_ref, gy_ref, gmlp_ref, e_ref, ss, rs, down, *, scale,
):
    place = Place(1)
    meet([place.sibling, place.across] + [place.gr_peer(d) for d in (1, 2, 3)])
    spread = Spread(place, e_ref, (ss, rs))
    spread.down = down
    p = place
    e_ref[p.g, p.c] = emb_ref[...]
    part, width = emb_ref.shape
    spread.own(0, False)
    spread.own(1, False)
    spread.relay(0, False)
    sib = p.u * 2 + 1 - p.core
    far = (1 - p.u) * 2 + 1 - p.core
    spread.arrive([p.g], [sib, far])
    left_rows = dot(e_ref[p.g].reshape(4 * part, width), left_ref[...]).astype(BF)
    spread.own(2, False)
    spread.relay(1, False)
    spread.own(3, False)
    right_cols = dot(e_ref[:, p.c].reshape(4 * part, width), right_ref[...]).astype(BF)
    spread.relay(2, False)
    logits_ref[...] = mask_ref[...].astype(F32) * dot(left_rows, right_cols, NT) * scale
    spread.relay(3, False)
    for d in range(1, 4):
        spread.arrive([lax.rem(p.g + d, 4)], [sib, far])
    row_sum = jnp.zeros((part, width), F32)
    col_sum = jnp.zeros((part, width), F32)
    for n in range(4):
        row_sum = row_sum + dot(rowp_ref[n], e_ref[:, n].reshape(4 * part, width))
        col_sum = col_sum + dot(colp_ref[n], e_ref[n].reshape(4 * part, width))

    def through(total, weight):
        high, low = hi_lo(total)
        return (dot(high, weight) + dot(low, weight)).astype(BF)

    g_left = through(row_sum, right_ref[...])
    g_right = through(col_sum, left_ref[...])
    emb_t = emb_ref[...].astype(F32).T.astype(BF)
    gleft_ref[...] = dot(emb_t, g_left).astype(BF)
    gright_ref[...] = dot(emb_t, g_right).astype(BF)
    g_emb = dot(g_left, left_ref[...], NT) + dot(g_right, right_ref[...], NT)
    seqs, length = seg_ref.shape
    slots = part // seqs
    for n in range(seqs):
        members = slot_members(seg_ref[n : n + 1, :], slots)
        g_seg = g_emb[n * slots : (n + 1) * slots] / jnp.sum(members, axis=1, keepdims=True)
        high, low = hi_lo(g_seg)
        twice = jnp.concatenate([members, members], axis=0).T.astype(BF)
        sl = slice(n * length, (n + 1) * length)
        g_y = cot_ref[sl, :].astype(F32) + dot(twice, jnp.concatenate([high, low], axis=0))
        gy_ref[sl, :] = g_y
        gmlp_ref[sl, :] = g_y.astype(BF)
    for step in range(4):
        spread.own(step, True)
        spread.relay(step, True)


def pair_head(emb, rel_left, rel_right, row_panel, col_panel, mask, cot_out, seg_ids, scale):
    part, width = emb.shape
    size = mask.shape[0]
    vm = pl.BlockSpec(memory_space=pltpu.VMEM)
    dma = pltpu.SemaphoreType.DMA
    return pl.pallas_call(
        functools.partial(pair_kernel, scale=scale),
        in_specs=[vm] * 8,
        out_specs=[vm] * 5,
        out_shape=[
            jax.ShapeDtypeStruct((size, size), F32), jax.ShapeDtypeStruct(rel_left.shape, BF),
            jax.ShapeDtypeStruct(rel_right.shape, BF), jax.ShapeDtypeStruct(cot_out.shape, F32),
            jax.ShapeDtypeStruct(cot_out.shape, BF),
        ],
        scratch_shapes=Spread.scratch((part, width)) + [dma((1,))],
        compiler_params=pltpu.CompilerParams(
            collective_id=5, has_side_effects=True, vmem_limit_bytes=50 << 20
        ),
        name="pair_head",
    )(emb, rel_left, rel_right, row_panel, col_panel, mask, cot_out, seg_ids)


def norm_back_chunk(g_out, rows, gain):
    average, inverse = norm_stats(rows)
    z = (rows - average) * inverse
    g_z = g_out * gain
    mean_g = jnp.mean(g_z, axis=-1, keepdims=True)
    mean_gz = jnp.mean(g_z * z, axis=-1, keepdims=True)
    return inverse * (g_z - mean_g - z * mean_gz), jnp.sum(g_out * z, axis=0, keepdims=True)


def turn(source, target):
    @pl.loop(0, source.shape[0] // 128, unroll=2)
    def _(c):
        sl = pl.ds(pl.multiple_of(c * 128, 128), 128)
        target[:, sl] = source[sl, :].astype(F32).T.astype(BF)


def put_lines(ref, at, row):
    for j in range(row.shape[1] // 128):
        ref[at + j : at + j + 1, :] = row[:, j * 128 : (j + 1) * 128]


def mlp_back_kernel(*refs, n_ext, units, n_rows, comm, window):
    (slope_ref, wd_ref, wu_ref, gmlp_ref, h2_ref, r1_ref, gy_ref, ctx_ref, wo_ref, gain_ref) = refs[:10]
    at = 10
    arrays = refs[at : at + n_ext]
    at += n_ext
    gup_ref, gr1_ref, gout_ref, gctx_ref, small_ref = refs[at : at + 5]
    at += 5
    carried = refs[at : at + 2]
    at += 2 if comm else 0
    h2t_ref, acc_ref, r1_buf, gy_buf, ctx_buf, ctxt_ref, wo_buf, gatt_ref, in_sem = refs[at : at + 9]
    at += 9
    n_step = pl.num_programs(0)
    step = pl.program_id(0)
    count, feats = acc_ref.shape
    lines = feats // 128
    steps = (small_ref.shape[0] - 16) // lines - 4
    if comm:
        place = Place(n_rows)
        shares = Shares(
            place, units, PIECE, arrays, None, carried, (), (), refs[at : at + 7],
            refs[at + 7 : at + 10], (None, None),
        )
        done = on_the_way(units, 3)

    def inputs():
        pairs = (
            (ctx_ref, ctx_buf), (r1_ref, r1_buf), (gy_ref, gy_buf), (wo_ref, wo_buf),
        )
        return [pltpu.make_async_copy(a, b, in_sem.at[i]) for i, (a, b) in enumerate(pairs)]

    @pl.when(step == 0)
    def _():
        for copy in inputs():
            copy.start()
        if comm:
            meet(place.peers())
            shares.begin(window)
        acc_ref[...] = jnp.zeros_like(acc_ref)
        small_ref[...] = jnp.zeros_like(small_ref)

    def beat(part):
        if comm:
            by_step(step, 0, steps, lambda n: shares.tick(2 * n + part, window, done))

    g_act = dot(gmlp_ref[...], wd_ref[...], NT)
    g_wide = g_act * slope_ref[...].astype(F32)
    g_u = g_wide.astype(BF)
    bias = jnp.sum(g_u.astype(F32), axis=0, keepdims=True)
    acc_ref[...] += dot(g_u, wu_ref[...], NT)
    beat(0)

    @pl.when(step == 0)
    def _():
        turn(h2_ref, h2t_ref)

    gup_ref[...] = dot(h2t_ref[...], g_u).astype(BF)
    for at_step in range(steps):
        @pl.when(step == at_step)
        def _(at_step=at_step):
            put_lines(small_ref, (4 + at_step) * lines, bias)
    beat(1)

    @pl.when(step == n_step - 1)
    def _():
        for copy in inputs():
            copy.wait()
        chunk = 256

        def back(c, sums):
            sl = pl.ds(pl.multiple_of(c * chunk, chunk), chunk)
            g_out = acc_ref[sl, :]
            g_in, part = norm_back_chunk(g_out, r1_buf[sl, :], gain_ref[...].reshape(1, -1))
            g_r1 = gy_buf[sl, :] + g_in
            gr1_ref[sl, :] = g_r1
            gatt_ref[sl, :] = g_r1.astype(BF)
            return sums[0] + part, sums[1] + jnp.sum(g_out, axis=0, keepdims=True)

        nothing = jnp.zeros((1, feats), F32)
        gain_sum, bias_sum = lax.fori_loop(0, count // chunk, back, (nothing, nothing), unroll=2)
        put_lines(small_ref, 2 * lines, gain_sum)
        put_lines(small_ref, 3 * lines, bias_sum)
        if comm:
            shares.tick(2 * steps, window, done)
        turn(ctx_buf, ctxt_ref)
        gctx_ref[...] = dot(gatt_ref[...], wo_buf[...], NT).astype(BF)
        if comm:
            shares.tick(2 * steps + 1, window, done)
        gout_ref[...] = dot(ctxt_ref[...], gatt_ref[...]).astype(BF)
        if comm:
            for t in range(2 * steps + 2, shares.ticks()):
                shares.tick(t, window, done)
            shares.wait_sends()


def early_units():
    order = ((0, 0, False), (1, 0, True), (2, 0, True), (2, 1, False), (2, 2, True), (2, 3, False))
    left = [0, 0]
    units = []
    for n, (k, s, first) in enumerate(order):
        beats = {0: 1 + n // 2 * 2, 1: 4 + n // 2 * 2}
        kind = 0 if first else 1
        units.append(Unit(k, s, 0, first, beats, leave=(kind, left[kind])))
        left[kind] += 1
    return tuple(units)


def mlp_backward(
    slope, w_down, w_up, g_mlp, h2, r1, g_y, ctx, w_out, gain, small_rows, left, right, down, n_rows, comm
):
    count, feats = g_mlp.shape
    hidden = slope.shape[1]
    steps = hidden // feats
    vm = pl.BlockSpec(memory_space=pltpu.VMEM)
    any_ref = pl.BlockSpec(memory_space=pl.ANY)
    views = [view(g, n_rows) for g in (left, right, down)] if comm else []
    units = early_units()
    extra = []
    if comm:
        extra = [
            jax.ShapeDtypeStruct((3, 4, 2, 48, PIECE), BF),
            jax.ShapeDtypeStruct((3, n_rows, 4, 48, PIECE), BF),
        ]
    scratch = [
        pltpu.VMEM((feats, count), BF), pltpu.VMEM((count, feats), F32),
        pltpu.VMEM((count, feats), F32), pltpu.VMEM((count, feats), F32), pltpu.VMEM((count, feats), BF),
        pltpu.VMEM((feats, count), BF), pltpu.VMEM((feats, feats), BF), pltpu.VMEM((count, feats), BF),
        pltpu.SemaphoreType.DMA((4,)),
    ]
    params = dict(vmem_limit_bytes=63 << 20, dimension_semantics=("arbitrary",))
    if comm:
        scratch += Shares.scratch(units, PIECE, n_rows)
        params.update(collective_id=3, has_side_effects=True)
    return pl.pallas_call(
        functools.partial(
            mlp_back_kernel, n_ext=len(views), units=units, n_rows=n_rows, comm=comm, window=2,
        ),
        grid=(steps,),
        in_specs=[
            pl.BlockSpec((count, feats), lambda f: (0, f)),
            pl.BlockSpec((feats, feats), lambda f: (f, 0)),
            pl.BlockSpec((feats, feats), lambda f: (0, f)),
            vm, vm, any_ref, any_ref, any_ref, any_ref, vm,
        ] + [any_ref] * len(views),
        out_specs=[pl.BlockSpec((feats, feats), lambda f: (0, f)), vm, vm, vm, vm] + [vm] * len(extra),
        out_shape=[
            jax.ShapeDtypeStruct((feats, hidden), BF), jax.ShapeDtypeStruct((count, feats), F32),
            jax.ShapeDtypeStruct((feats, feats), BF), jax.ShapeDtypeStruct((count, feats), BF),
            jax.ShapeDtypeStruct((small_rows, 128), F32),
        ] + extra,
        scratch_shapes=scratch,
        compiler_params=pltpu.CompilerParams(**params),
        name="mlp_backward",
    )(slope, w_down, w_up, g_mlp, h2, r1, g_y, ctx, w_out, gain, *views)


def deliver_kernel(gx_ref, small_ref, *refs, parts, heads):
    n_in = sum(parts)
    ins, outs = refs[:n_in], refs[n_in:]
    outs[0][...] = gx_ref[...]

    @pl.when(pl.program_id(0) == 0)
    def _():
        at = 0
        for k, n in enumerate(parts):
            out = outs[1 + k]
            row = 0
            for ref in ins[at : at + n]:
                rows, x = ref.shape
                per = x // 128
                for j in range(per):
                    out[pl.ds(row + j, rows, stride=per), :] = ref[:, j * 128 : (j + 1) * 128]
                row += rows * per
            at += n
        line = 0
        for out in outs[1 + len(parts) :]:
            if len(out.shape) == 1:
                for j in range(out.shape[0] // 128):
                    out[j * 128 : (j + 1) * 128] = small_ref[line]
                    line += 1
            else:
                out[...] = small_ref[line : line + out.shape[0], :]


def deliver(g_tokens, small, shares, features, hidden, heads):
    count = g_tokens.shape[0]
    flat = [p for group in shares for p in group]
    vm = pl.BlockSpec(memory_space=pltpu.VMEM)
    block = count // 2
    sizes = [sum(p.size for p in group) for group in shares]
    results = pl.pallas_call(
        functools.partial(deliver_kernel, parts=tuple(len(group) for group in shares), heads=heads),
        grid=(2,),
        in_specs=[pl.BlockSpec((block, features), lambda i: (i, 0)), vm] + [vm] * len(flat),
        out_specs=[pl.BlockSpec((block, features), lambda i: (i, 0))] + [vm] * (len(shares) + 6),
        out_shape=[jax.ShapeDtypeStruct(g_tokens.shape, F32)]
        + [jax.ShapeDtypeStruct((size // 128, 128), F32) for size in sizes]
        + [jax.ShapeDtypeStruct((features,), F32)] * 4
        + [jax.ShapeDtypeStruct((hidden,), F32), jax.ShapeDtypeStruct((heads, 128), F32)],
        name="deliver",
    )(g_tokens, small, *flat)
    return (
        results[0], [r.reshape(-1) for r in results[1 : 1 + len(shares)]], results[1 + len(shares) :]
    )


def back_kernel(*refs, n_ext, units, tail, spans, n_rows, comm, window):
    (q_ref, k_ref, v_ref, e_ref, linv_ref, ctx_ref, gctx_ref, boxr_ref, boxc_ref, w_ref, h1_ref,
     x_ref, gr1_ref, gain_ref, small_ref) = refs[:15]
    at = 15
    arrays = refs[at : at + n_ext]
    at += n_ext
    carried = refs[at : at + 2] if comm else ()
    at += len(carried)
    n_out = len(spans)
    gx_ref = refs[at]
    small_out = refs[at + 1]
    at += 2
    if comm:
        outs = refs[at : at + n_out]
        at += n_out
    else:
        grad_ref = refs[at]
        at += 1
    (oha_ref, ohbt_ref, cx_ref, cy_ref, g_ref, gcx_ref, gcy_ref, lt_ref, gt_ref, gall_ref, h1t_ref,
     hist_ref, h1_buf, x_buf, gr1_buf, w_buf, pack_ref, in_sem) = refs[at : at + 18]
    at += 18
    length = q_ref.shape[0]
    half, quarter = 64, 32
    pairs, seqs = pl.num_programs(0), pl.num_programs(1)
    hp = pl.program_id(0)
    s_id = pl.program_id(1)
    n_seq = cx_ref.shape[0]
    n_pair = hist_ref.shape[0] // 2
    lane = lax.broadcasted_iota(jnp.int32, (1, 128), 1)
    low = lane < 64
    if comm:
        place = Place(n_rows)
        staging = refs[at]
        fins = refs[at + 1 : at + n_out + 1]
        at += n_out + 1
        got = refs[at : at + n_out]
        at += n_out
        known = (None,) * 3 + tuple(arrays) + (None,)
        ends = refs[at : at + 2]
        at += 2
        shares = Shares(
            place, units, PIECE, known, staging, carried, fins, got, refs[at : at + 7],
            refs[at + 7 : at + 10], ends,
        )
        at += 10
        thirds = Shares(
            place, tail, PIECE // 3, known, staging, carried, fins, got, refs[at : at + 7],
            refs[at + 7 : at + 10], ends,
        )
        at += 10
        done = on_the_way(units + tail, n_out)
        total = Total(place, pack_ref, small_out, refs[at : at + 5], refs[at + 5 : at + 7])

    def inputs():
        return (
            pltpu.make_async_copy(h1_ref, h1_buf, in_sem.at[0]),
            pltpu.make_async_copy(x_ref, x_buf, in_sem.at[1]),
            pltpu.make_async_copy(gr1_ref, gr1_buf, in_sem.at[2]),
            pltpu.make_async_copy(w_ref, w_buf, in_sem.at[3]),
        )

    @pl.when((hp == 0) & (s_id == 0))
    def _():
        for copy in inputs():
            copy.start()
        hist_ref[...] = jnp.zeros_like(hist_ref)
        if comm:
            meet(place.peers())
            shares.begin(window)

    @pl.when(hp == 0)
    def _():
        bc = boxc_ref[...]
        ax, _ = key_side(bc[:, 0:1], bc[:, 2:3], half)
        ay, _ = key_side(bc[:, 1:2], bc[:, 3:4], half)
        _, fbx = query_side(bc[:, 0:1], bc[:, 2:3], half)
        _, fby = query_side(bc[:, 1:2], bc[:, 3:4], half)
        spot = (lane % quarter).astype(F32)
        is_x = (lane % half) < quarter
        oha = jnp.where(jnp.where(is_x, ax, ay) == spot, jnp.where(low, 1.0, 0.0), 0.0)
        oha_ref[s_id] = oha.astype(BF)
        br = boxr_ref[...]
        _, gax = key_side(br[0:1], br[2:3], half)
        _, gay = key_side(br[1:2], br[3:4], half)
        rbx, _ = query_side(br[0:1], br[2:3], half)
        rby, _ = query_side(br[1:2], br[3:4], half)
        row = lax.broadcasted_iota(jnp.int32, (half, length), 0)
        rspot = (row % quarter).astype(F32)
        ohbt_ref[s_id] = jnp.where(jnp.where(row < quarter, rbx, rby) == rspot, 1.0, 0.0).astype(BF)
        cx_ref[s_id] = jnp.where(gax + fbx >= SPAN, 1.0, 0.0).astype(BF)
        cy_ref[s_id] = jnp.where(gay + fby >= SPAN, 1.0, 0.0).astype(BF)

    @pl.when((hp == 0) & (s_id == n_seq - 1))
    def _():
        inputs()[0].wait()
        turn(h1_buf, h1t_ref)

    k = k_ref[...]
    v = v_ref[...]
    lt_ref[...] = q_ref[...].astype(F32).T.astype(BF)
    gc = gctx_ref[...].astype(F32) * linv_ref[...]
    gcb = gc.astype(BF)
    gt_ref[...] = gcb.astype(F32).T.astype(BF)
    prod = gc * ctx_ref[...].astype(F32)
    ohbt = ohbt_ref[s_id]
    kts = []
    vts = []
    rows = 256
    n_step = n_pair * n_seq
    step = hp * n_seq + s_id
    for a in range(2):
        if comm and a == 1:
            by_step(step, 0, n_step, lambda n: shares.tick(2 * n, window, done))
        mine = low if a == 0 else jnp.logical_not(low)
        other = 64 - 64 * a
        d = jnp.sum(jnp.where(mine, prod, 0.0), axis=1, keepdims=True)
        dhi = d.astype(BF).astype(F32)
        extra = jnp.where(lane == other, dhi, jnp.where(lane == other + 1, d - dhi, 0.0))
        lhs = jnp.where(mine, gcb.astype(F32), extra).astype(BF)
        minus = jnp.where((lane == other) | (lane == other + 1), -1.0, 0.0).astype(BF)
        rhs = jnp.where(mine, v, minus)
        for c in range(length // rows):
            sl = slice(c * rows, (c + 1) * rows)
            gp = dot(lhs[sl], rhs, NT)
            g = (gp * e_ref[a, sl, :].astype(F32)).astype(BF)
            g_ref[a, sl, :] = g
            gcx_ref[a, sl, :] = g * cx_ref[s_id, sl, :]
            gcy_ref[a, sl, :] = g * cy_ref[s_id, sl, :]
        left = jnp.concatenate([lt_ref[64 * a : 64 * a + 64, :], ohbt], axis=0)
        r0 = dot(left, g_ref[a])
        rx = dot(ohbt[:quarter], gcx_ref[a])
        ry = dot(ohbt[quarter:], gcy_ref[a])
        vts.append(dot(gt_ref[64 * a : 64 * a + 64, :], e_ref[a]))
        kts.append(r0[:64])
        w = jnp.concatenate([r0[64:], rx, ry], axis=0)
        whi, wlo = hi_lo(w)
        red = dot(jnp.concatenate([whi, wlo], axis=0), oha_ref[s_id])
        hist_ref[2 * hp + a] += red[:128] + red[128:]
    zero = jnp.zeros_like(k)
    gq = dot(g_ref[0], jnp.where(low, k, zero)) + dot(g_ref[1], jnp.where(low, zero, k))
    own_rows = pl.ds(pl.multiple_of(s_id * length, length), length)
    feats = h1_buf.shape[1]
    parts = [pl.ds(pl.multiple_of(p * feats + hp * 128, 128), 128) for p in range(3)]
    gall_ref[own_rows, parts[0]] = (gq * 0.125).astype(BF)
    gall_ref[own_rows, parts[1]] = (jnp.concatenate(kts, axis=0) * 0.125).T.astype(BF)
    gall_ref[own_rows, parts[2]] = jnp.concatenate(vts, axis=0).T.astype(BF)

    @pl.when(s_id == n_seq - 1)
    def _():
        g_pair = jnp.concatenate([gall_ref[:, part] for part in parts], axis=1)
        piece = dot(h1t_ref[...], g_pair).astype(BF)
        if comm:
            staging[lax.div(hp, 2), lax.rem(hp, 2)] = piece.reshape(staging.shape[2:])
        else:
            grad_ref[0] = piece[:, :128]
            grad_ref[1] = piece[:, 128:256]
            grad_ref[2] = piece[:, 256:]

    if comm:
        def beat_of(at_step):
            for part in (shares, thirds):
                for i, unit in enumerate(part.units):
                    source = unit.source or ("", 0)
                    if source[0] == "own" and (2 * source[1] + 2) * n_seq - 1 == at_step:
                        part.start(i, 0)
            if at_step < n_step - 1:
                shares.tick(2 * at_step + 1, window, done)

        by_step(step, 0, n_step, beat_of)

    @pl.when((hp == n_pair - 1) & (s_id == n_seq - 1))
    def _():
        for copy in inputs()[1:]:
            copy.wait()
        gain = gain_ref[...].reshape(1, -1)
        count = x_buf.shape[0]
        chunk = 256
        beat = 2 * n_step - 1
        gain_sum = jnp.zeros((1, feats), F32)
        bias_sum = jnp.zeros((1, feats), F32)
        pack_ref[...] = small_ref[...]
        base = pack_ref.shape[0] - 16
        for h in range(2 * n_pair):
            w = hist_ref[h]
            line = jnp.zeros((1, 128), F32)
            for axis in range(2):
                plain = w[axis * quarter : (axis + 1) * quarter]
                carry = w[half + axis * quarter : half + (axis + 1) * quarter]
                keep = (lane >= axis * quarter) & (lane < (axis + 1) * quarter)
                stay = jnp.where(keep, plain - carry, 0.0)
                move = jnp.where(keep, carry, 0.0)
                shift = axis * (half - quarter)
                stay = pltpu.roll(stay, shift, 1, stride=1, stride_axis=0)
                move = pltpu.roll(move, shift + 1, 1, stride=1, stride_axis=0)
                line = line + jnp.sum(stay + move, axis=0, keepdims=True)
            pack_ref[base + h : base + h + 1, :] = line
        for c in range(count // chunk):
            sl = slice(c * chunk, (c + 1) * chunk)
            g_out = dot(gall_ref[sl, :], w_buf[...], NT)
            g_in, part = norm_back_chunk(g_out, x_buf[sl, :].astype(F32), gain)
            gx_ref[sl, :] = gr1_buf[sl, :] + g_in
            gain_sum = gain_sum + part
            bias_sum = bias_sum + jnp.sum(g_out, axis=0, keepdims=True)
            if comm:
                for t in range(beat, beat + 2):
                    shares.tick(t, window, done)
                    thirds.tick(t, window, done)
                beat += 2
        lines = feats // 128
        put_lines(pack_ref, 0, gain_sum)
        put_lines(pack_ref, lines, bias_sum)
        if comm:
            total.start(0)
            stage = 0
            for t in range(beat, max(shares.ticks(), thirds.ticks())):
                shares.tick(t, window, done)
                thirds.tick(t, window, done)
                if t in SUM_BEATS:
                    total.finish(stage)
                    if stage < 3:
                        total.start(stage + 1)
                    stage += 1
            for stage in range(stage, 4):
                total.finish(stage)
                if stage < 3:
                    total.start(stage + 1)
            for n, out in enumerate(outs):
                shares.deliver(n, out, spans[n])
            thirds.wait_sends()
            total.wait_sends()
            shares.wait_sends()
        else:
            small_out[...] = pack_ref[...]


SUM_BEATS = (35, 39, 43, 47)


def late_units():
    rest = ((0, 4, 7), (3, 8, 17), (0, 4, 9), (3, 8, 15), (1, 6, 13), (1, 6, 11))
    units = [
        Unit(
            unit.array, unit.part, 0, unit.rows_first, {"in": enter, 2: second, 3: third},
            source=("mid",) + unit.leave,
        )
        for unit, (enter, second, third) in zip(early_units(), rest)
    ]
    whole = (
        (4, 0, True, (5, 12, 18, 21)), (4, 1, True, (9, 16, 20, 23)), (3, 0, False, (5, 12, 22, 23)),
        (4, 2, False, (9, 16, 23, 29)), (4, 3, True, (21, 27, 34, 44)),
    )
    units += [Unit(k, 0, j, first, dict(enumerate(beats))) for k, j, first, beats in whole]
    own = ((True, (10, 20, 25, 32)), (False, (19, 23, 31, 38)))
    units += [
        Unit(5, 0, t, first, dict(enumerate(beats)), source=("own", t, 0))
        for t, (first, beats) in enumerate(own)
    ]
    thirds = ((True, (27, 33, 40, 45)), (False, (27, 37, 42, 48)), (True, (27, 36, 41, 46)))
    tail = tuple(
        Unit(5, 0, 6 + n, first, dict(enumerate(beats)), source=("own", 2, n * PIECE // 3))
        for n, (first, beats) in enumerate(thirds)
    )
    return tuple(units), tail


def attend_and_project_backward(
    qkv, e, linv, ctx, gctx, boxes_r, boxes_c, weight, h1, tokens, g_r1, gain, small, arrays,
    carried, n_rows, comm
):
    count, width = qkv.shape
    feats = width // 3
    heads, seqs, length, _ = e.shape
    pairs = heads // 2
    rows_of = lambda off: pl.BlockSpec((length, 128), lambda h, s: (s, off + h))
    any_ref = pl.BlockSpec(memory_space=pl.ANY)
    vm = pl.BlockSpec(memory_space=pltpu.VMEM)
    views = [view(g, n_rows) for g in arrays] if comm else []
    n_ext = len(views)
    units, tail = late_units() if comm else ((), ())
    out_shape = [jax.ShapeDtypeStruct((count, feats), F32), jax.ShapeDtypeStruct(small.shape, F32)]
    out_specs = [vm, vm]
    spans = []
    scratch = [
        pltpu.VMEM((seqs, length, 128), BF), pltpu.VMEM((seqs, 64, length), BF),
        pltpu.VMEM((seqs, length, length), BF), pltpu.VMEM((seqs, length, length), BF),
        pltpu.VMEM((2, length, length), BF), pltpu.VMEM((2, length, length), BF),
        pltpu.VMEM((2, length, length), BF), pltpu.VMEM((128, length), BF),
        pltpu.VMEM((128, length), BF), pltpu.VMEM((count, width), BF), pltpu.VMEM((feats, count), BF),
        pltpu.VMEM((heads, 128, 128), F32), pltpu.VMEM((count, feats), BF),
        pltpu.VMEM((count, feats), BF), pltpu.VMEM((count, feats), F32), pltpu.VMEM((feats, width), BF),
        pltpu.VMEM(small.shape, F32), pltpu.SemaphoreType.DMA((4,)),
    ]
    params = dict(vmem_limit_bytes=63 << 20, dimension_semantics=("arbitrary", "arbitrary"))
    if comm:
        hidden = views[-1].shape[5]
        sizes = [(24, feats), (24, feats), (24 * hidden // feats, feats), (24, feats), (24, hidden), (24, width)]
        for rows, x in sizes[:-1]:
            spans.append([(j * 2 * PIECE, PIECE, PIECE) for j in range(x // (2 * PIECE))])
        spans.append(
            [(p * feats + t * 256, 128, 128) for t in range(pairs // 2) for p in range(3)]
        )
        out_shape += [jax.ShapeDtypeStruct(size, F32) for size in sizes]
        out_specs += [vm] * len(sizes)
        tbufs, tsems = Total.scratch(small.shape, n_rows)
        scratch += [pltpu.VMEM((pairs // 2, 2, n_rows, 4, 2, 48, PIECE), BF)]
        scratch += Shares.result_scratch(sizes) + Shares.scratch(units, PIECE, n_rows)
        scratch += Shares.scratch(tail, PIECE // 3, n_rows) + tbufs + tsems
        params.update(collective_id=2, has_side_effects=True)
    else:
        out_shape.append(jax.ShapeDtypeStruct((3, feats, feats), BF))
        out_specs.append(pl.BlockSpec((3, feats, 128), lambda h, s: (0, 0, h)))
    results = pl.pallas_call(
        functools.partial(
            back_kernel, n_ext=n_ext, units=units, tail=tail, spans=spans, n_rows=n_rows, comm=comm, window=3,
        ),
        grid=(pairs, seqs),
        in_specs=[
            rows_of(0), rows_of(pairs), rows_of(2 * pairs),
            pl.BlockSpec((2, None, length, length), lambda h, s: (h, s, 0, 0)),
            rows_of(0), rows_of(0), rows_of(0),
            pl.BlockSpec((4, length), lambda h, s: (0, s)),
            pl.BlockSpec((length, 128), lambda h, s: (s, 0)),
            any_ref, any_ref, any_ref, any_ref, vm, vm,
        ] + [any_ref] * (n_ext + len(carried)),
        out_specs=out_specs,
        out_shape=out_shape,
        scratch_shapes=scratch,
        compiler_params=pltpu.CompilerParams(**params),
        name="attend_backward",
    )(
        qkv, qkv, qkv, e, linv, ctx, gctx, boxes_r, boxes_c, weight, h1, tokens, g_r1,
        gain, small, *views, *carried,
    )
    return results


EPSILON = 1e-05


def norm_stats(rows):
    average = jnp.mean(rows, axis=-1, keepdims=True)
    centred = rows - average
    variance = jnp.mean(centred * centred, axis=-1, keepdims=True)
    return average, lax.rsqrt(variance + EPSILON)


def gelu_pair(u):
    bell = jnp.exp2(u * u * (-0.5 * LOG2E))
    below = 0.5 + 0.5 * lax.erf(u * math.sqrt(0.5))
    return u * below, below + u * bell * (1.0 / math.sqrt(2.0 * math.pi))


def body(
    tokens, boxes, page_ids, seg_ids, pair_mask, ln1_gain, ln1_bias, query_key_value_weight,
    attention_output_weight, ln2_gain, ln2_bias, up_projection_weight, up_projection_bias,
    down_projection_weight, box_table, rel_left, rel_right, cot_out, cot_logits,
):
    features = tokens.shape[1]
    h1, qkv, boxes_c = project_forward(
        tokens, ln1_gain, ln1_bias, query_key_value_weight, boxes, page_ids
    )
    pair_scale = 1.0 / math.sqrt(rel_left.shape[1])
    ctx, e, linv, row_panel, col_panel = attend_forward(
        qkv, boxes, boxes_c, page_ids.shape[0], box_table, pair_mask[0], cot_logits[0], pair_scale
    )
    r1, h2, act, slope, layer_out, embedded = mlp_forward(
        ctx, attention_output_weight, tokens, ln2_gain, ln2_bias, up_projection_weight,
        up_projection_bias, down_projection_weight, seg_ids, SLOTS,
    )
    pair_logits, grad_rel_left, grad_rel_right, g_y, g_mlp = pair_head(
        embedded, rel_left, rel_right, row_panel, col_panel, pair_mask[0], cot_out, seg_ids, pair_scale
    )
    grad_down = dot(act, g_mlp, (((0,), (0,)), ((), ()))).astype(BF)
    n_rows = lax.axis_size("rows")
    comm = n_rows * 8 * 48 <= features
    heads = box_table.shape[0]
    hidden = slope.shape[1]
    small_rows = (4 * features + hidden) // 128 + 16
    grad_up, g_r1, grad_out, g_ctx, small, *early = mlp_backward(
        slope, down_projection_weight, up_projection_weight, g_mlp, h2, r1, g_y, ctx,
        attention_output_weight, ln2_gain, small_rows, grad_rel_left, grad_rel_right, grad_down,
        n_rows, comm,
    )
    g_tokens, small, *late = attend_and_project_backward(
        qkv, e, linv, ctx, g_ctx, boxes, boxes_c, query_key_value_weight, h1, tokens, g_r1, ln1_gain,
        small, (grad_out, grad_up), early, n_rows, comm,
    )
    if comm:
        left, right, down, out, up, qkv_part = late
        shares = [[left], [right], [out], [down], [up], [qkv_part]]
    else:
        grad_qkv = jnp.concatenate([late[0][0], late[0][1], late[0][2]], axis=1)
        flats = [
            lax.psum_scatter(g, AXES, scatter_dimension=0, tiled=True).astype(F32).reshape(-1)
            for g in (grad_rel_left, grad_rel_right, grad_out, grad_down, grad_up, grad_qkv)
        ]
        shares = [[flat.reshape(-1, 128)] for flat in flats]
        small = lax.psum(small, AXES)
    grad_tokens, flats, vectors = deliver(g_tokens, small, shares, features, hidden, heads)
    left_share, right_share, out_share, down_share, up_share, qkv_share = flats
    return (
        layer_out, pair_logits[None], grad_tokens, vectors[0], vectors[1], qkv_share, out_share,
        vectors[2], vectors[3], up_share, vectors[4], down_share, vectors[5], left_share, right_share,
    )


def solution(mesh):
    whole = P(AXES, None)
    tile = P("rows", "gr", "gc")
    flat = P(AXES)
    one = P()
    in_specs = (
        whole, P(None, AXES), whole, whole, tile, one, one, one, one, one, one, one, one, one, one,
        one, one, whole, tile,
    )
    out_specs = (
        whole, tile, whole, one, one, flat, flat, one, one, flat, one, flat, one, flat, flat,
    )
    return jax.shard_map(body, mesh=mesh, in_specs=in_specs, out_specs=out_specs, check_vma=False)
```

```python
import functools
import math

import jax
import jax.numpy as jnp
from jax import lax
from jax.experimental import pallas as pl
from jax.experimental.pallas import tpu as pltpu
from jax.sharding import PartitionSpec as P

COORD=1000
SPAN=2*COORD+1
LOG2E=1.4426950408889634
BARRED=-2.0**99
SLOTS=64
BF=jnp.bfloat16
F32=jnp.float32
NT=(((1,),(1,)),((),()))
NN=(((1,),(0,)),((),()))
def dot(a,b,dims=NN):
    return lax.dot_general(a,b,dims,preferred_element_type=F32)

def whole_and_rest(scaled):
    whole=jnp.floor((scaled+0.5)*(1.0/SPAN))
    return whole, scaled-SPAN*whole

def key_side(low, high, half):
    c=jnp.floor((low+high).astype(F32)*0.5)
    return whole_and_rest(c*half)
def query_side(low, high, half):
    c=jnp.floor((low+high).astype(F32)*0.5)
    return whole_and_rest((COORD-c)*half)

def hi_lo(v):
    hi=v.astype(BF)
    return hi, (v-hi.astype(F32)).astype(BF)

def fwd_kernel(q_ref,k_ref,v_ref,boxr_ref,boxc_ref,tab_ref,mask_ref,cot_ref,
               ctx_ref,e_ref,linv_ref,rowp_ref,colp_ref,
               ohb_ref,oha_ref,kg_ref,rxy_ref,pg_ref,cx_ref,cy_ref,*panel_refs,rows,pair_scale):
    length=q_ref.shape[0]
    half=tab_ref.shape[1]//2
    quarter=half//2
    hp=pl.program_id(1)
    seq=pl.program_id(0)
    place=Place(1)
    mask_buf,cot_buf,in_sem=panel_refs[:3]
    panels=Panels(place,*panel_refs[3:7],panel_refs[7:])
    def inputs():
        return (pltpu.make_async_copy(mask_ref,mask_buf,in_sem.at[0]),
                pltpu.make_async_copy(cot_ref,cot_buf,in_sem.at[1]))
    @pl.when((hp==0)&(seq==0))
    def _():
        for copy in inputs():
            copy.start()
    @pl.when((hp==1)&(seq==0))
    def _():
        for copy in inputs():
            copy.wait()
        panels.fill(mask_buf,cot_buf,pair_scale)
        meet([place.gc_peer(d) for d in (1,2,3)]+[place.gr_peer(d) for d in (1,2,3)])
    @pl.when((hp==2)&(seq==0))
    def _():
        panels.start()
    lane=lax.broadcasted_iota(jnp.int32,(1,128),1)
    low=lane<64
    @pl.when(hp==0)
    def _():
        bc=boxc_ref[...]
        ax,fax=key_side(bc[:,0:1],bc[:,2:3],half)
        ay,fay=key_side(bc[:,1:2],bc[:,3:4],half)
        bx,fbx=query_side(bc[:,0:1],bc[:,2:3],half)
        by,fby=query_side(bc[:,1:2],bc[:,3:4],half)
        spot=(lane%quarter).astype(F32)
        is_x=(lane%half)<quarter
        oha=jnp.where(jnp.where(is_x,ax,ay)==spot,1.0,0.0)
        ohb=jnp.where(jnp.where(is_x,bx,by)==(quarter-1)-spot,1.0,0.0)
        ohb_ref[...]=jnp.where(low,ohb,0.0).astype(BF)
        oha_ref[...]=oha.astype(BF)
        page=bc[:,4:5].astype(jnp.int32)
        mine=(lane%64)==page
        barred=jnp.where((lane%64)<4,jnp.where(mine,0.0,BARRED),0.0)
        kg_ref[0]=jnp.where(low,oha,barred).astype(BF)
        kg_ref[1]=jnp.where(low,barred,oha).astype(BF)
        pg_ref[...]=jnp.where(mine,1.0,0.0).astype(BF)
        ohx=jnp.where(ax==spot,1.0,0.0)
        ohy=jnp.where(ay==spot,1.0,0.0)
        rxy_ref[pl.ds(0,length),:]=jnp.where(low,ohx,0.0).astype(BF)
        rxy_ref[pl.ds(length,length),:]=jnp.where(low,0.0,ohy).astype(BF)
        br=boxr_ref[...]
        _,gax=key_side(br[0:1],br[2:3],half)
        _,gay=key_side(br[1:2],br[3:4],half)
        cx_ref[...]=jnp.where(gax+fbx>=SPAN,1.0,0.0)
        cy_ref[...]=jnp.where(gay+fby>=SPAN,1.0,0.0)
    k=k_ref[...]
    v=v_ref[...]
    oha=oha_ref[...]
    b_row=lax.broadcasted_iota(jnp.int32,(half,128),0)
    l_col=lax.broadcasted_iota(jnp.int32,(half,128),1)
    row_x=b_row<quarter
    same_axis=row_x==((l_col%half)<quarter)
    d_axis=row_x==(l_col<half)
    heads=[]
    for a in range(2):
        t=tab_ref[pl.ds(2*hp+a,1),:]
        both=[jnp.where(low,t,0.0)+pltpu.roll(jnp.where(low,t,0.0),64,1),
              jnp.where(low,0.0,t)+pltpu.roll(jnp.where(low,0.0,t),64,1)]
        tiles=[]
        for b in both:
            spreads=[]
            for first in (0,1):
                whole=jnp.broadcast_to(b,(quarter,128))
                turned=pltpu.roll(whole,128-(quarter-1)-first,1,stride=1,stride_axis=0)
                lowq=jnp.where(lane<quarter,turned,0.0)
                pair=lowq+pltpu.roll(lowq,quarter,1)
                spreads.append(pair+pltpu.roll(pair,64,1))
            tiles.append(spreads)
        base=jnp.concatenate([tiles[0][0],tiles[1][0]],axis=0)
        nxt=jnp.concatenate([tiles[0][1],tiles[1][1]],axis=0)
        hi,lo=hi_lo(base)
        dhi,dlo=hi_lo(nxt-base)
        z=jnp.zeros_like(hi)
        is_hi=(l_col<64)==(a==1)
        g0=jnp.where(same_axis,jnp.where(is_hi,hi.astype(F32),lo.astype(F32)),0.0).astype(BF)
        g1=jnp.where(d_axis,jnp.where((l_col%half)<quarter,dhi.astype(F32),dlo.astype(F32)),0.0).astype(BF)
        hk=jnp.concatenate([g0,g1],axis=1)
        left=dot(ohb_ref[:,0:half],hk).astype(BF)
        if a==0:
            rhs=jnp.concatenate([jnp.where(low,k,oha),kg_ref[0]],axis=1)
            vv=jnp.where(low,v,jnp.ones_like(v))
        else:
            rhs=jnp.concatenate([jnp.where(low,oha,k),kg_ref[1]],axis=1)
            vv=jnp.where(low,jnp.ones_like(v),v)
        heads.append((left,rhs,vv))
    for c in range(length//rows):
        sl=pl.ds(c*rows,rows)
        q=q_ref[sl,:]*jnp.asarray(0.125,BF)
        pg=pg_ref[sl,:]
        outs=[]
        for a in range(2):
            left,rhs,vv=heads[a]
            lc=left[c*rows:(c+1)*rows]
            g0=lc[:,:128]
            if a==0:
                lhs=jnp.concatenate([jnp.where(low,q,g0),jnp.where(low,g0,pg)],axis=1)
            else:
                lhs=jnp.concatenate([jnp.where(low,g0,q),jnp.where(low,pg,g0)],axis=1)
            s=dot(lhs,rhs,NT)
            s=s+cx_ref[sl,:]*dot(lc[:,128:],rxy_ref[pl.ds(0,length),:],NT)
            s=s+cy_ref[sl,:]*dot(lc[:,128:],rxy_ref[pl.ds(length,length),:],NT)
            m=jnp.max(s,axis=1,keepdims=True)
            e=jnp.exp2((s-m)*LOG2E).astype(BF)
            e_ref[a,sl,:]=e
            outs.append(dot(e,vv))
        ctx=jnp.where(low,outs[0],outs[1])
        tot=jnp.where(low,pltpu.roll(outs[0],64,1),pltpu.roll(outs[1],64,1))
        linv=1.0/tot
        linv_ref[sl,:]=linv
        ctx_ref[sl,:]=(ctx*linv).astype(BF)
    @pl.when((hp==pl.num_programs(1)-1)&(seq==pl.num_programs(0)-1))
    def _():
        panels.collect(rowp_ref,colp_ref)

def attend_forward(qkv,boxes_r,boxes_c,seqs,table,mask,cot,pair_scale,rows=512):
    tokens,width=qkv.shape
    feats=width//3
    length=tokens//seqs
    heads=table.shape[0]
    pairs=heads//2
    return pl.pallas_call(
        functools.partial(fwd_kernel,rows=rows,pair_scale=pair_scale),
        grid=(seqs,pairs),
        in_specs=[
            pl.BlockSpec((length,128),lambda s,h:(s,h)),
            pl.BlockSpec((length,128),lambda s,h:(s,pairs+h)),
            pl.BlockSpec((length,128),lambda s,h:(s,2*pairs+h)),
            pl.BlockSpec((4,length),lambda s,h:(0,s)),
            pl.BlockSpec((length,128),lambda s,h:(s,0)),
            pl.BlockSpec(table.shape,lambda s,h:(0,0)),
            pl.BlockSpec(memory_space=pl.ANY),
            pl.BlockSpec(memory_space=pl.ANY),
        ],
        out_specs=[
            pl.BlockSpec((length,128),lambda s,h:(s,h)),
            pl.BlockSpec((2,None,length,length),lambda s,h:(h,s,0,0)),
            pl.BlockSpec((length,128),lambda s,h:(s,h)),
            pl.BlockSpec(memory_space=pltpu.VMEM),
            pl.BlockSpec(memory_space=pltpu.VMEM),
        ],
        out_shape=[jax.ShapeDtypeStruct((tokens,feats),BF),
                   jax.ShapeDtypeStruct((heads,seqs,length,length),BF),
                   jax.ShapeDtypeStruct((tokens,feats),F32)]
                  +[jax.ShapeDtypeStruct((4,mask.shape[0]//4,mask.shape[0]),BF)]*2,
        scratch_shapes=[pltpu.VMEM((length,128),BF),pltpu.VMEM((length,128),BF),
                        pltpu.VMEM((2,length,128),BF),pltpu.VMEM((2*length,128),BF),
                        pltpu.VMEM((length,128),BF),
                        pltpu.VMEM((length,length),F32),pltpu.VMEM((length,length),F32)]
                       +[pltpu.VMEM(mask.shape,jnp.int32),pltpu.VMEM(cot.shape,BF),pltpu.SemaphoreType.DMA((2,))]
                       +Panels.scratch(mask.shape[0]),
        compiler_params=pltpu.CompilerParams(collective_id=4,has_side_effects=True,vmem_limit_bytes=60<<20),
        name="attend_forward",
    )(qkv,qkv,qkv,boxes_r,boxes_c,table,mask,cot)


AXES = ("rows", "gr", "gc")
MESH = pl.DeviceIdType.MESH
PIECE = 384


class Place:
    def __init__(self, n_rows):
        self.n_rows = n_rows
        self.r = lax.axis_index("rows")
        self.g = lax.axis_index("gr")
        self.c = lax.axis_index("gc")
        self.core = lax.rem(self.c, 2)
        self.u = lax.div(self.c, 2)
        self.sibling = {"gc": self.u * 2 + 1 - self.core}
        self.across = {"gc": (1 - self.u) * 2 + self.core}

    def row_peer(self, d):
        return {"rows": lax.rem(self.r + d, self.n_rows)}

    def gr_peer(self, d):
        return {"gr": lax.rem(self.g + d, 4)}

    def gc_peer(self, d):
        return {"gc": lax.rem(self.c + d, 4)}

    def peers(self):
        return (
            [self.sibling, self.across]
            + [self.row_peer(d) for d in range(1, self.n_rows)]
            + [self.gr_peer(d) for d in range(1, 4)]
        )


def meet(peers):
    barrier = pltpu.get_barrier_semaphore()
    for peer in peers:
        pl.semaphore_signal(barrier, inc=1, device_id=peer, device_id_type=MESH)
    pl.semaphore_wait(barrier, len(peers))


def send(src, dst, send_sem, recv_sem, peer):
    return pltpu.make_async_remote_copy(
        src_ref=src, dst_ref=dst, send_sem=send_sem, recv_sem=recv_sem, device_id=peer,
        device_id_type=MESH,
    )


def by_step(step, first, end, action):
    if end - first == 1:
        action(first)
        return
    middle = (first + end) // 2
    pl.when(step < middle)(lambda: by_step(step, first, middle, action))
    pl.when(step >= middle)(lambda: by_step(step, middle, end, action))


class Unit:
    def __init__(self, array, part, block, rows_first, beats, source=None, leave=None):
        self.array, self.part, self.block = array, part, block
        self.rows_first, self.beats, self.source, self.leave = rows_first, beats, source, leave
        self.stages = sorted(stage for stage in beats if stage != "in")
        self.fresh = self.stages[0] == 0

    def does(self, stage):
        return stage in self.beats


class Shares:
    def __init__(self, place, units, piece, arrays, staging, carried, fins, got, bufs, sems, ends):
        self.p = place
        self.units = units
        self.piece = piece
        self.arrays = arrays
        self.staging = staging
        self.carried = carried
        self.fin = fins
        self.got = got
        self.own, self.b0, self.b1r, self.b1u, self.b2r, self.b2u, self.b3 = bufs
        self.ls, self.ss, self.rs = sems
        self.fs, self.fr = ends
        external = [i for i, unit in enumerate(units) if unit.source is None]
        self.external = sorted(external, key=lambda i: units[i].beats[0])

    def number(self, i, test):
        return sum(test(unit) for unit in self.units[:i])

    @staticmethod
    def kinds():
        return (
            lambda unit: True,
            lambda unit: unit.does(0),
            lambda unit: unit.does(1) and unit.rows_first,
            lambda unit: unit.does(1) and not unit.rows_first,
            lambda unit: unit.does(2) and not unit.rows_first,
            lambda unit: unit.does(2) and unit.rows_first,
            lambda unit: unit.does(3),
        )

    @staticmethod
    def scratch(units, piece, n_rows):
        n, m, r = len(units), 48, n_rows
        shapes = (
            (r, 4, 2, m), (r, 4, 2, m), (r - 1, 4, 2, m), (r, 4, m), (r - 1, 4, m), (4, m), (3, m),
        )
        bufs = [
            pltpu.VMEM((max(1, sum(map(test, units))),) + shape + (piece,), BF)
            for test, shape in zip(Shares.kinds(), shapes)
        ]
        dma = pltpu.SemaphoreType.DMA
        return bufs + [dma((n,)), dma((n, r + 4)), dma((n, r + 4))]

    @staticmethod
    def result_scratch(sizes):
        dma = pltpu.SemaphoreType.DMA
        k = len(sizes)
        fins = [pltpu.VMEM((2, rows, x // 2), F32) for rows, x in sizes]
        got = [pltpu.VMEM((rows, x // 2), F32) for rows, x in sizes]
        return fins + got + [dma((k,)), dma((k,))]

    def buffer(self, kind, i):
        bufs = (self.own, self.b0, self.b1r, self.b1u, self.b2r, self.b2u, self.b3)
        return bufs[kind].at[self.number(i, self.kinds()[kind])]

    def piece_of(self, i, core):
        unit = self.units[i]
        if unit.source is None:
            at = unit.block * 2 * self.piece + core * self.piece
            columns = pl.ds(pl.multiple_of(at, 128), self.piece)
            return self.arrays[unit.array].at[:, :, :, unit.part, :, columns]
        _, n, column = unit.source
        return self.staging.at[n, core, :, :, :, :, column : column + self.piece]

    def swap(self, i):
        src = self.piece_of(i, 1 - self.p.core)
        return send(src, self.buffer(1, i), self.ss.at[i, 0], self.rs.at[i, 0], self.p.sibling)

    def keep(self, i):
        unit, p = self.units[i], self.p
        if unit.source is None:
            src, to = self.piece_of(i, p.core), self.own.at[i]
        else:
            src = self.carried[unit.source[1]].at[unit.source[2]]
            if unit.does(2):
                to = self.own.at[i, p.r] if unit.rows_first else self.own.at[i, :, :, p.u]
            else:
                to = self.own.at[i, p.r, :, p.u]
        return pltpu.make_async_copy(src, to, self.ls.at[i])

    def along_rows(self, i, first):
        p = self.p
        out = []
        for d in range(1, p.n_rows):
            to = lax.rem(p.r + d, p.n_rows)
            src = self.own.at[i, to] if first else self.own.at[i, to, :, p.u]
            dst = self.buffer(2 if first else 4, i).at[d - 1]
            out.append(send(src, dst, self.ss.at[i, 1 + d], self.rs.at[i, 1 + d], p.row_peer(d)))
        return out

    def across(self, i, first):
        p = self.p
        src = self.own.at[i, :, :, 1 - p.u] if first else self.own.at[i, p.r, :, 1 - p.u]
        dst = self.buffer(3 if first else 5, i)
        return [send(src, dst, self.ss.at[i, 1], self.rs.at[i, 1], p.across)]

    def along_gr(self, i):
        p = self.p
        out = []
        for d in range(1, 4):
            src = self.own.at[i, p.r, lax.rem(p.g + d, 4), p.u]
            at = p.n_rows + d
            dst = self.buffer(6, i).at[d - 1]
            out.append(send(src, dst, self.ss.at[i, at], self.rs.at[i, at], p.gr_peer(d)))
        return out

    def copies(self, i, stage):
        if stage == 0:
            return [self.swap(i)]
        if stage == 3:
            return self.along_gr(i)
        if self.units[i].rows_first == (stage == 1):
            return self.along_rows(i, stage == 1)
        return self.across(i, stage == 1)

    def start(self, i, stage):
        if stage == 0 and self.units[i].source is None:
            self.keep(i).start()
        for copy in self.copies(i, stage):
            copy.start()

    def finish(self, i, stage):
        p, unit = self.p, self.units[i]
        if stage == 0 and unit.source is None:
            self.keep(i).wait()
        for copy in self.copies(i, stage):
            copy.wait_recv()
        if stage == 0:
            to = self.own.at[i]
            mine = to if unit.source is None else self.piece_of(i, p.core)
            theirs = self.buffer(1, i)

            @pl.loop(0, 4)
            def _(n):
                to[:, n] = mine[:, n] + theirs[:, n]

            return
        if stage == 3:
            total = self.own[i, p.r, p.g, p.u].astype(F32)
            for d in range(3):
                total = total + self.buffer(6, i)[d].astype(F32)
            m = total.shape[0]
            fin = self.fin[unit.array]
            rows = fin.shape[1]
            span = slice(unit.block * self.piece, (unit.block + 1) * self.piece)
            if rows < m:
                fin[0, :, span] = total[:rows]
                fin[1, :, span] = total[rows:]
            else:
                per = rows // m
                row = (unit.part % per) * m
                fin[unit.part // per, row : row + m, span] = total
            return
        if stage == 2:
            to = self.own.at[i, p.r, :, p.u]
        else:
            to = self.own.at[i, p.r] if unit.rows_first else self.own.at[i, :, :, p.u]
        if unit.rows_first == (stage == 1):
            terms = [self.buffer(2 if stage == 1 else 4, i).at[d] for d in range(p.n_rows - 1)]
        else:
            terms = [self.buffer(3 if stage == 1 else 5, i)]
        out = to
        if unit.leave is not None and stage == unit.stages[-1]:
            out = self.carried[unit.leave[0]].at[unit.leave[1]]
        if stage == 1:
            @pl.loop(0, 4)
            def _(n):
                at = n if unit.rows_first else (slice(None), n)
                total = to[at]
                for term in terms:
                    total = total + term[at]
                out[at] = total
        else:
            total = to[...]
            for term in terms:
                total = total + term[...]
            out[...] = total

    def last(self, k):
        return send(
            self.fin[k].at[1 - self.p.core], self.got[k], self.fs.at[k], self.fr.at[k],
            self.p.sibling,
        )

    def begin(self, window):
        for i, unit in enumerate(self.units):
            if not unit.fresh:
                self.keep(i).start()
        for i in self.external[:window]:
            self.start(i, 0)

    def tick(self, t, window, done):
        due = []
        for i, unit in enumerate(self.units):
            for stage, beat in unit.beats.items():
                if beat == t:
                    due.append((-1 if stage == "in" else stage, i))
        for stage, i in sorted(due, key=lambda entry: (-entry[0], entry[1])):
            unit = self.units[i]
            if stage < 0:
                self.keep(i).wait()
                self.start(i, unit.stages[0])
                continue
            self.finish(i, stage)
            if stage == 0 and i in self.external:
                later = self.external.index(i) + window
                if later < len(self.external):
                    self.start(self.external[later], 0)
            if stage == 3:
                final, count = done[unit.array]
                if t == final:
                    done[unit.array] = final, count - 1
                    if count == 1:
                        self.last(unit.array).start()
            elif stage < unit.stages[-1]:
                self.start(i, stage + 1)

    def ticks(self):
        return 1 + max(beat for unit in self.units for beat in unit.beats.values())

    def deliver(self, k, out, spans):
        core = self.p.core
        self.last(k).wait()
        for value, owner in ((self.fin[k][core], core), (self.got[k][...], 1 - core)):
            at = 0
            for base, step, width in spans:
                where = pl.ds(pl.multiple_of(base + owner * step, 128), width)
                out[:, where] = value[:, at : at + width]
                at += width

    def wait_sends(self):
        for i, unit in enumerate(self.units):
            for stage in unit.stages:
                for copy in self.copies(i, stage):
                    copy.wait_send()


def on_the_way(units, arrays):
    beats = [[unit.beats[3] for unit in units if unit.array == k and unit.does(3)] for k in range(arrays)]
    return [(max(of), of.count(max(of))) if of else (-1, 0) for of in beats]


class Total:
    def __init__(self, place, source, out, bufs, sems):
        self.p = place
        self.src = source
        self.out = out
        self.part, self.pair, self.high, self.rows, self.quad = bufs
        self.ss, self.rs = sems

    @staticmethod
    def scratch(shape, n_rows):
        dma = pltpu.SemaphoreType.DMA
        bufs = [
            pltpu.VMEM((3,) + shape, F32), pltpu.VMEM(shape, F32), pltpu.VMEM(shape, F32),
            pltpu.VMEM((n_rows,) + shape, F32), pltpu.VMEM((4,) + shape, F32),
        ]
        return bufs, [dma((n_rows + 4,)), dma((n_rows + 4,))]

    def copies(self, stage):
        p = self.p
        if stage == 0:
            return [send(self.src, self.pair, self.ss.at[0], self.rs.at[0], p.sibling)]
        if stage == 1:
            return [send(self.part.at[0], self.high, self.ss.at[1], self.rs.at[1], p.across)]
        if stage == 2:
            return [
                send(
                    self.part.at[1], self.rows.at[p.r], self.ss.at[1 + d], self.rs.at[1 + d],
                    p.row_peer(d),
                )
                for d in range(1, p.n_rows)
            ]
        return [
            send(
                self.part.at[2], self.quad.at[p.g], self.ss.at[p.n_rows + d],
                self.rs.at[p.n_rows + d], p.gr_peer(d),
            )
            for d in range(1, 4)
        ]

    def start(self, stage):
        for copy in self.copies(stage):
            copy.start()

    def finish(self, stage):
        p = self.p
        for copy in self.copies(stage):
            copy.wait_recv()
        if stage == 0:
            self.part[0] = self.src[...] + self.pair[...]
        elif stage == 1:
            self.part[1] = self.part[0] + self.high[...]
        elif stage == 2:
            self.rows[p.r] = self.part[1]
            total = self.rows[0]
            for d in range(1, p.n_rows):
                total = total + self.rows[d]
            self.part[2] = total
        else:
            self.quad[p.g] = self.part[2]
            self.out[...] = (self.quad[0] + self.quad[1]) + (self.quad[2] + self.quad[3])

    def wait_sends(self):
        for stage in range(4):
            for copy in self.copies(stage):
                copy.wait_send()


def view(g, n_rows):
    rows, x = g.shape
    per = rows // (n_rows * 8)
    return g.reshape(n_rows, 4, 2, per // 48, 48, x)


def project_kernel(x_ref, gain_ref, bias_ref, w_ref, box_ref, page_ref, h1_ref, qkv_ref, cols_ref):
    @pl.when(pl.program_id(0) == 0)
    def _():
        chunk = 256
        count = x_ref.shape[0]

        @pl.loop(0, count // chunk)
        def _(c):
            sl = pl.ds(pl.multiple_of(c * chunk, chunk), chunk)
            x = x_ref[sl, :].astype(F32)
            average, inverse = norm_stats(x)
            h1_ref[sl, :] = ((x - average) * inverse * gain_ref[...].reshape(1, -1) + bias_ref[...].reshape(1, -1)).astype(BF)
        pages = jnp.concatenate([page_ref[s : s + 1, :] for s in range(page_ref.shape[0])], axis=1)
        lines = jnp.concatenate(
            [box_ref[...].astype(F32), pages.astype(F32), jnp.zeros((123, count), F32)], axis=0
        )
        cols_ref[...] = lines.T

    qkv_ref[...] = dot(h1_ref[...], w_ref[...]).astype(BF)


def project_forward(tokens, gain, bias, weight, boxes, page_ids):
    count, feats = tokens.shape
    width = weight.shape[1]
    block = feats
    vm = pl.BlockSpec(memory_space=pltpu.VMEM)
    return pl.pallas_call(
        project_kernel,
        grid=(width // block,),
        in_specs=[
            pl.BlockSpec((count, feats), lambda j: (0, 0)), vm, vm,
            pl.BlockSpec((feats, block), lambda j: (0, j)), vm, vm,
        ],
        out_specs=[vm, pl.BlockSpec((count, block), lambda j: (0, j)), vm],
        out_shape=[
            jax.ShapeDtypeStruct((count, feats), BF), jax.ShapeDtypeStruct((count, width), BF),
            jax.ShapeDtypeStruct((count, 128), F32),
        ],
        compiler_params=pltpu.CompilerParams(vmem_limit_bytes=63 << 20),
        name="project_forward",
    )(tokens, gain, bias, weight, boxes, page_ids)


def slot_members(seg_row, slots):
    ids = lax.broadcasted_iota(jnp.int32, (slots, seg_row.shape[1]), 0)
    return jnp.where(ids == seg_row, 1.0, 0.0)


def mlp_forward_kernel(
    ctx_ref, wo_ref, x_ref, gain_ref, bias_ref, wu_ref, bu_ref, wd_ref, seg_ref,
    r1_ref, h2_ref, act_ref, slope_ref, out_ref, emb_ref, acc_ref,
):
    step = pl.program_id(0)
    count = x_ref.shape[0]
    chunk = 512

    @pl.when(step == 0)
    def _():
        @pl.loop(0, count // chunk)
        def _(c):
            sl = pl.ds(pl.multiple_of(c * chunk, chunk), chunk)
            r1 = x_ref[sl, :].astype(F32) + dot(ctx_ref[sl, :], wo_ref[...])
            average, inverse = norm_stats(r1)
            r1_ref[sl, :] = r1
            acc_ref[sl, :] = r1
            h2_ref[sl, :] = ((r1 - average) * inverse * gain_ref[...].reshape(1, -1) + bias_ref[...].reshape(1, -1)).astype(BF)

    for c in range(count // chunk):
        sl = slice(c * chunk, (c + 1) * chunk)
        act, slope = gelu_pair(dot(h2_ref[sl, :], wu_ref[...]) + bu_ref[...])
        act = act.astype(BF)
        act_ref[sl, :] = act
        slope_ref[sl, :] = slope.astype(BF)
        acc_ref[sl, :] += dot(act, wd_ref[...])

    @pl.when(step == pl.num_programs(0) - 1)
    def _():
        out_ref[...] = acc_ref[...].astype(BF)
        seqs, length = seg_ref.shape
        slots = emb_ref.shape[0] // seqs
        for s in range(seqs):
            members = slot_members(seg_ref[s : s + 1, :], slots)
            total = dot(members.astype(BF), out_ref[s * length : (s + 1) * length, :])
            sizes = jnp.sum(members, axis=1, keepdims=True)
            emb_ref[s * slots : (s + 1) * slots, :] = (total / sizes).astype(BF)


def mlp_forward(ctx, w_out, tokens, gain, bias, w_up, b_up, w_down, seg_ids, slots):
    count, feats = tokens.shape
    hidden = w_up.shape[1]
    vm = pl.BlockSpec(memory_space=pltpu.VMEM)
    return pl.pallas_call(
        mlp_forward_kernel,
        grid=(hidden // feats,),
        in_specs=[
            vm, vm, vm, vm, vm, pl.BlockSpec((feats, feats), lambda f: (0, f)),
            pl.BlockSpec((1, feats), lambda f: (0, f)), pl.BlockSpec((feats, feats), lambda f: (f, 0)), vm,
        ],
        out_specs=[
            vm, vm, pl.BlockSpec((count, feats), lambda f: (0, f)),
            pl.BlockSpec((count, feats), lambda f: (0, f)), vm, vm,
        ],
        out_shape=[
            jax.ShapeDtypeStruct((count, feats), F32), jax.ShapeDtypeStruct((count, feats), BF),
            jax.ShapeDtypeStruct((count, hidden), BF), jax.ShapeDtypeStruct((count, hidden), BF),
            jax.ShapeDtypeStruct((count, feats), BF),
            jax.ShapeDtypeStruct((seg_ids.shape[0] * slots, feats), BF),
        ],
        scratch_shapes=[pltpu.VMEM((count, feats), F32)],
        compiler_params=pltpu.CompilerParams(vmem_limit_bytes=50 << 20),
        name="mlp_forward",
    )(
        ctx, w_out, tokens, gain, bias, w_up,
        b_up.reshape(1, hidden), w_down, seg_ids,
    )


class Panels:
    def __init__(self, place, tile, tile_t, rows, cols, sems):
        self.p = place
        self.tile, self.tile_t, self.rows, self.cols = tile, tile_t, rows, cols
        self.ss, self.rs = sems

    @staticmethod
    def scratch(size):
        dma = pltpu.SemaphoreType.DMA
        part = size // 4
        return [
            pltpu.VMEM((4, part, size), BF), pltpu.VMEM((4, part, size), BF),
            pltpu.VMEM((3, part, size), BF), pltpu.VMEM((3, part, size), BF), dma((6,)), dma((6,)),
        ]

    def copies(self):
        p = self.p
        out = []
        for d in range(1, 4):
            for n, (src, dst, peer, at) in enumerate((
                (self.tile, self.rows, p.gc_peer(d), p.c), (self.tile_t, self.cols, p.gr_peer(d), p.g),
            )):
                at_sem = 3 * n + d - 1
                out.append(
                    send(
                        src.at[lax.rem(at + d, 4)], dst.at[d - 1], self.ss.at[at_sem],
                        self.rs.at[at_sem], peer,
                    )
                )
        return out

    def fill(self, mask, cot, scale):
        g_raw = cot[...].astype(F32) * scale * mask[...].astype(F32)
        self.tile[...] = g_raw.astype(BF).reshape(self.tile.shape)
        self.tile_t[...] = g_raw.T.astype(BF).reshape(self.tile_t.shape)

    def start(self):
        for copy in self.copies():
            copy.start()

    def collect(self, row_out, col_out):
        p = self.p
        for copy in self.copies():
            copy.wait()
        row_out[p.c] = self.tile[p.c]
        col_out[p.g] = self.tile_t[p.g]
        for d in range(1, 4):
            row_out[lax.rem(p.c + 4 - d, 4)] = self.rows[d - 1]
            col_out[lax.rem(p.g + 4 - d, 4)] = self.cols[d - 1]


class Spread:
    def __init__(self, place, blocks, sems):
        self.p = place
        self.e = blocks
        self.ss, self.rs = sems
        self.near = lax.rem(place.c + 2, 4)

    @staticmethod
    def scratch(shape):
        dma = pltpu.SemaphoreType.DMA
        return [pltpu.VMEM((4, 4) + shape, BF), dma((4, 4, 3)), dma((4, 4))]

    def hop(self, row, col, kind, peer):
        block = self.e.at[row, col]
        return send(block, block, self.ss.at[row, col, kind], self.rs.at[row, col], peer)

    def own(self, step, waiting):
        p = self.p
        for sign in (1, -1) if step else (0,):
            row = p.g + sign * step
            inside = (row >= 0) & (row <= 3)

            @pl.when(inside)
            def _(row=row, sign=sign):
                if step and not waiting:
                    self.hop(row, p.c, 0, p.sibling).wait_recv()
                go = "wait_send" if waiting else "start"
                getattr(self.hop(row, p.c, 0, p.sibling), go)()
                getattr(self.hop(row, p.c, 1, p.across), go)()
                for way in (1, -1) if step == 0 else (-sign,):
                    to = p.g + way

                    @pl.when((to >= 0) & (to <= 3))
                    def _(to=to, way=way):
                        if step == 0 and way == -1:
                            copy = send(
                                self.e.at[row, p.c], self.e.at[row, p.c], self.down.at[0],
                                self.rs.at[row, p.c], {"gr": to},
                            )
                        else:
                            copy = self.hop(row, p.c, 2, {"gr": to})
                        getattr(copy, go)()

    def relay(self, step, waiting):
        p = self.p
        for sign in (1, -1) if step else (0,):
            row = p.g + sign * step

            @pl.when((row >= 0) & (row <= 3))
            def _(row=row):
                copy = self.hop(row, self.near, 0, p.sibling)
                if waiting:
                    copy.wait_send()
                else:
                    copy.wait_recv()
                    copy.start()

    def arrive(self, rows, cols):
        for row in rows:
            for col in cols:
                self.hop(row, col, 0, self.p.sibling).wait_recv()


def pair_kernel(
    emb_ref, left_ref, right_ref, rowp_ref, colp_ref, mask_ref, cot_ref, seg_ref,
    logits_ref, gleft_ref, gright_ref, gy_ref, gmlp_ref, e_ref, ss, rs, down, *, scale,
):
    place = Place(1)
    meet([place.sibling, place.across] + [place.gr_peer(d) for d in (1, 2, 3)])
    spread = Spread(place, e_ref, (ss, rs))
    spread.down = down
    p = place
    e_ref[p.g, p.c] = emb_ref[...]
    part, width = emb_ref.shape
    spread.own(0, False)
    spread.own(1, False)
    spread.relay(0, False)
    sib = p.u * 2 + 1 - p.core
    far = (1 - p.u) * 2 + 1 - p.core
    spread.arrive([p.g], [sib, far])
    left_rows = dot(e_ref[p.g].reshape(4 * part, width), left_ref[...]).astype(BF)
    spread.own(2, False)
    spread.relay(1, False)
    spread.own(3, False)
    right_cols = dot(e_ref[:, p.c].reshape(4 * part, width), right_ref[...]).astype(BF)
    spread.relay(2, False)
    logits_ref[...] = mask_ref[...].astype(F32) * dot(left_rows, right_cols, NT) * scale
    spread.relay(3, False)
    for d in range(1, 4):
        spread.arrive([lax.rem(p.g + d, 4)], [sib, far])
    row_sum = jnp.zeros((part, width), F32)
    col_sum = jnp.zeros((part, width), F32)
    for n in range(4):
        row_sum = row_sum + dot(rowp_ref[n], e_ref[:, n].reshape(4 * part, width))
        col_sum = col_sum + dot(colp_ref[n], e_ref[n].reshape(4 * part, width))

    def through(total, weight):
        high, low = hi_lo(total)
        return (dot(high, weight) + dot(low, weight)).astype(BF)

    g_left = through(row_sum, right_ref[...])
    g_right = through(col_sum, left_ref[...])
    emb_t = emb_ref[...].astype(F32).T.astype(BF)
    gleft_ref[...] = dot(emb_t, g_left).astype(BF)
    gright_ref[...] = dot(emb_t, g_right).astype(BF)
    g_emb = dot(g_left, left_ref[...], NT) + dot(g_right, right_ref[...], NT)
    seqs, length = seg_ref.shape
    slots = part // seqs
    for n in range(seqs):
        members = slot_members(seg_ref[n : n + 1, :], slots)
        g_seg = g_emb[n * slots : (n + 1) * slots] / jnp.sum(members, axis=1, keepdims=True)
        high, low = hi_lo(g_seg)
        twice = jnp.concatenate([members, members], axis=0).T.astype(BF)
        sl = slice(n * length, (n + 1) * length)
        g_y = cot_ref[sl, :].astype(F32) + dot(twice, jnp.concatenate([high, low], axis=0))
        gy_ref[sl, :] = g_y
        gmlp_ref[sl, :] = g_y.astype(BF)
    for step in range(4):
        spread.own(step, True)
        spread.relay(step, True)


def pair_head(emb, rel_left, rel_right, row_panel, col_panel, mask, cot_out, seg_ids, scale):
    part, width = emb.shape
    size = mask.shape[0]
    vm = pl.BlockSpec(memory_space=pltpu.VMEM)
    dma = pltpu.SemaphoreType.DMA
    return pl.pallas_call(
        functools.partial(pair_kernel, scale=scale),
        in_specs=[vm] * 8,
        out_specs=[vm] * 5,
        out_shape=[
            jax.ShapeDtypeStruct((size, size), F32), jax.ShapeDtypeStruct(rel_left.shape, BF),
            jax.ShapeDtypeStruct(rel_right.shape, BF), jax.ShapeDtypeStruct(cot_out.shape, F32),
            jax.ShapeDtypeStruct(cot_out.shape, BF),
        ],
        scratch_shapes=Spread.scratch((part, width)) + [dma((1,))],
        compiler_params=pltpu.CompilerParams(
            collective_id=5, has_side_effects=True, vmem_limit_bytes=50 << 20
        ),
        name="pair_head",
    )(emb, rel_left, rel_right, row_panel, col_panel, mask, cot_out, seg_ids)


def norm_back_chunk(g_out, rows, gain):
    average, inverse = norm_stats(rows)
    z = (rows - average) * inverse
    g_z = g_out * gain
    mean_g = jnp.mean(g_z, axis=-1, keepdims=True)
    mean_gz = jnp.mean(g_z * z, axis=-1, keepdims=True)
    return inverse * (g_z - mean_g - z * mean_gz), jnp.sum(g_out * z, axis=0, keepdims=True)


def turn(source, target):
    @pl.loop(0, source.shape[0] // 128)
    def _(c):
        sl = pl.ds(pl.multiple_of(c * 128, 128), 128)
        target[:, sl] = source[sl, :].astype(F32).T.astype(BF)


def put_lines(ref, at, row):
    for j in range(row.shape[1] // 128):
        ref[at + j : at + j + 1, :] = row[:, j * 128 : (j + 1) * 128]


def mlp_back_kernel(*refs, n_ext, units, n_rows, comm, window):
    (slope_ref, wd_ref, wu_ref, gmlp_ref, h2_ref, r1_ref, gy_ref, ctx_ref, wo_ref, gain_ref) = refs[:10]
    at = 10
    arrays = refs[at : at + n_ext]
    at += n_ext
    gup_ref, gr1_ref, gout_ref, gctx_ref, small_ref = refs[at : at + 5]
    at += 5
    carried = refs[at : at + 3]
    at += 3 if comm else 0
    h2t_ref, acc_ref, r1_buf, gy_buf, ctx_buf, ctxt_ref, wo_buf, gatt_ref, in_sem = refs[at : at + 9]
    at += 9
    n_step = pl.num_programs(0)
    step = pl.program_id(0)
    count, feats = acc_ref.shape
    lines = feats // 128
    steps = (small_ref.shape[0] - 16) // lines - 4
    if comm:
        place = Place(n_rows)
        shares = Shares(
            place, units, PIECE, arrays, None, carried, (), (), refs[at : at + 7],
            refs[at + 7 : at + 10], (None, None),
        )
        done = on_the_way(units, 3)

    def inputs():
        pairs = (
            (ctx_ref, ctx_buf), (r1_ref, r1_buf), (gy_ref, gy_buf), (wo_ref, wo_buf),
        )
        return [pltpu.make_async_copy(a, b, in_sem.at[i]) for i, (a, b) in enumerate(pairs)]

    @pl.when(step == 0)
    def _():
        for copy in inputs():
            copy.start()
        if comm:
            meet(place.peers())
            shares.begin(window)
        acc_ref[...] = jnp.zeros_like(acc_ref)
        small_ref[...] = jnp.zeros_like(small_ref)

    def beat(part):
        if comm:
            by_step(step, 0, steps, lambda n: shares.tick(2 * n + part, window, done))

    g_act = dot(gmlp_ref[...], wd_ref[...], NT)
    g_wide = g_act * slope_ref[...].astype(F32)
    g_u = g_wide.astype(BF)
    bias = jnp.sum(g_u.astype(F32), axis=0, keepdims=True)
    acc_ref[...] += dot(g_u, wu_ref[...], NT)
    beat(0)

    @pl.when(step == 0)
    def _():
        turn(h2_ref, h2t_ref)

    gup_ref[...] = dot(h2t_ref[...], g_u).astype(BF)
    for at_step in range(steps):
        @pl.when(step == at_step)
        def _(at_step=at_step):
            put_lines(small_ref, (4 + at_step) * lines, bias)
    beat(1)

    @pl.when(step == n_step - 1)
    def _():
        for copy in inputs():
            copy.wait()
        chunk = 256

        def back(c, sums):
            sl = pl.ds(pl.multiple_of(c * chunk, chunk), chunk)
            g_out = acc_ref[sl, :]
            g_in, part = norm_back_chunk(g_out, r1_buf[sl, :], gain_ref[...].reshape(1, -1))
            g_r1 = gy_buf[sl, :] + g_in
            gr1_ref[sl, :] = g_r1
            gatt_ref[sl, :] = g_r1.astype(BF)
            return sums[0] + part, sums[1] + jnp.sum(g_out, axis=0, keepdims=True)

        nothing = jnp.zeros((1, feats), F32)
        gain_sum, bias_sum = lax.fori_loop(0, count // chunk, back, (nothing, nothing))
        put_lines(small_ref, 2 * lines, gain_sum)
        put_lines(small_ref, 3 * lines, bias_sum)
        if comm:
            shares.tick(2 * steps, window, done)
        turn(ctx_buf, ctxt_ref)
        gctx_ref[...] = dot(gatt_ref[...], wo_buf[...], NT).astype(BF)
        if comm:
            shares.tick(2 * steps + 1, window, done)
        gout_ref[...] = dot(ctxt_ref[...], gatt_ref[...]).astype(BF)
        if comm:
            for t in range(2 * steps + 2, shares.ticks()):
                shares.tick(t, window, done)
            shares.wait_sends()


def early_units():
    return (
        Unit(0, 0, 0, False, {0: 1, 1: 4, 2: 7}, leave=(2, 0)),
        Unit(1, 0, 0, True, {0: 1, 1: 4, 2: 7}, leave=(2, 1)),
        Unit(2, 0, 0, False, {0: 2, 1: 6}, leave=(1, 0)),
        Unit(2, 1, 0, True, {0: 2, 1: 6}, leave=(0, 0)),
        Unit(2, 2, 0, False, {0: 5, 1: 9}, leave=(1, 1)),
        Unit(2, 3, 0, True, {0: 5, 1: 9}, leave=(0, 1)),
    )


def mlp_backward(
    slope, w_down, w_up, g_mlp, h2, r1, g_y, ctx, w_out, gain, small_rows, left, right, down, n_rows, comm
):
    count, feats = g_mlp.shape
    hidden = slope.shape[1]
    steps = hidden // feats
    vm = pl.BlockSpec(memory_space=pltpu.VMEM)
    any_ref = pl.BlockSpec(memory_space=pl.ANY)
    views = [view(g, n_rows) for g in (left, right, down)] if comm else []
    units = early_units()
    extra = []
    if comm:
        extra = [
            jax.ShapeDtypeStruct((2, 4, 2, 48, PIECE), BF),
            jax.ShapeDtypeStruct((2, n_rows, 4, 48, PIECE), BF),
            jax.ShapeDtypeStruct((2, 4, 48, PIECE), BF),
        ]
    scratch = [
        pltpu.VMEM((feats, count), BF), pltpu.VMEM((count, feats), F32),
        pltpu.VMEM((count, feats), F32), pltpu.VMEM((count, feats), F32), pltpu.VMEM((count, feats), BF),
        pltpu.VMEM((feats, count), BF), pltpu.VMEM((feats, feats), BF), pltpu.VMEM((count, feats), BF),
        pltpu.SemaphoreType.DMA((4,)),
    ]
    params = dict(vmem_limit_bytes=63 << 20, dimension_semantics=("arbitrary",))
    if comm:
        scratch += Shares.scratch(units, PIECE, n_rows)
        params.update(collective_id=3, has_side_effects=True)
    return pl.pallas_call(
        functools.partial(
            mlp_back_kernel, n_ext=len(views), units=units, n_rows=n_rows, comm=comm, window=3,
        ),
        grid=(steps,),
        in_specs=[
            pl.BlockSpec((count, feats), lambda f: (0, f)),
            pl.BlockSpec((feats, feats), lambda f: (f, 0)),
            pl.BlockSpec((feats, feats), lambda f: (0, f)),
            vm, vm, any_ref, any_ref, any_ref, any_ref, vm,
        ] + [any_ref] * len(views),
        out_specs=[pl.BlockSpec((feats, feats), lambda f: (0, f)), vm, vm, vm, vm] + [vm] * len(extra),
        out_shape=[
            jax.ShapeDtypeStruct((feats, hidden), BF), jax.ShapeDtypeStruct((count, feats), F32),
            jax.ShapeDtypeStruct((feats, feats), BF), jax.ShapeDtypeStruct((count, feats), BF),
            jax.ShapeDtypeStruct((small_rows, 128), F32),
        ] + extra,
        scratch_shapes=scratch,
        compiler_params=pltpu.CompilerParams(**params),
        name="mlp_backward",
    )(slope, w_down, w_up, g_mlp, h2, r1, g_y, ctx, w_out, gain, *views)


def deliver_kernel(gx_ref, small_ref, *refs, parts, heads):
    n_in = sum(parts)
    ins, outs = refs[:n_in], refs[n_in:]
    outs[0][...] = gx_ref[...]

    @pl.when(pl.program_id(0) == 0)
    def _():
        at = 0
        for k, n in enumerate(parts):
            out = outs[1 + k]
            row = 0
            for ref in ins[at : at + n]:
                rows, x = ref.shape
                per = x // 128
                for j in range(per):
                    out[pl.ds(row + j, rows, stride=per), :] = ref[:, j * 128 : (j + 1) * 128]
                row += rows * per
            at += n
        line = 0
        for out in outs[1 + len(parts) :]:
            if len(out.shape) == 1:
                for j in range(out.shape[0] // 128):
                    out[j * 128 : (j + 1) * 128] = small_ref[line]
                    line += 1
            else:
                out[...] = small_ref[line : line + out.shape[0], :]


def deliver(g_tokens, small, shares, features, hidden, heads):
    count = g_tokens.shape[0]
    flat = [p for group in shares for p in group]
    vm = pl.BlockSpec(memory_space=pltpu.VMEM)
    block = count // 2
    sizes = [sum(p.size for p in group) for group in shares]
    results = pl.pallas_call(
        functools.partial(deliver_kernel, parts=tuple(len(group) for group in shares), heads=heads),
        grid=(2,),
        in_specs=[pl.BlockSpec((block, features), lambda i: (i, 0)), vm] + [vm] * len(flat),
        out_specs=[pl.BlockSpec((block, features), lambda i: (i, 0))] + [vm] * (len(shares) + 6),
        out_shape=[jax.ShapeDtypeStruct(g_tokens.shape, F32)]
        + [jax.ShapeDtypeStruct((size // 128, 128), F32) for size in sizes]
        + [jax.ShapeDtypeStruct((features,), F32)] * 4
        + [jax.ShapeDtypeStruct((hidden,), F32), jax.ShapeDtypeStruct((heads, 128), F32)],
        name="deliver",
    )(g_tokens, small, *flat)
    return (
        results[0], [r.reshape(-1) for r in results[1 : 1 + len(shares)]], results[1 + len(shares) :]
    )


def back_kernel(*refs, n_ext, units, tail, spans, n_rows, comm, window):
    (q_ref, k_ref, v_ref, e_ref, linv_ref, ctx_ref, gctx_ref, boxr_ref, boxc_ref, w_ref, h1_ref,
     x_ref, gr1_ref, gain_ref, small_ref) = refs[:15]
    at = 15
    arrays = refs[at : at + n_ext]
    at += n_ext
    carried = refs[at : at + 3] if comm else ()
    at += len(carried)
    n_out = len(spans)
    gx_ref = refs[at]
    small_out = refs[at + 1]
    at += 2
    if comm:
        outs = refs[at : at + n_out]
        at += n_out
    else:
        grad_ref = refs[at]
        at += 1
    (oha_ref, ohbt_ref, cx_ref, cy_ref, g_ref, gcx_ref, gcy_ref, lt_ref, gt_ref, gall_ref, h1t_ref,
     hist_ref, h1_buf, x_buf, gr1_buf, w_buf, pack_ref, in_sem) = refs[at : at + 18]
    at += 18
    length = q_ref.shape[0]
    half, quarter = 64, 32
    pairs, seqs = pl.num_programs(0), pl.num_programs(1)
    hp = pl.program_id(0)
    s_id = pl.program_id(1)
    n_seq = cx_ref.shape[0]
    n_pair = hist_ref.shape[0] // 2
    lane = lax.broadcasted_iota(jnp.int32, (1, 128), 1)
    low = lane < 64
    if comm:
        place = Place(n_rows)
        staging = refs[at]
        fins = refs[at + 1 : at + n_out + 1]
        at += n_out + 1
        got = refs[at : at + n_out]
        at += n_out
        known = (None,) * 3 + tuple(arrays) + (None,)
        ends = refs[at : at + 2]
        at += 2
        shares = Shares(
            place, units, PIECE, known, staging, carried, fins, got, refs[at : at + 7],
            refs[at + 7 : at + 10], ends,
        )
        at += 10
        thirds = Shares(
            place, tail, PIECE // 3, known, staging, carried, fins, got, refs[at : at + 7],
            refs[at + 7 : at + 10], ends,
        )
        at += 10
        done = on_the_way(units + tail, n_out)
        total = Total(place, pack_ref, small_out, refs[at : at + 5], refs[at + 5 : at + 7])

    def inputs():
        return (
            pltpu.make_async_copy(h1_ref, h1_buf, in_sem.at[0]),
            pltpu.make_async_copy(x_ref, x_buf, in_sem.at[1]),
            pltpu.make_async_copy(gr1_ref, gr1_buf, in_sem.at[2]),
            pltpu.make_async_copy(w_ref, w_buf, in_sem.at[3]),
        )

    @pl.when((hp == 0) & (s_id == 0))
    def _():
        for copy in inputs():
            copy.start()
        hist_ref[...] = jnp.zeros_like(hist_ref)
        if comm:
            meet(place.peers())
            shares.begin(window)

    @pl.when(hp == 0)
    def _():
        bc = boxc_ref[...]
        ax, _ = key_side(bc[:, 0:1], bc[:, 2:3], half)
        ay, _ = key_side(bc[:, 1:2], bc[:, 3:4], half)
        _, fbx = query_side(bc[:, 0:1], bc[:, 2:3], half)
        _, fby = query_side(bc[:, 1:2], bc[:, 3:4], half)
        spot = (lane % quarter).astype(F32)
        is_x = (lane % half) < quarter
        oha = jnp.where(jnp.where(is_x, ax, ay) == spot, jnp.where(low, 1.0, 0.0), 0.0)
        oha_ref[s_id] = oha.astype(BF)
        br = boxr_ref[...]
        _, gax = key_side(br[0:1], br[2:3], half)
        _, gay = key_side(br[1:2], br[3:4], half)
        rbx, _ = query_side(br[0:1], br[2:3], half)
        rby, _ = query_side(br[1:2], br[3:4], half)
        row = lax.broadcasted_iota(jnp.int32, (half, length), 0)
        rspot = (row % quarter).astype(F32)
        ohbt_ref[s_id] = jnp.where(jnp.where(row < quarter, rbx, rby) == rspot, 1.0, 0.0).astype(BF)
        cx_ref[s_id] = jnp.where(gax + fbx >= SPAN, 1.0, 0.0).astype(BF)
        cy_ref[s_id] = jnp.where(gay + fby >= SPAN, 1.0, 0.0).astype(BF)

    @pl.when((hp == 0) & (s_id == n_seq - 1))
    def _():
        inputs()[0].wait()
        turn(h1_buf, h1t_ref)

    k = k_ref[...]
    v = v_ref[...]
    lt_ref[...] = q_ref[...].astype(F32).T.astype(BF)
    gc = gctx_ref[...].astype(F32) * linv_ref[...]
    gcb = gc.astype(BF)
    gt_ref[...] = gcb.astype(F32).T.astype(BF)
    prod = gc * ctx_ref[...].astype(F32)
    ohbt = ohbt_ref[s_id]
    kts = []
    vts = []
    rows = 256
    n_step = n_pair * n_seq
    step = hp * n_seq + s_id
    for a in range(2):
        if comm and a == 1:
            by_step(step, 0, n_step, lambda n: shares.tick(2 * n, window, done))
        mine = low if a == 0 else jnp.logical_not(low)
        other = 64 - 64 * a
        d = jnp.sum(jnp.where(mine, prod, 0.0), axis=1, keepdims=True)
        dhi = d.astype(BF).astype(F32)
        extra = jnp.where(lane == other, dhi, jnp.where(lane == other + 1, d - dhi, 0.0))
        lhs = jnp.where(mine, gcb.astype(F32), extra).astype(BF)
        minus = jnp.where((lane == other) | (lane == other + 1), -1.0, 0.0).astype(BF)
        rhs = jnp.where(mine, v, minus)
        for c in range(length // rows):
            sl = slice(c * rows, (c + 1) * rows)
            gp = dot(lhs[sl], rhs, NT)
            g = (gp * e_ref[a, sl, :].astype(F32)).astype(BF)
            g_ref[a, sl, :] = g
            gcx_ref[a, sl, :] = g * cx_ref[s_id, sl, :]
            gcy_ref[a, sl, :] = g * cy_ref[s_id, sl, :]
        left = jnp.concatenate([lt_ref[64 * a : 64 * a + 64, :], ohbt], axis=0)
        r0 = dot(left, g_ref[a])
        rx = dot(ohbt[:quarter], gcx_ref[a])
        ry = dot(ohbt[quarter:], gcy_ref[a])
        vts.append(dot(gt_ref[64 * a : 64 * a + 64, :], e_ref[a]))
        kts.append(r0[:64])
        w = jnp.concatenate([r0[64:], rx, ry], axis=0)
        whi, wlo = hi_lo(w)
        red = dot(jnp.concatenate([whi, wlo], axis=0), oha_ref[s_id])
        hist_ref[2 * hp + a] += red[:128] + red[128:]
    zero = jnp.zeros_like(k)
    gq = dot(g_ref[0], jnp.where(low, k, zero)) + dot(g_ref[1], jnp.where(low, zero, k))
    own_rows = pl.ds(pl.multiple_of(s_id * length, length), length)
    feats = h1_buf.shape[1]
    parts = [pl.ds(pl.multiple_of(p * feats + hp * 128, 128), 128) for p in range(3)]
    gall_ref[own_rows, parts[0]] = (gq * 0.125).astype(BF)
    gall_ref[own_rows, parts[1]] = (jnp.concatenate(kts, axis=0) * 0.125).T.astype(BF)
    gall_ref[own_rows, parts[2]] = jnp.concatenate(vts, axis=0).T.astype(BF)

    @pl.when(s_id == n_seq - 1)
    def _():
        g_pair = jnp.concatenate([gall_ref[:, part] for part in parts], axis=1)
        piece = dot(h1t_ref[...], g_pair).astype(BF)
        if comm:
            staging[lax.div(hp, 2), lax.rem(hp, 2)] = piece.reshape(staging.shape[2:])
        else:
            grad_ref[0] = piece[:, :128]
            grad_ref[1] = piece[:, 128:256]
            grad_ref[2] = piece[:, 256:]

    if comm:
        def beat_of(at_step):
            for part in (shares, thirds):
                for i, unit in enumerate(part.units):
                    source = unit.source or ("", 0)
                    if source[0] == "own" and (2 * source[1] + 2) * n_seq - 1 == at_step:
                        part.start(i, 0)
            if at_step < n_step - 1:
                shares.tick(2 * at_step + 1, window, done)

        by_step(step, 0, n_step, beat_of)

    @pl.when((hp == n_pair - 1) & (s_id == n_seq - 1))
    def _():
        for copy in inputs()[1:]:
            copy.wait()
        gain = gain_ref[...].reshape(1, -1)
        count = x_buf.shape[0]
        chunk = 256
        beat = 2 * n_step - 1
        gain_sum = jnp.zeros((1, feats), F32)
        bias_sum = jnp.zeros((1, feats), F32)
        pack_ref[...] = small_ref[...]
        base = pack_ref.shape[0] - 16
        for h in range(2 * n_pair):
            w = hist_ref[h]
            line = jnp.zeros((1, 128), F32)
            for axis in range(2):
                plain = w[axis * quarter : (axis + 1) * quarter]
                carry = w[half + axis * quarter : half + (axis + 1) * quarter]
                keep = (lane >= axis * quarter) & (lane < (axis + 1) * quarter)
                stay = jnp.where(keep, plain - carry, 0.0)
                move = jnp.where(keep, carry, 0.0)
                shift = axis * (half - quarter)
                stay = pltpu.roll(stay, shift, 1, stride=1, stride_axis=0)
                move = pltpu.roll(move, shift + 1, 1, stride=1, stride_axis=0)
                line = line + jnp.sum(stay + move, axis=0, keepdims=True)
            pack_ref[base + h : base + h + 1, :] = line
        for c in range(count // chunk):
            sl = slice(c * chunk, (c + 1) * chunk)
            g_out = dot(gall_ref[sl, :], w_buf[...], NT)
            g_in, part = norm_back_chunk(g_out, x_buf[sl, :].astype(F32), gain)
            gx_ref[sl, :] = gr1_buf[sl, :] + g_in
            gain_sum = gain_sum + part
            bias_sum = bias_sum + jnp.sum(g_out, axis=0, keepdims=True)
            if comm:
                for t in range(beat, beat + 2):
                    shares.tick(t, window, done)
                    thirds.tick(t, window, done)
                beat += 2
        lines = feats // 128
        put_lines(pack_ref, 0, gain_sum)
        put_lines(pack_ref, lines, bias_sum)
        if comm:
            total.start(0)
            stage = 0
            for t in range(beat, max(shares.ticks(), thirds.ticks())):
                shares.tick(t, window, done)
                thirds.tick(t, window, done)
                if t in SUM_BEATS:
                    total.finish(stage)
                    if stage < 3:
                        total.start(stage + 1)
                    stage += 1
            for stage in range(stage, 4):
                total.finish(stage)
                if stage < 3:
                    total.start(stage + 1)
            for n, out in enumerate(outs):
                shares.deliver(n, out, spans[n])
            thirds.wait_sends()
            total.wait_sends()
            shares.wait_sends()
        else:
            small_out[...] = pack_ref[...]


SUM_BEATS = (34, 38, 43, 47)


def late_units():
    rest = (
        {'in': 2, 3: 6},
        {'in': 0, 3: 4},
        {'in': 0, 2: 4, 3: 8},
        {'in': 0, 2: 4, 3: 10},
        {'in': 2, 2: 6, 3: 12},
        {'in': 2, 2: 6, 3: 14},
    )
    units = [
        Unit(
            unit.array, unit.part, 0, unit.rows_first, beats, source=("mid",) + unit.leave
        )
        for unit, beats in zip(early_units(), rest)
    ]
    units += [
        Unit(4, 0, 0, True, {0: 4, 1: 10, 2: 16, 3: 20}),
        Unit(4, 0, 1, False, {0: 4, 1: 10, 2: 16, 3: 22}),
        Unit(3, 0, 0, True, {0: 8, 1: 14, 2: 22, 3: 25}),
        Unit(4, 0, 2, False, {0: 8, 1: 14, 2: 18, 3: 23}),
        Unit(4, 0, 3, True, {0: 16, 1: 22, 2: 25, 3: 31}),
        Unit(5, 0, 0, False, {0: 11, 1: 20, 2: 27, 3: 36}, source=("own", 0, 0)),
        Unit(5, 0, 1, True, {0: 19, 1: 25, 2: 32, 3: 41}, source=("own", 1, 0)),
    ]
    tail = (
        Unit(5, 0, 6, False, {0: 26, 1: 35, 2: 39, 3: 44}, source=("own", 2, 0 * PIECE // 3)),
        Unit(5, 0, 7, False, {0: 27, 1: 37, 2: 42, 3: 46}, source=("own", 2, 1 * PIECE // 3)),
        Unit(5, 0, 8, True, {0: 27, 1: 33, 2: 40, 3: 45}, source=("own", 2, 2 * PIECE // 3)),
    )
    return tuple(units), tail


def attend_and_project_backward(
    qkv, e, linv, ctx, gctx, boxes_r, boxes_c, weight, h1, tokens, g_r1, gain, small, arrays,
    carried, n_rows, comm
):
    count, width = qkv.shape
    feats = width // 3
    heads, seqs, length, _ = e.shape
    pairs = heads // 2
    rows_of = lambda off: pl.BlockSpec((length, 128), lambda h, s: (s, off + h))
    any_ref = pl.BlockSpec(memory_space=pl.ANY)
    vm = pl.BlockSpec(memory_space=pltpu.VMEM)
    views = [view(g, n_rows) for g in arrays] if comm else []
    n_ext = len(views)
    units, tail = late_units() if comm else ((), ())
    out_shape = [jax.ShapeDtypeStruct((count, feats), F32), jax.ShapeDtypeStruct(small.shape, F32)]
    out_specs = [vm, vm]
    spans = []
    scratch = [
        pltpu.VMEM((seqs, length, 128), BF), pltpu.VMEM((seqs, 64, length), BF),
        pltpu.VMEM((seqs, length, length), BF), pltpu.VMEM((seqs, length, length), BF),
        pltpu.VMEM((2, length, length), BF), pltpu.VMEM((2, length, length), BF),
        pltpu.VMEM((2, length, length), BF), pltpu.VMEM((128, length), BF),
        pltpu.VMEM((128, length), BF), pltpu.VMEM((count, width), BF), pltpu.VMEM((feats, count), BF),
        pltpu.VMEM((heads, 128, 128), F32), pltpu.VMEM((count, feats), BF),
        pltpu.VMEM((count, feats), BF), pltpu.VMEM((count, feats), F32), pltpu.VMEM((feats, width), BF),
        pltpu.VMEM(small.shape, F32), pltpu.SemaphoreType.DMA((4,)),
    ]
    params = dict(vmem_limit_bytes=63 << 20, dimension_semantics=("arbitrary", "arbitrary"))
    if comm:
        hidden = views[-1].shape[5]
        sizes = [(24, feats), (24, feats), (24 * hidden // feats, feats), (24, feats), (24, hidden), (24, width)]
        for rows, x in sizes[:-1]:
            spans.append([(j * 2 * PIECE, PIECE, PIECE) for j in range(x // (2 * PIECE))])
        spans.append(
            [(p * feats + t * 256, 128, 128) for t in range(pairs // 2) for p in range(3)]
        )
        out_shape += [jax.ShapeDtypeStruct(size, F32) for size in sizes]
        out_specs += [vm] * len(sizes)
        tbufs, tsems = Total.scratch(small.shape, n_rows)
        scratch += [pltpu.VMEM((pairs // 2, 2, n_rows, 4, 2, 48, PIECE), BF)]
        scratch += Shares.result_scratch(sizes) + Shares.scratch(units, PIECE, n_rows)
        scratch += Shares.scratch(tail, PIECE // 3, n_rows) + tbufs + tsems
        params.update(collective_id=2, has_side_effects=True)
    else:
        out_shape.append(jax.ShapeDtypeStruct((3, feats, feats), BF))
        out_specs.append(pl.BlockSpec((3, feats, 128), lambda h, s: (0, 0, h)))
    results = pl.pallas_call(
        functools.partial(
            back_kernel, n_ext=n_ext, units=units, tail=tail, spans=spans, n_rows=n_rows, comm=comm, window=3,
        ),
        grid=(pairs, seqs),
        in_specs=[
            rows_of(0), rows_of(pairs), rows_of(2 * pairs),
            pl.BlockSpec((2, None, length, length), lambda h, s: (h, s, 0, 0)),
            rows_of(0), rows_of(0), rows_of(0),
            pl.BlockSpec((4, length), lambda h, s: (0, s)),
            pl.BlockSpec((length, 128), lambda h, s: (s, 0)),
            any_ref, any_ref, any_ref, any_ref, vm, vm,
        ] + [any_ref] * (n_ext + len(carried)),
        out_specs=out_specs,
        out_shape=out_shape,
        scratch_shapes=scratch,
        compiler_params=pltpu.CompilerParams(**params),
        name="attend_backward",
    )(
        qkv, qkv, qkv, e, linv, ctx, gctx, boxes_r, boxes_c, weight, h1, tokens, g_r1,
        gain, small, *views, *carried,
    )
    return results


EPSILON = 1e-05


def norm_stats(rows):
    average = jnp.mean(rows, axis=-1, keepdims=True)
    centred = rows - average
    variance = jnp.mean(centred * centred, axis=-1, keepdims=True)
    return average, lax.rsqrt(variance + EPSILON)


def gelu_pair(u):
    bell = jnp.exp2(u * u * (-0.5 * LOG2E))
    below = 0.5 + 0.5 * lax.erf(u * math.sqrt(0.5))
    return u * below, below + u * bell * (1.0 / math.sqrt(2.0 * math.pi))


def body(
    tokens, boxes, page_ids, seg_ids, pair_mask, ln1_gain, ln1_bias, query_key_value_weight,
    attention_output_weight, ln2_gain, ln2_bias, up_projection_weight, up_projection_bias,
    down_projection_weight, box_table, rel_left, rel_right, cot_out, cot_logits,
):
    features = tokens.shape[1]
    h1, qkv, boxes_c = project_forward(
        tokens, ln1_gain, ln1_bias, query_key_value_weight, boxes, page_ids
    )
    pair_scale = 1.0 / math.sqrt(rel_left.shape[1])
    ctx, e, linv, row_panel, col_panel = attend_forward(
        qkv, boxes, boxes_c, page_ids.shape[0], box_table, pair_mask[0], cot_logits[0], pair_scale
    )
    r1, h2, act, slope, layer_out, embedded = mlp_forward(
        ctx, attention_output_weight, tokens, ln2_gain, ln2_bias, up_projection_weight,
        up_projection_bias, down_projection_weight, seg_ids, SLOTS,
    )
    pair_logits, grad_rel_left, grad_rel_right, g_y, g_mlp = pair_head(
        embedded, rel_left, rel_right, row_panel, col_panel, pair_mask[0], cot_out, seg_ids, pair_scale
    )
    grad_down = dot(act, g_mlp, (((0,), (0,)), ((), ()))).astype(BF)
    n_rows = lax.axis_size("rows")
    comm = n_rows * 8 * 48 <= features
    heads = box_table.shape[0]
    hidden = slope.shape[1]
    small_rows = (4 * features + hidden) // 128 + 16
    grad_up, g_r1, grad_out, g_ctx, small, *early = mlp_backward(
        slope, down_projection_weight, up_projection_weight, g_mlp, h2, r1, g_y, ctx,
        attention_output_weight, ln2_gain, small_rows, grad_rel_left, grad_rel_right, grad_down,
        n_rows, comm,
    )
    g_tokens, small, *late = attend_and_project_backward(
        qkv, e, linv, ctx, g_ctx, boxes, boxes_c, query_key_value_weight, h1, tokens, g_r1, ln1_gain,
        small, (grad_out, grad_up), early, n_rows, comm,
    )
    if comm:
        left, right, down, out, up, qkv_part = late
        shares = [[left], [right], [out], [down], [up], [qkv_part]]
    else:
        grad_qkv = jnp.concatenate([late[0][0], late[0][1], late[0][2]], axis=1)
        flats = [
            lax.psum_scatter(g, AXES, scatter_dimension=0, tiled=True).astype(F32).reshape(-1)
            for g in (grad_rel_left, grad_rel_right, grad_out, grad_down, grad_up, grad_qkv)
        ]
        shares = [[flat.reshape(-1, 128)] for flat in flats]
        small = lax.psum(small, AXES)
    grad_tokens, flats, vectors = deliver(g_tokens, small, shares, features, hidden, heads)
    left_share, right_share, out_share, down_share, up_share, qkv_share = flats
    return (
        layer_out, pair_logits[None], grad_tokens, vectors[0], vectors[1], qkv_share, out_share,
        vectors[2], vectors[3], up_share, vectors[4], down_share, vectors[5], left_share, right_share,
    )


def solution(mesh):
    whole = P(AXES, None)
    tile = P("rows", "gr", "gc")
    flat = P(AXES)
    one = P()
    in_specs = (
        whole, P(None, AXES), whole, whole, tile, one, one, one, one, one, one, one, one, one, one,
        one, one, whole, tile,
    )
    out_specs = (
        whole, tile, whole, one, one, flat, flat, one, one, flat, one, flat, one, flat, flat,
    )
    return jax.shard_map(body, mesh=mesh, in_specs=in_specs, out_specs=out_specs, check_vma=False)
```

```python
import functools
import math

import jax
import jax.numpy as jnp
from jax import lax
from jax.experimental import pallas as pl
from jax.experimental.pallas import tpu as pltpu
from jax.sharding import PartitionSpec as P

COORD=1000
SPAN=2*COORD+1
LOG2E=1.4426950408889634
BARRED=-2.0**99
SLOTS=64
BF=jnp.bfloat16
F32=jnp.float32
NT=(((1,),(1,)),((),()))
NN=(((1,),(0,)),((),()))
def dot(a,b,dims=NN):
    return lax.dot_general(a,b,dims,preferred_element_type=F32)

def whole_and_rest(scaled):
    whole=jnp.floor((scaled+0.5)*(1.0/SPAN))
    return whole, scaled-SPAN*whole

def key_side(low, high, half):
    c=jnp.floor((low+high).astype(F32)*0.5)
    return whole_and_rest(c*half)
def query_side(low, high, half):
    c=jnp.floor((low+high).astype(F32)*0.5)
    return whole_and_rest((COORD-c)*half)

def hi_lo(v):
    hi=v.astype(BF)
    return hi, (v-hi.astype(F32)).astype(BF)

def fwd_kernel(q_ref,k_ref,v_ref,boxr_ref,boxc_ref,tab_ref,mask_ref,cot_ref,
               ctx_ref,e_ref,linv_ref,rowp_ref,colp_ref,
               ohb_ref,oha_ref,kg_ref,rxy_ref,pg_ref,cx_ref,cy_ref,*panel_refs,rows,pair_scale):
    length=q_ref.shape[0]
    half=tab_ref.shape[1]//2
    quarter=half//2
    hp=pl.program_id(1)
    seq=pl.program_id(0)
    place=Place(1)
    mask_buf,cot_buf,in_sem=panel_refs[:3]
    panels=Panels(place,*panel_refs[3:7],panel_refs[7:])
    def inputs():
        return (pltpu.make_async_copy(mask_ref,mask_buf,in_sem.at[0]),
                pltpu.make_async_copy(cot_ref,cot_buf,in_sem.at[1]))
    @pl.when((hp==0)&(seq==0))
    def _():
        for copy in inputs():
            copy.start()
    @pl.when((hp==1)&(seq==0))
    def _():
        for copy in inputs():
            copy.wait()
        panels.fill(mask_buf,cot_buf,pair_scale)
        meet([place.gc_peer(d) for d in (1,2,3)]+[place.gr_peer(d) for d in (1,2,3)])
    @pl.when((hp==2)&(seq==0))
    def _():
        panels.start()
    lane=lax.broadcasted_iota(jnp.int32,(1,128),1)
    low=lane<64
    @pl.when(hp==0)
    def _():
        bc=boxc_ref[...]
        ax,fax=key_side(bc[:,0:1],bc[:,2:3],half)
        ay,fay=key_side(bc[:,1:2],bc[:,3:4],half)
        bx,fbx=query_side(bc[:,0:1],bc[:,2:3],half)
        by,fby=query_side(bc[:,1:2],bc[:,3:4],half)
        spot=(lane%quarter).astype(F32)
        is_x=(lane%half)<quarter
        oha=jnp.where(jnp.where(is_x,ax,ay)==spot,1.0,0.0)
        ohb=jnp.where(jnp.where(is_x,bx,by)==(quarter-1)-spot,1.0,0.0)
        ohb_ref[...]=jnp.where(low,ohb,0.0).astype(BF)
        oha_ref[...]=oha.astype(BF)
        page=bc[:,4:5].astype(jnp.int32)
        mine=(lane%64)==page
        barred=jnp.where((lane%64)<4,jnp.where(mine,0.0,BARRED),0.0)
        kg_ref[0]=jnp.where(low,oha,barred).astype(BF)
        kg_ref[1]=jnp.where(low,barred,oha).astype(BF)
        pg_ref[...]=jnp.where(mine,1.0,0.0).astype(BF)
        ohx=jnp.where(ax==spot,1.0,0.0)
        ohy=jnp.where(ay==spot,1.0,0.0)
        rxy_ref[pl.ds(0,length),:]=jnp.where(low,ohx,0.0).astype(BF)
        rxy_ref[pl.ds(length,length),:]=jnp.where(low,0.0,ohy).astype(BF)
        br=boxr_ref[...]
        _,gax=key_side(br[0:1],br[2:3],half)
        _,gay=key_side(br[1:2],br[3:4],half)
        cx_ref[...]=jnp.where(gax+fbx>=SPAN,1.0,0.0)
        cy_ref[...]=jnp.where(gay+fby>=SPAN,1.0,0.0)
    k=k_ref[...]
    v=v_ref[...]
    oha=oha_ref[...]
    b_row=lax.broadcasted_iota(jnp.int32,(half,128),0)
    l_col=lax.broadcasted_iota(jnp.int32,(half,128),1)
    row_x=b_row<quarter
    same_axis=row_x==((l_col%half)<quarter)
    d_axis=row_x==(l_col<half)
    heads=[]
    for a in range(2):
        t=tab_ref[pl.ds(2*hp+a,1),:]
        both=[jnp.where(low,t,0.0)+pltpu.roll(jnp.where(low,t,0.0),64,1),
              jnp.where(low,0.0,t)+pltpu.roll(jnp.where(low,0.0,t),64,1)]
        tiles=[]
        for b in both:
            spreads=[]
            for first in (0,1):
                whole=jnp.broadcast_to(b,(quarter,128))
                turned=pltpu.roll(whole,128-(quarter-1)-first,1,stride=1,stride_axis=0)
                lowq=jnp.where(lane<quarter,turned,0.0)
                pair=lowq+pltpu.roll(lowq,quarter,1)
                spreads.append(pair+pltpu.roll(pair,64,1))
            tiles.append(spreads)
        base=jnp.concatenate([tiles[0][0],tiles[1][0]],axis=0)
        nxt=jnp.concatenate([tiles[0][1],tiles[1][1]],axis=0)
        hi,lo=hi_lo(base)
        dhi,dlo=hi_lo(nxt-base)
        z=jnp.zeros_like(hi)
        is_hi=(l_col<64)==(a==1)
        g0=jnp.where(same_axis,jnp.where(is_hi,hi.astype(F32),lo.astype(F32)),0.0).astype(BF)
        g1=jnp.where(d_axis,jnp.where((l_col%half)<quarter,dhi.astype(F32),dlo.astype(F32)),0.0).astype(BF)
        hk=jnp.concatenate([g0,g1],axis=1)
        left=dot(ohb_ref[:,0:half],hk).astype(BF)
        if a==0:
            rhs=jnp.concatenate([jnp.where(low,k,oha),kg_ref[0]],axis=1)
            vv=jnp.where(low,v,jnp.ones_like(v))
        else:
            rhs=jnp.concatenate([jnp.where(low,oha,k),kg_ref[1]],axis=1)
            vv=jnp.where(low,jnp.ones_like(v),v)
        heads.append((left,rhs,vv))
    for c in range(length//rows):
        sl=pl.ds(c*rows,rows)
        q=q_ref[sl,:]*jnp.asarray(0.125,BF)
        pg=pg_ref[sl,:]
        outs=[]
        for a in range(2):
            left,rhs,vv=heads[a]
            lc=left[c*rows:(c+1)*rows]
            g0=lc[:,:128]
            if a==0:
                lhs=jnp.concatenate([jnp.where(low,q,g0),jnp.where(low,g0,pg)],axis=1)
            else:
                lhs=jnp.concatenate([jnp.where(low,g0,q),jnp.where(low,pg,g0)],axis=1)
            s=dot(lhs,rhs,NT)
            s=s+cx_ref[sl,:]*dot(lc[:,128:],rxy_ref[pl.ds(0,length),:],NT)
            s=s+cy_ref[sl,:]*dot(lc[:,128:],rxy_ref[pl.ds(length,length),:],NT)
            m=jnp.max(s,axis=1,keepdims=True)
            e=jnp.exp2((s-m)*LOG2E).astype(BF)
            e_ref[a,sl,:]=e
            outs.append(dot(e,vv))
        ctx=jnp.where(low,outs[0],outs[1])
        tot=jnp.where(low,pltpu.roll(outs[0],64,1),pltpu.roll(outs[1],64,1))
        linv=1.0/tot
        linv_ref[sl,:]=linv
        ctx_ref[sl,:]=(ctx*linv).astype(BF)
    @pl.when((hp==pl.num_programs(1)-1)&(seq==pl.num_programs(0)-1))
    def _():
        panels.collect(rowp_ref,colp_ref)

def attend_forward(qkv,boxes_r,boxes_c,seqs,table,mask,cot,pair_scale,rows=512):
    tokens,width=qkv.shape
    feats=width//3
    length=tokens//seqs
    heads=table.shape[0]
    pairs=heads//2
    return pl.pallas_call(
        functools.partial(fwd_kernel,rows=rows,pair_scale=pair_scale),
        grid=(seqs,pairs),
        in_specs=[
            pl.BlockSpec((length,128),lambda s,h:(s,h)),
            pl.BlockSpec((length,128),lambda s,h:(s,pairs+h)),
            pl.BlockSpec((length,128),lambda s,h:(s,2*pairs+h)),
            pl.BlockSpec((4,length),lambda s,h:(0,s)),
            pl.BlockSpec((length,128),lambda s,h:(s,0)),
            pl.BlockSpec(table.shape,lambda s,h:(0,0)),
            pl.BlockSpec(memory_space=pl.ANY),
            pl.BlockSpec(memory_space=pl.ANY),
        ],
        out_specs=[
            pl.BlockSpec((length,128),lambda s,h:(s,h)),
            pl.BlockSpec((2,None,length,length),lambda s,h:(h,s,0,0)),
            pl.BlockSpec((length,128),lambda s,h:(s,h)),
            pl.BlockSpec(memory_space=pltpu.VMEM),
            pl.BlockSpec(memory_space=pltpu.VMEM),
        ],
        out_shape=[jax.ShapeDtypeStruct((tokens,feats),BF),
                   jax.ShapeDtypeStruct((heads,seqs,length,length),BF),
                   jax.ShapeDtypeStruct((tokens,feats),F32)]
                  +[jax.ShapeDtypeStruct((4,mask.shape[0]//4,mask.shape[0]),BF)]*2,
        scratch_shapes=[pltpu.VMEM((length,128),BF),pltpu.VMEM((length,128),BF),
                        pltpu.VMEM((2,length,128),BF),pltpu.VMEM((2*length,128),BF),
                        pltpu.VMEM((length,128),BF),
                        pltpu.VMEM((length,length),F32),pltpu.VMEM((length,length),F32)]
                       +[pltpu.VMEM(mask.shape,jnp.int32),pltpu.VMEM(cot.shape,BF),pltpu.SemaphoreType.DMA((2,))]
                       +Panels.scratch(mask.shape[0]),
        compiler_params=pltpu.CompilerParams(collective_id=4,has_side_effects=True,vmem_limit_bytes=60<<20),
        name="attend_forward",
    )(qkv,qkv,qkv,boxes_r,boxes_c,table,mask,cot)


AXES = ("rows", "gr", "gc")
MESH = pl.DeviceIdType.MESH
PIECE = 384


class Place:
    def __init__(self, n_rows):
        self.n_rows = n_rows
        self.r = lax.axis_index("rows")
        self.g = lax.axis_index("gr")
        self.c = lax.axis_index("gc")
        self.core = lax.rem(self.c, 2)
        self.u = lax.div(self.c, 2)
        self.sibling = {"gc": self.u * 2 + 1 - self.core}
        self.across = {"gc": (1 - self.u) * 2 + self.core}

    def row_peer(self, d):
        return {"rows": lax.rem(self.r + d, self.n_rows)}

    def gr_peer(self, d):
        return {"gr": lax.rem(self.g + d, 4)}

    def gc_peer(self, d):
        return {"gc": lax.rem(self.c + d, 4)}

    def peers(self):
        return (
            [self.sibling, self.across]
            + [self.row_peer(d) for d in range(1, self.n_rows)]
            + [self.gr_peer(d) for d in range(1, 4)]
        )


def meet(peers):
    barrier = pltpu.get_barrier_semaphore()
    for peer in peers:
        pl.semaphore_signal(barrier, inc=1, device_id=peer, device_id_type=MESH)
    pl.semaphore_wait(barrier, len(peers))


def send(src, dst, send_sem, recv_sem, peer):
    return pltpu.make_async_remote_copy(
        src_ref=src, dst_ref=dst, send_sem=send_sem, recv_sem=recv_sem, device_id=peer,
        device_id_type=MESH,
    )


def by_step(step, first, end, action):
    if end - first == 1:
        action(first)
        return
    middle = (first + end) // 2
    pl.when(step < middle)(lambda: by_step(step, first, middle, action))
    pl.when(step >= middle)(lambda: by_step(step, middle, end, action))


class Unit:
    def __init__(self, array, part, block, rows_first, beats, source=None, leave=None):
        self.array, self.part, self.block = array, part, block
        self.rows_first, self.beats, self.source, self.leave = rows_first, beats, source, leave
        self.stages = sorted(stage for stage in beats if stage != "in")
        self.fresh = self.stages[0] == 0

    def does(self, stage):
        return stage in self.beats


class Shares:
    def __init__(self, place, units, piece, arrays, staging, carried, fins, got, bufs, sems, ends):
        self.p = place
        self.units = units
        self.piece = piece
        self.arrays = arrays
        self.staging = staging
        self.carried = carried
        self.fin = fins
        self.got = got
        self.own, self.b0, self.b1r, self.b1u, self.b2r, self.b2u, self.b3 = bufs
        self.ls, self.ss, self.rs = sems
        self.fs, self.fr = ends
        external = [i for i, unit in enumerate(units) if unit.source is None]
        self.external = sorted(external, key=lambda i: units[i].beats[0])

    def number(self, i, test):
        return sum(test(unit) for unit in self.units[:i])

    @staticmethod
    def kinds():
        return (
            lambda unit: True,
            lambda unit: unit.does(0),
            lambda unit: unit.does(1) and unit.rows_first,
            lambda unit: unit.does(1) and not unit.rows_first,
            lambda unit: unit.does(2) and not unit.rows_first,
            lambda unit: unit.does(2) and unit.rows_first,
            lambda unit: unit.does(3),
        )

    @staticmethod
    def scratch(units, piece, n_rows):
        n, m, r = len(units), 48, n_rows
        shapes = (
            (r, 4, 2, m), (r, 4, 2, m), (r - 1, 4, 2, m), (r, 4, m), (r - 1, 4, m), (4, m), (3, m),
        )
        bufs = [
            pltpu.VMEM((max(1, sum(map(test, units))),) + shape + (piece,), BF)
            for test, shape in zip(Shares.kinds(), shapes)
        ]
        dma = pltpu.SemaphoreType.DMA
        return bufs + [dma((n,)), dma((n, r + 4)), dma((n, r + 4))]

    @staticmethod
    def result_scratch(sizes):
        dma = pltpu.SemaphoreType.DMA
        k = len(sizes)
        fins = [pltpu.VMEM((2, rows, x // 2), F32) for rows, x in sizes]
        got = [pltpu.VMEM((rows, x // 2), F32) for rows, x in sizes]
        return fins + got + [dma((k,)), dma((k,))]

    def buffer(self, kind, i):
        bufs = (self.own, self.b0, self.b1r, self.b1u, self.b2r, self.b2u, self.b3)
        return bufs[kind].at[self.number(i, self.kinds()[kind])]

    def piece_of(self, i, core):
        unit = self.units[i]
        if unit.source is None:
            at = unit.block * 2 * self.piece + core * self.piece
            columns = pl.ds(pl.multiple_of(at, 128), self.piece)
            return self.arrays[unit.array].at[:, :, :, unit.part, :, columns]
        _, n, column = unit.source
        return self.staging.at[n, core, :, :, :, :, column : column + self.piece]

    def swap(self, i):
        src = self.piece_of(i, 1 - self.p.core)
        return send(src, self.buffer(1, i), self.ss.at[i, 0], self.rs.at[i, 0], self.p.sibling)

    def keep(self, i):
        unit, p = self.units[i], self.p
        if unit.source is None:
            src, to = self.piece_of(i, p.core), self.own.at[i]
        else:
            src = self.carried[unit.source[1]].at[unit.source[2]]
            if unit.does(2):
                to = self.own.at[i, p.r] if unit.rows_first else self.own.at[i, :, :, p.u]
            else:
                to = self.own.at[i, p.r, :, p.u]
        return pltpu.make_async_copy(src, to, self.ls.at[i])

    def along_rows(self, i, first):
        p = self.p
        out = []
        for d in range(1, p.n_rows):
            to = lax.rem(p.r + d, p.n_rows)
            src = self.own.at[i, to] if first else self.own.at[i, to, :, p.u]
            dst = self.buffer(2 if first else 4, i).at[d - 1]
            out.append(send(src, dst, self.ss.at[i, 1 + d], self.rs.at[i, 1 + d], p.row_peer(d)))
        return out

    def across(self, i, first):
        p = self.p
        src = self.own.at[i, :, :, 1 - p.u] if first else self.own.at[i, p.r, :, 1 - p.u]
        dst = self.buffer(3 if first else 5, i)
        return [send(src, dst, self.ss.at[i, 1], self.rs.at[i, 1], p.across)]

    def along_gr(self, i):
        p = self.p
        out = []
        for d in range(1, 4):
            src = self.own.at[i, p.r, lax.rem(p.g + d, 4), p.u]
            at = p.n_rows + d
            dst = self.buffer(6, i).at[d - 1]
            out.append(send(src, dst, self.ss.at[i, at], self.rs.at[i, at], p.gr_peer(d)))
        return out

    def copies(self, i, stage):
        if stage == 0:
            return [self.swap(i)]
        if stage == 3:
            return self.along_gr(i)
        if self.units[i].rows_first == (stage == 1):
            return self.along_rows(i, stage == 1)
        return self.across(i, stage == 1)

    def start(self, i, stage):
        if stage == 0 and self.units[i].source is None:
            self.keep(i).start()
        for copy in self.copies(i, stage):
            copy.start()

    def finish(self, i, stage):
        p, unit = self.p, self.units[i]
        if stage == 0 and unit.source is None:
            self.keep(i).wait()
        for copy in self.copies(i, stage):
            copy.wait_recv()
        if stage == 0:
            to = self.own.at[i]
            mine = to if unit.source is None else self.piece_of(i, p.core)
            theirs = self.buffer(1, i)

            @pl.loop(0, 4)
            def _(n):
                to[:, n] = mine[:, n] + theirs[:, n]

            return
        if stage == 3:
            total = self.own[i, p.r, p.g, p.u].astype(F32)
            for d in range(3):
                total = total + self.buffer(6, i)[d].astype(F32)
            m = total.shape[0]
            fin = self.fin[unit.array]
            rows = fin.shape[1]
            span = slice(unit.block * self.piece, (unit.block + 1) * self.piece)
            if rows < m:
                fin[0, :, span] = total[:rows]
                fin[1, :, span] = total[rows:]
            else:
                per = rows // m
                row = (unit.part % per) * m
                fin[unit.part // per, row : row + m, span] = total
            return
        if stage == 2:
            to = self.own.at[i, p.r, :, p.u]
        else:
            to = self.own.at[i, p.r] if unit.rows_first else self.own.at[i, :, :, p.u]
        if unit.rows_first == (stage == 1):
            terms = [self.buffer(2 if stage == 1 else 4, i).at[d] for d in range(p.n_rows - 1)]
        else:
            terms = [self.buffer(3 if stage == 1 else 5, i)]
        out = to
        if unit.leave is not None and stage == unit.stages[-1]:
            out = self.carried[unit.leave[0]].at[unit.leave[1]]
        if stage == 1:
            @pl.loop(0, 4)
            def _(n):
                at = n if unit.rows_first else (slice(None), n)
                total = to[at]
                for term in terms:
                    total = total + term[at]
                out[at] = total
        else:
            total = to[...]
            for term in terms:
                total = total + term[...]
            out[...] = total

    def last(self, k):
        return send(
            self.fin[k].at[1 - self.p.core], self.got[k], self.fs.at[k], self.fr.at[k],
            self.p.sibling,
        )

    def begin(self, window):
        for i, unit in enumerate(self.units):
            if not unit.fresh:
                self.keep(i).start()
        for i in self.external[:window]:
            self.start(i, 0)

    def tick(self, t, window, done):
        due = []
        for i, unit in enumerate(self.units):
            for stage, beat in unit.beats.items():
                if beat == t:
                    due.append((-1 if stage == "in" else stage, i))
        for stage, i in sorted(due, key=lambda entry: (-entry[0], entry[1])):
            unit = self.units[i]
            if stage < 0:
                self.keep(i).wait()
                self.start(i, unit.stages[0])
                continue
            self.finish(i, stage)
            if stage == 0 and i in self.external:
                later = self.external.index(i) + window
                if later < len(self.external):
                    self.start(self.external[later], 0)
            if stage == 3:
                final, count = done[unit.array]
                if t == final:
                    done[unit.array] = final, count - 1
                    if count == 1:
                        self.last(unit.array).start()
            elif stage < unit.stages[-1]:
                self.start(i, stage + 1)

    def ticks(self):
        return 1 + max(beat for unit in self.units for beat in unit.beats.values())

    def deliver(self, k, out, spans):
        core = self.p.core
        self.last(k).wait()
        for value, owner in ((self.fin[k][core], core), (self.got[k][...], 1 - core)):
            at = 0
            for base, step, width in spans:
                where = pl.ds(pl.multiple_of(base + owner * step, 128), width)
                out[:, where] = value[:, at : at + width]
                at += width

    def wait_sends(self):
        for i, unit in enumerate(self.units):
            for stage in unit.stages:
                for copy in self.copies(i, stage):
                    copy.wait_send()


def on_the_way(units, arrays):
    beats = [[unit.beats[3] for unit in units if unit.array == k and unit.does(3)] for k in range(arrays)]
    return [(max(of), of.count(max(of))) if of else (-1, 0) for of in beats]


class Total:
    def __init__(self, place, source, out, bufs, sems):
        self.p = place
        self.src = source
        self.out = out
        self.part, self.pair, self.high, self.rows, self.quad = bufs
        self.ss, self.rs = sems

    @staticmethod
    def scratch(shape, n_rows):
        dma = pltpu.SemaphoreType.DMA
        bufs = [
            pltpu.VMEM((3,) + shape, F32), pltpu.VMEM(shape, F32), pltpu.VMEM(shape, F32),
            pltpu.VMEM((n_rows,) + shape, F32), pltpu.VMEM((4,) + shape, F32),
        ]
        return bufs, [dma((n_rows + 4,)), dma((n_rows + 4,))]

    def copies(self, stage):
        p = self.p
        if stage == 0:
            return [send(self.src, self.pair, self.ss.at[0], self.rs.at[0], p.sibling)]
        if stage == 1:
            return [send(self.part.at[0], self.high, self.ss.at[1], self.rs.at[1], p.across)]
        if stage == 2:
            return [
                send(
                    self.part.at[1], self.rows.at[p.r], self.ss.at[1 + d], self.rs.at[1 + d],
                    p.row_peer(d),
                )
                for d in range(1, p.n_rows)
            ]
        return [
            send(
                self.part.at[2], self.quad.at[p.g], self.ss.at[p.n_rows + d],
                self.rs.at[p.n_rows + d], p.gr_peer(d),
            )
            for d in range(1, 4)
        ]

    def start(self, stage):
        for copy in self.copies(stage):
            copy.start()

    def finish(self, stage):
        p = self.p
        for copy in self.copies(stage):
            copy.wait_recv()
        if stage == 0:
            self.part[0] = self.src[...] + self.pair[...]
        elif stage == 1:
            self.part[1] = self.part[0] + self.high[...]
        elif stage == 2:
            self.rows[p.r] = self.part[1]
            total = self.rows[0]
            for d in range(1, p.n_rows):
                total = total + self.rows[d]
            self.part[2] = total
        else:
            self.quad[p.g] = self.part[2]
            self.out[...] = (self.quad[0] + self.quad[1]) + (self.quad[2] + self.quad[3])

    def wait_sends(self):
        for stage in range(4):
            for copy in self.copies(stage):
                copy.wait_send()


def view(g, n_rows):
    rows, x = g.shape
    per = rows // (n_rows * 8)
    return g.reshape(n_rows, 4, 2, per // 48, 48, x)


def project_kernel(x_ref, gain_ref, bias_ref, w_ref, box_ref, page_ref, h1_ref, qkv_ref, cols_ref):
    @pl.when(pl.program_id(0) == 0)
    def _():
        chunk = 256
        count = x_ref.shape[0]

        @pl.loop(0, count // chunk)
        def _(c):
            sl = pl.ds(pl.multiple_of(c * chunk, chunk), chunk)
            x = x_ref[sl, :].astype(F32)
            average, inverse = norm_stats(x)
            h1_ref[sl, :] = ((x - average) * inverse * gain_ref[...].reshape(1, -1) + bias_ref[...].reshape(1, -1)).astype(BF)
        pages = jnp.concatenate([page_ref[s : s + 1, :] for s in range(page_ref.shape[0])], axis=1)
        lines = jnp.concatenate(
            [box_ref[...].astype(F32), pages.astype(F32), jnp.zeros((123, count), F32)], axis=0
        )
        cols_ref[...] = lines.T

    qkv_ref[...] = dot(h1_ref[...], w_ref[...]).astype(BF)


def project_forward(tokens, gain, bias, weight, boxes, page_ids):
    count, feats = tokens.shape
    width = weight.shape[1]
    block = feats
    vm = pl.BlockSpec(memory_space=pltpu.VMEM)
    return pl.pallas_call(
        project_kernel,
        grid=(width // block,),
        in_specs=[
            pl.BlockSpec((count, feats), lambda j: (0, 0)), vm, vm,
            pl.BlockSpec((feats, block), lambda j: (0, j)), vm, vm,
        ],
        out_specs=[vm, pl.BlockSpec((count, block), lambda j: (0, j)), vm],
        out_shape=[
            jax.ShapeDtypeStruct((count, feats), BF), jax.ShapeDtypeStruct((count, width), BF),
            jax.ShapeDtypeStruct((count, 128), F32),
        ],
        compiler_params=pltpu.CompilerParams(vmem_limit_bytes=63 << 20),
        name="project_forward",
    )(tokens, gain, bias, weight, boxes, page_ids)


def slot_members(seg_row, slots):
    ids = lax.broadcasted_iota(jnp.int32, (slots, seg_row.shape[1]), 0)
    return jnp.where(ids == seg_row, 1.0, 0.0)


def mlp_forward_kernel(
    ctx_ref, wo_ref, x_ref, gain_ref, bias_ref, wu_ref, bu_ref, wd_ref, seg_ref,
    r1_ref, h2_ref, act_ref, slope_ref, out_ref, emb_ref, acc_ref,
):
    step = pl.program_id(0)
    count = x_ref.shape[0]
    chunk = 512

    @pl.when(step == 0)
    def _():
        @pl.loop(0, count // chunk)
        def _(c):
            sl = pl.ds(pl.multiple_of(c * chunk, chunk), chunk)
            r1 = x_ref[sl, :].astype(F32) + dot(ctx_ref[sl, :], wo_ref[...])
            average, inverse = norm_stats(r1)
            r1_ref[sl, :] = r1
            acc_ref[sl, :] = r1
            h2_ref[sl, :] = ((r1 - average) * inverse * gain_ref[...].reshape(1, -1) + bias_ref[...].reshape(1, -1)).astype(BF)

    for c in range(count // chunk):
        sl = slice(c * chunk, (c + 1) * chunk)
        act, slope = gelu_pair(dot(h2_ref[sl, :], wu_ref[...]) + bu_ref[...])
        act = act.astype(BF)
        act_ref[sl, :] = act
        slope_ref[sl, :] = slope.astype(BF)
        acc_ref[sl, :] += dot(act, wd_ref[...])

    @pl.when(step == pl.num_programs(0) - 1)
    def _():
        out_ref[...] = acc_ref[...].astype(BF)
        seqs, length = seg_ref.shape
        slots = emb_ref.shape[0] // seqs
        for s in range(seqs):
            members = slot_members(seg_ref[s : s + 1, :], slots)
            total = dot(members.astype(BF), out_ref[s * length : (s + 1) * length, :])
            sizes = jnp.sum(members, axis=1, keepdims=True)
            emb_ref[s * slots : (s + 1) * slots, :] = (total / sizes).astype(BF)


def mlp_forward(ctx, w_out, tokens, gain, bias, w_up, b_up, w_down, seg_ids, slots):
    count, feats = tokens.shape
    hidden = w_up.shape[1]
    vm = pl.BlockSpec(memory_space=pltpu.VMEM)
    return pl.pallas_call(
        mlp_forward_kernel,
        grid=(hidden // feats,),
        in_specs=[
            vm, vm, vm, vm, vm, pl.BlockSpec((feats, feats), lambda f: (0, f)),
            pl.BlockSpec((1, feats), lambda f: (0, f)), pl.BlockSpec((feats, feats), lambda f: (f, 0)), vm,
        ],
        out_specs=[
            vm, vm, pl.BlockSpec((count, feats), lambda f: (0, f)),
            pl.BlockSpec((count, feats), lambda f: (0, f)), vm, vm,
        ],
        out_shape=[
            jax.ShapeDtypeStruct((count, feats), F32), jax.ShapeDtypeStruct((count, feats), BF),
            jax.ShapeDtypeStruct((count, hidden), BF), jax.ShapeDtypeStruct((count, hidden), BF),
            jax.ShapeDtypeStruct((count, feats), BF),
            jax.ShapeDtypeStruct((seg_ids.shape[0] * slots, feats), BF),
        ],
        scratch_shapes=[pltpu.VMEM((count, feats), F32)],
        compiler_params=pltpu.CompilerParams(vmem_limit_bytes=50 << 20),
        name="mlp_forward",
    )(
        ctx, w_out, tokens, gain, bias, w_up,
        b_up.reshape(1, hidden), w_down, seg_ids,
    )


class Panels:
    def __init__(self, place, tile, tile_t, rows, cols, sems):
        self.p = place
        self.tile, self.tile_t, self.rows, self.cols = tile, tile_t, rows, cols
        self.ss, self.rs = sems

    @staticmethod
    def scratch(size):
        dma = pltpu.SemaphoreType.DMA
        part = size // 4
        return [
            pltpu.VMEM((4, part, size), BF), pltpu.VMEM((4, part, size), BF),
            pltpu.VMEM((3, part, size), BF), pltpu.VMEM((3, part, size), BF), dma((6,)), dma((6,)),
        ]

    def copies(self):
        p = self.p
        out = []
        for d in range(1, 4):
            for n, (src, dst, peer, at) in enumerate((
                (self.tile, self.rows, p.gc_peer(d), p.c), (self.tile_t, self.cols, p.gr_peer(d), p.g),
            )):
                at_sem = 3 * n + d - 1
                out.append(
                    send(
                        src.at[lax.rem(at + d, 4)], dst.at[d - 1], self.ss.at[at_sem],
                        self.rs.at[at_sem], peer,
                    )
                )
        return out

    def fill(self, mask, cot, scale):
        g_raw = cot[...].astype(F32) * scale * mask[...].astype(F32)
        self.tile[...] = g_raw.astype(BF).reshape(self.tile.shape)
        self.tile_t[...] = g_raw.T.astype(BF).reshape(self.tile_t.shape)

    def start(self):
        for copy in self.copies():
            copy.start()

    def collect(self, row_out, col_out):
        p = self.p
        for copy in self.copies():
            copy.wait()
        row_out[p.c] = self.tile[p.c]
        col_out[p.g] = self.tile_t[p.g]
        for d in range(1, 4):
            row_out[lax.rem(p.c + 4 - d, 4)] = self.rows[d - 1]
            col_out[lax.rem(p.g + 4 - d, 4)] = self.cols[d - 1]


class Spread:
    def __init__(self, place, blocks, sems):
        self.p = place
        self.e = blocks
        self.ss, self.rs = sems
        self.near = lax.rem(place.c + 2, 4)

    @staticmethod
    def scratch(shape):
        dma = pltpu.SemaphoreType.DMA
        return [pltpu.VMEM((4, 4) + shape, BF), dma((4, 4, 3)), dma((4, 4))]

    def hop(self, row, col, kind, peer):
        block = self.e.at[row, col]
        return send(block, block, self.ss.at[row, col, kind], self.rs.at[row, col], peer)

    def own(self, step, waiting):
        p = self.p
        for sign in (1, -1) if step else (0,):
            row = p.g + sign * step
            inside = (row >= 0) & (row <= 3)

            @pl.when(inside)
            def _(row=row, sign=sign):
                if step and not waiting:
                    self.hop(row, p.c, 0, p.sibling).wait_recv()
                go = "wait_send" if waiting else "start"
                getattr(self.hop(row, p.c, 0, p.sibling), go)()
                getattr(self.hop(row, p.c, 1, p.across), go)()
                for way in (1, -1) if step == 0 else (-sign,):
                    to = p.g + way

                    @pl.when((to >= 0) & (to <= 3))
                    def _(to=to, way=way):
                        if step == 0 and way == -1:
                            copy = send(
                                self.e.at[row, p.c], self.e.at[row, p.c], self.down.at[0],
                                self.rs.at[row, p.c], {"gr": to},
                            )
                        else:
                            copy = self.hop(row, p.c, 2, {"gr": to})
                        getattr(copy, go)()

    def relay(self, step, waiting):
        p = self.p
        for sign in (1, -1) if step else (0,):
            row = p.g + sign * step

            @pl.when((row >= 0) & (row <= 3))
            def _(row=row):
                copy = self.hop(row, self.near, 0, p.sibling)
                if waiting:
                    copy.wait_send()
                else:
                    copy.wait_recv()
                    copy.start()

    def arrive(self, rows, cols):
        for row in rows:
            for col in cols:
                self.hop(row, col, 0, self.p.sibling).wait_recv()


def pair_kernel(
    emb_ref, left_ref, right_ref, rowp_ref, colp_ref, mask_ref, cot_ref, seg_ref,
    logits_ref, gleft_ref, gright_ref, gy_ref, gmlp_ref, e_ref, ss, rs, down, *, scale,
):
    place = Place(1)
    meet([place.sibling, place.across] + [place.gr_peer(d) for d in (1, 2, 3)])
    spread = Spread(place, e_ref, (ss, rs))
    spread.down = down
    p = place
    e_ref[p.g, p.c] = emb_ref[...]
    part, width = emb_ref.shape
    spread.own(0, False)
    spread.own(1, False)
    spread.relay(0, False)
    sib = p.u * 2 + 1 - p.core
    far = (1 - p.u) * 2 + 1 - p.core
    spread.arrive([p.g], [sib, far])
    left_rows = dot(e_ref[p.g].reshape(4 * part, width), left_ref[...]).astype(BF)
    spread.own(2, False)
    spread.relay(1, False)
    spread.own(3, False)
    right_cols = dot(e_ref[:, p.c].reshape(4 * part, width), right_ref[...]).astype(BF)
    spread.relay(2, False)
    logits_ref[...] = mask_ref[...].astype(F32) * dot(left_rows, right_cols, NT) * scale
    spread.relay(3, False)
    for d in range(1, 4):
        spread.arrive([lax.rem(p.g + d, 4)], [sib, far])
    row_sum = jnp.zeros((part, width), F32)
    col_sum = jnp.zeros((part, width), F32)
    for n in range(4):
        row_sum = row_sum + dot(rowp_ref[n], e_ref[:, n].reshape(4 * part, width))
        col_sum = col_sum + dot(colp_ref[n], e_ref[n].reshape(4 * part, width))

    def through(total, weight):
        high, low = hi_lo(total)
        return (dot(high, weight) + dot(low, weight)).astype(BF)

    g_left = through(row_sum, right_ref[...])
    g_right = through(col_sum, left_ref[...])
    emb_t = emb_ref[...].astype(F32).T.astype(BF)
    gleft_ref[...] = dot(emb_t, g_left).astype(BF)
    gright_ref[...] = dot(emb_t, g_right).astype(BF)
    g_emb = dot(g_left, left_ref[...], NT) + dot(g_right, right_ref[...], NT)
    seqs, length = seg_ref.shape
    slots = part // seqs
    for n in range(seqs):
        members = slot_members(seg_ref[n : n + 1, :], slots)
        g_seg = g_emb[n * slots : (n + 1) * slots] / jnp.sum(members, axis=1, keepdims=True)
        high, low = hi_lo(g_seg)
        twice = jnp.concatenate([members, members], axis=0).T.astype(BF)
        sl = slice(n * length, (n + 1) * length)
        g_y = cot_ref[sl, :].astype(F32) + dot(twice, jnp.concatenate([high, low], axis=0))
        gy_ref[sl, :] = g_y
        gmlp_ref[sl, :] = g_y.astype(BF)
    for step in range(4):
        spread.own(step, True)
        spread.relay(step, True)


def pair_head(emb, rel_left, rel_right, row_panel, col_panel, mask, cot_out, seg_ids, scale):
    part, width = emb.shape
    size = mask.shape[0]
    vm = pl.BlockSpec(memory_space=pltpu.VMEM)
    dma = pltpu.SemaphoreType.DMA
    return pl.pallas_call(
        functools.partial(pair_kernel, scale=scale),
        in_specs=[vm] * 8,
        out_specs=[vm] * 5,
        out_shape=[
            jax.ShapeDtypeStruct((size, size), F32), jax.ShapeDtypeStruct(rel_left.shape, BF),
            jax.ShapeDtypeStruct(rel_right.shape, BF), jax.ShapeDtypeStruct(cot_out.shape, F32),
            jax.ShapeDtypeStruct(cot_out.shape, BF),
        ],
        scratch_shapes=Spread.scratch((part, width)) + [dma((1,))],
        compiler_params=pltpu.CompilerParams(
            collective_id=5, has_side_effects=True, vmem_limit_bytes=50 << 20
        ),
        name="pair_head",
    )(emb, rel_left, rel_right, row_panel, col_panel, mask, cot_out, seg_ids)


def norm_back_chunk(g_out, rows, gain):
    average, inverse = norm_stats(rows)
    z = (rows - average) * inverse
    g_z = g_out * gain
    mean_g = jnp.mean(g_z, axis=-1, keepdims=True)
    mean_gz = jnp.mean(g_z * z, axis=-1, keepdims=True)
    return inverse * (g_z - mean_g - z * mean_gz), jnp.sum(g_out * z, axis=0, keepdims=True)


def turn(source, target):
    @pl.loop(0, source.shape[0] // 128)
    def _(c):
        sl = pl.ds(pl.multiple_of(c * 128, 128), 128)
        target[:, sl] = source[sl, :].astype(F32).T.astype(BF)


def put_lines(ref, at, row):
    for j in range(row.shape[1] // 128):
        ref[at + j : at + j + 1, :] = row[:, j * 128 : (j + 1) * 128]


def mlp_back_kernel(*refs, n_ext, units, n_rows, comm, window):
    (slope_ref, wd_ref, wu_ref, gmlp_ref, h2_ref, r1_ref, gy_ref, ctx_ref, wo_ref, gain_ref) = refs[:10]
    at = 10
    arrays = refs[at : at + n_ext]
    at += n_ext
    gup_ref, gr1_ref, gout_ref, gctx_ref, small_ref = refs[at : at + 5]
    at += 5
    carried = refs[at : at + 3]
    at += 3 if comm else 0
    h2t_ref, acc_ref, r1_buf, gy_buf, ctx_buf, ctxt_ref, wo_buf, gatt_ref, in_sem = refs[at : at + 9]
    at += 9
    n_step = pl.num_programs(0)
    step = pl.program_id(0)
    count, feats = acc_ref.shape
    lines = feats // 128
    steps = (small_ref.shape[0] - 16) // lines - 4
    if comm:
        place = Place(n_rows)
        shares = Shares(
            place, units, PIECE, arrays, None, carried, (), (), refs[at : at + 7],
            refs[at + 7 : at + 10], (None, None),
        )
        done = on_the_way(units, 3)

    def inputs():
        pairs = (
            (ctx_ref, ctx_buf), (r1_ref, r1_buf), (gy_ref, gy_buf), (wo_ref, wo_buf),
        )
        return [pltpu.make_async_copy(a, b, in_sem.at[i]) for i, (a, b) in enumerate(pairs)]

    @pl.when(step == 0)
    def _():
        for copy in inputs():
            copy.start()
        if comm:
            meet(place.peers())
            shares.begin(window)
        acc_ref[...] = jnp.zeros_like(acc_ref)
        small_ref[...] = jnp.zeros_like(small_ref)

    def beat(part):
        if comm:
            by_step(step, 0, steps, lambda n: shares.tick(2 * n + part, window, done))

    g_act = dot(gmlp_ref[...], wd_ref[...], NT)
    g_wide = g_act * slope_ref[...].astype(F32)
    g_u = g_wide.astype(BF)
    bias = jnp.sum(g_u.astype(F32), axis=0, keepdims=True)
    acc_ref[...] += dot(g_u, wu_ref[...], NT)
    beat(0)

    @pl.when(step == 0)
    def _():
        turn(h2_ref, h2t_ref)

    gup_ref[...] = dot(h2t_ref[...], g_u).astype(BF)
    for at_step in range(steps):
        @pl.when(step == at_step)
        def _(at_step=at_step):
            put_lines(small_ref, (4 + at_step) * lines, bias)
    beat(1)

    @pl.when(step == n_step - 1)
    def _():
        for copy in inputs():
            copy.wait()
        chunk = 256

        def back(c, sums):
            sl = pl.ds(pl.multiple_of(c * chunk, chunk), chunk)
            g_out = acc_ref[sl, :]
            g_in, part = norm_back_chunk(g_out, r1_buf[sl, :], gain_ref[...].reshape(1, -1))
            g_r1 = gy_buf[sl, :] + g_in
            gr1_ref[sl, :] = g_r1
            gatt_ref[sl, :] = g_r1.astype(BF)
            return sums[0] + part, sums[1] + jnp.sum(g_out, axis=0, keepdims=True)

        nothing = jnp.zeros((1, feats), F32)
        gain_sum, bias_sum = lax.fori_loop(0, count // chunk, back, (nothing, nothing))
        put_lines(small_ref, 2 * lines, gain_sum)
        put_lines(small_ref, 3 * lines, bias_sum)
        if comm:
            shares.tick(2 * steps, window, done)
        turn(ctx_buf, ctxt_ref)
        gctx_ref[...] = dot(gatt_ref[...], wo_buf[...], NT).astype(BF)
        if comm:
            shares.tick(2 * steps + 1, window, done)
        gout_ref[...] = dot(ctxt_ref[...], gatt_ref[...]).astype(BF)
        if comm:
            for t in range(2 * steps + 2, shares.ticks()):
                shares.tick(t, window, done)
            shares.wait_sends()


def early_units():
    return (
        Unit(0, 0, 0, False, {0: 1, 1: 4, 2: 7}, leave=(2, 0)),
        Unit(1, 0, 0, True, {0: 1, 1: 4, 2: 7}, leave=(2, 1)),
        Unit(2, 0, 0, False, {0: 2, 1: 6}, leave=(1, 0)),
        Unit(2, 1, 0, True, {0: 2, 1: 6}, leave=(0, 0)),
        Unit(2, 2, 0, False, {0: 5, 1: 9}, leave=(1, 1)),
        Unit(2, 3, 0, True, {0: 5, 1: 9}, leave=(0, 1)),
    )


def mlp_backward(
    slope, w_down, w_up, g_mlp, h2, r1, g_y, ctx, w_out, gain, small_rows, left, right, down, n_rows, comm
):
    count, feats = g_mlp.shape
    hidden = slope.shape[1]
    steps = hidden // feats
    vm = pl.BlockSpec(memory_space=pltpu.VMEM)
    any_ref = pl.BlockSpec(memory_space=pl.ANY)
    views = [view(g, n_rows) for g in (left, right, down)] if comm else []
    units = early_units()
    extra = []
    if comm:
        extra = [
            jax.ShapeDtypeStruct((2, 4, 2, 48, PIECE), BF),
            jax.ShapeDtypeStruct((2, n_rows, 4, 48, PIECE), BF),
            jax.ShapeDtypeStruct((2, 4, 48, PIECE), BF),
        ]
    scratch = [
        pltpu.VMEM((feats, count), BF), pltpu.VMEM((count, feats), F32),
        pltpu.VMEM((count, feats), F32), pltpu.VMEM((count, feats), F32), pltpu.VMEM((count, feats), BF),
        pltpu.VMEM((feats, count), BF), pltpu.VMEM((feats, feats), BF), pltpu.VMEM((count, feats), BF),
        pltpu.SemaphoreType.DMA((4,)),
    ]
    params = dict(vmem_limit_bytes=63 << 20, dimension_semantics=("arbitrary",))
    if comm:
        scratch += Shares.scratch(units, PIECE, n_rows)
        params.update(collective_id=3, has_side_effects=True)
    return pl.pallas_call(
        functools.partial(
            mlp_back_kernel, n_ext=len(views), units=units, n_rows=n_rows, comm=comm, window=3,
        ),
        grid=(steps,),
        in_specs=[
            pl.BlockSpec((count, feats), lambda f: (0, f)),
            pl.BlockSpec((feats, feats), lambda f: (f, 0)),
            pl.BlockSpec((feats, feats), lambda f: (0, f)),
            vm, vm, any_ref, any_ref, any_ref, any_ref, vm,
        ] + [any_ref] * len(views),
        out_specs=[pl.BlockSpec((feats, feats), lambda f: (0, f)), vm, vm, vm, vm] + [vm] * len(extra),
        out_shape=[
            jax.ShapeDtypeStruct((feats, hidden), BF), jax.ShapeDtypeStruct((count, feats), F32),
            jax.ShapeDtypeStruct((feats, feats), BF), jax.ShapeDtypeStruct((count, feats), BF),
            jax.ShapeDtypeStruct((small_rows, 128), F32),
        ] + extra,
        scratch_shapes=scratch,
        compiler_params=pltpu.CompilerParams(**params),
        name="mlp_backward",
    )(slope, w_down, w_up, g_mlp, h2, r1, g_y, ctx, w_out, gain, *views)


def deliver_kernel(gx_ref, small_ref, *refs, parts, heads):
    n_in = sum(parts)
    ins, outs = refs[:n_in], refs[n_in:]
    outs[0][...] = gx_ref[...]

    @pl.when(pl.program_id(0) == 0)
    def _():
        at = 0
        for k, n in enumerate(parts):
            out = outs[1 + k]
            row = 0
            for ref in ins[at : at + n]:
                rows, x = ref.shape
                per = x // 128
                for j in range(per):
                    out[pl.ds(row + j, rows, stride=per), :] = ref[:, j * 128 : (j + 1) * 128]
                row += rows * per
            at += n
        line = 0
        for out in outs[1 + len(parts) :]:
            if len(out.shape) == 1:
                for j in range(out.shape[0] // 128):
                    out[j * 128 : (j + 1) * 128] = small_ref[line]
                    line += 1
            else:
                out[...] = small_ref[line : line + out.shape[0], :]


def deliver(g_tokens, small, shares, features, hidden, heads):
    count = g_tokens.shape[0]
    flat = [p for group in shares for p in group]
    vm = pl.BlockSpec(memory_space=pltpu.VMEM)
    block = count
    sizes = [sum(p.size for p in group) for group in shares]
    results = pl.pallas_call(
        functools.partial(deliver_kernel, parts=tuple(len(group) for group in shares), heads=heads),
        grid=(1,),
        in_specs=[pl.BlockSpec((block, features), lambda i: (i, 0)), vm] + [vm] * len(flat),
        out_specs=[pl.BlockSpec((block, features), lambda i: (i, 0))] + [vm] * (len(shares) + 6),
        out_shape=[jax.ShapeDtypeStruct(g_tokens.shape, F32)]
        + [jax.ShapeDtypeStruct((size // 128, 128), F32) for size in sizes]
        + [jax.ShapeDtypeStruct((features,), F32)] * 4
        + [jax.ShapeDtypeStruct((hidden,), F32), jax.ShapeDtypeStruct((heads, 128), F32)],
        name="deliver",
    )(g_tokens, small, *flat)
    return (
        results[0], [r.reshape(-1) for r in results[1 : 1 + len(shares)]], results[1 + len(shares) :]
    )


def back_kernel(*refs, n_ext, units, tail, spans, n_rows, comm, window):
    (q_ref, k_ref, v_ref, e_ref, linv_ref, ctx_ref, gctx_ref, boxr_ref, boxc_ref, w_ref, h1_ref,
     x_ref, gr1_ref, gain_ref, small_ref) = refs[:15]
    at = 15
    arrays = refs[at : at + n_ext]
    at += n_ext
    carried = refs[at : at + 3] if comm else ()
    at += len(carried)
    n_out = len(spans)
    gx_ref = refs[at]
    small_out = refs[at + 1]
    at += 2
    if comm:
        outs = refs[at : at + n_out]
        at += n_out
    else:
        grad_ref = refs[at]
        at += 1
    (oha_ref, ohbt_ref, cx_ref, cy_ref, g_ref, gcx_ref, gcy_ref, lt_ref, gt_ref, gall_ref, h1t_ref,
     hist_ref, h1_buf, x_buf, gr1_buf, w_buf, pack_ref, in_sem) = refs[at : at + 18]
    at += 18
    length = q_ref.shape[0]
    half, quarter = 64, 32
    pairs, seqs = pl.num_programs(0), pl.num_programs(1)
    hp = pl.program_id(0)
    s_id = pl.program_id(1)
    n_seq = cx_ref.shape[0]
    n_pair = hist_ref.shape[0] // 2
    lane = lax.broadcasted_iota(jnp.int32, (1, 128), 1)
    low = lane < 64
    if comm:
        place = Place(n_rows)
        staging = refs[at]
        fins = refs[at + 1 : at + n_out + 1]
        at += n_out + 1
        got = refs[at : at + n_out]
        at += n_out
        known = (None,) * 3 + tuple(arrays) + (None,)
        ends = refs[at : at + 2]
        at += 2
        shares = Shares(
            place, units, PIECE, known, staging, carried, fins, got, refs[at : at + 7],
            refs[at + 7 : at + 10], ends,
        )
        at += 10
        thirds = Shares(
            place, tail, PIECE // 3, known, staging, carried, fins, got, refs[at : at + 7],
            refs[at + 7 : at + 10], ends,
        )
        at += 10
        done = on_the_way(units + tail, n_out)
        total = Total(place, pack_ref, small_out, refs[at : at + 5], refs[at + 5 : at + 7])

    def inputs():
        return (
            pltpu.make_async_copy(h1_ref, h1_buf, in_sem.at[0]),
            pltpu.make_async_copy(x_ref, x_buf, in_sem.at[1]),
            pltpu.make_async_copy(gr1_ref, gr1_buf, in_sem.at[2]),
            pltpu.make_async_copy(w_ref, w_buf, in_sem.at[3]),
        )

    @pl.when((hp == 0) & (s_id == 0))
    def _():
        for copy in inputs():
            copy.start()
        hist_ref[...] = jnp.zeros_like(hist_ref)
        if comm:
            meet(place.peers())
            shares.begin(window)

    @pl.when(hp == 0)
    def _():
        bc = boxc_ref[...]
        ax, _ = key_side(bc[:, 0:1], bc[:, 2:3], half)
        ay, _ = key_side(bc[:, 1:2], bc[:, 3:4], half)
        _, fbx = query_side(bc[:, 0:1], bc[:, 2:3], half)
        _, fby = query_side(bc[:, 1:2], bc[:, 3:4], half)
        spot = (lane % quarter).astype(F32)
        is_x = (lane % half) < quarter
        oha = jnp.where(jnp.where(is_x, ax, ay) == spot, jnp.where(low, 1.0, 0.0), 0.0)
        oha_ref[s_id] = oha.astype(BF)
        br = boxr_ref[...]
        _, gax = key_side(br[0:1], br[2:3], half)
        _, gay = key_side(br[1:2], br[3:4], half)
        rbx, _ = query_side(br[0:1], br[2:3], half)
        rby, _ = query_side(br[1:2], br[3:4], half)
        row = lax.broadcasted_iota(jnp.int32, (half, length), 0)
        rspot = (row % quarter).astype(F32)
        ohbt_ref[s_id] = jnp.where(jnp.where(row < quarter, rbx, rby) == rspot, 1.0, 0.0).astype(BF)
        cx_ref[s_id] = jnp.where(gax + fbx >= SPAN, 1.0, 0.0).astype(BF)
        cy_ref[s_id] = jnp.where(gay + fby >= SPAN, 1.0, 0.0).astype(BF)

    @pl.when((hp == 0) & (s_id == n_seq - 1))
    def _():
        inputs()[0].wait()
        turn(h1_buf, h1t_ref)

    k = k_ref[...]
    v = v_ref[...]
    lt_ref[...] = q_ref[...].astype(F32).T.astype(BF)
    gc = gctx_ref[...].astype(F32) * linv_ref[...]
    gcb = gc.astype(BF)
    gt_ref[...] = gcb.astype(F32).T.astype(BF)
    prod = gc * ctx_ref[...].astype(F32)
    ohbt = ohbt_ref[s_id]
    kts = []
    vts = []
    rows = 256
    n_step = n_pair * n_seq
    step = hp * n_seq + s_id
    for a in range(2):
        if comm and a == 1:
            by_step(step, 0, n_step, lambda n: shares.tick(2 * n, window, done))
        mine = low if a == 0 else jnp.logical_not(low)
        other = 64 - 64 * a
        d = jnp.sum(jnp.where(mine, prod, 0.0), axis=1, keepdims=True)
        dhi = d.astype(BF).astype(F32)
        extra = jnp.where(lane == other, dhi, jnp.where(lane == other + 1, d - dhi, 0.0))
        lhs = jnp.where(mine, gcb.astype(F32), extra).astype(BF)
        minus = jnp.where((lane == other) | (lane == other + 1), -1.0, 0.0).astype(BF)
        rhs = jnp.where(mine, v, minus)
        for c in range(length // rows):
            sl = slice(c * rows, (c + 1) * rows)
            gp = dot(lhs[sl], rhs, NT)
            g = (gp * e_ref[a, sl, :].astype(F32)).astype(BF)
            g_ref[a, sl, :] = g
            gcx_ref[a, sl, :] = g * cx_ref[s_id, sl, :]
            gcy_ref[a, sl, :] = g * cy_ref[s_id, sl, :]
        left = jnp.concatenate([lt_ref[64 * a : 64 * a + 64, :], ohbt], axis=0)
        r0 = dot(left, g_ref[a])
        rx = dot(ohbt[:quarter], gcx_ref[a])
        ry = dot(ohbt[quarter:], gcy_ref[a])
        vts.append(dot(gt_ref[64 * a : 64 * a + 64, :], e_ref[a]))
        kts.append(r0[:64])
        w = jnp.concatenate([r0[64:], rx, ry], axis=0)
        whi, wlo = hi_lo(w)
        red = dot(jnp.concatenate([whi, wlo], axis=0), oha_ref[s_id])
        hist_ref[2 * hp + a] += red[:128] + red[128:]
    zero = jnp.zeros_like(k)
    gq = dot(g_ref[0], jnp.where(low, k, zero)) + dot(g_ref[1], jnp.where(low, zero, k))
    own_rows = pl.ds(pl.multiple_of(s_id * length, length), length)
    feats = h1_buf.shape[1]
    parts = [pl.ds(pl.multiple_of(p * feats + hp * 128, 128), 128) for p in range(3)]
    gall_ref[own_rows, parts[0]] = (gq * 0.125).astype(BF)
    gall_ref[own_rows, parts[1]] = (jnp.concatenate(kts, axis=0) * 0.125).T.astype(BF)
    gall_ref[own_rows, parts[2]] = jnp.concatenate(vts, axis=0).T.astype(BF)

    @pl.when(s_id == n_seq - 1)
    def _():
        g_pair = jnp.concatenate([gall_ref[:, part] for part in parts], axis=1)
        piece = dot(h1t_ref[...], g_pair).astype(BF)
        if comm:
            staging[lax.div(hp, 2), lax.rem(hp, 2)] = piece.reshape(staging.shape[2:])
        else:
            grad_ref[0] = piece[:, :128]
            grad_ref[1] = piece[:, 128:256]
            grad_ref[2] = piece[:, 256:]

    if comm:
        def beat_of(at_step):
            for part in (shares, thirds):
                for i, unit in enumerate(part.units):
                    source = unit.source or ("", 0)
                    if source[0] == "own" and (2 * source[1] + 2) * n_seq - 1 == at_step:
                        part.start(i, 0)
            if at_step < n_step - 1:
                shares.tick(2 * at_step + 1, window, done)

        by_step(step, 0, n_step, beat_of)

    @pl.when((hp == n_pair - 1) & (s_id == n_seq - 1))
    def _():
        for copy in inputs()[1:]:
            copy.wait()
        gain = gain_ref[...].reshape(1, -1)
        count = x_buf.shape[0]
        chunk = 256
        beat = 2 * n_step - 1
        gain_sum = jnp.zeros((1, feats), F32)
        bias_sum = jnp.zeros((1, feats), F32)
        pack_ref[...] = small_ref[...]
        base = pack_ref.shape[0] - 16
        for h in range(2 * n_pair):
            w = hist_ref[h]
            line = jnp.zeros((1, 128), F32)
            for axis in range(2):
                plain = w[axis * quarter : (axis + 1) * quarter]
                carry = w[half + axis * quarter : half + (axis + 1) * quarter]
                keep = (lane >= axis * quarter) & (lane < (axis + 1) * quarter)
                stay = jnp.where(keep, plain - carry, 0.0)
                move = jnp.where(keep, carry, 0.0)
                shift = axis * (half - quarter)
                stay = pltpu.roll(stay, shift, 1, stride=1, stride_axis=0)
                move = pltpu.roll(move, shift + 1, 1, stride=1, stride_axis=0)
                line = line + jnp.sum(stay + move, axis=0, keepdims=True)
            pack_ref[base + h : base + h + 1, :] = line
        for c in range(count // chunk):
            sl = slice(c * chunk, (c + 1) * chunk)
            g_out = dot(gall_ref[sl, :], w_buf[...], NT)
            g_in, part = norm_back_chunk(g_out, x_buf[sl, :].astype(F32), gain)
            gx_ref[sl, :] = gr1_buf[sl, :] + g_in
            gain_sum = gain_sum + part
            bias_sum = bias_sum + jnp.sum(g_out, axis=0, keepdims=True)
            if comm:
                for t in range(beat, beat + 2):
                    shares.tick(t, window, done)
                    thirds.tick(t, window, done)
                beat += 2
        lines = feats // 128
        put_lines(pack_ref, 0, gain_sum)
        put_lines(pack_ref, lines, bias_sum)
        if comm:
            total.start(0)
            stage = 0
            for t in range(beat, max(shares.ticks(), thirds.ticks())):
                shares.tick(t, window, done)
                thirds.tick(t, window, done)
                if t in SUM_BEATS:
                    total.finish(stage)
                    if stage < 3:
                        total.start(stage + 1)
                    stage += 1
            for stage in range(stage, 4):
                total.finish(stage)
                if stage < 3:
                    total.start(stage + 1)
            for n, out in enumerate(outs):
                shares.deliver(n, out, spans[n])
            thirds.wait_sends()
            total.wait_sends()
            shares.wait_sends()
        else:
            small_out[...] = pack_ref[...]


SUM_BEATS = (34, 38, 43, 47)


def late_units():
    rest = (
        {'in': 2, 3: 6},
        {'in': 0, 3: 4},
        {'in': 0, 2: 4, 3: 8},
        {'in': 0, 2: 4, 3: 10},
        {'in': 2, 2: 6, 3: 12},
        {'in': 2, 2: 6, 3: 14},
    )
    units = [
        Unit(
            unit.array, unit.part, 0, unit.rows_first, beats, source=("mid",) + unit.leave
        )
        for unit, beats in zip(early_units(), rest)
    ]
    units += [
        Unit(4, 0, 0, True, {0: 4, 1: 10, 2: 16, 3: 20}),
        Unit(4, 0, 1, False, {0: 4, 1: 10, 2: 16, 3: 22}),
        Unit(3, 0, 0, True, {0: 8, 1: 14, 2: 22, 3: 25}),
        Unit(4, 0, 2, False, {0: 8, 1: 14, 2: 18, 3: 23}),
        Unit(4, 0, 3, True, {0: 16, 1: 22, 2: 25, 3: 31}),
        Unit(5, 0, 0, False, {0: 11, 1: 20, 2: 27, 3: 36}, source=("own", 0, 0)),
        Unit(5, 0, 1, True, {0: 19, 1: 25, 2: 32, 3: 41}, source=("own", 1, 0)),
    ]
    tail = (
        Unit(5, 0, 6, False, {0: 26, 1: 35, 2: 39, 3: 44}, source=("own", 2, 0 * PIECE // 3)),
        Unit(5, 0, 7, False, {0: 27, 1: 37, 2: 42, 3: 46}, source=("own", 2, 1 * PIECE // 3)),
        Unit(5, 0, 8, True, {0: 27, 1: 33, 2: 40, 3: 45}, source=("own", 2, 2 * PIECE // 3)),
    )
    return tuple(units), tail


def attend_and_project_backward(
    qkv, e, linv, ctx, gctx, boxes_r, boxes_c, weight, h1, tokens, g_r1, gain, small, arrays,
    carried, n_rows, comm
):
    count, width = qkv.shape
    feats = width // 3
    heads, seqs, length, _ = e.shape
    pairs = heads // 2
    rows_of = lambda off: pl.BlockSpec((length, 128), lambda h, s: (s, off + h))
    any_ref = pl.BlockSpec(memory_space=pl.ANY)
    vm = pl.BlockSpec(memory_space=pltpu.VMEM)
    views = [view(g, n_rows) for g in arrays] if comm else []
    n_ext = len(views)
    units, tail = late_units() if comm else ((), ())
    out_shape = [jax.ShapeDtypeStruct((count, feats), F32), jax.ShapeDtypeStruct(small.shape, F32)]
    out_specs = [vm, vm]
    spans = []
    scratch = [
        pltpu.VMEM((seqs, length, 128), BF), pltpu.VMEM((seqs, 64, length), BF),
        pltpu.VMEM((seqs, length, length), BF), pltpu.VMEM((seqs, length, length), BF),
        pltpu.VMEM((2, length, length), BF), pltpu.VMEM((2, length, length), BF),
        pltpu.VMEM((2, length, length), BF), pltpu.VMEM((128, length), BF),
        pltpu.VMEM((128, length), BF), pltpu.VMEM((count, width), BF), pltpu.VMEM((feats, count), BF),
        pltpu.VMEM((heads, 128, 128), F32), pltpu.VMEM((count, feats), BF),
        pltpu.VMEM((count, feats), BF), pltpu.VMEM((count, feats), F32), pltpu.VMEM((feats, width), BF),
        pltpu.VMEM(small.shape, F32), pltpu.SemaphoreType.DMA((4,)),
    ]
    params = dict(vmem_limit_bytes=63 << 20, dimension_semantics=("arbitrary", "arbitrary"))
    if comm:
        hidden = views[-1].shape[5]
        sizes = [(24, feats), (24, feats), (24 * hidden // feats, feats), (24, feats), (24, hidden), (24, width)]
        for rows, x in sizes[:-1]:
            spans.append([(j * 2 * PIECE, PIECE, PIECE) for j in range(x // (2 * PIECE))])
        spans.append(
            [(p * feats + t * 256, 128, 128) for t in range(pairs // 2) for p in range(3)]
        )
        out_shape += [jax.ShapeDtypeStruct(size, F32) for size in sizes]
        out_specs += [vm] * len(sizes)
        tbufs, tsems = Total.scratch(small.shape, n_rows)
        scratch += [pltpu.VMEM((pairs // 2, 2, n_rows, 4, 2, 48, PIECE), BF)]
        scratch += Shares.result_scratch(sizes) + Shares.scratch(units, PIECE, n_rows)
        scratch += Shares.scratch(tail, PIECE // 3, n_rows) + tbufs + tsems
        params.update(collective_id=2, has_side_effects=True)
    else:
        out_shape.append(jax.ShapeDtypeStruct((3, feats, feats), BF))
        out_specs.append(pl.BlockSpec((3, feats, 128), lambda h, s: (0, 0, h)))
    results = pl.pallas_call(
        functools.partial(
            back_kernel, n_ext=n_ext, units=units, tail=tail, spans=spans, n_rows=n_rows, comm=comm, window=3,
        ),
        grid=(pairs, seqs),
        in_specs=[
            rows_of(0), rows_of(pairs), rows_of(2 * pairs),
            pl.BlockSpec((2, None, length, length), lambda h, s: (h, s, 0, 0)),
            rows_of(0), rows_of(0), rows_of(0),
            pl.BlockSpec((4, length), lambda h, s: (0, s)),
            pl.BlockSpec((length, 128), lambda h, s: (s, 0)),
            any_ref, any_ref, any_ref, any_ref, vm, vm,
        ] + [any_ref] * (n_ext + len(carried)),
        out_specs=out_specs,
        out_shape=out_shape,
        scratch_shapes=scratch,
        compiler_params=pltpu.CompilerParams(**params),
        name="attend_backward",
    )(
        qkv, qkv, qkv, e, linv, ctx, gctx, boxes_r, boxes_c, weight, h1, tokens, g_r1,
        gain, small, *views, *carried,
    )
    return results


EPSILON = 1e-05


def norm_stats(rows):
    average = jnp.mean(rows, axis=-1, keepdims=True)
    centred = rows - average
    variance = jnp.mean(centred * centred, axis=-1, keepdims=True)
    return average, lax.rsqrt(variance + EPSILON)


def gelu_pair(u):
    bell = jnp.exp2(u * u * (-0.5 * LOG2E))
    below = 0.5 + 0.5 * lax.erf(u * math.sqrt(0.5))
    return u * below, below + u * bell * (1.0 / math.sqrt(2.0 * math.pi))


def body(
    tokens, boxes, page_ids, seg_ids, pair_mask, ln1_gain, ln1_bias, query_key_value_weight,
    attention_output_weight, ln2_gain, ln2_bias, up_projection_weight, up_projection_bias,
    down_projection_weight, box_table, rel_left, rel_right, cot_out, cot_logits,
):
    features = tokens.shape[1]
    h1, qkv, boxes_c = project_forward(
        tokens, ln1_gain, ln1_bias, query_key_value_weight, boxes, page_ids
    )
    pair_scale = 1.0 / math.sqrt(rel_left.shape[1])
    ctx, e, linv, row_panel, col_panel = attend_forward(
        qkv, boxes, boxes_c, page_ids.shape[0], box_table, pair_mask[0], cot_logits[0], pair_scale
    )
    r1, h2, act, slope, layer_out, embedded = mlp_forward(
        ctx, attention_output_weight, tokens, ln2_gain, ln2_bias, up_projection_weight,
        up_projection_bias, down_projection_weight, seg_ids, SLOTS,
    )
    pair_logits, grad_rel_left, grad_rel_right, g_y, g_mlp = pair_head(
        embedded, rel_left, rel_right, row_panel, col_panel, pair_mask[0], cot_out, seg_ids, pair_scale
    )
    grad_down = dot(act, g_mlp, (((0,), (0,)), ((), ()))).astype(BF)
    n_rows = lax.axis_size("rows")
    comm = n_rows * 8 * 48 <= features
    heads = box_table.shape[0]
    hidden = slope.shape[1]
    small_rows = (4 * features + hidden) // 128 + 16
    grad_up, g_r1, grad_out, g_ctx, small, *early = mlp_backward(
        slope, down_projection_weight, up_projection_weight, g_mlp, h2, r1, g_y, ctx,
        attention_output_weight, ln2_gain, small_rows, grad_rel_left, grad_rel_right, grad_down,
        n_rows, comm,
    )
    g_tokens, small, *late = attend_and_project_backward(
        qkv, e, linv, ctx, g_ctx, boxes, boxes_c, query_key_value_weight, h1, tokens, g_r1, ln1_gain,
        small, (grad_out, grad_up), early, n_rows, comm,
    )
    if comm:
        left, right, down, out, up, qkv_part = late
        shares = [[left], [right], [out], [down], [up], [qkv_part]]
    else:
        grad_qkv = jnp.concatenate([late[0][0], late[0][1], late[0][2]], axis=1)
        flats = [
            lax.psum_scatter(g, AXES, scatter_dimension=0, tiled=True).astype(F32).reshape(-1)
            for g in (grad_rel_left, grad_rel_right, grad_out, grad_down, grad_up, grad_qkv)
        ]
        shares = [[flat.reshape(-1, 128)] for flat in flats]
        small = lax.psum(small, AXES)
    grad_tokens, flats, vectors = deliver(g_tokens, small, shares, features, hidden, heads)
    left_share, right_share, out_share, down_share, up_share, qkv_share = flats
    return (
        layer_out, pair_logits[None], grad_tokens, vectors[0], vectors[1], qkv_share, out_share,
        vectors[2], vectors[3], up_share, vectors[4], down_share, vectors[5], left_share, right_share,
    )


def solution(mesh):
    whole = P(AXES, None)
    tile = P("rows", "gr", "gc")
    flat = P(AXES)
    one = P()
    in_specs = (
        whole, P(None, AXES), whole, whole, tile, one, one, one, one, one, one, one, one, one, one,
        one, one, whole, tile,
    )
    out_specs = (
        whole, tile, whole, one, one, flat, flat, one, one, flat, one, flat, one, flat, flat,
    )
    return jax.shard_map(body, mesh=mesh, in_specs=in_specs, out_specs=out_specs, check_vma=False)
```
